32 devices in a mesh: rep: 4 (over z), fsdp: 8 (over y, x, core).
Axes of the slice: x: 2, y: 2, z: 4, core: 2. Of those that a mesh axis runs over, the one named last changes fastest.
Arguments:
- hidden_in: bfloat16 [4, 1024, 2048], P('rep', 'fsdp'), may hold values from -6 to 6
- segments: int32 [4, 1024], P('rep', 'fsdp'), may hold values from 0 to 7, never falling along the last dimension, each value on 1 to 768 neighbouring positions
- routes: int32 [4, 1024, 8], P('rep', 'fsdp'), may hold values from 0 to 15, all different within a row; in each aligned block of 128 rows (0 to 127, 128 to 255, ..., all dimensions but the last counted through in order) at most 96 rows name the same one
- doc_sets: int32 [4, 8], P('rep'), may hold values from 0 to 7, each once within a row
- cotangent: bfloat16 [4, 1024, 2048], P('rep', 'fsdp'), may hold values from -6 to 6
- w_qkv: bfloat16 [3, 2048, 2048], P(None, 'fsdp'), may hold values from -0.125 to 0.125
- w_out: bfloat16 [2048, 2048], P('fsdp'), may hold values from -0.5 to 0.5
- gain_attn: bfloat16 [2048], P('fsdp'), may hold values from 0.25 to 1.75
- gain_moe: bfloat16 [2048], P('fsdp'), may hold values from 0.25 to 1.75
- router: bfloat16 [2048, 16], P('fsdp'), may hold values from -0.0625 to 0.0625
- w_gate: bfloat16 [16, 2048, 1024], P('fsdp'), may hold values from -0.125 to 0.125
- w_up: bfloat16 [16, 2048, 1024], P('fsdp'), may hold values from -0.125 to 0.125
- w_down: bfloat16 [16, 1024, 2048], P('fsdp'), may hold values from -0.75 to 0.75
- a_attn: bfloat16 [4, 2048, 128], P(None, 'fsdp'), may hold values from -0.125 to 0.125
- b_attn: bfloat16 [4, 2048, 128], P(None, 'fsdp'), may hold values from -0.75 to 0.75
- exp_a_in: bfloat16 [16, 2, 2048, 128], P('fsdp'), may hold values from -0.125 to 0.125
- exp_b_in: bfloat16 [16, 2, 128, 1024], P('fsdp'), may hold values from -0.75 to 0.75
- exp_a_down: bfloat16 [16, 1024, 128], P('fsdp'), may hold values from -0.1875 to 0.1875
- exp_b_down: bfloat16 [16, 128, 2048], P('fsdp'), may hold values from -0.75 to 0.75
Outputs:
- layer_out: bfloat16 [4, 1024, 2048], P('rep', 'fsdp')
- grad_in: bfloat16 [4, 1024, 2048], P('rep', 'fsdp')
- grad_a_attn: float32 [4, 2048, 128], P(None, 'fsdp')
- grad_b_attn: float32 [4, 2048, 128], P(None, 'fsdp')
- grad_exp_a_in: float32 [16, 2, 2048, 128], P('fsdp')
- grad_exp_b_in: float32 [16, 2, 128, 1024], P('fsdp')
- grad_exp_a_down: float32 [16, 1024, 128], P('fsdp')
- grad_exp_b_down: float32 [16, 128, 2048], P('fsdp')
The draws below stay inside these ranges and needn't reach their ends.
Inputs may be any that keep to these rules, and one draw needn't show every extreme that they name: `segments`: a sequence's document numbers never fall; each of the 8 documents is present and at most 768 tokens long, and one of them is exactly that long. `routes`: each token names 8 different experts; among the tokens of one device at most 96 name the same expert, and in every draw some expert is named by exactly 96 tokens of one device. `doc_sets`: the documents of a sequence take the 8 adapter sets in some order.
All inputs are finite; a program needn't handle non-finite values.
Results may differ from the reference program's by a relative error of at most 0.035.
Values may be sent and summed in bfloat16 or wider, within the bound.
No kernel may reach another device: no remote copies, remote signals or barrier semaphores. Data moves between devices by JAX's collectives and lax.ppermute only.
A program may use at most 384 MiB of HBM per device.

```python
import math
import jax
import jax.numpy as jnp
import numpy as np
from jax import lax

D = 2048
H = 16
HD = 128
F = 1024
TOP = 8
R = 16
SETS = 8
TOK_DEV = 128
EXPERTS = 16
SEQ = 1024
SEQS = 4
SR = 128
CAP = 96
N_FSDP = 8


def steps_of(own_key, extent, pieces, low, top_value):
    level = 1.0
    for dim, blocks in pieces:
        draws = jax.random.uniform(jax.random.fold_in(jax.random.fold_in(own_key, 6), dim), (blocks,), jnp.float32, low / len(pieces), top_value / len(pieces))
        level = level * jnp.repeat(jnp.exp(draws), extent[dim] // blocks).reshape((-1,) + (1,) * (len(extent) - 1 - dim))
    return level


def split_up(amount, total, most, lean):
    weights = [(1 << 20) // math.isqrt(rank ** lean) + 1 for rank in range(2, amount + 1)]
    surplus, counts = total - most - (amount - 1), [1] * (amount - 1)
    while surplus > 0:
        free = [i for i in range(amount - 1) if counts[i] < most]
        whole, remaining = sum([weights[i] for i in free]), surplus
        for i in free:
            more = min(most - counts[i], max(1, remaining * weights[i] // whole), surplus)
            counts[i] = counts[i] + more
            surplus = surplus - more
    return np.array([most] + counts)


def uneven(stream_key, number_of, total, most, lean):
    if number_of == 2:
        one = jax.random.randint(stream_key, (), max(1, total - most), min(most, total - 1) + 1)
        return jnp.stack([one, total - one])
    sizes = jnp.asarray(split_up(number_of, total, most, lean), jnp.int32)
    pairs = (number_of - 1) // 2
    giver, receiver = sizes[1:1 + 2 * pairs:2], sizes[2:2 + 2 * pairs:2]
    slack = jnp.minimum(giver - 1, most - receiver)
    shifted = jax.random.randint(jax.random.fold_in(stream_key, 1), (pairs,), 0, 1 << 20) % (slack + 1)
    sizes = sizes.at[1:1 + 2 * pairs:2].set(giver - shifted).at[2:2 + 2 * pairs:2].set(receiver + shifted)
    return sizes[jax.random.permutation(jax.random.fold_in(stream_key, 2), number_of)]


def shared_out(key, own, number, rows, count, top, limit, lean):
    order = jax.random.permutation(key, count)
    heavy_load, usual = portions_of(count, rows * top, limit, lean, True), portions_of(count, rows * top, limit, lean, False)
    places = jnp.arange(count)

    def named(tallies, offset_by):
        used = int((tallies > 0).sum())
        fixed = max(1, used // 4)
        passed = fixed + (places - fixed + offset_by * (used - fixed)) % max(1, count - fixed)
        return jnp.zeros((count,), jnp.int32).at[order[jnp.where(places < fixed, places, passed)]].set(jnp.asarray(tallies, jnp.int32))

    tallies = jnp.where(number % 4 == 0, named(heavy_load, number // 4), named(usual, number - number // 4 - 1))
    mixed = jax.random.permutation(jax.random.fold_in(own, 3), count)
    giver, sink = mixed[0:count // 2 * 2:2], mixed[1:count // 2 * 2:2]
    margin = jnp.minimum(tallies[giver] - 1, limit - tallies[sink]) // 2
    margin = jnp.where((giver == order[0]) | (sink == order[0]) | (tallies[sink] == 0), 0, jnp.maximum(margin, 0))
    passed = jax.random.randint(jax.random.fold_in(own, 4), (count // 2,), 0, 1 << 20) % (margin + 1)
    tallies = tallies.at[giver].add(-passed).at[sink].add(passed)
    items = jnp.searchsorted(jnp.cumsum(tallies), jnp.arange(rows * top), side="right").astype(jnp.int32)
    listing = items.reshape(top, rows).T
    listing = listing[jax.random.permutation(jax.random.fold_in(own, 1), rows)]
    offset_by = jax.random.randint(jax.random.fold_in(own, 2), (rows, 1), 0, top)
    return jnp.take_along_axis(listing, (jnp.arange(top)[None, :] + offset_by) % top, axis=1)


def portions_of(count, total, limit, slope, full):
    weights = [(1 << 20) // math.isqrt(rank ** slope) + 1 for rank in range(1, count + 1)]
    largest = limit if full else min(limit, max(-(-total // count), total * weights[0] // sum(weights)))
    least = 1 if total - largest >= count - 1 else 0
    holding, spare = [largest] + [least] * (count - 1), total - largest - least * (count - 1)
    while spare > 0:
        movable = [i for i in range(1, count) if holding[i] < largest] or [i for i in range(1, count) if holding[i] < limit]
        pool, remaining = sum([weights[i] for i in movable]), spare
        for i in movable:
            more = min(limit - holding[i], max(1, remaining * weights[i] // pool), spare)
            holding[i] = holding[i] + more
            spare = spare - more
    return np.array(holding)


def centred(stream_key, extent, scale, limit, cuts=(), kind=jnp.bfloat16):
    entries = jax.random.normal(stream_key, extent, jnp.float32) * scale
    if len(cuts) > 0:
        entries = steps_of(stream_key, extent, cuts, -0.22, 0.18) * entries
    return jnp.clip(entries, min=-limit, max=limit).astype(kind)


def setup_inputs(seed: int = 0) -> dict:
    key_of = jax.random.split(jax.random.key(seed), 20)
    hidden_in = centred(key_of[0], (SEQS, SEQ, D), 1.0, 6.0, ((0, 4), (1, 8)))
    segments = jax.vmap(lambda own: jnp.searchsorted(jnp.cumsum(uneven(own, SETS, SEQ, 3 * SEQ // 4, 2)), jnp.arange(SEQ), side="right"))(jax.random.split(key_of[1], SEQS)).reshape((SEQS, SEQ)).astype(jnp.int32)
    routes_keys = jax.random.split(jax.random.fold_in(key_of[2], 1), SEQS * SEQ // TOK_DEV)
    routes_turns = jax.random.permutation(jax.random.fold_in(key_of[2], 3), SEQS * SEQ // TOK_DEV)
    routes = jax.vmap(lambda own, number: shared_out(jax.random.fold_in(key_of[2], 2), own, number, TOK_DEV, EXPERTS, TOP, CAP, 1))(routes_keys, routes_turns).reshape((SEQS, SEQ, TOP))
    doc_sets = jax.vmap(lambda own: jax.random.permutation(own, SETS))(jax.random.split(key_of[3], SEQS)).reshape((SEQS, SETS)).astype(jnp.int32)
    cotangent = centred(key_of[4], (SEQS, SEQ, D), 1.0, 6.0, ((0, 4), (1, 8)))
    w_qkv = centred(key_of[5], (3, D, D), D ** -0.5, 0.125, ((1, 8),))
    w_out = centred(key_of[6], (D, D), (D // 16) ** -0.5, 0.5, ((0, 8),))
    gain_attn = jnp.clip(1.0 + 0.15 * jax.random.normal(key_of[7], (D,), jnp.float32), 0.25, 1.75).astype(jnp.bfloat16)
    gain_moe = jnp.clip(1.0 + 0.15 * jax.random.normal(key_of[8], (D,), jnp.float32), 0.25, 1.75).astype(jnp.bfloat16)
    router = centred(key_of[9], (D, EXPERTS), (4 * D) ** -0.5, 0.0625, ((0, 8),))
    w_gate = centred(key_of[10], (EXPERTS, D, F), D ** -0.5, 0.125, ((0, 8),))
    w_up = centred(key_of[11], (EXPERTS, D, F), D ** -0.5, 0.125, ((0, 8),))
    w_down = centred(key_of[12], (EXPERTS, F, D), (F // 16) ** -0.5, 0.75, ((0, 8),))
    a_attn = centred(key_of[13], (4, D, SR), D ** -0.5, 0.125, ((1, 8),))
    b_attn = centred(key_of[14], (4, D, SR), (4 * R) ** -0.5, 0.75, ((1, 8),))
    exp_a_in = centred(key_of[15], (EXPERTS, 2, D, SR), D ** -0.5, 0.125, ((0, 8),))
    exp_b_in = centred(key_of[16], (EXPERTS, 2, SR, F), (4 * R) ** -0.5, 0.75, ((0, 8),))
    exp_a_down = centred(key_of[17], (EXPERTS, F, SR), F ** -0.5, 0.1875, ((0, 8),))
    exp_b_down = centred(key_of[18], (EXPERTS, SR, D), (4 * R) ** -0.5, 0.75, ((0, 8),))
    return dict(hidden_in=hidden_in, segments=segments, routes=routes, doc_sets=doc_sets, cotangent=cotangent, w_qkv=w_qkv, w_out=w_out, gain_attn=gain_attn, gain_moe=gain_moe, router=router, w_gate=w_gate, w_up=w_up, w_down=w_down, a_attn=a_attn, b_attn=b_attn, exp_a_in=exp_a_in, exp_b_in=exp_b_in, exp_a_down=exp_a_down, exp_b_down=exp_b_down)


EPSILON = 1e-05
MASKED = -1e+30
HIGHEST = lax.Precision.HIGHEST

@jax.custom_vjp
def low(v):
    return lax.optimization_barrier(v.astype(jnp.bfloat16)).astype(jnp.float32)

@jax.custom_vjp
def low_back(v):
    return v

def low_keep(v):
    return (low(v), None)

def low_pass(kept, grad):
    return (grad,)

def back_keep(v):
    return (v, None)

def back_low(kept, grad):
    return (low(grad),)
low.defvjp(low_keep, low_pass)
low_back.defvjp(back_keep, back_low)

def matmul(left_side, right_side):
    return jnp.dot(left_side, right_side, precision=HIGHEST, preferred_element_type=jnp.float32)

def rms_scale(values):
    return values * lax.rsqrt(lax.optimization_barrier(jnp.mean(values * values, axis=-1, keepdims=True)) + EPSILON)

def rope_tables(positions, head_size):
    half_size = head_size // 2
    inv_freq = jnp.exp(jnp.arange(half_size, dtype=jnp.float32) * (-2.0 * math.log(10000.0) / head_size))
    angles = positions.astype(jnp.float32)[:, None] * inv_freq[None, :]
    return (jnp.cos(angles), jnp.sin(angles))

def rotate(values, cosine, sine_table):
    half_size = values.shape[-1] // 2
    front_half = values[..., :half_size]
    back_half = values[..., half_size:]
    cos_rows = cosine[:, None, :]
    sin_rows = sine_table[:, None, :]
    return jnp.concatenate([front_half * cos_rows - back_half * sin_rows, back_half * cos_rows + front_half * sin_rows], axis=-1)

def adapted(inputs, weight, down_map, up_map, document_set_mask):
    low_rank = low_back(low(matmul(inputs, down_map) * document_set_mask))
    return matmul(inputs, weight) + matmul(low_rank, up_map.T)

def expert_adapted(inputs, weight, down_map, up_map, slot_mask):
    low_rank = low_back(low(jnp.einsum('erd,eds->ers', inputs, down_map, precision=HIGHEST) * slot_mask))
    return jnp.einsum('erd,edf->erf', inputs, weight, precision=HIGHEST) + jnp.einsum('ers,esf->erf', low_rank, up_map, precision=HIGHEST)

def layer_forward(hidden_f, adapters, frozen, seg_ids, route_ids, set_row):
    w_qkv, w_out, gain_attn, gain_moe, router, w_gate, w_up, w_down = frozen
    a_attn, b_attn, exp_a_in, exp_b_in, exp_a_down, exp_b_down = adapters
    length = hidden_f.shape[0]
    set_token = lax.optimization_barrier(jnp.sum(jnp.where(seg_ids[:, None] == jnp.arange(SETS)[None, :], set_row[None, :], 0), axis=1))
    document_set_mask = (set_token[:, None] == (jnp.arange(SETS * R) // R)[None, :]).astype(jnp.float32)
    first_normed_rows = low(rms_scale(hidden_f) * gain_attn)
    query_pre = low_back(adapted(first_normed_rows, w_qkv[0], a_attn[0], b_attn[0], document_set_mask))
    key_pre = low_back(adapted(first_normed_rows, w_qkv[1], a_attn[1], b_attn[1], document_set_mask))
    values = low_back(low(adapted(first_normed_rows, w_qkv[2], a_attn[2], b_attn[2], document_set_mask)))
    cosine, sine_table = rope_tables(jnp.arange(length), HD)
    queries = low(rotate(query_pre.reshape(length, H, HD), cosine, sine_table))
    keys_rot = low(rotate(key_pre.reshape(length, H, HD), cosine, sine_table))
    value_heads = values.reshape(length, H, HD)
    block_rows = math.gcd(length, 512)

    def attend(block_in):
        query_block, seg_block = block_in
        scores = jnp.einsum('qhd,khd->hqk', query_block, keys_rot, precision=HIGHEST) * HD ** (-0.5)
        scores = low_back(jnp.where((seg_block[:, None] == seg_ids[None, :])[None], scores, MASKED))
        soft_probs = low(jax.nn.softmax(scores, axis=-1))
        return jnp.einsum('hqk,khd->qhd', soft_probs, value_heads, precision=HIGHEST)
    attended = lax.map(jax.checkpoint(attend), (queries.reshape(length // block_rows, block_rows, H, HD), seg_ids.reshape(length // block_rows, block_rows)))
    attention_rounded_rows = low_back(low(attended.reshape(length, H * HD)))
    branch = low_back(adapted(attention_rounded_rows, w_out, a_attn[3], b_attn[3], document_set_mask))
    resid_one = hidden_f + branch
    normed_two = low(rms_scale(resid_one) * gain_moe)
    logits = low_back(matmul(normed_two, router))
    gate_weights = jax.nn.softmax(jnp.take_along_axis(logits, route_ids, axis=1), axis=-1)
    flat_routes = route_ids.reshape(-1)
    one_hot = (flat_routes[:, None] == jnp.arange(EXPERTS)[None, :]).astype(jnp.int32)
    slot_index = lax.optimization_barrier(jnp.sum((jnp.cumsum(one_hot, axis=0) - 1) * one_hot, axis=1)).astype(jnp.int32)
    token_index = (jnp.arange(flat_routes.shape[0]) // TOP).astype(jnp.int32)
    slot_rows = N_FSDP * CAP
    rows_in = low_back(jnp.zeros((EXPERTS, slot_rows, D), jnp.float32).at[flat_routes, slot_index].set(normed_two[token_index]))
    row_sets = jnp.zeros((EXPERTS, slot_rows), jnp.int32).at[flat_routes, slot_index].set(set_token[token_index].astype(jnp.int32))
    slot_mask = (row_sets[:, :, None] == (jnp.arange(SETS * R) // R)[None, None, :]).astype(jnp.float32)
    gate_h = low_back(expert_adapted(rows_in, w_gate, exp_a_in[:, 0], exp_b_in[:, 0], slot_mask))
    up_h = low_back(expert_adapted(rows_in, w_up, exp_a_in[:, 1], exp_b_in[:, 1], slot_mask))
    activation = low(jax.nn.silu(gate_h) * up_h)
    expert_out = low_back(low(expert_adapted(activation, w_down, exp_a_down, exp_b_down, slot_mask)))
    route_out = expert_out[flat_routes, slot_index].reshape(length, TOP, D)
    return resid_one + lax.optimization_barrier(jnp.sum(gate_weights[:, :, None] * route_out, axis=1))

def reference(hidden_in, segments, routes, doc_sets, cotangent, w_qkv, w_out, gain_attn, gain_moe, router, w_gate, w_up, w_down, a_attn, b_attn, exp_a_in, exp_b_in, exp_a_down, exp_b_down):
    frozen = tuple((array_in.astype(jnp.float32) for array_in in (w_qkv, w_out, gain_attn, gain_moe, router, w_gate, w_up, w_down)))
    adapters = tuple((array_in.astype(jnp.float32) for array_in in (a_attn, b_attn, exp_a_in, exp_b_in, exp_a_down, exp_b_down)))

    def per_sequence(running, inputs_now):
        hidden_now, seg_now, route_now, set_now, cot_now = inputs_now

        def forward(hidden_f, adapters_now):
            return layer_forward(hidden_f, adapters_now, frozen, seg_now, route_now, set_now)
        layer_value, pull_back = jax.vjp(forward, hidden_now.astype(jnp.float32), adapters)
        grad_hidden, grad_adapters = pull_back(cot_now.astype(jnp.float32))
        running = jax.tree.map(jnp.add, running, grad_adapters)
        return (running, (layer_value.astype(jnp.bfloat16), grad_hidden.astype(jnp.bfloat16)))
    start_sums = tuple((jnp.zeros(array_in.shape, jnp.float32) for array_in in adapters))
    grad_sums, (outputs, grads_in) = lax.scan(per_sequence, start_sums, (hidden_in, segments, routes, doc_sets, cotangent))
    return (outputs, grads_in, grad_sums[0], grad_sums[1], grad_sums[2], grad_sums[3], grad_sums[4], grad_sums[5])
```

```python
import math

import jax
import jax.numpy as jnp
from jax import lax
from jax.sharding import PartitionSpec as P

HD = 128
TOP = 8
R = 16
SETS = 8
SR = 128


EPSILON = 1e-05
MASKED = -1e30


def rms_scale(values):
    return values * lax.rsqrt(jnp.mean(values * values, axis=-1, keepdims=True) + EPSILON)


def norm_back(values, gain_row, upstream_grad):
    result, pull_back = jax.vjp(lambda inner_rows: rms_scale(inner_rows) * gain_row, values)
    return pull_back(upstream_grad)[0]


def rope_tables(positions, head_size):
    half_size = head_size // 2
    inv_freq = jnp.exp(
        jnp.arange(half_size, dtype=jnp.float32) * (-2.0 * math.log(10000.0) / head_size)
    )
    angles = positions.astype(jnp.float32)[:, None] * inv_freq[None, :]
    return (jnp.cos(angles), jnp.sin(angles))


def rotate(values, cosine, sine_table):
    half_size = values.shape[-1] // 2
    front_half = values[..., :half_size]
    back_half = values[..., half_size:]
    cos_rows = cosine[:, None, :]
    sin_rows = sine_table[:, None, :]
    return jnp.concatenate(
        [
            front_half * cos_rows - back_half * sin_rows,
            back_half * cos_rows + front_half * sin_rows,
        ],
        axis=-1,
    )


def gathered_layer(
    hidden_in,
    segments,
    routes,
    doc_sets,
    cotangent,
    w_qkv,
    w_out,
    gain_attn,
    gain_moe,
    router,
    w_gate,
    w_up,
    w_down,
    a_attn,
    b_attn,
    exp_a_in,
    exp_b_in,
    exp_a_down,
    exp_b_down,
):
    shard_count = lax.axis_size("fsdp")
    shard_index = lax.axis_index("fsdp")
    tok_rows = hidden_in.shape[1]
    model_width = hidden_in.shape[2]
    head_count = model_width // HD
    local_experts = w_gate.shape[0]
    experts_all = local_experts * shard_count
    capacity = max(2, 3 * tok_rows * TOP // (2 * experts_all))
    score_scale = HD ** (-0.5)
    (
        attention_weight_full,
        output_weight_full,
        adapter_down_weight,
        adapter_up_weight,
        first_norm_gain_full,
        second_norm_gain_full,
        router_weight_full,
    ) = (
        lax.all_gather(w_qkv, "fsdp", axis=1, tiled=True),
        lax.all_gather(w_out, "fsdp", axis=0, tiled=True),
        lax.all_gather(a_attn, "fsdp", axis=1, tiled=True),
        lax.all_gather(b_attn, "fsdp", axis=1, tiled=True),
        lax.all_gather(gain_attn, "fsdp", axis=0, tiled=True),
        lax.all_gather(gain_moe, "fsdp", axis=0, tiled=True),
        lax.all_gather(router, "fsdp", axis=0, tiled=True),
    )
    gain_one = first_norm_gain_full.astype(jnp.float32)
    gain_two = second_norm_gain_full.astype(jnp.float32)
    seg_local = segments[0]
    set_token = jnp.sum(
        jnp.where(seg_local[:, None] == jnp.arange(SETS)[None, :], doc_sets[0][None, :], 0), axis=1
    )
    document_set_mask = (set_token[:, None] == (jnp.arange(SR) // R)[None, :]).astype(jnp.float32)
    mask_half = document_set_mask.astype(jnp.bfloat16)
    hidden_f = hidden_in[0].astype(jnp.float32)
    first_normed_rows = (rms_scale(hidden_f) * gain_one).astype(jnp.bfloat16)
    attention_rank_branch = (
        jnp.einsum(
            "xj,zje->zxe",
            first_normed_rows,
            adapter_down_weight[:3],
            preferred_element_type=jnp.float32,
        )
        * document_set_mask[None]
    ).astype(jnp.bfloat16)
    projected = jnp.einsum(
        "td,pde->pte", first_normed_rows, attention_weight_full, preferred_element_type=jnp.float32
    ) + jnp.einsum(
        "nzv,nwv->nzw",
        attention_rank_branch,
        adapter_up_weight[:3],
        preferred_element_type=jnp.float32,
    )
    positions = shard_index * tok_rows + jnp.arange(tok_rows)
    cosine, sine_table = rope_tables(positions, HD)
    queries = rotate(projected[0].reshape(tok_rows, head_count, HD), cosine, sine_table).astype(
        jnp.bfloat16
    )
    keys_own = (
        rotate(projected[1].reshape(tok_rows, head_count, HD), cosine, sine_table)
        .astype(jnp.bfloat16)
        .reshape(tok_rows, model_width)
    )
    values_own = projected[2].astype(jnp.bfloat16)
    seg_own = seg_local.astype(jnp.bfloat16)
    run_max = jnp.full((head_count, tok_rows), MASKED, jnp.float32)
    key_piece = lax.all_gather(keys_own, "fsdp", axis=0, tiled=True)
    value_piece = lax.all_gather(values_own, "fsdp", axis=0, tiled=True)
    seg_piece = lax.all_gather(seg_own, "fsdp", axis=0, tiled=True)
    piece_rows = key_piece.shape[0]
    scores = (
        jnp.einsum(
            "qhd,khd->hqk",
            queries,
            key_piece.reshape(piece_rows, head_count, HD),
            preferred_element_type=jnp.float32,
        )
        * score_scale
    )
    same_doc = seg_local[:, None] == seg_piece.astype(jnp.int32)[None, :]
    scores = jnp.where(same_doc[None], scores, MASKED)
    new_max = jnp.maximum(run_max, jnp.max(scores, axis=2))
    exp_scores = jnp.exp(scores - new_max[:, :, None])
    new_sum = jnp.sum(exp_scores, axis=2)
    new_acc = jnp.einsum(
        "hqk,khd->qhd",
        exp_scores.astype(jnp.bfloat16),
        value_piece.reshape(piece_rows, head_count, HD),
        preferred_element_type=jnp.float32,
    )
    folded = (new_max, new_sum, new_acc)
    run_max, run_sum, run_acc = folded
    log_sum = run_max + jnp.log(run_sum)
    attended = run_acc / jnp.transpose(run_sum)[:, :, None]
    attention_rounded_rows = attended.reshape(tok_rows, model_width).astype(jnp.bfloat16)
    output_rank_branch = (
        jnp.dot(attention_rounded_rows, adapter_down_weight[3], preferred_element_type=jnp.float32)
        * document_set_mask
    ).astype(jnp.bfloat16)
    resid_one = hidden_f + (
        jnp.dot(attention_rounded_rows, output_weight_full, preferred_element_type=jnp.float32)
        + jnp.einsum(
            "nd,gd->ng",
            output_rank_branch,
            adapter_up_weight[3],
            preferred_element_type=jnp.float32,
        )
    )
    normed_two = (rms_scale(resid_one) * gain_two).astype(jnp.bfloat16)
    logits = jnp.dot(normed_two, router_weight_full, preferred_element_type=jnp.float32)
    my_routes = routes[0]
    gate_weights = jax.nn.softmax(jnp.take_along_axis(logits, my_routes, axis=1), axis=-1)
    flat_routes = my_routes.reshape(-1)
    one_hot = (flat_routes[:, None] == jnp.arange(experts_all)[None, :]).astype(jnp.int32)
    slot_index = jnp.sum((jnp.cumsum(one_hot, axis=0) - 1) * one_hot, axis=1)
    token_index = jnp.arange(tok_rows * TOP) // TOP
    send_rows = (
        jnp.zeros((experts_all, capacity, model_width), jnp.bfloat16)
        .at[flat_routes, slot_index]
        .set(normed_two[token_index])
    )
    send_sets = (
        jnp.zeros((experts_all, capacity), jnp.bfloat16)
        .at[flat_routes, slot_index]
        .set(set_token[token_index].astype(jnp.bfloat16))
    )
    rows_got = lax.all_to_all(
        send_rows.reshape(shard_count, local_experts, capacity, model_width),
        "fsdp",
        split_axis=0,
        concat_axis=0,
        tiled=True,
    )
    sets_got = lax.all_to_all(
        send_sets.reshape(shard_count, local_experts, capacity),
        "fsdp",
        split_axis=0,
        concat_axis=0,
        tiled=True,
    )
    slot_mask = (sets_got.astype(jnp.int32)[..., None] == jnp.arange(SR) // R).astype(jnp.float32)
    low_in = (
        jnp.einsum("necd,eids->necis", rows_got, exp_a_in, preferred_element_type=jnp.float32)
        * slot_mask[:, :, :, None, :]
    ).astype(jnp.bfloat16)
    gate_h = jnp.einsum(
        "necd,edf->necf", rows_got, w_gate, preferred_element_type=jnp.float32
    ) + jnp.einsum(
        "necs,esf->necf", low_in[:, :, :, 0], exp_b_in[:, 0], preferred_element_type=jnp.float32
    )
    up_h = jnp.einsum(
        "necd,edf->necf", rows_got, w_up, preferred_element_type=jnp.float32
    ) + jnp.einsum(
        "necs,esf->necf", low_in[:, :, :, 1], exp_b_in[:, 1], preferred_element_type=jnp.float32
    )
    activation = (jax.nn.silu(gate_h) * up_h).astype(jnp.bfloat16)
    low_down = (
        jnp.einsum("necf,efs->necs", activation, exp_a_down, preferred_element_type=jnp.float32)
        * slot_mask
    ).astype(jnp.bfloat16)
    expert_out = (
        jnp.einsum("necf,efd->necd", activation, w_down, preferred_element_type=jnp.float32)
        + jnp.einsum("necs,esd->necd", low_down, exp_b_down, preferred_element_type=jnp.float32)
    ).astype(jnp.bfloat16)
    expert_out, rows_got, slot_mask, low_in, gate_h, up_h, activation, low_down = (
        expert_out,
        rows_got,
        slot_mask,
        low_in,
        gate_h,
        up_h,
        activation,
        low_down,
    )
    returned = lax.all_to_all(expert_out, "fsdp", split_axis=0, concat_axis=0, tiled=True)
    route_out = (
        returned.reshape(experts_all, capacity, model_width)[flat_routes, slot_index]
        .reshape(tok_rows, TOP, model_width)
        .astype(jnp.float32)
    )
    layer_value = resid_one + jnp.sum(gate_weights[:, :, None] * route_out, axis=1)
    (
        attention_weight_full,
        output_weight_full,
        adapter_down_weight,
        adapter_up_weight,
        first_norm_gain_full,
        second_norm_gain_full,
        router_weight_full,
    ) = (
        lax.all_gather(w_qkv, "fsdp", axis=1, tiled=True),
        lax.all_gather(w_out, "fsdp", axis=0, tiled=True),
        lax.all_gather(a_attn, "fsdp", axis=1, tiled=True),
        lax.all_gather(b_attn, "fsdp", axis=1, tiled=True),
        lax.all_gather(gain_attn, "fsdp", axis=0, tiled=True),
        lax.all_gather(gain_moe, "fsdp", axis=0, tiled=True),
        lax.all_gather(router, "fsdp", axis=0, tiled=True),
    )
    gain_one = first_norm_gain_full.astype(jnp.float32)
    gain_two = second_norm_gain_full.astype(jnp.float32)
    upstream = cotangent[0].astype(jnp.float32)
    d_route = (gate_weights[:, :, None] * upstream[:, None, :]).astype(jnp.bfloat16)
    d_gates = jnp.sum(upstream[:, None, :] * route_out, axis=2)
    d_chosen = gate_weights * (d_gates - jnp.sum(gate_weights * d_gates, axis=1, keepdims=True))
    d_logits = jnp.sum(
        jnp.where(
            my_routes[:, :, None] == jnp.arange(experts_all)[None, None, :],
            d_chosen[:, :, None],
            0.0,
        ),
        axis=1,
    ).astype(jnp.bfloat16)
    send_grads = (
        jnp.zeros((experts_all, capacity, model_width), jnp.bfloat16)
        .at[flat_routes, slot_index]
        .set(d_route.reshape(tok_rows * TOP, model_width))
    )
    grads_got = lax.all_to_all(
        send_grads.reshape(shard_count, local_experts, capacity, model_width),
        "fsdp",
        split_axis=0,
        concat_axis=0,
        tiled=True,
    )
    slot_half = slot_mask.astype(jnp.bfloat16)
    d_low_down = (
        jnp.einsum(
            "necd,esd->necs", grads_got, exp_b_down, preferred_element_type=jnp.float32
        ).astype(jnp.bfloat16)
        * slot_half
    )
    d_activation = jnp.einsum(
        "necd,efd->necf", grads_got, w_down, preferred_element_type=jnp.float32
    ) + jnp.einsum("necs,efs->necf", d_low_down, exp_a_down, preferred_element_type=jnp.float32)
    silu_value, silu_pull = jax.vjp(
        lambda gate_in, up_in: jax.nn.silu(gate_in) * up_in, gate_h, up_h
    )
    d_gate_h, d_up_h = silu_pull(d_activation)
    d_gate_h = d_gate_h.astype(jnp.bfloat16)
    d_up_h = d_up_h.astype(jnp.bfloat16)
    d_both = jnp.stack([d_gate_h, d_up_h], axis=3)
    d_low_in = (
        jnp.einsum(
            "necif,eisf->necis", d_both, exp_b_in, preferred_element_type=jnp.float32
        ).astype(jnp.bfloat16)
        * slot_half[:, :, :, None, :]
    )
    d_rows = (
        jnp.einsum("necf,edf->necd", d_gate_h, w_gate, preferred_element_type=jnp.float32)
        + jnp.einsum("necf,edf->necd", d_up_h, w_up, preferred_element_type=jnp.float32)
        + jnp.einsum("necis,eids->necd", d_low_in, exp_a_in, preferred_element_type=jnp.float32)
    )
    returned_grads = lax.all_to_all(
        d_rows.astype(jnp.bfloat16), "fsdp", split_axis=0, concat_axis=0, tiled=True
    )
    g_exp_b_down = jnp.einsum(
        "necs,necd->esd", low_down, grads_got, preferred_element_type=jnp.float32
    )
    g_exp_a_down = jnp.einsum(
        "necf,necs->efs", activation, d_low_down, preferred_element_type=jnp.float32
    )
    g_exp_b_in = jnp.einsum("necis,necif->eisf", low_in, d_both, preferred_element_type=jnp.float32)
    g_exp_a_in = jnp.einsum(
        "necd,necis->eids", rows_got, d_low_in, preferred_element_type=jnp.float32
    )
    d_normed_two = jnp.sum(
        returned_grads.reshape(experts_all, capacity, model_width)[flat_routes, slot_index]
        .reshape(tok_rows, TOP, model_width)
        .astype(jnp.float32),
        axis=1,
    ) + jnp.einsum("te,de->td", d_logits, router_weight_full, preferred_element_type=jnp.float32)
    d_resid_one = upstream + norm_back(resid_one, gain_two, d_normed_two)
    branch_gradient = d_resid_one.astype(jnp.bfloat16)
    output_adapter_gradient = (
        jnp.dot(branch_gradient, adapter_up_weight[3], preferred_element_type=jnp.float32).astype(
            jnp.bfloat16
        )
        * mask_half
    )
    d_att = (
        jnp.einsum(
            "te,de->td", branch_gradient, output_weight_full, preferred_element_type=jnp.float32
        )
        + jnp.einsum(
            "cr,ar->ca",
            output_adapter_gradient,
            adapter_down_weight[3],
            preferred_element_type=jnp.float32,
        )
    ).astype(jnp.bfloat16)
    output_up_gradient = jnp.einsum(
        "ts,te->es", output_rank_branch, branch_gradient, preferred_element_type=jnp.float32
    )
    output_down_gradient = jnp.einsum(
        "td,ts->ds",
        attention_rounded_rows,
        output_adapter_gradient,
        preferred_element_type=jnp.float32,
    )
    d_att_heads = d_att.reshape(tok_rows, head_count, HD)
    delta_rows = jnp.transpose(jnp.sum(d_att_heads.astype(jnp.float32) * attended, axis=2))
    key_piece = lax.all_gather(keys_own, "fsdp", axis=0, tiled=True)
    value_piece = lax.all_gather(values_own, "fsdp", axis=0, tiled=True)
    seg_piece = lax.all_gather(seg_own, "fsdp", axis=0, tiled=True)
    piece_rows = key_piece.shape[0]
    key_heads = key_piece.reshape(piece_rows, head_count, HD)
    value_heads = value_piece.reshape(piece_rows, head_count, HD)
    scores = (
        jnp.einsum("qhd,khd->hqk", queries, key_heads, preferred_element_type=jnp.float32)
        * score_scale
    )
    same_doc = seg_local[:, None] == seg_piece.astype(jnp.int32)[None, :]
    scores = jnp.where(same_doc[None], scores, MASKED)
    soft_probs = jnp.exp(scores - log_sum[:, :, None])
    d_probs = jnp.einsum(
        "qhd,khd->hqk", d_att_heads, value_heads, preferred_element_type=jnp.float32
    )
    d_scores = (soft_probs * (d_probs - delta_rows[:, :, None])).astype(jnp.bfloat16)
    soft_probs, d_scores = (soft_probs, d_scores)
    d_query_part = jnp.einsum(
        "hqk,khd->qhd", d_scores, key_heads, preferred_element_type=jnp.float32
    )
    d_key_part = jnp.einsum(
        "hqk,qhd->khd", d_scores, queries, preferred_element_type=jnp.float32
    ).reshape(piece_rows, model_width)
    d_value_part = jnp.einsum(
        "hqk,qhd->khd",
        soft_probs.astype(jnp.bfloat16),
        d_att_heads,
        preferred_element_type=jnp.float32,
    ).reshape(piece_rows, model_width)
    back_state = (d_query_part, d_key_part, d_value_part)
    d_query, d_keys_all, d_values_all = back_state
    d_keys_mine, d_values_mine = (
        lax.psum_scatter(
            d_keys_all.astype(jnp.bfloat16), "fsdp", scatter_dimension=0, tiled=True
        ).astype(jnp.float32),
        lax.psum_scatter(
            d_values_all.astype(jnp.bfloat16), "fsdp", scatter_dimension=0, tiled=True
        ).astype(jnp.float32),
    )
    d_query_pre = (
        rotate(d_query * score_scale, cosine, -sine_table)
        .reshape(tok_rows, model_width)
        .astype(jnp.bfloat16)
    )
    d_key_pre = (
        rotate((d_keys_mine * score_scale).reshape(tok_rows, head_count, HD), cosine, -sine_table)
        .reshape(tok_rows, model_width)
        .astype(jnp.bfloat16)
    )
    projected_gradient = jnp.stack([d_query_pre, d_key_pre, d_values_mine.astype(jnp.bfloat16)])
    projection_adapter_gradient = (
        jnp.einsum(
            "jah,jho->jao",
            projected_gradient,
            adapter_up_weight[:3],
            preferred_element_type=jnp.float32,
        ).astype(jnp.bfloat16)
        * mask_half[None]
    )
    d_normed_one = jnp.einsum(
        "pte,pde->td", projected_gradient, attention_weight_full, preferred_element_type=jnp.float32
    ) + jnp.einsum(
        "czn,cvn->zv",
        projection_adapter_gradient,
        adapter_down_weight[:3],
        preferred_element_type=jnp.float32,
    )
    attention_up_gradient = jnp.einsum(
        "pts,pte->pes",
        attention_rank_branch,
        projected_gradient,
        preferred_element_type=jnp.float32,
    )
    attention_down_gradient = jnp.einsum(
        "td,pts->pds",
        first_normed_rows,
        projection_adapter_gradient,
        preferred_element_type=jnp.float32,
    )
    d_hidden = d_resid_one + norm_back(hidden_f, gain_one, d_normed_one)
    adapter_down_gradient = jnp.concatenate(
        [attention_down_gradient, output_down_gradient[None]], axis=0
    )
    adapter_up_gradient = jnp.concatenate([attention_up_gradient, output_up_gradient[None]], axis=0)
    part_down, part_up = (
        lax.psum_scatter(
            adapter_down_gradient.astype(jnp.bfloat16), "fsdp", scatter_dimension=1, tiled=True
        ).astype(jnp.float32),
        lax.psum_scatter(
            adapter_up_gradient.astype(jnp.bfloat16), "fsdp", scatter_dimension=1, tiled=True
        ).astype(jnp.float32),
    )
    summed = (
        lax.psum(part_down.astype(jnp.bfloat16), "rep").astype(jnp.float32),
        lax.psum(part_up.astype(jnp.bfloat16), "rep").astype(jnp.float32),
        lax.psum(g_exp_a_in.astype(jnp.bfloat16), "rep").astype(jnp.float32),
        lax.psum(g_exp_b_in.astype(jnp.bfloat16), "rep").astype(jnp.float32),
        lax.psum(g_exp_a_down.astype(jnp.bfloat16), "rep").astype(jnp.float32),
        lax.psum(g_exp_b_down.astype(jnp.bfloat16), "rep").astype(jnp.float32),
    )
    return (
        layer_value.astype(jnp.bfloat16)[None],
        d_hidden.astype(jnp.bfloat16)[None],
        summed[0],
        summed[1],
        summed[2],
        summed[3],
        summed[4],
        summed[5],
    )


EVERY = 8


def swap(values, bits):
    return lax.ppermute(values, "fsdp", [(i, i ^ bits) for i in range(EVERY)])


def gather_relative(values):
    half = values.shape[0] // 2
    side, over = swap(values, 2), swap(values, 4)
    far = jnp.concatenate([swap(side[:half], 4), swap(over[half:], 2)], axis=0)
    mine = [values, side, over, far]
    other = [swap(block, 1) for block in mine]
    return [mine[0], other[0], mine[1], other[1], mine[2], other[2], mine[3], other[3]]


def add_half(left, right):
    return (left.astype(jnp.float32) + right.astype(jnp.float32)).astype(jnp.bfloat16)


def scatter_relative(blocks):
    got = [swap(blocks[j], 1) for j in (7, 3, 5, 1)]
    far = add_half(blocks[6], got[0])
    half = far.shape[0] // 2
    far_side, far_over = swap(far[:half], 2), swap(far[half:], 4)
    side = blocks[2].astype(jnp.float32) + got[1].astype(jnp.float32)
    over = blocks[4].astype(jnp.float32) + got[2].astype(jnp.float32)
    side = jnp.concatenate([side[:half], side[half:] + far_over.astype(jnp.float32)], axis=0)
    over = jnp.concatenate([over[:half] + far_side.astype(jnp.float32), over[half:]], axis=0)
    side, over = swap(side.astype(jnp.bfloat16), 2), swap(over.astype(jnp.bfloat16), 4)
    return (
        blocks[0].astype(jnp.float32)
        + got[3].astype(jnp.float32)
        + side.astype(jnp.float32)
        + over.astype(jnp.float32)
    )


def exchange_relative(blocks):
    return [blocks[0]] + [swap(blocks[j], j) for j in range(1, EVERY)]


def rep_swap(values, bits):
    return lax.ppermute(values, "rep", [(i, i ^ bits) for i in range(4)])


def pick(pair, index):
    return lax.dynamic_index_in_dim(pair, index, 0, keepdims=False)


def joined(own, other, index):
    return jnp.where(index == 0, jnp.stack([own, other]), jnp.stack([other, own]))


def sum_rep(values):
    where = lax.axis_index("rep")
    low_bit, high_bit = where % 2, where // 2
    rows, columns = values.shape
    halves = values.reshape(2, rows // 2, columns)
    half = add_half(pick(halves, low_bit), rep_swap(pick(halves, 1 - low_bit), 1))
    parts = half.reshape(2, rows // 4, columns)
    part = add_half(pick(parts, high_bit), rep_swap(pick(parts, 1 - high_bit), 2))
    half = joined(part, rep_swap(part, 2), high_bit).reshape(rows // 2, columns)
    return joined(half, rep_swap(half, 1), low_bit).reshape(rows, columns)


def dot32(left, right):
    return jnp.dot(left, right, preferred_element_type=jnp.float32)


def dot_nt(left, right):
    return lax.dot_general(left, right, (((1,), (1,)), ((), ())), preferred_element_type=jnp.float32)


def dot_tn(left, right):
    return lax.dot_general(left, right, (((0,), (0,)), ((), ())), preferred_element_type=jnp.float32)


def in_order(blocks, me):
    rows = blocks[0].shape[0]
    whole = jnp.zeros((rows * EVERY, blocks[0].shape[1]), blocks[0].dtype)
    for j, block in enumerate(blocks):
        whole = lax.dynamic_update_slice(whole, block, ((me ^ j) * rows, 0))
    return whole


def block_of(values, index, rows):
    return lax.dynamic_slice_in_dim(values, index * rows, rows, axis=0)


def after(value, gate):
    return lax.optimization_barrier((value, gate))[0]


def set_masks(seg, doc_sets):
    set_token = jnp.sum(
        jnp.where(seg[:, None] == jnp.arange(SETS)[None, :], doc_sets[0][None, :], 0), axis=1
    )
    return (set_token[:, None] == (jnp.arange(SR) // R)[None, :]).astype(jnp.float32)


def split_layer(
    hidden_in,
    segments,
    routes,
    doc_sets,
    cotangent,
    w_qkv,
    w_out,
    gain_attn,
    gain_moe,
    router,
    w_gate,
    w_up,
    w_down,
    a_attn,
    b_attn,
    exp_a_in,
    exp_b_in,
    exp_a_down,
    exp_b_down,
):
    bf16, f32 = jnp.bfloat16, jnp.float32
    me = lax.axis_index("fsdp")
    rows = hidden_in.shape[1]
    width = hidden_in.shape[2]
    wide = width // EVERY
    heads = wide // HD
    experts_all = w_gate.shape[0] * EVERY
    score_scale = HD ** (-0.5)
    tokens = rows * EVERY
    meta = jnp.concatenate([routes[0], segments[0][:, None]], axis=1).astype(bf16)
    meta = jnp.pad(meta, ((0, 0), (0, 128 - meta.shape[1])))
    hidden_blocks = gather_relative(jnp.concatenate([hidden_in[0], meta], axis=1))
    w_own = lax.all_to_all(
        w_qkv.reshape(3, wide, EVERY, wide).transpose(2, 0, 1, 3),
        "fsdp",
        split_axis=0,
        concat_axis=0,
        tiled=True,
    )
    w_own = w_own.transpose(1, 0, 2, 3).reshape(3, width, wide)
    small = jnp.concatenate(
        [a_attn[0], a_attn[1], a_attn[2], a_attn[3], b_attn[3], router, gain_attn[:, None], gain_moe[:, None]],
        axis=1,
    )
    small = jnp.pad(small, ((0, 0), (0, 768 - small.shape[1])))
    small_blocks = gather_relative(small)
    small_all = in_order(small_blocks, me)
    a_qkv, b_out = small_all[:, : 3 * SR], small_all[:, 4 * SR : 5 * SR]
    router_all = small_all[:, 5 * SR : 5 * SR + experts_all]
    gain_one = small_all[:, 5 * SR + experts_all].astype(f32)
    gain_two = small_all[:, 5 * SR + experts_all + 1].astype(f32)
    a_out = jnp.concatenate([block[:, 3 * SR : 4 * SR] for block in small_blocks], axis=0)
    hidden_ext = jnp.concatenate(hidden_blocks, axis=0)
    hidden_f = hidden_ext[:, :width].astype(f32)
    routes_all = hidden_ext[:, width : width + TOP].astype(jnp.int32)
    seg_all = hidden_ext[:, width + TOP].astype(jnp.int32)
    mask = set_masks(seg_all, doc_sets)
    mask_own = set_masks(segments[0], doc_sets)
    mask_half, mask_own_half = mask.astype(bf16), mask_own.astype(bf16)
    normed_one = (rms_scale(hidden_f) * gain_one).astype(bf16)
    w_out_rel = jnp.concatenate(gather_relative(after(w_out, normed_one)), axis=0)
    low_qkv = (
        dot32(normed_one, a_qkv).reshape(tokens, 3, SR) * mask[:, None, :]
    ).astype(bf16)
    proj = [dot32(normed_one, w_own[i]) + dot_nt(low_qkv[:, i], b_attn[i]) for i in range(3)]
    order = me ^ jnp.arange(EVERY)
    positions = (order[:, None] * rows + jnp.arange(rows)[None, :]).reshape(-1)
    cosine, sine_table = rope_tables(positions, HD)
    queries = rotate(proj[0].reshape(tokens, heads, HD), cosine, sine_table).astype(bf16)
    keys = rotate(proj[1].reshape(tokens, heads, HD), cosine, sine_table).astype(bf16)
    values = proj[2].reshape(tokens, heads, HD).astype(bf16)
    same_doc = (seg_all[:, None] == seg_all[None, :])[None]
    scores = jnp.einsum("qhd,khd->hqk", queries, keys, preferred_element_type=f32) * score_scale
    scores = jnp.where(same_doc, scores, MASKED)
    top_score = jnp.max(scores, axis=2)
    exp_scores = jnp.exp(scores - top_score[:, :, None])
    score_sum = jnp.sum(exp_scores, axis=2)
    log_sum = top_score + jnp.log(score_sum)
    attended = jnp.einsum(
        "hqk,khd->qhd", exp_scores.astype(bf16), values, preferred_element_type=f32
    ) / jnp.transpose(score_sum)[:, :, None]
    att_half = attended.reshape(tokens, wide).astype(bf16)
    att_own = jnp.concatenate(
        exchange_relative([att_half[j * rows : (j + 1) * rows] for j in range(EVERY)]), axis=1
    )
    low_out = (dot32(att_own, a_out) * mask_own).astype(bf16)
    resid_one = hidden_in[0].astype(f32) + (dot32(att_own, w_out_rel) + dot_nt(low_out, b_out))
    normed_own = (rms_scale(resid_one) * gain_two).astype(bf16)
    normed_two = jnp.concatenate(gather_relative(normed_own), axis=0)
    cot_all = jnp.concatenate(gather_relative(after(cotangent[0], normed_two)), axis=0)
    logits = dot32(normed_two, router_all)
    ids = jnp.arange(experts_all)
    named = jnp.any(routes_all[:, :, None] == ids[None, None, :], axis=1)
    gates = jax.nn.softmax(jnp.where(named, logits, -jnp.inf), axis=-1)
    own_gates = lax.dynamic_slice_in_dim(gates, me * 2, 2, axis=1)
    out_sum, row_sum, gate_cols, grads = 0.0, 0.0, 0.0, []
    cot_f = cot_all.astype(f32)
    for k in range(2):
        gate = own_gates[:, k : k + 1]
        a_in = jnp.concatenate([exp_a_in[k, 0], exp_a_in[k, 1]], axis=1)
        low_in = (dot32(normed_two, a_in).reshape(tokens, 2, SR) * mask[:, None, :]).astype(bf16)
        gate_h = dot32(normed_two, w_gate[k]) + dot32(low_in[:, 0], exp_b_in[k, 0])
        up_h = dot32(normed_two, w_up[k]) + dot32(low_in[:, 1], exp_b_in[k, 1])
        activation = (jax.nn.silu(gate_h) * up_h).astype(bf16)
        low_down = (dot32(activation, exp_a_down[k]) * mask).astype(bf16)
        expert_out = (
            (dot32(activation, w_down[k]) + dot32(low_down, exp_b_down[k])).astype(bf16).astype(f32)
        )
        out_sum = out_sum + gate * expert_out
        d_gate = jnp.sum(cot_f * expert_out, axis=1, keepdims=True)
        high = d_gate.astype(bf16)
        gate_cols = (
            gate_cols
            + jnp.where(jnp.arange(128)[None, :] == 2 * me + k, high.astype(f32), 0.0)
            + jnp.where(jnp.arange(128)[None, :] == 2 * me + k + experts_all, d_gate - high.astype(f32), 0.0)
        )
        d_out = (gate * cot_f).astype(bf16)
        d_low_down = dot_nt(d_out, exp_b_down[k]).astype(bf16) * mask_half
        d_act = dot_nt(d_out, w_down[k]) + dot_nt(d_low_down, exp_a_down[k])
        _, pull = jax.vjp(lambda a, b: jax.nn.silu(a) * b, gate_h, up_h)
        d_gate_h, d_up_h = pull(d_act)
        d_gate_h, d_up_h = d_gate_h.astype(bf16), d_up_h.astype(bf16)
        d_low_in = [
            dot_nt(d_gate_h, exp_b_in[k, 0]).astype(bf16) * mask_half,
            dot_nt(d_up_h, exp_b_in[k, 1]).astype(bf16) * mask_half,
        ]
        d_low_both = jnp.concatenate(d_low_in, axis=1)
        d_row = dot_nt(d_gate_h, w_gate[k]) + dot_nt(d_up_h, w_up[k]) + dot_nt(d_low_both, a_in)
        row_sum = row_sum + d_row.astype(bf16).astype(f32)
        g_a_in = dot_tn(d_low_both, normed_two).reshape(2, SR, width)
        g_b_in = jnp.stack([dot_tn(low_in[:, 0], d_gate_h), dot_tn(low_in[:, 1], d_up_h)])
        g_a_down = dot_tn(d_low_down, activation)
        g_b_down = dot_tn(low_down, d_out)
        packed = jnp.concatenate(
            [
                g_a_in.reshape(2 * SR, width),
                g_b_down,
                g_b_in.reshape(SR, width),
                g_a_down.reshape(SR // 2, width),
            ],
            axis=0,
        ).astype(bf16)
        grads.append(sum_rep(packed).astype(f32))
    out_ext = jnp.concatenate([out_sum, gate_cols], axis=1).astype(bf16)
    blocks = [out_ext[j * rows : (j + 1) * rows] for j in range(EVERY)]
    out_got = scatter_relative(blocks)
    layer_out = resid_one + out_got[:, :width]
    d_gates = out_got[:, width : width + experts_all] + out_got[:, width + experts_all : width + 2 * experts_all]
    gates_own_tok = gates[:rows]
    d_chosen = gates_own_tok * (d_gates - jnp.sum(gates_own_tok * d_gates, axis=1, keepdims=True))
    d_logits = d_chosen.astype(bf16)
    row_half = row_sum.astype(bf16)
    d_normed_two = scatter_relative(
        [row_half[j * rows : (j + 1) * rows] for j in range(EVERY)]
    ) + dot_nt(d_logits, router_all)
    upstream = cotangent[0].astype(f32)
    d_resid = upstream + norm_back(resid_one, gain_two, d_normed_two)
    d_branch = d_resid.astype(bf16)
    d_low_out = dot32(d_branch, b_out).astype(bf16) * mask_own_half
    d_att_own = (dot_nt(d_branch, w_out_rel) + dot_nt(d_low_out, a_out)).astype(bf16)
    d_att = jnp.concatenate(
        exchange_relative([d_att_own[:, j * wide : (j + 1) * wide] for j in range(EVERY)]), axis=0
    ).reshape(tokens, heads, HD)
    g_b_out = dot_tn(d_branch, low_out)
    g_a_out = dot_tn(att_own, d_low_out)
    delta = jnp.transpose(jnp.sum(d_att.astype(f32) * attended, axis=2))
    scores = jnp.einsum("qhd,khd->hqk", queries, keys, preferred_element_type=f32) * score_scale
    scores = jnp.where(same_doc, scores, MASKED)
    probs = jnp.exp(scores - log_sum[:, :, None])
    d_probs = jnp.einsum("qhd,khd->hqk", d_att, values, preferred_element_type=f32)
    d_scores = (probs * (d_probs - delta[:, :, None])).astype(bf16)
    d_queries = jnp.einsum("hqk,khd->qhd", d_scores, keys, preferred_element_type=f32)
    d_keys = jnp.einsum("hqk,qhd->khd", d_scores, queries, preferred_element_type=f32)
    d_values = jnp.einsum("hqk,qhd->khd", probs.astype(bf16), d_att, preferred_element_type=f32)
    d_proj = [
        rotate(d_queries * score_scale, cosine, -sine_table).reshape(tokens, wide).astype(bf16),
        rotate(d_keys * score_scale, cosine, -sine_table).reshape(tokens, wide).astype(bf16),
        d_values.reshape(tokens, wide).astype(bf16),
    ]
    d_low = jnp.concatenate(
        [dot32(d_proj[i], b_attn[i]).astype(bf16) * mask_half for i in range(3)], axis=1
    )
    d_normed = dot_nt(d_low, a_qkv)
    for i in range(3):
        d_normed = d_normed + dot_nt(d_proj[i], w_own[i])
    d_normed = d_normed.astype(bf16)
    d_normed_own = scatter_relative([d_normed[j * rows : (j + 1) * rows] for j in range(EVERY)])
    grad_in = d_resid + norm_back(hidden_in[0].astype(f32), gain_one, d_normed_own)
    g_a_qkv = dot_tn(normed_one, d_low)
    g_b_qkv = [dot_tn(d_proj[i], low_qkv[:, i]) for i in range(3)]
    sums = []
    for j in range(EVERY):
        sums.append(
            jnp.concatenate(
                [
                    block_of(g_a_qkv, me ^ j, wide),
                    g_a_out[j * wide : (j + 1) * wide],
                    block_of(g_b_out, me ^ j, wide),
                ],
                axis=1,
            ).astype(bf16)
        )
    g_sum = jnp.concatenate([scatter_relative(sums)] + g_b_qkv, axis=1)
    g_sum = sum_rep(g_sum.astype(bf16)).astype(f32)
    cut = [g_sum[:, i * SR : (i + 1) * SR] for i in range(8)]
    grad_a = jnp.stack([cut[0], cut[1], cut[2], cut[3]])
    grad_b = jnp.stack([cut[5], cut[6], cut[7], cut[4]])
    at = [2 * SR, 3 * SR, 4 * SR]
    return (
        layer_out.astype(bf16)[None],
        grad_in.astype(bf16)[None],
        grad_a,
        grad_b,
        jnp.stack([g[: at[0]].reshape(2, SR, width).transpose(0, 2, 1) for g in grads]),
        jnp.stack([g[at[1] : at[2]].reshape(2, SR, w_gate.shape[2]) for g in grads]),
        jnp.stack([g[at[2] :].reshape(SR, w_gate.shape[2]).T for g in grads]),
        jnp.stack([g[at[0] : at[1]] for g in grads]),
    )


def solution(mesh):
    shape = dict(mesh.shape)
    shards = split_layer if shape == {"rep": 4, "fsdp": EVERY} else gathered_layer
    return jax.shard_map(
        shards,
        mesh=mesh,
        in_specs=(
            P("rep", "fsdp", None),
            P("rep", "fsdp"),
            P("rep", "fsdp", None),
            P("rep", None),
            P("rep", "fsdp", None),
            P(None, "fsdp", None),
            P("fsdp", None),
            P("fsdp"),
            P("fsdp"),
            P("fsdp", None),
            P("fsdp", None, None),
            P("fsdp", None, None),
            P("fsdp", None, None),
            P(None, "fsdp", None),
            P(None, "fsdp", None),
            P("fsdp", None, None, None),
            P("fsdp", None, None, None),
            P("fsdp", None, None),
            P("fsdp", None, None),
        ),
        out_specs=(
            P("rep", "fsdp", None),
            P("rep", "fsdp", None),
            P(None, "fsdp", None),
            P(None, "fsdp", None),
            P("fsdp", None, None, None),
            P("fsdp", None, None, None),
            P("fsdp", None, None),
            P("fsdp", None, None),
        ),
        check_vma=False,
    )
```

```python
import functools
import math

import jax
import jax.numpy as jnp
from jax import lax
from jax.experimental import pallas as pl
from jax.experimental.pallas import tpu as pltpu
from jax.sharding import PartitionSpec as P

HD = 128
TOP = 8
R = 16
SETS = 8
SR = 128


EPSILON = 1e-05
MASKED = -1e30


def rms_scale(values):
    return values * lax.rsqrt(jnp.mean(values * values, axis=-1, keepdims=True) + EPSILON)


def norm_back(values, gain_row, upstream_grad):
    result, pull_back = jax.vjp(lambda inner_rows: rms_scale(inner_rows) * gain_row, values)
    return pull_back(upstream_grad)[0]


def rope_tables(positions, head_size):
    half_size = head_size // 2
    inv_freq = jnp.exp(
        jnp.arange(half_size, dtype=jnp.float32) * (-2.0 * math.log(10000.0) / head_size)
    )
    angles = positions.astype(jnp.float32)[:, None] * inv_freq[None, :]
    return (jnp.cos(angles), jnp.sin(angles))


def rotate(values, cosine, sine_table):
    half_size = values.shape[-1] // 2
    front_half = values[..., :half_size]
    back_half = values[..., half_size:]
    cos_rows = cosine[:, None, :]
    sin_rows = sine_table[:, None, :]
    return jnp.concatenate(
        [
            front_half * cos_rows - back_half * sin_rows,
            back_half * cos_rows + front_half * sin_rows,
        ],
        axis=-1,
    )


def gathered_layer(
    hidden_in,
    segments,
    routes,
    doc_sets,
    cotangent,
    w_qkv,
    w_out,
    gain_attn,
    gain_moe,
    router,
    w_gate,
    w_up,
    w_down,
    a_attn,
    b_attn,
    exp_a_in,
    exp_b_in,
    exp_a_down,
    exp_b_down,
):
    shard_count = lax.axis_size("fsdp")
    shard_index = lax.axis_index("fsdp")
    tok_rows = hidden_in.shape[1]
    model_width = hidden_in.shape[2]
    head_count = model_width // HD
    local_experts = w_gate.shape[0]
    experts_all = local_experts * shard_count
    capacity = max(2, 3 * tok_rows * TOP // (2 * experts_all))
    score_scale = HD ** (-0.5)
    (
        attention_weight_full,
        output_weight_full,
        adapter_down_weight,
        adapter_up_weight,
        first_norm_gain_full,
        second_norm_gain_full,
        router_weight_full,
    ) = (
        lax.all_gather(w_qkv, "fsdp", axis=1, tiled=True),
        lax.all_gather(w_out, "fsdp", axis=0, tiled=True),
        lax.all_gather(a_attn, "fsdp", axis=1, tiled=True),
        lax.all_gather(b_attn, "fsdp", axis=1, tiled=True),
        lax.all_gather(gain_attn, "fsdp", axis=0, tiled=True),
        lax.all_gather(gain_moe, "fsdp", axis=0, tiled=True),
        lax.all_gather(router, "fsdp", axis=0, tiled=True),
    )
    gain_one = first_norm_gain_full.astype(jnp.float32)
    gain_two = second_norm_gain_full.astype(jnp.float32)
    seg_local = segments[0]
    set_token = jnp.sum(
        jnp.where(seg_local[:, None] == jnp.arange(SETS)[None, :], doc_sets[0][None, :], 0), axis=1
    )
    document_set_mask = (set_token[:, None] == (jnp.arange(SR) // R)[None, :]).astype(jnp.float32)
    mask_half = document_set_mask.astype(jnp.bfloat16)
    hidden_f = hidden_in[0].astype(jnp.float32)
    first_normed_rows = (rms_scale(hidden_f) * gain_one).astype(jnp.bfloat16)
    attention_rank_branch = (
        jnp.einsum(
            "xj,zje->zxe",
            first_normed_rows,
            adapter_down_weight[:3],
            preferred_element_type=jnp.float32,
        )
        * document_set_mask[None]
    ).astype(jnp.bfloat16)
    projected = jnp.einsum(
        "td,pde->pte", first_normed_rows, attention_weight_full, preferred_element_type=jnp.float32
    ) + jnp.einsum(
        "nzv,nwv->nzw",
        attention_rank_branch,
        adapter_up_weight[:3],
        preferred_element_type=jnp.float32,
    )
    positions = shard_index * tok_rows + jnp.arange(tok_rows)
    cosine, sine_table = rope_tables(positions, HD)
    queries = rotate(projected[0].reshape(tok_rows, head_count, HD), cosine, sine_table).astype(
        jnp.bfloat16
    )
    keys_own = (
        rotate(projected[1].reshape(tok_rows, head_count, HD), cosine, sine_table)
        .astype(jnp.bfloat16)
        .reshape(tok_rows, model_width)
    )
    values_own = projected[2].astype(jnp.bfloat16)
    seg_own = seg_local.astype(jnp.bfloat16)
    run_max = jnp.full((head_count, tok_rows), MASKED, jnp.float32)
    key_piece = lax.all_gather(keys_own, "fsdp", axis=0, tiled=True)
    value_piece = lax.all_gather(values_own, "fsdp", axis=0, tiled=True)
    seg_piece = lax.all_gather(seg_own, "fsdp", axis=0, tiled=True)
    piece_rows = key_piece.shape[0]
    scores = (
        jnp.einsum(
            "qhd,khd->hqk",
            queries,
            key_piece.reshape(piece_rows, head_count, HD),
            preferred_element_type=jnp.float32,
        )
        * score_scale
    )
    same_doc = seg_local[:, None] == seg_piece.astype(jnp.int32)[None, :]
    scores = jnp.where(same_doc[None], scores, MASKED)
    new_max = jnp.maximum(run_max, jnp.max(scores, axis=2))
    exp_scores = jnp.exp(scores - new_max[:, :, None])
    new_sum = jnp.sum(exp_scores, axis=2)
    new_acc = jnp.einsum(
        "hqk,khd->qhd",
        exp_scores.astype(jnp.bfloat16),
        value_piece.reshape(piece_rows, head_count, HD),
        preferred_element_type=jnp.float32,
    )
    folded = (new_max, new_sum, new_acc)
    run_max, run_sum, run_acc = folded
    log_sum = run_max + jnp.log(run_sum)
    attended = run_acc / jnp.transpose(run_sum)[:, :, None]
    attention_rounded_rows = attended.reshape(tok_rows, model_width).astype(jnp.bfloat16)
    output_rank_branch = (
        jnp.dot(attention_rounded_rows, adapter_down_weight[3], preferred_element_type=jnp.float32)
        * document_set_mask
    ).astype(jnp.bfloat16)
    resid_one = hidden_f + (
        jnp.dot(attention_rounded_rows, output_weight_full, preferred_element_type=jnp.float32)
        + jnp.einsum(
            "nd,gd->ng",
            output_rank_branch,
            adapter_up_weight[3],
            preferred_element_type=jnp.float32,
        )
    )
    normed_two = (rms_scale(resid_one) * gain_two).astype(jnp.bfloat16)
    logits = jnp.dot(normed_two, router_weight_full, preferred_element_type=jnp.float32)
    my_routes = routes[0]
    gate_weights = jax.nn.softmax(jnp.take_along_axis(logits, my_routes, axis=1), axis=-1)
    flat_routes = my_routes.reshape(-1)
    one_hot = (flat_routes[:, None] == jnp.arange(experts_all)[None, :]).astype(jnp.int32)
    slot_index = jnp.sum((jnp.cumsum(one_hot, axis=0) - 1) * one_hot, axis=1)
    token_index = jnp.arange(tok_rows * TOP) // TOP
    send_rows = (
        jnp.zeros((experts_all, capacity, model_width), jnp.bfloat16)
        .at[flat_routes, slot_index]
        .set(normed_two[token_index])
    )
    send_sets = (
        jnp.zeros((experts_all, capacity), jnp.bfloat16)
        .at[flat_routes, slot_index]
        .set(set_token[token_index].astype(jnp.bfloat16))
    )
    rows_got = lax.all_to_all(
        send_rows.reshape(shard_count, local_experts, capacity, model_width),
        "fsdp",
        split_axis=0,
        concat_axis=0,
        tiled=True,
    )
    sets_got = lax.all_to_all(
        send_sets.reshape(shard_count, local_experts, capacity),
        "fsdp",
        split_axis=0,
        concat_axis=0,
        tiled=True,
    )
    slot_mask = (sets_got.astype(jnp.int32)[..., None] == jnp.arange(SR) // R).astype(jnp.float32)
    low_in = (
        jnp.einsum("necd,eids->necis", rows_got, exp_a_in, preferred_element_type=jnp.float32)
        * slot_mask[:, :, :, None, :]
    ).astype(jnp.bfloat16)
    gate_h = jnp.einsum(
        "necd,edf->necf", rows_got, w_gate, preferred_element_type=jnp.float32
    ) + jnp.einsum(
        "necs,esf->necf", low_in[:, :, :, 0], exp_b_in[:, 0], preferred_element_type=jnp.float32
    )
    up_h = jnp.einsum(
        "necd,edf->necf", rows_got, w_up, preferred_element_type=jnp.float32
    ) + jnp.einsum(
        "necs,esf->necf", low_in[:, :, :, 1], exp_b_in[:, 1], preferred_element_type=jnp.float32
    )
    activation = (jax.nn.silu(gate_h) * up_h).astype(jnp.bfloat16)
    low_down = (
        jnp.einsum("necf,efs->necs", activation, exp_a_down, preferred_element_type=jnp.float32)
        * slot_mask
    ).astype(jnp.bfloat16)
    expert_out = (
        jnp.einsum("necf,efd->necd", activation, w_down, preferred_element_type=jnp.float32)
        + jnp.einsum("necs,esd->necd", low_down, exp_b_down, preferred_element_type=jnp.float32)
    ).astype(jnp.bfloat16)
    expert_out, rows_got, slot_mask, low_in, gate_h, up_h, activation, low_down = (
        expert_out,
        rows_got,
        slot_mask,
        low_in,
        gate_h,
        up_h,
        activation,
        low_down,
    )
    returned = lax.all_to_all(expert_out, "fsdp", split_axis=0, concat_axis=0, tiled=True)
    route_out = (
        returned.reshape(experts_all, capacity, model_width)[flat_routes, slot_index]
        .reshape(tok_rows, TOP, model_width)
        .astype(jnp.float32)
    )
    layer_value = resid_one + jnp.sum(gate_weights[:, :, None] * route_out, axis=1)
    (
        attention_weight_full,
        output_weight_full,
        adapter_down_weight,
        adapter_up_weight,
        first_norm_gain_full,
        second_norm_gain_full,
        router_weight_full,
    ) = (
        lax.all_gather(w_qkv, "fsdp", axis=1, tiled=True),
        lax.all_gather(w_out, "fsdp", axis=0, tiled=True),
        lax.all_gather(a_attn, "fsdp", axis=1, tiled=True),
        lax.all_gather(b_attn, "fsdp", axis=1, tiled=True),
        lax.all_gather(gain_attn, "fsdp", axis=0, tiled=True),
        lax.all_gather(gain_moe, "fsdp", axis=0, tiled=True),
        lax.all_gather(router, "fsdp", axis=0, tiled=True),
    )
    gain_one = first_norm_gain_full.astype(jnp.float32)
    gain_two = second_norm_gain_full.astype(jnp.float32)
    upstream = cotangent[0].astype(jnp.float32)
    d_route = (gate_weights[:, :, None] * upstream[:, None, :]).astype(jnp.bfloat16)
    d_gates = jnp.sum(upstream[:, None, :] * route_out, axis=2)
    d_chosen = gate_weights * (d_gates - jnp.sum(gate_weights * d_gates, axis=1, keepdims=True))
    d_logits = jnp.sum(
        jnp.where(
            my_routes[:, :, None] == jnp.arange(experts_all)[None, None, :],
            d_chosen[:, :, None],
            0.0,
        ),
        axis=1,
    ).astype(jnp.bfloat16)
    send_grads = (
        jnp.zeros((experts_all, capacity, model_width), jnp.bfloat16)
        .at[flat_routes, slot_index]
        .set(d_route.reshape(tok_rows * TOP, model_width))
    )
    grads_got = lax.all_to_all(
        send_grads.reshape(shard_count, local_experts, capacity, model_width),
        "fsdp",
        split_axis=0,
        concat_axis=0,
        tiled=True,
    )
    slot_half = slot_mask.astype(jnp.bfloat16)
    d_low_down = (
        jnp.einsum(
            "necd,esd->necs", grads_got, exp_b_down, preferred_element_type=jnp.float32
        ).astype(jnp.bfloat16)
        * slot_half
    )
    d_activation = jnp.einsum(
        "necd,efd->necf", grads_got, w_down, preferred_element_type=jnp.float32
    ) + jnp.einsum("necs,efs->necf", d_low_down, exp_a_down, preferred_element_type=jnp.float32)
    silu_value, silu_pull = jax.vjp(
        lambda gate_in, up_in: jax.nn.silu(gate_in) * up_in, gate_h, up_h
    )
    d_gate_h, d_up_h = silu_pull(d_activation)
    d_gate_h = d_gate_h.astype(jnp.bfloat16)
    d_up_h = d_up_h.astype(jnp.bfloat16)
    d_both = jnp.stack([d_gate_h, d_up_h], axis=3)
    d_low_in = (
        jnp.einsum(
            "necif,eisf->necis", d_both, exp_b_in, preferred_element_type=jnp.float32
        ).astype(jnp.bfloat16)
        * slot_half[:, :, :, None, :]
    )
    d_rows = (
        jnp.einsum("necf,edf->necd", d_gate_h, w_gate, preferred_element_type=jnp.float32)
        + jnp.einsum("necf,edf->necd", d_up_h, w_up, preferred_element_type=jnp.float32)
        + jnp.einsum("necis,eids->necd", d_low_in, exp_a_in, preferred_element_type=jnp.float32)
    )
    returned_grads = lax.all_to_all(
        d_rows.astype(jnp.bfloat16), "fsdp", split_axis=0, concat_axis=0, tiled=True
    )
    g_exp_b_down = jnp.einsum(
        "necs,necd->esd", low_down, grads_got, preferred_element_type=jnp.float32
    )
    g_exp_a_down = jnp.einsum(
        "necf,necs->efs", activation, d_low_down, preferred_element_type=jnp.float32
    )
    g_exp_b_in = jnp.einsum("necis,necif->eisf", low_in, d_both, preferred_element_type=jnp.float32)
    g_exp_a_in = jnp.einsum(
        "necd,necis->eids", rows_got, d_low_in, preferred_element_type=jnp.float32
    )
    d_normed_two = jnp.sum(
        returned_grads.reshape(experts_all, capacity, model_width)[flat_routes, slot_index]
        .reshape(tok_rows, TOP, model_width)
        .astype(jnp.float32),
        axis=1,
    ) + jnp.einsum("te,de->td", d_logits, router_weight_full, preferred_element_type=jnp.float32)
    d_resid_one = upstream + norm_back(resid_one, gain_two, d_normed_two)
    branch_gradient = d_resid_one.astype(jnp.bfloat16)
    output_adapter_gradient = (
        jnp.dot(branch_gradient, adapter_up_weight[3], preferred_element_type=jnp.float32).astype(
            jnp.bfloat16
        )
        * mask_half
    )
    d_att = (
        jnp.einsum(
            "te,de->td", branch_gradient, output_weight_full, preferred_element_type=jnp.float32
        )
        + jnp.einsum(
            "cr,ar->ca",
            output_adapter_gradient,
            adapter_down_weight[3],
            preferred_element_type=jnp.float32,
        )
    ).astype(jnp.bfloat16)
    output_up_gradient = jnp.einsum(
        "ts,te->es", output_rank_branch, branch_gradient, preferred_element_type=jnp.float32
    )
    output_down_gradient = jnp.einsum(
        "td,ts->ds",
        attention_rounded_rows,
        output_adapter_gradient,
        preferred_element_type=jnp.float32,
    )
    d_att_heads = d_att.reshape(tok_rows, head_count, HD)
    delta_rows = jnp.transpose(jnp.sum(d_att_heads.astype(jnp.float32) * attended, axis=2))
    key_piece = lax.all_gather(keys_own, "fsdp", axis=0, tiled=True)
    value_piece = lax.all_gather(values_own, "fsdp", axis=0, tiled=True)
    seg_piece = lax.all_gather(seg_own, "fsdp", axis=0, tiled=True)
    piece_rows = key_piece.shape[0]
    key_heads = key_piece.reshape(piece_rows, head_count, HD)
    value_heads = value_piece.reshape(piece_rows, head_count, HD)
    scores = (
        jnp.einsum("qhd,khd->hqk", queries, key_heads, preferred_element_type=jnp.float32)
        * score_scale
    )
    same_doc = seg_local[:, None] == seg_piece.astype(jnp.int32)[None, :]
    scores = jnp.where(same_doc[None], scores, MASKED)
    soft_probs = jnp.exp(scores - log_sum[:, :, None])
    d_probs = jnp.einsum(
        "qhd,khd->hqk", d_att_heads, value_heads, preferred_element_type=jnp.float32
    )
    d_scores = (soft_probs * (d_probs - delta_rows[:, :, None])).astype(jnp.bfloat16)
    soft_probs, d_scores = (soft_probs, d_scores)
    d_query_part = jnp.einsum(
        "hqk,khd->qhd", d_scores, key_heads, preferred_element_type=jnp.float32
    )
    d_key_part = jnp.einsum(
        "hqk,qhd->khd", d_scores, queries, preferred_element_type=jnp.float32
    ).reshape(piece_rows, model_width)
    d_value_part = jnp.einsum(
        "hqk,qhd->khd",
        soft_probs.astype(jnp.bfloat16),
        d_att_heads,
        preferred_element_type=jnp.float32,
    ).reshape(piece_rows, model_width)
    back_state = (d_query_part, d_key_part, d_value_part)
    d_query, d_keys_all, d_values_all = back_state
    d_keys_mine, d_values_mine = (
        lax.psum_scatter(
            d_keys_all.astype(jnp.bfloat16), "fsdp", scatter_dimension=0, tiled=True
        ).astype(jnp.float32),
        lax.psum_scatter(
            d_values_all.astype(jnp.bfloat16), "fsdp", scatter_dimension=0, tiled=True
        ).astype(jnp.float32),
    )
    d_query_pre = (
        rotate(d_query * score_scale, cosine, -sine_table)
        .reshape(tok_rows, model_width)
        .astype(jnp.bfloat16)
    )
    d_key_pre = (
        rotate((d_keys_mine * score_scale).reshape(tok_rows, head_count, HD), cosine, -sine_table)
        .reshape(tok_rows, model_width)
        .astype(jnp.bfloat16)
    )
    projected_gradient = jnp.stack([d_query_pre, d_key_pre, d_values_mine.astype(jnp.bfloat16)])
    projection_adapter_gradient = (
        jnp.einsum(
            "jah,jho->jao",
            projected_gradient,
            adapter_up_weight[:3],
            preferred_element_type=jnp.float32,
        ).astype(jnp.bfloat16)
        * mask_half[None]
    )
    d_normed_one = jnp.einsum(
        "pte,pde->td", projected_gradient, attention_weight_full, preferred_element_type=jnp.float32
    ) + jnp.einsum(
        "czn,cvn->zv",
        projection_adapter_gradient,
        adapter_down_weight[:3],
        preferred_element_type=jnp.float32,
    )
    attention_up_gradient = jnp.einsum(
        "pts,pte->pes",
        attention_rank_branch,
        projected_gradient,
        preferred_element_type=jnp.float32,
    )
    attention_down_gradient = jnp.einsum(
        "td,pts->pds",
        first_normed_rows,
        projection_adapter_gradient,
        preferred_element_type=jnp.float32,
    )
    d_hidden = d_resid_one + norm_back(hidden_f, gain_one, d_normed_one)
    adapter_down_gradient = jnp.concatenate(
        [attention_down_gradient, output_down_gradient[None]], axis=0
    )
    adapter_up_gradient = jnp.concatenate([attention_up_gradient, output_up_gradient[None]], axis=0)
    part_down, part_up = (
        lax.psum_scatter(
            adapter_down_gradient.astype(jnp.bfloat16), "fsdp", scatter_dimension=1, tiled=True
        ).astype(jnp.float32),
        lax.psum_scatter(
            adapter_up_gradient.astype(jnp.bfloat16), "fsdp", scatter_dimension=1, tiled=True
        ).astype(jnp.float32),
    )
    summed = (
        lax.psum(part_down.astype(jnp.bfloat16), "rep").astype(jnp.float32),
        lax.psum(part_up.astype(jnp.bfloat16), "rep").astype(jnp.float32),
        lax.psum(g_exp_a_in.astype(jnp.bfloat16), "rep").astype(jnp.float32),
        lax.psum(g_exp_b_in.astype(jnp.bfloat16), "rep").astype(jnp.float32),
        lax.psum(g_exp_a_down.astype(jnp.bfloat16), "rep").astype(jnp.float32),
        lax.psum(g_exp_b_down.astype(jnp.bfloat16), "rep").astype(jnp.float32),
    )
    return (
        layer_value.astype(jnp.bfloat16)[None],
        d_hidden.astype(jnp.bfloat16)[None],
        summed[0],
        summed[1],
        summed[2],
        summed[3],
        summed[4],
        summed[5],
    )


EVERY = 8
TILE = 256
CUT = 512
VMEM_BYTES = 64000000


def mm(left, right):
    return jnp.dot(left, right, preferred_element_type=jnp.float32)


def mm_nt(left, right):
    return lax.dot_general(left, right, (((1,), (1,)), ((), ())), preferred_element_type=jnp.float32)


def whole():
    return pl.BlockSpec(memory_space=pltpu.VMEM)


def in_place():
    return pl.BlockSpec(memory_space=pl.ANY)


def scalars():
    return pl.BlockSpec(memory_space=pltpu.SMEM)


def params():
    return pltpu.CompilerParams(vmem_limit_bytes=VMEM_BYTES)


def cost(flops, moved):
    return pl.CostEstimate(flops=flops, bytes_accessed=moved, transcendentals=0)


def shape_of(shape, dtype=jnp.bfloat16):
    return jax.ShapeDtypeStruct(shape, dtype)


def swap(values, bits):
    return lax.ppermute(values, "fsdp", [(i, i ^ bits) for i in range(EVERY)])


def gather_relative(values):
    half = values.shape[0] // 2
    side, over = swap(values, 2), swap(values, 4)
    far = jnp.concatenate([swap(side[:half], 4), swap(over[half:], 2)], axis=0)
    mine = [values, side, over, far]
    other = [swap(block, 1) for block in mine]
    return [mine[0], other[0], mine[1], other[1], mine[2], other[2], mine[3], other[3]]


def add_half(left, right):
    return (left.astype(jnp.float32) + right.astype(jnp.float32)).astype(jnp.bfloat16)


def scatter_relative(even, odd):
    rows = even.shape[0] // 4
    half = rows // 2
    got = swap(odd, 1)

    def pair(start):
        return add_half(even[start : start + half], got[start : start + half])

    far_side = swap(pair(3 * rows), 2)
    far_over = swap(pair(3 * rows + half), 4)
    side_top = swap(pair(rows), 2)
    over_low = swap(pair(2 * rows + half), 4)
    side_low = swap(add_half(pair(rows + half), far_over), 2)
    over_top = swap(add_half(pair(2 * rows), far_side), 4)
    return even, got, side_top, side_low, over_top, over_low


def sum_pieces(even, got, side_top, side_low, over_top, over_low):
    f32 = jnp.float32
    top = side_top.astype(f32) + over_top.astype(f32)
    low = side_low.astype(f32) + over_low.astype(f32)
    return even.astype(f32) + got.astype(f32) + jnp.concatenate([top, low], axis=0)


def piece_specs(rows, columns, at=0):
    return [pl.BlockSpec((rows, columns), lambda i: (0, at))] * 2 + [
        pl.BlockSpec((rows // 2, columns), lambda i: (0, at))
    ] * 4


def rep_swap(values, bits):
    return lax.ppermute(values, "rep", [(i, i ^ bits) for i in range(4)])


def pick(pair, index):
    return lax.dynamic_index_in_dim(pair, index, 0, keepdims=False)


def joined(own, other, index):
    return jnp.where(index == 0, jnp.stack([own, other]), jnp.stack([other, own]))


def sum_rep(values):
    where = lax.axis_index("rep")
    low_bit, high_bit = where % 2, where // 2
    rows, columns = values.shape
    halves = values.reshape(2, rows // 2, columns)
    half = add_half(pick(halves, low_bit), rep_swap(pick(halves, 1 - low_bit), 1))
    parts = half.reshape(2, rows // 4, columns)
    part = add_half(pick(parts, high_bit), rep_swap(pick(parts, 1 - high_bit), 2))
    half = joined(part, rep_swap(part, 2), high_bit).reshape(rows // 2, columns)
    return joined(half, rep_swap(half, 1), low_bit).reshape(rows, columns)


def sum_rep_short(values):
    values = add_half(values, rep_swap(values, 1))
    return add_half(values, rep_swap(values, 2))


def turn(values, cosine, signed_sine):
    return values * cosine + pltpu.roll(values, HD // 2, 1) * signed_sine


def project_kernel(
    rows, width, wide,
    me_ref, gain_ref, mask_ref, cos_ref, sin_ref, up_ref, *refs,
):
    f32, bf16 = jnp.float32, jnp.bfloat16
    hidden_hbm, w_hbm, small_hbm = refs[:EVERY], refs[EVERY : 2 * EVERY], refs[2 * EVERY : 3 * EVERY]
    q_ref, k_ref, v_ref, normed_ref, low_ref, hidden, weight, down, sems = refs[3 * EVERY :]
    me = me_ref[0]
    copies = []
    for j in range(EVERY):
        at = pl.multiple_of((me ^ j) * wide, wide)
        copies.append(
            [
                pltpu.make_async_copy(hidden_hbm[j], hidden.at[j * rows : (j + 1) * rows], sems.at[j, 0]),
                pltpu.make_async_copy(
                    small_hbm[j].at[:, 0 : 3 * SR], down.at[pl.ds(at, wide), :], sems.at[j, 1]
                ),
            ]
            + [
                pltpu.make_async_copy(
                    w_hbm[j].at[i], weight.at[pl.ds(at, wide), i * wide : (i + 1) * wide], sems.at[j, 2 + i]
                )
                for i in range(3)
            ]
        )
    for group in copies:
        for item in group:
            item.start()
    for group in copies:
        for item in group:
            item.wait()
    gain = gain_ref[...]

    def chunk(c, _):
        at = pl.ds(pl.multiple_of(c * TILE, TILE), TILE)
        values = hidden[at, :].astype(f32)
        scale = lax.rsqrt(jnp.mean(values * values, axis=1, keepdims=True) + EPSILON)
        normed = (values * scale * gain).astype(bf16)
        normed_ref[at, :] = normed
        mask = mask_ref[at, :]
        low = (mm(normed, down[...]) * jnp.concatenate([mask] * 3, axis=1)).astype(bf16)
        low_ref[at, :] = low
        cosine, sine = cos_ref[at, :], sin_ref[at, :]
        for i, ref in enumerate((q_ref, k_ref, v_ref)):
            proj = mm(normed, weight[:, i * wide : (i + 1) * wide]) + mm_nt(
                low[:, i * SR : (i + 1) * SR], up_ref[i]
            )
            for h in range(wide // HD):
                part = proj[:, h * HD : (h + 1) * HD]
                ref[at, h * HD : (h + 1) * HD] = (turn(part, cosine, sine) if i < 2 else part).astype(bf16)
        return 0

    lax.fori_loop(0, EVERY * rows // TILE, chunk, 0)


def project(me, gain, mask, cosine, sine, up, hidden_blocks, w_blocks, small_blocks):
    rows, width = hidden_blocks[0].shape
    wide = width // EVERY
    tokens = rows * EVERY
    return pl.pallas_call(
        functools.partial(project_kernel, rows, width, wide),
        in_specs=[scalars()] + [whole()] * 5 + [in_place()] * (3 * EVERY),
        out_specs=[whole()] * 5,
        out_shape=[shape_of((tokens, wide))] * 3 + [shape_of((tokens, width)), shape_of((tokens, 3 * SR))],
        scratch_shapes=[
            pltpu.VMEM((tokens, width), jnp.bfloat16),
            pltpu.VMEM((width, 3 * wide), jnp.bfloat16),
            pltpu.VMEM((width, 3 * SR), jnp.bfloat16),
            pltpu.SemaphoreType.DMA((EVERY, 5)),
        ],
        compiler_params=params(),
        cost_estimate=cost(2 * tokens * width * 3 * (wide + SR), 16 << 20),
        name="project",
    )(me, gain, mask, cosine, sine, up, *hidden_blocks, *w_blocks, *small_blocks)


def attend_kernel(rows, q_ref, k_ref, v_ref, col_ref, row_ref, att_ref, lse_ref, *outs):
    f32, bf16 = jnp.float32, jnp.bfloat16
    scale = HD ** (-0.5)
    seg_row = row_ref[0:1, :]
    for h in range(q_ref.shape[1] // HD):
        lanes = slice(h * HD, (h + 1) * HD)
        for c in range(q_ref.shape[0] // TILE):
            at = slice(c * TILE, (c + 1) * TILE)
            scores = mm_nt(q_ref[at, lanes], k_ref[:, lanes]) * scale
            scores = jnp.where(col_ref[at, 0:1] == seg_row, scores, MASKED)
            top = jnp.max(scores, axis=1, keepdims=True)
            weights = jnp.exp(scores - top)
            total = jnp.sum(weights, axis=1, keepdims=True)
            att = mm(weights.astype(bf16), v_ref[:, lanes]) / total
            att_ref[at, lanes] = att
            log_sum = jnp.broadcast_to(top + jnp.log(total), (TILE, HD))
            lse_ref[h : h + 1, at] = log_sum.T[0:1, :]
            for part in range(TILE // rows):
                outs[c * (TILE // rows) + part][:, lanes] = att[part * rows : (part + 1) * rows].astype(bf16)


def attend(rows, queries, keys, values, seg_col, seg_row):
    tokens, wide = queries.shape
    return pl.pallas_call(
        functools.partial(attend_kernel, rows),
        in_specs=[whole()] * 5,
        out_specs=[whole()] * (2 + EVERY),
        out_shape=[shape_of((tokens, wide), jnp.float32), shape_of((8, tokens), jnp.float32)]
        + [shape_of((rows, wide))] * EVERY,
        compiler_params=params(),
        cost_estimate=cost(4 * tokens * tokens * wide, 4 << 20),
        name="attend",
    )(queries, keys, values, seg_col, seg_row)


def mix_kernel(
    wide,
    me_ref, hidden_ref, gain_ref, mask_ref, router_ref, named_ref, *refs,
):
    f32, bf16 = jnp.float32, jnp.bfloat16
    att_ref, w_hbm, small_hbm = refs[:EVERY], refs[EVERY : 2 * EVERY], refs[2 * EVERY : 3 * EVERY]
    resid_ref, normed_ref, low_ref, gates_ref, weight, down, up, sems = refs[3 * EVERY :]
    me = me_ref[0]
    width = hidden_ref.shape[1]
    copies = []
    for j in range(EVERY):
        at = pl.multiple_of((me ^ j) * wide, wide)
        here = slice(j * wide, (j + 1) * wide)
        copies.append(
            [
                pltpu.make_async_copy(small_hbm[j].at[:, 3 * SR : 4 * SR], down.at[here, :], sems.at[j, 0]),
                pltpu.make_async_copy(
                    small_hbm[j].at[:, 4 * SR : 5 * SR], up.at[pl.ds(at, wide), :], sems.at[j, 1]
                ),
                pltpu.make_async_copy(w_hbm[j], weight.at[here, :], sems.at[j, 2]),
            ]
        )
    for part in range(3):
        for group in copies:
            group[part].start()
    for part in range(2):
        for group in copies:
            group[part].wait()
    att = jnp.concatenate([ref[...] for ref in att_ref], axis=1)
    low = (mm(att, down[...]) * mask_ref[...]).astype(bf16)
    low_ref[...] = low
    total = mm_nt(low, up[...])
    for j in range(EVERY):
        copies[j][2].wait()
        total = total + mm(att_ref[j][...], weight[j * wide : (j + 1) * wide, :])
    resid = hidden_ref[...].astype(f32) + total
    resid_ref[...] = resid
    scale = lax.rsqrt(jnp.mean(resid * resid, axis=1, keepdims=True) + EPSILON)
    normed = (resid * scale * gain_ref[...]).astype(bf16)
    normed_ref[:, 0:width] = normed
    logits = jnp.where(named_ref[...] > 0.5, mm(normed, router_ref[...]), MASKED)
    share = jnp.exp(logits - jnp.max(logits, axis=1, keepdims=True)) * named_ref[...]
    gates = share / jnp.sum(share, axis=1, keepdims=True)
    gates_ref[...] = gates
    high = gates.astype(bf16).astype(f32)
    normed_ref[:, width : width + 128] = (high + pltpu.roll(gates - high, 64, 1)).astype(bf16)


def mix(me, hidden, gain, mask, router, named, att_blocks, w_blocks, small_blocks):
    rows, width = hidden.shape
    wide = width // EVERY
    f32 = jnp.float32
    return pl.pallas_call(
        functools.partial(mix_kernel, wide),
        in_specs=[scalars()] + [whole()] * 5 + [whole()] * EVERY + [in_place()] * (2 * EVERY),
        out_specs=[whole()] * 4,
        out_shape=[shape_of((rows, width), f32), shape_of((rows, width + 128)), shape_of((rows, SR)),
                   shape_of((rows, 128), f32)],
        scratch_shapes=[
            pltpu.VMEM((width, width), jnp.bfloat16),
            pltpu.VMEM((width, SR), jnp.bfloat16),
            pltpu.VMEM((width, SR), jnp.bfloat16),
            pltpu.SemaphoreType.DMA((EVERY, 3)),
        ],
        compiler_params=params(),
        cost_estimate=cost(2 * rows * width * width, 10 << 20),
        name="mix",
    )(me, hidden, gain, mask, router, named, *att_blocks, *w_blocks, *small_blocks)


def expert_kernel(k, first, width, hidden, blocks, mask_ref, pick_ref, *refs):
    f32, bf16 = jnp.float32, jnp.bfloat16
    rows_hbm, cot_hbm, refs = refs[:blocks], refs[blocks : 2 * blocks], refs[2 * blocks :]
    if not first:
        prev_out, prev_row, refs = refs[:2], refs[2:4], refs[4:]
    (
        w_gate_hbm, w_up_hbm, w_down_hbm, a_in_hbm, b_in_hbm, a_down_hbm, b_down_hbm,
        out_even, out_odd, row_even, row_odd, grad_ref,
        rows_s, cot_s, w_in, w_down, silu_s, slope_s,
        g_a_in, g_b_down, g_b_in, g_a_down, sems, block_sems,
    ) = refs
    out_refs, row_refs = (out_even, out_odd), (row_even, row_odd)
    step = pl.program_id(0)
    part = TILE // 2
    low_at, thin_at = 2 * hidden, width
    chunks = hidden // CUT
    early, late, given = [], [], []

    def copy(source, target, group):
        group.append(pltpu.make_async_copy(source, target, sems.at[len(early) + len(late)]))

    copy(a_in_hbm.at[k, 0], w_in.at[0:width, low_at : low_at + SR], early)
    copy(a_in_hbm.at[k, 1], w_in.at[0:width, low_at + SR : low_at + 2 * SR], early)
    copy(b_in_hbm.at[k, 0], w_in.at[width : width + SR, 0:hidden], early)
    copy(b_in_hbm.at[k, 1], w_in.at[width : width + SR, hidden:low_at], early)
    for j in range(chunks):
        at = slice(j * CUT, (j + 1) * CUT)
        copy(w_gate_hbm.at[k, :, at], w_in.at[0:width, at], early)
        copy(w_up_hbm.at[k, :, at], w_in.at[0:width, hidden + j * CUT : hidden + (j + 1) * CUT], early)
    copy(a_down_hbm.at[k], w_down.at[0:hidden, thin_at : thin_at + SR], late)
    copy(b_down_hbm.at[k], w_down.at[hidden : hidden + SR, 0:width], late)
    copy(w_down_hbm.at[k], w_down.at[0:hidden, 0:width], late)
    for j in range(blocks):
        at = slice(j * part, (j + 1) * part)
        given.append(pltpu.make_async_copy(rows_hbm[j], rows_s.at[at, :], block_sems.at[j, 0]))
        given.append(pltpu.make_async_copy(cot_hbm[j], cot_s.at[at, :], block_sems.at[j, 1]))

    def wait_for(group, when=0):
        @pl.when(step == when)
        def _():
            for item in group:
                item.wait()

    @pl.when(step == 0)
    def _():
        for item in given[0:4] + early + late + given[4:]:
            item.start()
        g_a_in[...] = jnp.zeros_like(g_a_in)
        g_b_down[...] = jnp.zeros_like(g_b_down)
        g_b_in[...] = jnp.zeros_like(g_b_in)
        g_a_down[...] = jnp.zeros_like(g_a_down)

    for i in range(blocks // 2):
        wait_for(given[4 * i : 4 * i + 4], i)
    wait_for(early[:2])
    at_rows = pl.ds(pl.multiple_of(step * TILE, TILE), TILE)
    mask = mask_ref[...]
    mask_two = jnp.concatenate([mask, mask], axis=1)
    rows = rows_s[at_rows, 0:width]
    gate = jnp.sum(rows_s[at_rows, width:].astype(f32) * pick_ref[0:1, :], axis=1, keepdims=True)
    low_in = (mm(rows, w_in[0:width, low_at:]) * mask_two).astype(bf16)
    rows_gate = jnp.concatenate([rows, low_in[:, :SR]], axis=1)
    rows_up = jnp.concatenate([rows, low_in[:, SR:]], axis=1)
    wait_for(early[2:4])
    act_parts = []
    for j in range(chunks):
        wait_for(early[4 + 2 * j : 6 + 2 * j])
        at = slice(j * CUT, (j + 1) * CUT)
        gate_h = mm(rows_gate, w_in[:, at])
        up_h = mm(rows_up, w_in[:, hidden + j * CUT : hidden + (j + 1) * CUT])
        share = 1.0 / (1.0 + jnp.exp(-gate_h))
        silu = gate_h * share
        silu_s[:, at] = silu
        slope_s[:, at] = up_h * (share * (1.0 + gate_h * (1.0 - share)))
        act_parts.append((silu * up_h).astype(bf16))
    act = jnp.concatenate(act_parts, axis=1)
    wait_for(late)

    low_down = (mm(act, w_down[0:hidden, thin_at:]) * mask).astype(bf16)
    act_low = jnp.concatenate([act, low_down], axis=1)
    d_gate = jnp.zeros((TILE, 1), f32)
    d_out_parts = []
    for j in range(width // CUT):
        at = slice(j * CUT, (j + 1) * CUT)
        out = mm(act_low, w_down[:, at]).astype(bf16).astype(f32)
        cot = cot_s[at_rows, at].astype(f32)
        d_out_parts.append((gate * cot).astype(bf16))
        weighted = gate * out
        for i in range(2):
            value = weighted[i * part : (i + 1) * part]
            if not first:
                value = value + prev_out[i][:, at].astype(f32)
            out_refs[i][:, at] = value.astype(bf16)
        d_gate = d_gate + jnp.sum(cot * out, axis=1, keepdims=True)
    high = d_gate.astype(bf16).astype(f32)
    extra = high * pick_ref[1:2, :] + (d_gate - high) * pick_ref[2:3, :]
    for i in range(2):
        value = extra[i * part : (i + 1) * part]
        if not first:
            value = value + prev_out[i][:, width:].astype(f32)
        out_refs[i][:, width:] = value.astype(bf16)

    mask_half = mask.astype(bf16)
    d_out = jnp.concatenate(d_out_parts, axis=1)
    d_low_down = mm_nt(d_out, w_down[hidden:, 0:width]).astype(bf16) * mask_half
    d_out_low = jnp.concatenate([d_out, d_low_down], axis=1)
    d_gate_parts, d_up_parts = [], []
    for j in range(chunks):
        at = slice(j * CUT, (j + 1) * CUT)
        d_act = mm_nt(d_out_low, w_down[at, :])
        d_gate_parts.append((d_act * slope_s[:, at]).astype(bf16))
        d_up_parts.append((d_act * silu_s[:, at]).astype(bf16))
    d_gate_h = jnp.concatenate(d_gate_parts, axis=1)
    d_up_h = jnp.concatenate(d_up_parts, axis=1)
    d_low_gate = mm_nt(d_gate_h, w_in[width:, 0:hidden]).astype(bf16) * mask_half
    d_low_up = mm_nt(d_up_h, w_in[width:, hidden:low_at]).astype(bf16) * mask_half
    d_low_in = jnp.concatenate([d_low_gate, d_low_up], axis=1)
    d_all = jnp.concatenate([d_gate_h, d_up_h, d_low_in], axis=1)
    d_low_in_t, low_down_t, low_in_t, d_low_down_t = d_low_in.T, low_down.T, low_in.T, d_low_down.T
    for j in range(width // CUT):
        at = slice(j * CUT, (j + 1) * CUT)
        d_row = mm_nt(d_all, w_in[at, :]).astype(bf16)
        for i in range(2):
            value = d_row[i * part : (i + 1) * part]
            if not first:
                value = (value.astype(f32) + prev_row[i][:, at].astype(f32)).astype(bf16)
            row_refs[i][:, at] = value
        g_a_in[:, at] += mm(d_low_in_t, rows[:, at])
        g_b_down[:, at] += mm(low_down_t, d_out[:, at])
    for j in range(chunks):
        at = slice(j * CUT, (j + 1) * CUT)
        g_b_in[0, :, at] += mm(low_in_t[:SR], d_gate_h[:, at])
        g_b_in[1, :, at] += mm(low_in_t[SR:], d_up_h[:, at])
        g_a_down[:, at] += mm(d_low_down_t, act[:, at])

    @pl.when(step == pl.num_programs(0) - 1)
    def _():
        grad_ref[0 : 2 * SR, :] = g_a_in[...].astype(bf16)
        grad_ref[2 * SR : 3 * SR, :] = g_b_down[...].astype(bf16)
        grad_ref[3 * SR : 4 * SR, 0:hidden] = g_b_in[0].astype(bf16)
        grad_ref[3 * SR : 4 * SR, hidden:] = g_b_in[1].astype(bf16)
        grad_ref[4 * SR : 4 * SR + SR // 2, 0:hidden] = g_a_down[: SR // 2].astype(bf16)
        grad_ref[4 * SR : 4 * SR + SR // 2, hidden:] = g_a_down[SR // 2 :].astype(bf16)


def expert_pass(k, rows, cot, mask, picks, prev, weights):
    f32, bf16 = jnp.float32, jnp.bfloat16
    blocks = len(rows)
    part, width = cot[0].shape
    hidden = weights[0].shape[2]
    tokens = blocks * part
    by_tile = lambda size, columns: pl.BlockSpec((size, columns), lambda i: (i, 0))
    in_specs = [by_tile(TILE, SR), pl.BlockSpec((8, 128), lambda i: (0, 0))] + [in_place()] * (2 * blocks)
    operands = [mask, picks, *rows, *cot]
    if prev is not None:
        in_specs += [by_tile(part, width + 128)] * 2 + [by_tile(part, width)] * 2
        operands += list(prev)
    in_specs += [in_place()] * 7
    flops = 2 * tokens * (6 * width * hidden + 9 * SR * (width + hidden))
    return pl.pallas_call(
        functools.partial(expert_kernel, k, prev is None, width, hidden, blocks),
        grid=(tokens // TILE,),
        in_specs=in_specs,
        out_specs=[by_tile(part, width + 128)] * 2
        + [by_tile(part, width)] * 2
        + [pl.BlockSpec((4 * SR + SR // 2, width), lambda i: (0, 0))],
        out_shape=[shape_of((tokens // 2, width + 128))] * 2
        + [shape_of((tokens // 2, width))] * 2
        + [shape_of((4 * SR + SR // 2, width))],
        scratch_shapes=[
            pltpu.VMEM((tokens, width + 128), bf16),
            pltpu.VMEM((tokens, width), bf16),
            pltpu.VMEM((width + SR, 2 * hidden + 2 * SR), bf16),
            pltpu.VMEM((hidden + SR, width + SR), bf16),
            pltpu.VMEM((TILE, hidden), f32),
            pltpu.VMEM((TILE, hidden), f32),
            pltpu.VMEM((2 * SR, width), f32),
            pltpu.VMEM((SR, width), f32),
            pltpu.VMEM((2, SR, hidden), f32),
            pltpu.VMEM((SR, hidden), f32),
            pltpu.SemaphoreType.DMA((7 + 2 * (hidden // CUT),)),
            pltpu.SemaphoreType.DMA((blocks, 2)),
        ],
        compiler_params=params(),
        cost_estimate=cost(flops, 40 << 20),
        name="expert",
    )(*operands, *weights)


def norm_grad(values, gain_row, upstream_grad):
    scale = lax.rsqrt(jnp.mean(values * values, axis=1, keepdims=True) + EPSILON)
    inner = gain_row * upstream_grad
    mean = jnp.mean(values * inner, axis=1, keepdims=True)
    return scale * inner - values * (scale * scale * scale * mean)


def unmix_kernel(
    wide,
    me_ref, resid_ref, cot_ref, gain_ref, mask_ref, router_ref, gates_ref, low_ref, *refs,
):
    f32, bf16 = jnp.float32, jnp.bfloat16
    row_pieces, out_pieces, extra_pieces, refs = refs[:6], refs[6:12], refs[12:18], refs[18:]
    att_ref, w_hbm, small_hbm = refs[:EVERY], refs[EVERY : 2 * EVERY], refs[2 * EVERY : 3 * EVERY]
    layer_ref, resid_grad_ref, grad_ref, *refs = refs[3 * EVERY :]
    att_grads, (weight, down, up, up_grad, sems) = refs[:EVERY], refs[EVERY:]
    me = me_ref[0]
    width = resid_ref.shape[1]
    copies = []
    for j in range(EVERY):
        at = pl.multiple_of((me ^ j) * wide, wide)
        here = slice(j * wide, (j + 1) * wide)
        copies.append(
            [
                pltpu.make_async_copy(
                    small_hbm[j].at[:, 4 * SR : 5 * SR], up.at[pl.ds(at, wide), :], sems.at[j, 1]
                ),
                pltpu.make_async_copy(small_hbm[j].at[:, 3 * SR : 4 * SR], down.at[here, :], sems.at[j, 0]),
                pltpu.make_async_copy(w_hbm[j], weight.at[here, :], sems.at[j, 2]),
            ]
        )
    for which in range(3):
        for group in copies:
            group[which].start()
    resid = resid_ref[...]
    layer_ref[...] = (resid + sum_pieces(*[ref[...] for ref in out_pieces])).astype(bf16)
    extra = sum_pieces(*[ref[...] for ref in extra_pieces])
    gates = gates_ref[...]
    d_gates = extra + pltpu.roll(extra, 64, 1)
    d_chosen = gates * (d_gates - jnp.sum(gates * d_gates, axis=1, keepdims=True))
    d_normed = sum_pieces(*[ref[...] for ref in row_pieces]) + mm_nt(d_chosen.astype(bf16), router_ref[...])
    d_resid = cot_ref[...].astype(f32) + norm_grad(resid, gain_ref[...], d_normed)
    resid_grad_ref[...] = d_resid
    branch = d_resid.astype(bf16)
    for group in copies:
        group[0].wait()
    d_low = (mm(branch, up[...]).astype(bf16).astype(f32) * mask_ref[...]).astype(bf16)
    low_t, d_low_t = low_ref[...].T, d_low.T
    up_grad[...] = mm(low_t, branch).astype(bf16)
    for group in copies:
        group[1].wait()
    for j in range(EVERY):
        here = slice(j * wide, (j + 1) * wide)
        copies[j][2].wait()
        att_grads[j][...] = (mm_nt(branch, weight[here, :]) + mm_nt(d_low, down[here, :])).astype(bf16)
        at = pl.multiple_of((me ^ j) * wide, wide)
        grad_ref[j * 2 * SR : j * 2 * SR + SR, :] = mm(d_low_t, att_ref[j][...]).astype(bf16)
        grad_ref[j * 2 * SR + SR : (j + 1) * 2 * SR, :] = up_grad[:, pl.ds(at, wide)]


def unmix(me, resid, cot, gain, mask, router, gates, low, row_pieces, out_pieces, att_blocks, w_blocks, small_blocks):
    rows, width = resid.shape
    wide = width // EVERY
    return pl.pallas_call(
        functools.partial(unmix_kernel, wide),
        grid=(1,),
        in_specs=[scalars()]
        + [whole()] * 7
        + piece_specs(rows, width)
        + piece_specs(rows, width)
        + piece_specs(rows, 128, width // 128)
        + [whole()] * EVERY
        + [in_place()] * (2 * EVERY),
        out_specs=[whole()] * (3 + EVERY),
        out_shape=[
            shape_of((rows, width)),
            shape_of((rows, width), jnp.float32),
            shape_of((EVERY * 2 * SR, wide)),
        ]
        + [shape_of((rows, wide))] * EVERY,
        scratch_shapes=[
            pltpu.VMEM((width, width), jnp.bfloat16),
            pltpu.VMEM((width, SR), jnp.bfloat16),
            pltpu.VMEM((width, SR), jnp.bfloat16),
            pltpu.VMEM((SR, width), jnp.bfloat16),
            pltpu.SemaphoreType.DMA((EVERY, 3)),
        ],
        compiler_params=params(),
        cost_estimate=cost(2 * rows * width * width, 14 << 20),
        name="unmix",
    )(me, resid, cot, gain, mask, router, gates, low, *row_pieces, *out_pieces, *out_pieces,
      *att_blocks, *w_blocks, *small_blocks)


def attend_back_kernel(
    rows, wide,
    me_ref, q_ref, k_ref, v_ref, att_ref, lse_ref, col_ref, row_ref, cos_ref, sin_ref, low_ref, mask_ref, up_ref,
    *refs,
):
    f32, bf16 = jnp.float32, jnp.bfloat16
    d_att_blocks, refs = refs[:EVERY], refs[EVERY:]
    normed_hbm, small_hbm, refs = refs[0], refs[1 : 1 + EVERY], refs[1 + EVERY :]
    d_proj_ref, d_low_ref, down_grad_ref, up_grad_ref, d_att, normed, down, sems = refs
    tokens = q_ref.shape[0]
    scale = HD ** (-0.5)
    me = me_ref[0]
    bring = pltpu.make_async_copy(normed_hbm, normed, sems.at[0])
    bring.start()
    for j in range(EVERY):
        d_att[j * rows : (j + 1) * rows, :] = d_att_blocks[j][...]
    seg_row = row_ref[0:1, :]
    for h in range(wide // HD):
        lanes = slice(h * HD, (h + 1) * HD)
        delta = jnp.sum(d_att[:, lanes].astype(f32) * att_ref[:, lanes], axis=1, keepdims=True)
        delta = jnp.broadcast_to(delta, (tokens, HD)).T[0:1, :]
        log_sum = lse_ref[h : h + 1, :]
        d_query = jnp.zeros((tokens, HD), f32)
        for c in range(tokens // TILE):
            at = slice(c * TILE, (c + 1) * TILE)
            scores = mm_nt(k_ref[at, lanes], q_ref[:, lanes]) * scale
            same = col_ref[at, 0:1] == seg_row
            probs = jnp.where(same, jnp.exp(jnp.where(same, scores - log_sum, 0.0)), 0.0)
            d_probs = mm_nt(v_ref[at, lanes], d_att[:, lanes])
            d_scores = (probs * (d_probs - delta)).astype(bf16)
            d_value = mm(probs.astype(bf16), d_att[:, lanes])
            d_key = mm(d_scores, q_ref[:, lanes])
            d_query = d_query + mm(d_scores.T, k_ref[at, lanes])
            d_proj_ref[at, wide + h * HD : wide + (h + 1) * HD] = turn(
                d_key * scale, cos_ref[at, :], -sin_ref[at, :]
            ).astype(bf16)
            d_proj_ref[at, 2 * wide + h * HD : 2 * wide + (h + 1) * HD] = d_value.astype(bf16)
        d_proj_ref[:, lanes] = turn(d_query * scale, cos_ref[...], -sin_ref[...]).astype(bf16)
    for i in range(3):
        part = d_proj_ref[:, i * wide : (i + 1) * wide]
        d_low = (mm(part, up_ref[i]).astype(bf16).astype(f32) * mask_ref[...]).astype(bf16)
        d_low_ref[:, i * SR : (i + 1) * SR] = d_low
        up_grad_ref[i * SR : (i + 1) * SR, :] = mm(low_ref[:, i * SR : (i + 1) * SR].T, part).astype(bf16)
    d_low_t = d_low_ref[...].T
    bring.wait()
    for j in range(EVERY):
        at = pl.multiple_of((me ^ j) * wide, wide)
        down_grad_ref[j * 3 * SR : (j + 1) * 3 * SR, :] = mm(d_low_t, normed[:, pl.ds(at, wide)]).astype(bf16)


def attend_back(rows, me, q, k, v, att, lse, seg_col, seg_row, cosine, sine, low, mask, up, d_att_blocks, normed, small):
    tokens, wide = q.shape
    width = wide * EVERY
    return pl.pallas_call(
        functools.partial(attend_back_kernel, rows, wide),
        in_specs=[scalars()] + [whole()] * 12 + [whole()] * EVERY + [in_place()] * (1 + EVERY),
        out_specs=[whole()] * 4,
        out_shape=[
            shape_of((tokens, 3 * wide)),
            shape_of((tokens, 3 * SR)),
            shape_of((EVERY * 3 * SR, wide)),
            shape_of((3 * SR, wide)),
        ],
        scratch_shapes=[
            pltpu.VMEM((tokens, wide), jnp.bfloat16),
            pltpu.VMEM((tokens, width), jnp.bfloat16),
            pltpu.VMEM((16, 128), jnp.bfloat16),
            pltpu.SemaphoreType.DMA((2,)),
        ],
        compiler_params=params(),
        cost_estimate=cost(10 * tokens * tokens * wide, 10 << 20),
        name="attend_back",
    )(me, q, k, v, att, lse, seg_col, seg_row, cosine, sine, low, mask, up, *d_att_blocks, normed, *small)


def unproject_kernel(rows, wide, me_ref, proj_ref, low_ref, *refs):
    bf16 = jnp.bfloat16
    w_hbm, small_hbm, (even_ref, odd_ref, weight, sems) = refs[:EVERY], refs[EVERY : 2 * EVERY], refs[2 * EVERY :]
    me = me_ref[0]
    copies = []
    for j in range(EVERY):
        at = pl.multiple_of((me ^ j) * wide, wide)
        for i in range(3):
            copies.append(
                pltpu.make_async_copy(
                    w_hbm[j].at[i], weight.at[pl.ds(at, wide), i * wide : (i + 1) * wide], sems.at[j, i]
                )
            )
        copies.append(
            pltpu.make_async_copy(
                small_hbm[j].at[:, 0 : 3 * SR],
                weight.at[pl.ds(at, wide), 3 * wide : 3 * wide + 3 * SR],
                sems.at[j, 3],
            )
        )
    for item in copies:
        item.start()
    for item in copies:
        item.wait()

    def chunk(c, _):
        at = pl.ds(pl.multiple_of(c * TILE, TILE), TILE)
        here = pl.ds(pl.multiple_of(c * rows, rows), rows)
        both = jnp.concatenate([proj_ref[at, :], low_ref[at, :]], axis=1)
        for j in range(EVERY * wide // CUT):
            lanes = slice(j * CUT, (j + 1) * CUT)
            value = mm_nt(both, weight[lanes, :]).astype(bf16)
            even_ref[here, lanes] = value[:rows]
            odd_ref[here, lanes] = value[rows:]
        return 0

    lax.fori_loop(0, EVERY * rows // TILE, chunk, 0)


def unproject(rows, me, d_proj, d_low, w_blocks, small_blocks):
    tokens = d_proj.shape[0]
    wide = d_proj.shape[1] // 3
    width = wide * EVERY
    return pl.pallas_call(
        functools.partial(unproject_kernel, rows, wide),
        in_specs=[scalars()] + [whole()] * 2 + [in_place()] * (2 * EVERY),
        out_specs=[whole()] * 2,
        out_shape=[shape_of((tokens // 2, width))] * 2,
        scratch_shapes=[
            pltpu.VMEM((width, 3 * wide + 3 * SR), jnp.bfloat16),
            pltpu.SemaphoreType.DMA((EVERY, 4)),
        ],
        compiler_params=params(),
        cost_estimate=cost(2 * tokens * width * 3 * (wide + SR), 12 << 20),
        name="unproject",
    )(me, d_proj, d_low, *w_blocks, *small_blocks)


def finish_kernel(hidden_ref, gain_ref, resid_grad_ref, *refs):
    pieces, out_ref = refs[:6], refs[6]
    d_normed = sum_pieces(*[ref[...] for ref in pieces])
    back = norm_grad(hidden_ref[...].astype(jnp.float32), gain_ref[...], d_normed)
    out_ref[...] = (resid_grad_ref[...] + back).astype(jnp.bfloat16)


def finish(hidden, gain, resid_grad, pieces):
    rows, width = hidden.shape
    return pl.pallas_call(
        finish_kernel,
        grid=(1,),
        in_specs=[whole()] * 3 + piece_specs(rows, width),
        out_specs=whole(),
        out_shape=shape_of((rows, width)),
        compiler_params=params(),
        cost_estimate=cost(20 * rows * width, 6 << 20),
        name="finish",
    )(hidden, gain, resid_grad, *pieces)


def set_masks(seg, doc_sets):
    set_token = jnp.sum(
        jnp.where(seg[:, None] == jnp.arange(SETS)[None, :], doc_sets[0][None, :], 0), axis=1
    )
    return (set_token[:, None] == (jnp.arange(SR) // R)[None, :]).astype(jnp.float32)


def after(value, gate):
    return lax.optimization_barrier((value, gate))[0]


def split_layer(
    hidden_in,
    segments,
    routes,
    doc_sets,
    cotangent,
    w_qkv,
    w_out,
    gain_attn,
    gain_moe,
    router,
    w_gate,
    w_up,
    w_down,
    a_attn,
    b_attn,
    exp_a_in,
    exp_b_in,
    exp_a_down,
    exp_b_down,
):
    bf16, f32 = jnp.bfloat16, jnp.float32
    index = lax.axis_index("fsdp")
    me = index.astype(jnp.int32).reshape(1)
    hidden, upstream = hidden_in[0], cotangent[0]
    rows, width = hidden.shape
    wide = width // EVERY
    experts_all = w_gate.shape[0] * EVERY
    order = index ^ jnp.arange(EVERY)

    thin = jnp.concatenate([gain_attn, gain_moe, router.reshape(-1)])
    thin = lax.all_to_all(
        jnp.broadcast_to(thin[None], (EVERY, thin.shape[0])), "fsdp", split_axis=0, concat_axis=0, tiled=True
    )
    gain_one = thin[:, :wide].reshape(1, width).astype(f32)
    gain_two = thin[:, wide : 2 * wide].reshape(1, width).astype(f32)
    router_all = thin[:, 2 * wide :].reshape(width, experts_all)
    router_all = jnp.pad(router_all, ((0, 0), (0, 128 - experts_all)))
    seg_own = segments[0].astype(bf16)
    seg_blocks = [seg_own] + [swap(seg_own, j) for j in range(1, EVERY)]
    seg_all = jnp.concatenate(seg_blocks).astype(jnp.int32)
    mask = set_masks(seg_all, doc_sets)
    mask_own = mask[:rows]
    seg_row = jnp.broadcast_to(seg_all.astype(f32)[None, :], (8, rows * EVERY))
    seg_col = jnp.broadcast_to(seg_all.astype(f32)[:, None], (rows * EVERY, 128))
    positions = (order[:, None] * rows + jnp.arange(rows)[None, :]).reshape(-1)
    cosine, sine = rope_tables(positions, HD)
    cosine, sine = jnp.concatenate([cosine, cosine], axis=1), jnp.concatenate([-sine, sine], axis=1)
    lanes = jnp.arange(128)
    named = jnp.any(routes[0][:, :, None] == lanes[None, None, :], axis=1).astype(f32)

    hidden_blocks = gather_relative(hidden)
    w_blocks = [
        lax.dynamic_slice_in_dim(w_qkv, order[j] * wide, wide, axis=2) for j in range(EVERY)
    ]
    w_blocks = [w_blocks[0]] + [swap(w_blocks[j], j) for j in range(1, EVERY)]
    small = jnp.concatenate([a_attn[0], a_attn[1], a_attn[2], a_attn[3], b_attn[3]], axis=1)
    small_blocks = gather_relative(small)

    queries, keys, values, normed_one, low_qkv = project(
        me, gain_one, mask, cosine, sine, b_attn, hidden_blocks, w_blocks, small_blocks
    )
    out_blocks = gather_relative(after(w_out, (hidden_blocks[6], w_blocks[7], w_blocks[6])))
    att, lse, *att_blocks = attend(rows, queries, keys, values, seg_col, seg_row)
    att_blocks = [att_blocks[0]] + [swap(att_blocks[j], j) for j in range(1, EVERY)]
    resid_one, normed_own, low_out, gates_own = mix(
        me, hidden, gain_two, mask_own, router_all, named, att_blocks, out_blocks, small_blocks
    )
    cot_blocks = gather_relative(after(upstream, out_blocks[6]))
    normed_blocks = gather_relative(normed_own)

    weights = (w_gate, w_up, w_down, exp_a_in, exp_b_in, exp_a_down, exp_b_down)
    state, sums = None, []
    for k in range(w_gate.shape[0]):
        high = (lanes == 2 * index + k).astype(f32)
        low = (lanes == 2 * index + k + 64).astype(f32)
        picks = jnp.stack([high + low, high, low] + [jnp.zeros_like(high)] * 5)
        *state, grads = expert_pass(k, normed_blocks, cot_blocks, mask, picks, state, weights)
        sums.append(sum_rep(grads).astype(f32))
    out_even, out_odd, row_even, row_odd = state
    row_pieces = scatter_relative(row_even, row_odd)
    out_pieces = scatter_relative(out_even, out_odd)
    layer_out, d_resid, out_grads, *d_att_blocks = unmix(
        me, resid_one, upstream, gain_two, mask_own, router_all, gates_own, low_out,
        row_pieces, out_pieces, att_blocks, out_blocks, small_blocks,
    )
    d_att_blocks = [d_att_blocks[0]] + [swap(d_att_blocks[j], j) for j in range(1, EVERY)]
    out_grads = out_grads.reshape(EVERY, 2 * SR, wide)
    d_proj, d_low, down_grads, up_grads = attend_back(
        rows, me, queries, keys, values, att, lse, seg_col, seg_row, cosine, sine, low_qkv, mask, b_attn,
        d_att_blocks, normed_one, small_blocks,
    )
    even, odd = unproject(rows, me, d_proj, d_low, w_blocks, small_blocks)
    pieces = scatter_relative(even, odd)
    grad_in = finish(hidden, gain_one, d_resid, pieces)

    def by_parity(values):
        pairs = values.reshape(4, 2, values.shape[0] // EVERY, wide)
        return pairs[:, 0].reshape(-1, wide), pairs[:, 1].reshape(-1, wide)

    def own_sum(values):
        size = values.shape[0] // EVERY
        even, got, *rest = scatter_relative(*by_parity(values))
        return sum_pieces(even[:size], got[:size], *rest).astype(bf16)

    out_sum = own_sum(out_grads.reshape(-1, wide))
    early = sum_rep_short(jnp.concatenate([out_sum, up_grads], axis=0))
    late = sum_rep_short(own_sum(down_grads))
    early, late = early.astype(f32).T, late.astype(f32).T
    cut = lambda values, i: values[:, i * SR : (i + 1) * SR]
    grad_a = jnp.stack([cut(late, 0), cut(late, 1), cut(late, 2), cut(early, 0)])
    grad_b = jnp.stack([cut(early, 2), cut(early, 3), cut(early, 4), cut(early, 1)])
    at = [2 * SR, 3 * SR, 4 * SR]
    half = w_gate.shape[2]
    return (
        layer_out[None],
        grad_in[None],
        grad_a,
        grad_b,
        jnp.stack([g[: at[0]].reshape(2, SR, width).transpose(0, 2, 1) for g in sums]),
        jnp.stack([jnp.stack([g[at[1] : at[2], :half], g[at[1] : at[2], half:]]) for g in sums]),
        jnp.stack([jnp.concatenate([g[at[2] :, :half], g[at[2] :, half:]]).T for g in sums]),
        jnp.stack([g[at[0] : at[1]] for g in sums]),
    )


def solution(mesh):
    shape = dict(mesh.shape)
    shards = split_layer if shape == {"rep": 4, "fsdp": EVERY} else gathered_layer
    return jax.shard_map(
        shards,
        mesh=mesh,
        in_specs=(
            P("rep", "fsdp", None),
            P("rep", "fsdp"),
            P("rep", "fsdp", None),
            P("rep", None),
            P("rep", "fsdp", None),
            P(None, "fsdp", None),
            P("fsdp", None),
            P("fsdp"),
            P("fsdp"),
            P("fsdp", None),
            P("fsdp", None, None),
            P("fsdp", None, None),
            P("fsdp", None, None),
            P(None, "fsdp", None),
            P(None, "fsdp", None),
            P("fsdp", None, None, None),
            P("fsdp", None, None, None),
            P("fsdp", None, None),
            P("fsdp", None, None),
        ),
        out_specs=(
            P("rep", "fsdp", None),
            P("rep", "fsdp", None),
            P(None, "fsdp", None),
            P(None, "fsdp", None),
            P("fsdp", None, None, None),
            P("fsdp", None, None, None),
            P("fsdp", None, None),
            P("fsdp", None, None),
        ),
        check_vma=False,
    )
```

```python
import functools
import math

import jax
import jax.numpy as jnp
from jax import lax
from jax.experimental import pallas as pl
from jax.experimental.pallas import tpu as pltpu
from jax.sharding import PartitionSpec as P

HD = 128
TOP = 8
R = 16
SETS = 8
SR = 128


EPSILON = 1e-05
MASKED = -1e30


def rms_scale(values):
    return values * lax.rsqrt(jnp.mean(values * values, axis=-1, keepdims=True) + EPSILON)


def norm_back(values, gain_row, upstream_grad):
    result, pull_back = jax.vjp(lambda inner_rows: rms_scale(inner_rows) * gain_row, values)
    return pull_back(upstream_grad)[0]


def rope_tables(positions, head_size):
    half_size = head_size // 2
    inv_freq = jnp.exp(
        jnp.arange(half_size, dtype=jnp.float32) * (-2.0 * math.log(10000.0) / head_size)
    )
    angles = positions.astype(jnp.float32)[:, None] * inv_freq[None, :]
    return (jnp.cos(angles), jnp.sin(angles))


def rotate(values, cosine, sine_table):
    half_size = values.shape[-1] // 2
    front_half = values[..., :half_size]
    back_half = values[..., half_size:]
    cos_rows = cosine[:, None, :]
    sin_rows = sine_table[:, None, :]
    return jnp.concatenate(
        [
            front_half * cos_rows - back_half * sin_rows,
            back_half * cos_rows + front_half * sin_rows,
        ],
        axis=-1,
    )


def gathered_layer(
    hidden_in,
    segments,
    routes,
    doc_sets,
    cotangent,
    w_qkv,
    w_out,
    gain_attn,
    gain_moe,
    router,
    w_gate,
    w_up,
    w_down,
    a_attn,
    b_attn,
    exp_a_in,
    exp_b_in,
    exp_a_down,
    exp_b_down,
):
    shard_count = lax.axis_size("fsdp")
    shard_index = lax.axis_index("fsdp")
    tok_rows = hidden_in.shape[1]
    model_width = hidden_in.shape[2]
    head_count = model_width // HD
    local_experts = w_gate.shape[0]
    experts_all = local_experts * shard_count
    capacity = max(2, 3 * tok_rows * TOP // (2 * experts_all))
    score_scale = HD ** (-0.5)
    (
        attention_weight_full,
        output_weight_full,
        adapter_down_weight,
        adapter_up_weight,
        first_norm_gain_full,
        second_norm_gain_full,
        router_weight_full,
    ) = (
        lax.all_gather(w_qkv, "fsdp", axis=1, tiled=True),
        lax.all_gather(w_out, "fsdp", axis=0, tiled=True),
        lax.all_gather(a_attn, "fsdp", axis=1, tiled=True),
        lax.all_gather(b_attn, "fsdp", axis=1, tiled=True),
        lax.all_gather(gain_attn, "fsdp", axis=0, tiled=True),
        lax.all_gather(gain_moe, "fsdp", axis=0, tiled=True),
        lax.all_gather(router, "fsdp", axis=0, tiled=True),
    )
    gain_one = first_norm_gain_full.astype(jnp.float32)
    gain_two = second_norm_gain_full.astype(jnp.float32)
    seg_local = segments[0]
    set_token = jnp.sum(
        jnp.where(seg_local[:, None] == jnp.arange(SETS)[None, :], doc_sets[0][None, :], 0), axis=1
    )
    document_set_mask = (set_token[:, None] == (jnp.arange(SR) // R)[None, :]).astype(jnp.float32)
    mask_half = document_set_mask.astype(jnp.bfloat16)
    hidden_f = hidden_in[0].astype(jnp.float32)
    first_normed_rows = (rms_scale(hidden_f) * gain_one).astype(jnp.bfloat16)
    attention_rank_branch = (
        jnp.einsum(
            "xj,zje->zxe",
            first_normed_rows,
            adapter_down_weight[:3],
            preferred_element_type=jnp.float32,
        )
        * document_set_mask[None]
    ).astype(jnp.bfloat16)
    projected = jnp.einsum(
        "td,pde->pte", first_normed_rows, attention_weight_full, preferred_element_type=jnp.float32
    ) + jnp.einsum(
        "nzv,nwv->nzw",
        attention_rank_branch,
        adapter_up_weight[:3],
        preferred_element_type=jnp.float32,
    )
    positions = shard_index * tok_rows + jnp.arange(tok_rows)
    cosine, sine_table = rope_tables(positions, HD)
    queries = rotate(projected[0].reshape(tok_rows, head_count, HD), cosine, sine_table).astype(
        jnp.bfloat16
    )
    keys_own = (
        rotate(projected[1].reshape(tok_rows, head_count, HD), cosine, sine_table)
        .astype(jnp.bfloat16)
        .reshape(tok_rows, model_width)
    )
    values_own = projected[2].astype(jnp.bfloat16)
    seg_own = seg_local.astype(jnp.bfloat16)
    run_max = jnp.full((head_count, tok_rows), MASKED, jnp.float32)
    key_piece = lax.all_gather(keys_own, "fsdp", axis=0, tiled=True)
    value_piece = lax.all_gather(values_own, "fsdp", axis=0, tiled=True)
    seg_piece = lax.all_gather(seg_own, "fsdp", axis=0, tiled=True)
    piece_rows = key_piece.shape[0]
    scores = (
        jnp.einsum(
            "qhd,khd->hqk",
            queries,
            key_piece.reshape(piece_rows, head_count, HD),
            preferred_element_type=jnp.float32,
        )
        * score_scale
    )
    same_doc = seg_local[:, None] == seg_piece.astype(jnp.int32)[None, :]
    scores = jnp.where(same_doc[None], scores, MASKED)
    new_max = jnp.maximum(run_max, jnp.max(scores, axis=2))
    exp_scores = jnp.exp(scores - new_max[:, :, None])
    new_sum = jnp.sum(exp_scores, axis=2)
    new_acc = jnp.einsum(
        "hqk,khd->qhd",
        exp_scores.astype(jnp.bfloat16),
        value_piece.reshape(piece_rows, head_count, HD),
        preferred_element_type=jnp.float32,
    )
    folded = (new_max, new_sum, new_acc)
    run_max, run_sum, run_acc = folded
    log_sum = run_max + jnp.log(run_sum)
    attended = run_acc / jnp.transpose(run_sum)[:, :, None]
    attention_rounded_rows = attended.reshape(tok_rows, model_width).astype(jnp.bfloat16)
    output_rank_branch = (
        jnp.dot(attention_rounded_rows, adapter_down_weight[3], preferred_element_type=jnp.float32)
        * document_set_mask
    ).astype(jnp.bfloat16)
    resid_one = hidden_f + (
        jnp.dot(attention_rounded_rows, output_weight_full, preferred_element_type=jnp.float32)
        + jnp.einsum(
            "nd,gd->ng",
            output_rank_branch,
            adapter_up_weight[3],
            preferred_element_type=jnp.float32,
        )
    )
    normed_two = (rms_scale(resid_one) * gain_two).astype(jnp.bfloat16)
    logits = jnp.dot(normed_two, router_weight_full, preferred_element_type=jnp.float32)
    my_routes = routes[0]
    gate_weights = jax.nn.softmax(jnp.take_along_axis(logits, my_routes, axis=1), axis=-1)
    flat_routes = my_routes.reshape(-1)
    one_hot = (flat_routes[:, None] == jnp.arange(experts_all)[None, :]).astype(jnp.int32)
    slot_index = jnp.sum((jnp.cumsum(one_hot, axis=0) - 1) * one_hot, axis=1)
    token_index = jnp.arange(tok_rows * TOP) // TOP
    send_rows = (
        jnp.zeros((experts_all, capacity, model_width), jnp.bfloat16)
        .at[flat_routes, slot_index]
        .set(normed_two[token_index])
    )
    send_sets = (
        jnp.zeros((experts_all, capacity), jnp.bfloat16)
        .at[flat_routes, slot_index]
        .set(set_token[token_index].astype(jnp.bfloat16))
    )
    rows_got = lax.all_to_all(
        send_rows.reshape(shard_count, local_experts, capacity, model_width),
        "fsdp",
        split_axis=0,
        concat_axis=0,
        tiled=True,
    )
    sets_got = lax.all_to_all(
        send_sets.reshape(shard_count, local_experts, capacity),
        "fsdp",
        split_axis=0,
        concat_axis=0,
        tiled=True,
    )
    slot_mask = (sets_got.astype(jnp.int32)[..., None] == jnp.arange(SR) // R).astype(jnp.float32)
    low_in = (
        jnp.einsum("necd,eids->necis", rows_got, exp_a_in, preferred_element_type=jnp.float32)
        * slot_mask[:, :, :, None, :]
    ).astype(jnp.bfloat16)
    gate_h = jnp.einsum(
        "necd,edf->necf", rows_got, w_gate, preferred_element_type=jnp.float32
    ) + jnp.einsum(
        "necs,esf->necf", low_in[:, :, :, 0], exp_b_in[:, 0], preferred_element_type=jnp.float32
    )
    up_h = jnp.einsum(
        "necd,edf->necf", rows_got, w_up, preferred_element_type=jnp.float32
    ) + jnp.einsum(
        "necs,esf->necf", low_in[:, :, :, 1], exp_b_in[:, 1], preferred_element_type=jnp.float32
    )
    activation = (jax.nn.silu(gate_h) * up_h).astype(jnp.bfloat16)
    low_down = (
        jnp.einsum("necf,efs->necs", activation, exp_a_down, preferred_element_type=jnp.float32)
        * slot_mask
    ).astype(jnp.bfloat16)
    expert_out = (
        jnp.einsum("necf,efd->necd", activation, w_down, preferred_element_type=jnp.float32)
        + jnp.einsum("necs,esd->necd", low_down, exp_b_down, preferred_element_type=jnp.float32)
    ).astype(jnp.bfloat16)
    expert_out, rows_got, slot_mask, low_in, gate_h, up_h, activation, low_down = (
        expert_out,
        rows_got,
        slot_mask,
        low_in,
        gate_h,
        up_h,
        activation,
        low_down,
    )
    returned = lax.all_to_all(expert_out, "fsdp", split_axis=0, concat_axis=0, tiled=True)
    route_out = (
        returned.reshape(experts_all, capacity, model_width)[flat_routes, slot_index]
        .reshape(tok_rows, TOP, model_width)
        .astype(jnp.float32)
    )
    layer_value = resid_one + jnp.sum(gate_weights[:, :, None] * route_out, axis=1)
    (
        attention_weight_full,
        output_weight_full,
        adapter_down_weight,
        adapter_up_weight,
        first_norm_gain_full,
        second_norm_gain_full,
        router_weight_full,
    ) = (
        lax.all_gather(w_qkv, "fsdp", axis=1, tiled=True),
        lax.all_gather(w_out, "fsdp", axis=0, tiled=True),
        lax.all_gather(a_attn, "fsdp", axis=1, tiled=True),
        lax.all_gather(b_attn, "fsdp", axis=1, tiled=True),
        lax.all_gather(gain_attn, "fsdp", axis=0, tiled=True),
        lax.all_gather(gain_moe, "fsdp", axis=0, tiled=True),
        lax.all_gather(router, "fsdp", axis=0, tiled=True),
    )
    gain_one = first_norm_gain_full.astype(jnp.float32)
    gain_two = second_norm_gain_full.astype(jnp.float32)
    upstream = cotangent[0].astype(jnp.float32)
    d_route = (gate_weights[:, :, None] * upstream[:, None, :]).astype(jnp.bfloat16)
    d_gates = jnp.sum(upstream[:, None, :] * route_out, axis=2)
    d_chosen = gate_weights * (d_gates - jnp.sum(gate_weights * d_gates, axis=1, keepdims=True))
    d_logits = jnp.sum(
        jnp.where(
            my_routes[:, :, None] == jnp.arange(experts_all)[None, None, :],
            d_chosen[:, :, None],
            0.0,
        ),
        axis=1,
    ).astype(jnp.bfloat16)
    send_grads = (
        jnp.zeros((experts_all, capacity, model_width), jnp.bfloat16)
        .at[flat_routes, slot_index]
        .set(d_route.reshape(tok_rows * TOP, model_width))
    )
    grads_got = lax.all_to_all(
        send_grads.reshape(shard_count, local_experts, capacity, model_width),
        "fsdp",
        split_axis=0,
        concat_axis=0,
        tiled=True,
    )
    slot_half = slot_mask.astype(jnp.bfloat16)
    d_low_down = (
        jnp.einsum(
            "necd,esd->necs", grads_got, exp_b_down, preferred_element_type=jnp.float32
        ).astype(jnp.bfloat16)
        * slot_half
    )
    d_activation = jnp.einsum(
        "necd,efd->necf", grads_got, w_down, preferred_element_type=jnp.float32
    ) + jnp.einsum("necs,efs->necf", d_low_down, exp_a_down, preferred_element_type=jnp.float32)
    silu_value, silu_pull = jax.vjp(
        lambda gate_in, up_in: jax.nn.silu(gate_in) * up_in, gate_h, up_h
    )
    d_gate_h, d_up_h = silu_pull(d_activation)
    d_gate_h = d_gate_h.astype(jnp.bfloat16)
    d_up_h = d_up_h.astype(jnp.bfloat16)
    d_both = jnp.stack([d_gate_h, d_up_h], axis=3)
    d_low_in = (
        jnp.einsum(
            "necif,eisf->necis", d_both, exp_b_in, preferred_element_type=jnp.float32
        ).astype(jnp.bfloat16)
        * slot_half[:, :, :, None, :]
    )
    d_rows = (
        jnp.einsum("necf,edf->necd", d_gate_h, w_gate, preferred_element_type=jnp.float32)
        + jnp.einsum("necf,edf->necd", d_up_h, w_up, preferred_element_type=jnp.float32)
        + jnp.einsum("necis,eids->necd", d_low_in, exp_a_in, preferred_element_type=jnp.float32)
    )
    returned_grads = lax.all_to_all(
        d_rows.astype(jnp.bfloat16), "fsdp", split_axis=0, concat_axis=0, tiled=True
    )
    g_exp_b_down = jnp.einsum(
        "necs,necd->esd", low_down, grads_got, preferred_element_type=jnp.float32
    )
    g_exp_a_down = jnp.einsum(
        "necf,necs->efs", activation, d_low_down, preferred_element_type=jnp.float32
    )
    g_exp_b_in = jnp.einsum("necis,necif->eisf", low_in, d_both, preferred_element_type=jnp.float32)
    g_exp_a_in = jnp.einsum(
        "necd,necis->eids", rows_got, d_low_in, preferred_element_type=jnp.float32
    )
    d_normed_two = jnp.sum(
        returned_grads.reshape(experts_all, capacity, model_width)[flat_routes, slot_index]
        .reshape(tok_rows, TOP, model_width)
        .astype(jnp.float32),
        axis=1,
    ) + jnp.einsum("te,de->td", d_logits, router_weight_full, preferred_element_type=jnp.float32)
    d_resid_one = upstream + norm_back(resid_one, gain_two, d_normed_two)
    branch_gradient = d_resid_one.astype(jnp.bfloat16)
    output_adapter_gradient = (
        jnp.dot(branch_gradient, adapter_up_weight[3], preferred_element_type=jnp.float32).astype(
            jnp.bfloat16
        )
        * mask_half
    )
    d_att = (
        jnp.einsum(
            "te,de->td", branch_gradient, output_weight_full, preferred_element_type=jnp.float32
        )
        + jnp.einsum(
            "cr,ar->ca",
            output_adapter_gradient,
            adapter_down_weight[3],
            preferred_element_type=jnp.float32,
        )
    ).astype(jnp.bfloat16)
    output_up_gradient = jnp.einsum(
        "ts,te->es", output_rank_branch, branch_gradient, preferred_element_type=jnp.float32
    )
    output_down_gradient = jnp.einsum(
        "td,ts->ds",
        attention_rounded_rows,
        output_adapter_gradient,
        preferred_element_type=jnp.float32,
    )
    d_att_heads = d_att.reshape(tok_rows, head_count, HD)
    delta_rows = jnp.transpose(jnp.sum(d_att_heads.astype(jnp.float32) * attended, axis=2))
    key_piece = lax.all_gather(keys_own, "fsdp", axis=0, tiled=True)
    value_piece = lax.all_gather(values_own, "fsdp", axis=0, tiled=True)
    seg_piece = lax.all_gather(seg_own, "fsdp", axis=0, tiled=True)
    piece_rows = key_piece.shape[0]
    key_heads = key_piece.reshape(piece_rows, head_count, HD)
    value_heads = value_piece.reshape(piece_rows, head_count, HD)
    scores = (
        jnp.einsum("qhd,khd->hqk", queries, key_heads, preferred_element_type=jnp.float32)
        * score_scale
    )
    same_doc = seg_local[:, None] == seg_piece.astype(jnp.int32)[None, :]
    scores = jnp.where(same_doc[None], scores, MASKED)
    soft_probs = jnp.exp(scores - log_sum[:, :, None])
    d_probs = jnp.einsum(
        "qhd,khd->hqk", d_att_heads, value_heads, preferred_element_type=jnp.float32
    )
    d_scores = (soft_probs * (d_probs - delta_rows[:, :, None])).astype(jnp.bfloat16)
    soft_probs, d_scores = (soft_probs, d_scores)
    d_query_part = jnp.einsum(
        "hqk,khd->qhd", d_scores, key_heads, preferred_element_type=jnp.float32
    )
    d_key_part = jnp.einsum(
        "hqk,qhd->khd", d_scores, queries, preferred_element_type=jnp.float32
    ).reshape(piece_rows, model_width)
    d_value_part = jnp.einsum(
        "hqk,qhd->khd",
        soft_probs.astype(jnp.bfloat16),
        d_att_heads,
        preferred_element_type=jnp.float32,
    ).reshape(piece_rows, model_width)
    back_state = (d_query_part, d_key_part, d_value_part)
    d_query, d_keys_all, d_values_all = back_state
    d_keys_mine, d_values_mine = (
        lax.psum_scatter(
            d_keys_all.astype(jnp.bfloat16), "fsdp", scatter_dimension=0, tiled=True
        ).astype(jnp.float32),
        lax.psum_scatter(
            d_values_all.astype(jnp.bfloat16), "fsdp", scatter_dimension=0, tiled=True
        ).astype(jnp.float32),
    )
    d_query_pre = (
        rotate(d_query * score_scale, cosine, -sine_table)
        .reshape(tok_rows, model_width)
        .astype(jnp.bfloat16)
    )
    d_key_pre = (
        rotate((d_keys_mine * score_scale).reshape(tok_rows, head_count, HD), cosine, -sine_table)
        .reshape(tok_rows, model_width)
        .astype(jnp.bfloat16)
    )
    projected_gradient = jnp.stack([d_query_pre, d_key_pre, d_values_mine.astype(jnp.bfloat16)])
    projection_adapter_gradient = (
        jnp.einsum(
            "jah,jho->jao",
            projected_gradient,
            adapter_up_weight[:3],
            preferred_element_type=jnp.float32,
        ).astype(jnp.bfloat16)
        * mask_half[None]
    )
    d_normed_one = jnp.einsum(
        "pte,pde->td", projected_gradient, attention_weight_full, preferred_element_type=jnp.float32
    ) + jnp.einsum(
        "czn,cvn->zv",
        projection_adapter_gradient,
        adapter_down_weight[:3],
        preferred_element_type=jnp.float32,
    )
    attention_up_gradient = jnp.einsum(
        "pts,pte->pes",
        attention_rank_branch,
        projected_gradient,
        preferred_element_type=jnp.float32,
    )
    attention_down_gradient = jnp.einsum(
        "td,pts->pds",
        first_normed_rows,
        projection_adapter_gradient,
        preferred_element_type=jnp.float32,
    )
    d_hidden = d_resid_one + norm_back(hidden_f, gain_one, d_normed_one)
    adapter_down_gradient = jnp.concatenate(
        [attention_down_gradient, output_down_gradient[None]], axis=0
    )
    adapter_up_gradient = jnp.concatenate([attention_up_gradient, output_up_gradient[None]], axis=0)
    part_down, part_up = (
        lax.psum_scatter(
            adapter_down_gradient.astype(jnp.bfloat16), "fsdp", scatter_dimension=1, tiled=True
        ).astype(jnp.float32),
        lax.psum_scatter(
            adapter_up_gradient.astype(jnp.bfloat16), "fsdp", scatter_dimension=1, tiled=True
        ).astype(jnp.float32),
    )
    summed = (
        lax.psum(part_down.astype(jnp.bfloat16), "rep").astype(jnp.float32),
        lax.psum(part_up.astype(jnp.bfloat16), "rep").astype(jnp.float32),
        lax.psum(g_exp_a_in.astype(jnp.bfloat16), "rep").astype(jnp.float32),
        lax.psum(g_exp_b_in.astype(jnp.bfloat16), "rep").astype(jnp.float32),
        lax.psum(g_exp_a_down.astype(jnp.bfloat16), "rep").astype(jnp.float32),
        lax.psum(g_exp_b_down.astype(jnp.bfloat16), "rep").astype(jnp.float32),
    )
    return (
        layer_value.astype(jnp.bfloat16)[None],
        d_hidden.astype(jnp.bfloat16)[None],
        summed[0],
        summed[1],
        summed[2],
        summed[3],
        summed[4],
        summed[5],
    )


EVERY = 8
TILE = 256
CUT = 512
VMEM_BYTES = 64000000


def mm(left, right):
    return jnp.dot(left, right, preferred_element_type=jnp.float32)


def mm_nt(left, right):
    return lax.dot_general(left, right, (((1,), (1,)), ((), ())), preferred_element_type=jnp.float32)


def whole():
    return pl.BlockSpec(memory_space=pltpu.VMEM)


def in_place():
    return pl.BlockSpec(memory_space=pl.ANY)


def scalars():
    return pl.BlockSpec(memory_space=pltpu.SMEM)


def params():
    return pltpu.CompilerParams(vmem_limit_bytes=VMEM_BYTES)


def cost(flops, moved):
    return pl.CostEstimate(flops=flops, bytes_accessed=moved, transcendentals=0)


def shape_of(shape, dtype=jnp.bfloat16):
    return jax.ShapeDtypeStruct(shape, dtype)


def swap(values, bits):
    return lax.ppermute(values, "fsdp", [(i, i ^ bits) for i in range(EVERY)])


def tie(*values):
    return lax.optimization_barrier(values)


def gather_first(values):
    return [values, swap(values, 2), swap(values, 4)]


def gather_second(values, side, over):
    half = values.shape[0] // 2
    far = [swap(side[:half], 4), swap(over[half:], 2)]
    return far, swap(values, 1), swap(jnp.concatenate([side, over], axis=0), 1)


def gather_third(first, far, own, pair):
    far = jnp.concatenate(far, axis=0)
    return [*first, far, own, pair, swap(far, 1)]


GATHERED = 7


def blocks_of(refs):
    values, side, over, far, own, pair, last = refs
    rows = values.shape[0]
    return [values, own, side, pair.at[0:rows], over, pair.at[rows : 2 * rows], far, last]


def gather_relative(values):
    first = gather_first(values)
    return gather_third(first, *gather_second(*first))


def add_half(left, right):
    return (left.astype(jnp.float32) + right.astype(jnp.float32)).astype(jnp.bfloat16)


def scatter_second(even, got):
    rows = even.shape[0] // 4
    half = rows // 2
    far = 3 * rows
    return [
        swap(add_half(even[far : far + half], got[far : far + half]), 2),
        swap(add_half(even[far + half :], got[far + half :]), 4),
    ]


def scatter_third(even, got, far_side, far_over):
    rows = even.shape[0] // 4
    half = rows // 2
    f32 = jnp.float32
    side = even[rows : 2 * rows].astype(f32) + got[rows : 2 * rows].astype(f32)
    over = even[2 * rows : 3 * rows].astype(f32) + got[2 * rows : 3 * rows].astype(f32)
    side = jnp.concatenate([side[:half], side[half:] + far_over.astype(f32)], axis=0)
    over = jnp.concatenate([over[:half] + far_side.astype(f32), over[half:]], axis=0)
    return even, got, swap(side.astype(jnp.bfloat16), 2), swap(over.astype(jnp.bfloat16), 4)


def scatter_relative(even, odd):
    got = swap(odd, 1)
    return scatter_third(even, got, *scatter_second(even, got))


def sum_pieces(*pieces):
    return sum([piece.astype(jnp.float32) for piece in pieces[1:]], pieces[0].astype(jnp.float32))


PIECES = 4


def piece_specs(rows, columns, at=0):
    return [pl.BlockSpec((rows, columns), lambda i: (0, at))] * PIECES


def rep_swap(values, bits):
    return lax.ppermute(values, "rep", [(i, i ^ bits) for i in range(4)])


def turn(values, cosine, signed_sine):
    return values * cosine + pltpu.roll(values, HD // 2, 1) * signed_sine


SPOT = 16


def relayout_kernel(wide, source_ref, out_ref):
    for j in range(EVERY):
        out_ref[j, 0] = source_ref[0, :, j * wide : (j + 1) * wide]


def by_columns(values, wide):
    count, rows, width = values.shape
    half = rows // 2
    return pl.pallas_call(
        functools.partial(relayout_kernel, wide),
        grid=(count, 2),
        in_specs=[pl.BlockSpec((1, half, width), lambda i, j: (i, j, 0))],
        out_specs=pl.BlockSpec((EVERY, 1, half, wide), lambda i, j: (0, i, j, 0)),
        out_shape=shape_of((EVERY, count, rows, wide)),
        cost_estimate=cost(1 << 20, 1 << 16),
        name="by_columns",
    )(values)


def project_kernel(
    rows, width, wide,
    me_ref, sets_ref, cos_ref, sin_ref, up_ref, *refs,
):
    f32, bf16 = jnp.float32, jnp.bfloat16
    hidden_hbm, given, w_hbm = blocks_of(refs[:GATHERED]), blocks_of(refs[GATHERED : 2 * GATHERED]), refs[2 * GATHERED]
    refs = refs[2 * GATHERED + 1 :]
    q_ref, k_ref, v_ref, normed_ref, low_ref, mask_ref, col_ref, row_ref, gains_ref, router_ref, *refs = refs
    hidden, extra, weight, down, sems, w_sems = refs
    me, step = me_ref[0], pl.program_id(0)
    thin = 3 * SR
    copies = []
    for j in range(EVERY):
        at = pl.multiple_of((me ^ j) * wide, wide)
        here = slice(j * rows, (j + 1) * rows)
        copies.append(
            [
                pltpu.make_async_copy(hidden_hbm[j], hidden.at[here], sems.at[j, 0]),
                pltpu.make_async_copy(given[j].at[:, 2 * thin :], extra.at[here], sems.at[j, 1]),
                pltpu.make_async_copy(
                    given[j].at[:, 0:thin], down.at[pl.ds(at, rows), :], sems.at[j, 2]
                ),
                pltpu.make_async_copy(
                    given[j].at[:, thin : 2 * thin], down.at[pl.ds(at + rows, rows), :], sems.at[j, 3]
                ),
            ]
        )
    w_copies = [
        pltpu.make_async_copy(
            w_hbm.at[j, i], weight.at[j * wide : (j + 1) * wide, i * wide : (i + 1) * wide], w_sems.at[j, i]
        )
        for i in range(3)
        for j in range(EVERY)
    ]

    @pl.when(step == 0)
    def _():
        for which in (1, 0, 2, 3):
            for group in copies:
                group[which].start()
        for item in w_copies:
            item.start()
        for group in copies:
            group[1].wait()
        for j in range(EVERY):
            at = pl.multiple_of((me ^ j) * wide, wide)
            for part in range(wide // rows):
                spot = pl.multiple_of(at + part * rows, rows)
                router_ref[pl.ds(spot, rows), :] = extra[j * rows : (j + 1) * rows, part * 128 : (part + 1) * 128]
                for i in range(2):
                    line = extra[j * rows : j * rows + 16, 256:384].astype(f32)
                    gains_ref[i : i + 1, pl.ds(spot, rows)] = line[2 * i + part : 2 * i + part + 1, :]
        for group in copies:
            for which in (0, 2, 3):
                group[which].wait()
        for item in w_copies:
            item.wait()

    at = pl.ds(pl.multiple_of(step * TILE, TILE), TILE)
    seg = jnp.broadcast_to(extra[at, 0:1].astype(f32), (TILE, 128))
    col_ref[...] = seg
    row_ref[...] = seg.T[0:8, :]
    chosen = jnp.zeros_like(seg)
    for i in range(SETS):
        chosen = jnp.where(seg == float(i), sets_ref[0, i].astype(f32), chosen)
    lane_set = (lax.broadcasted_iota(jnp.int32, (TILE, SR), 1) // R).astype(f32)
    mask = (chosen == lane_set).astype(f32)
    mask_ref[...] = mask
    values = hidden[at, :].astype(f32)
    scale = lax.rsqrt(jnp.mean(values * values, axis=1, keepdims=True) + EPSILON)
    normed = (values * scale * gains_ref[0:1, :]).astype(bf16)
    normed_ref[...] = normed
    low = (mm(normed, down[...]) * jnp.concatenate([mask] * 3, axis=1)).astype(bf16)
    low_ref[...] = low
    cosine, sine = cos_ref[...], sin_ref[...]
    for i, ref in enumerate((q_ref, k_ref, v_ref)):
        proj = mm(normed, weight[:, i * wide : (i + 1) * wide]) + mm_nt(
            low[:, i * SR : (i + 1) * SR], up_ref[i]
        )
        for h in range(wide // HD):
            part = proj[:, h * HD : (h + 1) * HD]
            ref[:, h * HD : (h + 1) * HD] = (turn(part, cosine, sine) if i < 2 else part).astype(bf16)


def by_tile(rows, columns):
    return pl.BlockSpec((rows, columns), lambda i: (i, 0))


def project(me, sets, cosine, sine, up, hidden_given, given, w_got):
    rows, width = hidden_given[0].shape
    wide = width // EVERY
    tokens = rows * EVERY
    f32 = jnp.float32
    return pl.pallas_call(
        functools.partial(project_kernel, rows, width, wide),
        grid=(tokens // TILE,),
        in_specs=[scalars(), scalars(), by_tile(TILE, 128), by_tile(TILE, 128), whole()] + [in_place()] * (2 * GATHERED + 1),
        out_specs=[by_tile(TILE, wide)] * 3
        + [by_tile(TILE, width), by_tile(TILE, 3 * SR), by_tile(TILE, SR), by_tile(TILE, 128)]
        + [
            pl.BlockSpec((8, TILE), lambda i: (0, i)),
            pl.BlockSpec((8, width), lambda i: (0, 0)),
            pl.BlockSpec((width, 128), lambda i: (0, 0)),
        ],
        out_shape=[shape_of((tokens, wide))] * 3
        + [shape_of((tokens, width)), shape_of((tokens, 3 * SR)), shape_of((tokens, SR), f32)]
        + [shape_of((tokens, 128), f32), shape_of((8, tokens), f32), shape_of((8, width), f32), shape_of((width, 128))],
        scratch_shapes=[
            pltpu.VMEM((tokens, width), jnp.bfloat16),
            pltpu.VMEM((tokens, 384), jnp.bfloat16),
            pltpu.VMEM((width, 3 * wide), jnp.bfloat16),
            pltpu.VMEM((width, 3 * SR), jnp.bfloat16),
            pltpu.SemaphoreType.DMA((EVERY, 4)),
            pltpu.SemaphoreType.DMA((EVERY, 3)),
        ],
        compiler_params=params(),
        cost_estimate=cost(1 << 20, 1 << 16),
        name="project",
    )(me, sets, cosine, sine, up, *hidden_given, *given, w_got)


def attend_kernel(rows, me_ref, q_ref, k_ref, v_ref, col_ref, row_ref, att_ref, lse_ref, send_ref):
    f32, bf16 = jnp.float32, jnp.bfloat16
    scale = HD ** (-0.5)
    seg_row = row_ref[0:1, :]
    for h in range(q_ref.shape[1] // HD):
        lanes = slice(h * HD, (h + 1) * HD)
        for c in range(q_ref.shape[0] // TILE):
            at = slice(c * TILE, (c + 1) * TILE)
            scores = mm_nt(q_ref[at, lanes], k_ref[:, lanes]) * scale
            scores = jnp.where(col_ref[at, 0:1] == seg_row, scores, MASKED)
            top = jnp.max(scores, axis=1, keepdims=True)
            weights = jnp.exp(scores - top)
            total = jnp.sum(weights, axis=1, keepdims=True)
            att = mm(weights.astype(bf16), v_ref[:, lanes]) / total
            att_ref[at, lanes] = att
            log_sum = jnp.broadcast_to(top + jnp.log(total), (TILE, HD))
            lse_ref[h : h + 1, at] = log_sum.T[0:1, :]
            for part in range(TILE // rows):
                j = c * (TILE // rows) + part
                send_ref[me_ref[0] ^ j, :, lanes] = att[part * rows : (part + 1) * rows].astype(bf16)


def attend(rows, me, queries, keys, values, seg_col, seg_row):
    tokens, wide = queries.shape
    return pl.pallas_call(
        functools.partial(attend_kernel, rows),
        in_specs=[scalars()] + [whole()] * 5,
        out_specs=[whole()] * 3,
        out_shape=[
            shape_of((tokens, wide), jnp.float32),
            shape_of((8, tokens), jnp.float32),
            shape_of((EVERY, rows, wide)),
        ],
        compiler_params=params(),
        cost_estimate=cost(1 << 20, 1 << 16),
        name="attend",
    )(me, queries, keys, values, seg_col, seg_row)


def output_copies(me, wide, given, weight, down, up, sems):
    width = weight.shape[1]
    copies = []
    for j in range(EVERY):
        at = pl.multiple_of((me ^ j) * wide, wide)
        here = slice(j * wide, (j + 1) * wide)
        copies.append(
            [
                pltpu.make_async_copy(given[j].at[:, width : width + SR], down.at[here, :], sems.at[j, 0]),
                pltpu.make_async_copy(given[j].at[:, width + SR :], up.at[pl.ds(at, wide), :], sems.at[j, 1]),
                pltpu.make_async_copy(given[j].at[:, 0:width], weight.at[here, :], sems.at[j, 2]),
            ]
        )
    return copies


def output_scratch(width):
    return [
        pltpu.VMEM((width, width), jnp.bfloat16),
        pltpu.VMEM((width, SR), jnp.bfloat16),
        pltpu.VMEM((width, SR), jnp.bfloat16),
        pltpu.SemaphoreType.DMA((EVERY, 3)),
    ]


def mix_kernel(
    wide,
    me_ref, hidden_ref, gains_ref, mask_ref, router_ref, named_ref, att_ref, *refs,
):
    f32, bf16 = jnp.float32, jnp.bfloat16
    given = blocks_of(refs[:GATHERED])
    resid_ref, normed_ref, low_ref, gates_ref, weight, down, up, sems = refs[GATHERED:]
    me = me_ref[0]
    width = hidden_ref.shape[1]
    copies = output_copies(me, wide, given, weight, down, up, sems)
    for part in range(3):
        for group in copies:
            group[part].start()
    for part in range(2):
        for group in copies:
            group[part].wait()
    blocks = [att_ref[me ^ j] for j in range(EVERY)]
    low = (mm(jnp.concatenate(blocks, axis=1), down[...]) * mask_ref[...]).astype(bf16)
    low_ref[...] = low
    total = mm_nt(low, up[...])
    for j in range(EVERY):
        copies[j][2].wait()
        total = total + mm(blocks[j], weight[j * wide : (j + 1) * wide, :])
    resid = hidden_ref[...].astype(f32) + total
    resid_ref[...] = resid
    scale = lax.rsqrt(jnp.mean(resid * resid, axis=1, keepdims=True) + EPSILON)
    normed = (resid * scale * gains_ref[1:2, :]).astype(bf16)
    normed_ref[:, 0:width] = normed
    logits = jnp.where(named_ref[...] > 0.5, mm(normed, router_ref[...]), MASKED)
    share = jnp.exp(logits - jnp.max(logits, axis=1, keepdims=True)) * named_ref[...]
    gates = share / jnp.sum(share, axis=1, keepdims=True)
    gates_ref[...] = gates
    high = gates.astype(bf16).astype(f32)
    normed_ref[:, width : width + 128] = (high + pltpu.roll(gates - high, 64, 1)).astype(bf16)


def mix(me, hidden, gains, mask, router, named, att_got, given):
    rows, width = hidden.shape
    wide = width // EVERY
    f32 = jnp.float32
    return pl.pallas_call(
        functools.partial(mix_kernel, wide),
        grid=(1,),
        in_specs=[scalars(), whole(), whole(), pl.BlockSpec((rows, SR), lambda i: (0, 0))]
        + [whole()] * 3
        + [in_place()] * GATHERED,
        out_specs=[whole()] * 4,
        out_shape=[shape_of((rows, width), f32), shape_of((rows, width + 128)), shape_of((rows, SR)),
                   shape_of((rows, 128), f32)],
        scratch_shapes=output_scratch(width),
        compiler_params=params(),
        cost_estimate=cost(1 << 20, 1 << 16),
        name="mix",
    )(me, hidden, gains, mask, router, named, att_got, *given)


def expert_kernel(k, first, width, hidden, blocks, where_ref, mask_ref, pick_ref, *refs):
    f32, bf16 = jnp.float32, jnp.bfloat16
    rows_hbm, cot_hbm = blocks_of(refs[:GATHERED]), blocks_of(refs[GATHERED : 2 * GATHERED])
    refs = refs[2 * GATHERED :]
    if not first:
        prev_out, refs = refs[:2], refs[2:]
    (
        w_gate_hbm, w_up_hbm, w_down_hbm, a_in_hbm, b_in_hbm, a_down_hbm, b_down_hbm,
        out_even, out_odd, d_all_ref, extra_ref, *refs,
    ) = refs
    *grad_refs, rows_s, cot_s, w_in, w_down, silu_s, slope_s, g_a_in, g_b_down, g_b_in, g_a_down, packed, sems, block_sems = refs
    out_refs = (out_even, out_odd)
    step = pl.program_id(0)
    part = TILE // 2
    low_at, thin_at = 2 * hidden, width
    chunks = hidden // CUT
    early, late, given = [], [], []

    def copy(source, target, group):
        group.append(pltpu.make_async_copy(source, target, sems.at[len(early) + len(late)]))

    copy(a_in_hbm.at[k, 0], w_in.at[0:width, low_at : low_at + SR], early)
    copy(a_in_hbm.at[k, 1], w_in.at[0:width, low_at + SR : low_at + 2 * SR], early)
    copy(b_in_hbm.at[k, 0], w_in.at[width : width + SR, 0:hidden], early)
    copy(b_in_hbm.at[k, 1], w_in.at[width : width + SR, hidden:low_at], early)
    for j in range(chunks):
        at = slice(j * CUT, (j + 1) * CUT)
        copy(w_gate_hbm.at[k, :, at], w_in.at[0:width, at], early)
        copy(w_up_hbm.at[k, :, at], w_in.at[0:width, hidden + j * CUT : hidden + (j + 1) * CUT], early)
    copy(a_down_hbm.at[k], w_down.at[0:hidden, thin_at : thin_at + SR], late)
    copy(b_down_hbm.at[k], w_down.at[hidden : hidden + SR, 0:width], late)
    copy(w_down_hbm.at[k], w_down.at[0:hidden, 0:width], late)
    for j in range(blocks):
        at = slice(j * part, (j + 1) * part)
        given.append(pltpu.make_async_copy(rows_hbm[j], rows_s.at[at, :], block_sems.at[j, 0]))
        given.append(pltpu.make_async_copy(cot_hbm[j], cot_s.at[at, :], block_sems.at[j, 1]))

    def wait_for(group, when=0):
        @pl.when(step == when)
        def _():
            for item in group:
                item.wait()

    @pl.when(step == 0)
    def _():
        for item in given[0:4] + early + late + given[4:]:
            item.start()
        g_a_in[...] = jnp.zeros_like(g_a_in)
        g_b_down[...] = jnp.zeros_like(g_b_down)
        g_b_in[...] = jnp.zeros_like(g_b_in)
        g_a_down[...] = jnp.zeros_like(g_a_down)

    for i in range(blocks // 2):
        wait_for(given[4 * i : 4 * i + 4], i)
    wait_for(early[:2])
    at_rows = pl.ds(pl.multiple_of(step * TILE, TILE), TILE)
    mask = mask_ref[...]
    mask_two = jnp.concatenate([mask, mask], axis=1)
    rows = rows_s[at_rows, 0:width]
    gate = jnp.sum(rows_s[at_rows, width:].astype(f32) * pick_ref[0:1, :], axis=1, keepdims=True)
    low_in = (mm(rows, w_in[0:width, low_at:]) * mask_two).astype(bf16)
    rows_gate = jnp.concatenate([rows, low_in[:, :SR]], axis=1)
    rows_up = jnp.concatenate([rows, low_in[:, SR:]], axis=1)
    wait_for(early[2:4])
    act_parts = []
    for j in range(chunks):
        wait_for(early[4 + 2 * j : 6 + 2 * j])
        at = slice(j * CUT, (j + 1) * CUT)
        gate_h = mm(rows_gate, w_in[:, at])
        up_h = mm(rows_up, w_in[:, hidden + j * CUT : hidden + (j + 1) * CUT])
        share = 1.0 / (1.0 + jnp.exp(-gate_h))
        silu = gate_h * share
        silu_s[:, at] = silu
        slope_s[:, at] = up_h * (share * (1.0 + gate_h * (1.0 - share)))
        act_parts.append((silu * up_h).astype(bf16))
    act = jnp.concatenate(act_parts, axis=1)
    wait_for(late)

    low_down = (mm(act, w_down[0:hidden, thin_at:]) * mask).astype(bf16)
    act_low = jnp.concatenate([act, low_down], axis=1)
    d_gate = jnp.zeros((TILE, 1), f32)
    d_out_parts = []
    for j in range(width // CUT):
        at = slice(j * CUT, (j + 1) * CUT)
        out = mm(act_low, w_down[:, at]).astype(bf16).astype(f32)
        cot = cot_s[at_rows, at].astype(f32)
        d_out_parts.append((gate * cot).astype(bf16))
        weighted = gate * out
        for i in range(2):
            value = weighted[i * part : (i + 1) * part]
            if not first:
                value = value + prev_out[i][:, at].astype(f32)
            out_refs[i][:, at] = value.astype(bf16)
        d_gate = d_gate + jnp.sum(cot * out, axis=1, keepdims=True)
    high = d_gate.astype(bf16).astype(f32)
    extra_ref[...] = high * pick_ref[1:2, :] + (d_gate - high) * pick_ref[2:3, :]

    mask_half = mask.astype(bf16)
    d_out = jnp.concatenate(d_out_parts, axis=1)
    d_low_down = mm_nt(d_out, w_down[hidden:, 0:width]).astype(bf16) * mask_half
    d_out_low = jnp.concatenate([d_out, d_low_down], axis=1)
    d_gate_parts, d_up_parts = [], []
    for j in range(chunks):
        at = slice(j * CUT, (j + 1) * CUT)
        d_act = mm_nt(d_out_low, w_down[at, :])
        d_gate_parts.append((d_act * slope_s[:, at]).astype(bf16))
        d_up_parts.append((d_act * silu_s[:, at]).astype(bf16))
    d_gate_h = jnp.concatenate(d_gate_parts, axis=1)
    d_up_h = jnp.concatenate(d_up_parts, axis=1)
    d_low_gate = mm_nt(d_gate_h, w_in[width:, 0:hidden]).astype(bf16) * mask_half
    d_low_up = mm_nt(d_up_h, w_in[width:, hidden:low_at]).astype(bf16) * mask_half
    d_low_in = jnp.concatenate([d_low_gate, d_low_up], axis=1)
    d_all_ref[:, 0:hidden] = d_gate_h
    d_all_ref[:, hidden:low_at] = d_up_h
    d_all_ref[:, low_at:] = d_low_in
    d_low_in_t, low_down_t, low_in_t, d_low_down_t = d_low_in.T, low_down.T, low_in.T, d_low_down.T
    for j in range(width // CUT):
        at = slice(j * CUT, (j + 1) * CUT)
        g_a_in[:, at] += mm(d_low_in_t, rows[:, at])
        g_b_down[:, at] += mm(low_down_t, d_out[:, at])
    for j in range(chunks):
        at = slice(j * CUT, (j + 1) * CUT)
        g_b_in[0, :, at] += mm(low_in_t[:SR], d_gate_h[:, at])
        g_b_in[1, :, at] += mm(low_in_t[SR:], d_up_h[:, at])
        g_a_down[:, at] += mm(d_low_down_t, act[:, at])

    @pl.when(step == pl.num_programs(0) - 1)
    def _():
        packed[0 : 2 * SR, :] = g_a_in[...].astype(bf16)
        packed[2 * SR : 3 * SR, :] = g_b_down[...].astype(bf16)
        packed[3 * SR : 4 * SR, 0:hidden] = g_b_in[0].astype(bf16)
        packed[3 * SR : 4 * SR, hidden:] = g_b_in[1].astype(bf16)
        packed[4 * SR :, 0:hidden] = g_a_down[: SR // 2].astype(bf16)
        packed[4 * SR :, hidden:] = g_a_down[SR // 2 :].astype(bf16)
        size = packed.shape[0] // 4
        for spot, b in enumerate((0, 2, 1, 3)):
            quarter = packed[pl.ds(pl.multiple_of((where_ref[0] ^ b) * size, 16), size), :]
            per = 4 // len(grad_refs)
            grad_refs[spot // per][(spot % per) * size : (spot % per + 1) * size, :] = quarter


def expert_pass(k, where, rows, cot, mask, picks, prev, weights):
    f32, bf16 = jnp.float32, jnp.bfloat16
    blocks = EVERY
    part, width = cot[0].shape
    hidden = weights[0].shape[2]
    tokens = blocks * part
    shares = 2
    grad_shape = ((4 * SR + SR // 2) // shares, width)
    in_specs = [scalars(), by_tile(TILE, SR), pl.BlockSpec((8, 128), lambda i: (0, 0))] + [in_place()] * (2 * GATHERED)
    operands = [where, mask, picks, *rows, *cot]
    if prev is not None:
        in_specs += [by_tile(part, width)] * 2
        operands += list(prev)
    in_specs += [in_place()] * 7
    flops = 2 * tokens * (4 * width * hidden + 7 * SR * (width + hidden))
    return pl.pallas_call(
        functools.partial(expert_kernel, k, prev is None, width, hidden, blocks),
        grid=(tokens // TILE,),
        in_specs=in_specs,
        out_specs=[by_tile(part, width)] * 2
        + [by_tile(TILE, 2 * hidden + 2 * SR), by_tile(TILE, 128)]
        + [pl.BlockSpec(grad_shape, lambda i: (0, 0))] * shares,
        out_shape=[shape_of((tokens // 2, width))] * 2
        + [shape_of((tokens, 2 * hidden + 2 * SR)), shape_of((tokens, 128), f32)]
        + [shape_of(grad_shape)] * shares,
        scratch_shapes=[
            pltpu.VMEM((tokens, width + 128), bf16),
            pltpu.VMEM((tokens, width), bf16),
            pltpu.VMEM((width + SR, 2 * hidden + 2 * SR), bf16),
            pltpu.VMEM((hidden + SR, width + SR), bf16),
            pltpu.VMEM((TILE, hidden), f32),
            pltpu.VMEM((TILE, hidden), f32),
            pltpu.VMEM((2 * SR, width), f32),
            pltpu.VMEM((SR, width), f32),
            pltpu.VMEM((2, SR, hidden), f32),
            pltpu.VMEM((SR, hidden), f32),
            pltpu.VMEM((4 * SR + SR // 2, width), bf16),
            pltpu.SemaphoreType.DMA((7 + 2 * (hidden // CUT),)),
            pltpu.SemaphoreType.DMA((blocks, 2)),
        ],
        compiler_params=params(),
        cost_estimate=cost(flops, 40 << 20),
        name="expert",
    )(*operands, *weights)


def rows_kernel(part, width, hidden, local, *refs):
    bf16 = jnp.bfloat16
    d_all, extra, (w_gate_hbm, w_up_hbm, a_in_hbm) = refs[:local], refs[local : 2 * local], refs[2 * local : 2 * local + 3]
    even_ref, odd_ref, weight, sems = refs[2 * local + 3 :]
    step = pl.program_id(0)
    span = 2 * hidden + 2 * SR
    chunks = width // CUT
    copies = []
    for j in range(chunks):
        at = slice(j * CUT, (j + 1) * CUT)
        group = []
        for k in range(local):
            base = k * span
            targets = [
                (w_gate_hbm.at[k, at], base, hidden),
                (w_up_hbm.at[k, at], base + hidden, hidden),
                (a_in_hbm.at[k, 0, at], base + 2 * hidden, SR),
                (a_in_hbm.at[k, 1, at], base + 2 * hidden + SR, SR),
            ]
            for i, (source, start, size) in enumerate(targets):
                group.append(
                    pltpu.make_async_copy(source, weight.at[at, start : start + size], sems.at[j, 4 * k + i])
                )
        copies.append(group)

    @pl.when(step == 0)
    def _():
        for group in copies:
            for item in group:
                item.start()

    both = jnp.concatenate([ref[...] for ref in d_all], axis=1)
    for j in range(chunks):

        @pl.when(step == 0)
        def _():
            for item in copies[j]:
                item.wait()

        at = slice(j * CUT, (j + 1) * CUT)
        value = mm_nt(both, weight[at, :]).astype(bf16)
        even_ref[:, at] = value[:part]
        odd_ref[:, at] = value[part:]
    total = sum([ref[...] for ref in extra[1:]], extra[0][...]).astype(bf16)
    even_ref[:, width:] = total[:part]
    odd_ref[:, width:] = total[part:]


def rows_pass(part, d_all, extra, w_gate, w_up, a_in):
    local, width, hidden = w_gate.shape
    tokens, span = d_all[0].shape
    return pl.pallas_call(
        functools.partial(rows_kernel, part, width, hidden, local),
        grid=(tokens // TILE,),
        in_specs=[by_tile(TILE, span)] * local + [by_tile(TILE, 128)] * local + [in_place()] * 3,
        out_specs=[by_tile(part, width + 128)] * 2,
        out_shape=[shape_of((tokens // 2, width + 128))] * 2,
        scratch_shapes=[
            pltpu.VMEM((width, local * span), jnp.bfloat16),
            pltpu.SemaphoreType.DMA((width // CUT, 4 * local)),
        ],
        compiler_params=params(),
        cost_estimate=cost(2 * tokens * width * span * local, 40 << 20),
        name="rows",
    )(*d_all, *extra, w_gate, w_up, a_in)


def norm_grad(values, gain_row, upstream_grad):
    scale = lax.rsqrt(jnp.mean(values * values, axis=1, keepdims=True) + EPSILON)
    inner = gain_row * upstream_grad
    mean = jnp.mean(values * inner, axis=1, keepdims=True)
    return scale * inner - values * (scale * scale * scale * mean)


def unmix_kernel(
    wide,
    me_ref, resid_ref, cot_ref, gains_ref, mask_ref, router_ref, gates_ref, low_ref, att_ref, *refs,
):
    f32, bf16 = jnp.float32, jnp.bfloat16
    pieces, given, refs = refs[:PIECES], blocks_of(refs[PIECES : PIECES + GATHERED]), refs[PIECES + GATHERED :]
    resid_grad_ref, grad_ref, send_ref, weight, down, up, up_grad, sems = refs
    me = me_ref[0]
    width = resid_ref.shape[1]
    copies = output_copies(me, wide, given, weight, down, up, sems)
    for which in (1, 0, 2):
        for group in copies:
            group[which].start()
    resid = resid_ref[...]
    total = sum_pieces(*[ref[...] for ref in pieces])
    extra = total[:, width:]
    gates = gates_ref[...]
    d_gates = extra + pltpu.roll(extra, 64, 1)
    d_chosen = gates * (d_gates - jnp.sum(gates * d_gates, axis=1, keepdims=True))
    d_normed = total[:, :width] + mm_nt(d_chosen.astype(bf16), router_ref[...])
    d_resid = cot_ref[...].astype(f32) + norm_grad(resid, gains_ref[1:2, :], d_normed)
    resid_grad_ref[...] = d_resid
    branch = d_resid.astype(bf16)
    for group in copies:
        group[1].wait()
    d_low = (mm(branch, up[...]).astype(bf16).astype(f32) * mask_ref[...]).astype(bf16)
    low_t, d_low_t = low_ref[...].T, d_low.T
    up_grad[...] = mm(low_t, branch).astype(bf16)
    for group in copies:
        group[0].wait()
    for j in range(EVERY):
        here = slice(j * wide, (j + 1) * wide)
        copies[j][2].wait()
        send_ref[me ^ j] = (mm_nt(branch, weight[here, :]) + mm_nt(d_low, down[here, :])).astype(bf16)
        at = pl.multiple_of((me ^ j) * wide, wide)
        grad_ref[me ^ j, 0:SR, :] = mm(d_low_t, att_ref[me ^ j]).astype(bf16)
        grad_ref[me ^ j, SR:, :] = up_grad[:, pl.ds(at, wide)]


def unmix(me, resid, cot, gains, mask, router, gates, low, att_got, pieces, given):
    rows, width = resid.shape
    wide = width // EVERY
    return pl.pallas_call(
        functools.partial(unmix_kernel, wide),
        grid=(1,),
        in_specs=[scalars()]
        + [whole()] * 3
        + [pl.BlockSpec((rows, SR), lambda i: (0, 0))]
        + [whole()] * 4
        + piece_specs(rows, width + 128)
        + [in_place()] * GATHERED,
        out_specs=[whole()] * 3,
        out_shape=[
            shape_of((rows, width), jnp.float32),
            shape_of((EVERY, 2 * SR, wide)),
            shape_of((EVERY, rows, wide)),
        ],
        scratch_shapes=output_scratch(width)[:3]
        + [pltpu.VMEM((SR, width), jnp.bfloat16)]
        + output_scratch(width)[3:],
        compiler_params=params(),
        cost_estimate=cost(1 << 20, 1 << 16),
        name="unmix",
    )(me, resid, cot, gains, mask, router, gates, low, att_got, *pieces, *given)


def attend_back_kernel(
    rows, wide,
    me_ref, q_ref, k_ref, v_ref, att_ref, lse_ref, col_ref, row_ref, cos_ref, sin_ref, low_ref, mask_ref, up_ref,
    got_ref, out_grad_ref, normed_hbm, d_proj_ref, d_low_ref, even_ref, odd_ref, up_grad_ref, d_att, normed, sems,
):
    f32, bf16 = jnp.float32, jnp.bfloat16
    tokens = q_ref.shape[0]
    scale = HD ** (-0.5)
    me = me_ref[0]
    bring = pltpu.make_async_copy(normed_hbm, normed, sems.at[0])
    bring.start()
    for j in range(EVERY):
        d_att[j * rows : (j + 1) * rows, :] = got_ref[me ^ j]
    seg_row = row_ref[0:1, :]
    for h in range(wide // HD):
        lanes = slice(h * HD, (h + 1) * HD)
        delta = jnp.sum(d_att[:, lanes].astype(f32) * att_ref[:, lanes], axis=1, keepdims=True)
        delta = jnp.broadcast_to(delta, (tokens, HD)).T[0:1, :]
        log_sum = lse_ref[h : h + 1, :]
        d_query = jnp.zeros((tokens, HD), f32)
        for c in range(tokens // TILE):
            at = slice(c * TILE, (c + 1) * TILE)
            scores = mm_nt(k_ref[at, lanes], q_ref[:, lanes]) * scale - log_sum
            probs = jnp.exp(jnp.where(col_ref[at, 0:1] == seg_row, scores, MASKED))
            d_probs = mm_nt(v_ref[at, lanes], d_att[:, lanes])
            d_scores = (probs * (d_probs - delta)).astype(bf16)
            d_value = mm(probs.astype(bf16), d_att[:, lanes])
            d_key = mm(d_scores, q_ref[:, lanes])
            d_query = d_query + mm(d_scores.T, k_ref[at, lanes])
            d_proj_ref[at, wide + h * HD : wide + (h + 1) * HD] = turn(
                d_key * scale, cos_ref[at, :], -sin_ref[at, :]
            ).astype(bf16)
            d_proj_ref[at, 2 * wide + h * HD : 2 * wide + (h + 1) * HD] = d_value.astype(bf16)
        d_proj_ref[:, lanes] = turn(d_query * scale, cos_ref[...], -sin_ref[...]).astype(bf16)
    for i in range(3):
        part = d_proj_ref[:, i * wide : (i + 1) * wide]
        d_low = (mm(part, up_ref[i]).astype(bf16).astype(f32) * mask_ref[...]).astype(bf16)
        d_low_ref[:, i * SR : (i + 1) * SR] = d_low
        up_grad_ref[i * SR : (i + 1) * SR, :] = mm(low_ref[:, i * SR : (i + 1) * SR].T, part).astype(bf16)
    d_low_t = d_low_ref[...].T
    bring.wait()
    for j in range(EVERY):
        at = pl.multiple_of((me ^ j) * wide, wide)
        spot = (j // 2) * 5 * SR
        ref = (even_ref, odd_ref)[j % 2]
        ref[spot : spot + 2 * SR, :] = out_grad_ref[me ^ j]
        ref[spot + 2 * SR : spot + 5 * SR, :] = mm(d_low_t, normed[:, pl.ds(at, wide)]).astype(bf16)


def attend_back(rows, me, q, k, v, att, lse, seg_col, seg_row, cosine, sine, low, mask, up, got, out_grad, normed):
    tokens, wide = q.shape
    width = wide * EVERY
    return pl.pallas_call(
        functools.partial(attend_back_kernel, rows, wide),
        in_specs=[scalars()] + [whole()] * 14 + [in_place()],
        out_specs=[whole()] * 5,
        out_shape=[
            shape_of((tokens, 3 * wide)),
            shape_of((tokens, 3 * SR)),
            shape_of((4 * 5 * SR, wide)),
            shape_of((4 * 5 * SR, wide)),
            shape_of((3 * SR, wide)),
        ],
        scratch_shapes=[
            pltpu.VMEM((tokens, wide), jnp.bfloat16),
            pltpu.VMEM((tokens, width), jnp.bfloat16),
            pltpu.SemaphoreType.DMA((1,)),
        ],
        compiler_params=params(),
        cost_estimate=cost(1 << 20, 1 << 16),
        name="attend_back",
    )(me, q, k, v, att, lse, seg_col, seg_row, cosine, sine, low, mask, up, got, out_grad, normed)


def unproject_kernel(rows, width, wide, me_ref, proj_ref, low_ref, *refs):
    bf16 = jnp.bfloat16
    given, w_hbm = blocks_of(refs[:GATHERED]), refs[GATHERED]
    even_ref, odd_ref, weight, sems, w_sems = refs[GATHERED + 1 :]
    me, thin = me_ref[0], 3 * SR

    @pl.when(pl.program_id(0) == 0)
    def _():
        copies = []
        for j in range(EVERY):
            at = pl.multiple_of((me ^ j) * wide, wide)
            for i in range(3):
                copies.append(
                    pltpu.make_async_copy(
                        w_hbm.at[j, i],
                        weight.at[j * wide : (j + 1) * wide, i * wide : (i + 1) * wide],
                        w_sems.at[j, i],
                    )
                )
            for part in range(2):
                start = part * thin
                copies.append(
                    pltpu.make_async_copy(
                        given[j].at[:, start : start + thin],
                        weight.at[pl.ds(at + part * rows, rows), 3 * wide : 3 * wide + thin],
                        sems.at[j, part],
                    )
                )
        for item in copies:
            item.start()
        for item in copies:
            item.wait()

    both = jnp.concatenate([proj_ref[...], low_ref[...]], axis=1)
    for j in range(width // CUT):
        lanes = slice(j * CUT, (j + 1) * CUT)
        value = mm_nt(both, weight[lanes, :]).astype(bf16)
        even_ref[:, lanes] = value[:rows]
        odd_ref[:, lanes] = value[rows:]


def unproject(rows, me, d_proj, d_low, given, w_got):
    tokens = d_proj.shape[0]
    wide = d_proj.shape[1] // 3
    width = wide * EVERY
    return pl.pallas_call(
        functools.partial(unproject_kernel, rows, width, wide),
        grid=(tokens // TILE,),
        in_specs=[scalars(), by_tile(TILE, 3 * wide), by_tile(TILE, 3 * SR)] + [in_place()] * (GATHERED + 1),
        out_specs=[by_tile(rows, width)] * 2,
        out_shape=[shape_of((tokens // 2, width))] * 2,
        scratch_shapes=[
            pltpu.VMEM((width, 3 * wide + 3 * SR), jnp.bfloat16),
            pltpu.SemaphoreType.DMA((EVERY, 2)),
            pltpu.SemaphoreType.DMA((EVERY, 3)),
        ],
        compiler_params=params(),
        cost_estimate=cost(1 << 20, 1 << 16),
        name="unproject",
    )(me, d_proj, d_low, *given, w_got)


def finish_kernel(hidden_ref, gains_ref, resid_grad_ref, *refs):
    pieces, out_ref = refs[:PIECES], refs[PIECES]
    d_normed = sum_pieces(*[ref[...] for ref in pieces])
    back = norm_grad(hidden_ref[...].astype(jnp.float32), gains_ref[0:1, :], d_normed)
    out_ref[...] = (resid_grad_ref[...] + back).astype(jnp.bfloat16)


def finish(hidden, gains, resid_grad, pieces):
    rows, width = hidden.shape
    return pl.pallas_call(
        finish_kernel,
        grid=(1,),
        in_specs=[whole()] * 3 + piece_specs(rows, width),
        out_specs=whole(),
        out_shape=shape_of((rows, width)),
        compiler_params=params(),
        cost_estimate=cost(1 << 20, 1 << 16),
        name="finish",
    )(hidden, gains, resid_grad, *pieces)


def layer_kernel(resid_ref, *refs):
    pieces, out_ref = refs[:PIECES], refs[PIECES]
    out_ref[...] = (resid_ref[...] + sum_pieces(*[ref[...] for ref in pieces])).astype(jnp.bfloat16)


def layer(resid, pieces):
    rows, width = resid.shape
    return pl.pallas_call(
        layer_kernel,
        grid=(1,),
        in_specs=[whole()] + piece_specs(rows, width),
        out_specs=whole(),
        out_shape=shape_of((rows, width)),
        compiler_params=params(),
        cost_estimate=cost(1 << 20, 1 << 16),
        name="layer",
    )(resid, *pieces)


def unpack_kernel(hidden, first, where_ref, *refs):
    f32 = jnp.float32
    parts, refs = refs[:8], refs[8:]
    refs = refs if first else refs[4:]
    a_in_ref, b_in_ref, a_down_ref, b_down_ref, packed = refs
    size = packed.shape[0] // 4
    for b in range(4):
        for i in range(2):
            spot = pl.multiple_of((where_ref[0] ^ b) * size + i * (size // 2), 8)
            packed[pl.ds(spot, size // 2), :] = parts[2 * b + i][...].astype(f32)
    for i in range(2):
        a_in_ref[0, i] = packed[i * SR : (i + 1) * SR, :].T
        b_in_ref[0, i] = packed[3 * SR : 4 * SR, i * hidden : (i + 1) * hidden]
    b_down_ref[0] = packed[2 * SR : 3 * SR, :]
    a_down_ref[0, :, 0 : SR // 2] = packed[4 * SR :, 0:hidden].T
    a_down_ref[0, :, SR // 2 :] = packed[4 * SR :, hidden:].T


def unpack(k, where, quarters, hidden, experts, before):
    quarters = [part for quarter in quarters for part in quarter]
    width = quarters[0].shape[1]
    f32 = jnp.float32
    first = before is None
    shapes = [(experts, 2, width, SR), (experts, 2, SR, hidden), (experts, hidden, SR), (experts, SR, width)]
    given = [] if first else list(before)
    return pl.pallas_call(
        functools.partial(unpack_kernel, hidden, first),
        grid=(1,),
        in_specs=[scalars()] + [whole()] * 8 + [in_place()] * len(given),
        out_specs=[
            pl.BlockSpec((1,) + shape[1:], lambda i, n=len(shape): (k,) + (0,) * (n - 1)) for shape in shapes
        ],
        out_shape=[shape_of(shape, f32) for shape in shapes],
        input_output_aliases={} if first else {9 + i: i for i in range(4)},
        scratch_shapes=[pltpu.VMEM((4 * SR + SR // 2, width), f32)],
        compiler_params=params(),
        cost_estimate=cost(1 << 20, 1 << 16),
        name="unpack",
    )(where, *quarters, *given)


def thin_kernel(left_ref, right_ref, a_ref, b_ref):
    total = left_ref[...].astype(jnp.float32) + right_ref[...].astype(jnp.float32)
    for i in range(4):
        at = (2 + i) * SR if i < 3 else 0
        a_ref[i] = total[at : at + SR, :].T
        at = (5 + i) * SR if i < 3 else SR
        b_ref[i] = total[at : at + SR, :].T


def thin_grads(left, right):
    wide = left.shape[1]
    return pl.pallas_call(
        thin_kernel,
        in_specs=[whole()] * 2,
        out_specs=[whole()] * 2,
        out_shape=[shape_of((4, wide, SR), jnp.float32)] * 2,
        compiler_params=params(),
        cost_estimate=cost(1 << 20, 1 << 16),
        name="thin_grads",
    )(left, right)


def split_layer(
    hidden_in,
    segments,
    routes,
    doc_sets,
    cotangent,
    w_qkv,
    w_out,
    gain_attn,
    gain_moe,
    router,
    w_gate,
    w_up,
    w_down,
    a_attn,
    b_attn,
    exp_a_in,
    exp_b_in,
    exp_a_down,
    exp_b_down,
):
    bf16, f32 = jnp.bfloat16, jnp.float32
    index = lax.axis_index("fsdp")
    me = index.astype(jnp.int32).reshape(1)
    where = lax.axis_index("rep").astype(jnp.int32).reshape(1)
    hidden, upstream = hidden_in[0], cotangent[0]
    rows, width = hidden.shape
    wide = width // EVERY
    local, _, inner = w_gate.shape
    experts_all = local * EVERY

    order = index ^ jnp.arange(EVERY)
    positions = (order[:, None] * rows + jnp.arange(rows)[None, :]).reshape(-1)
    cosine, sine = rope_tables(positions, HD)
    cosine, sine = jnp.concatenate([cosine, cosine], axis=1), jnp.concatenate([-sine, sine], axis=1)
    lanes = jnp.arange(128)
    named = jnp.any(routes[0][:, :, None] + SPOT == lanes[None, None, :], axis=1).astype(f32)
    out_own = jnp.concatenate([w_out, a_attn[3], b_attn[3]], axis=1)

    def picks(k):
        high = (lanes == SPOT + 2 * index + k).astype(f32)
        low = (lanes == SPOT + 2 * index + k + 64).astype(f32)
        return jnp.stack([high + low, high, low] + [jnp.zeros_like(high)] * 5)

    hidden_first = gather_first(hidden)
    narrow = jnp.concatenate([a_attn[0], a_attn[1], a_attn[2]], axis=1)
    at_spot = ((0, 0), (SPOT, 128 - SPOT - experts_all))
    meta = jnp.pad(router[:rows], at_spot) + jnp.pad(segments[0].astype(bf16)[:, None], ((0, 0), (0, 127)))
    lines = jnp.concatenate([gain_attn.reshape(2, 128), gain_moe.reshape(2, 128)], axis=0)
    lines = jnp.pad(lines, ((0, rows - 4), (0, 0)))
    given = jnp.concatenate([narrow[:rows], narrow[rows:], meta, jnp.pad(router[rows:], at_spot), lines], axis=1)
    given_first = gather_first(given)
    w_got = lax.all_to_all(by_columns(w_qkv, wide), "fsdp", split_axis=0, concat_axis=0, tiled=True)
    hidden_first, cosine, sine, out_own, named, pick_rows = tie(
        hidden_first, cosine, sine, out_own, named, [picks(0), picks(1)]
    )
    hidden_given = gather_third(hidden_first, *gather_second(*hidden_first))
    given = gather_third(given_first, *gather_second(*given_first))

    hidden_given, given, w_got, out_own = tie(hidden_given, given, w_got, out_own)
    out_first = gather_first(out_own)
    queries, keys, values, normed_one, low_qkv, mask, seg_col, seg_row, gains, router_all = project(
        me, doc_sets, cosine, sine, b_attn, hidden_given, given, w_got
    )
    att, lse, att_send = attend(rows, me, queries, keys, values, seg_col, seg_row)
    att_send, out_first = tie(att_send, out_first)
    att_got = lax.all_to_all(att_send, "fsdp", split_axis=0, concat_axis=0, tiled=True)
    far, *others = gather_second(*out_first)
    far, others, att_got, upstream_now = tie(far, others, att_got, upstream)
    cot_first = gather_first(upstream_now)
    out_given = gather_third(out_first, far, *others)
    resid_one, normed_own, low_out, gates_own = mix(
        me, hidden, gains, mask, router_all, named, att_got, out_given
    )
    normed_own, cot_first = tie(normed_own, cot_first)
    normed_given = gather_relative(normed_own)
    cot_given = gather_third(cot_first, *gather_second(*cot_first))

    weights = (w_gate, w_up, w_down, exp_a_in, exp_b_in, exp_a_down, exp_b_down)
    *state, d_all_a, extra_a, kept_a, sent_a = expert_pass(
        0, where, normed_given, cot_given, mask, pick_rows[0], None, weights
    )
    def in_two(values):
        return [values[: values.shape[0] // 2], values[values.shape[0] // 2 :]]

    def later(values, anchor):
        return tie(values, anchor)[0]

    def in_two(values):
        return [values[: values.shape[0] // 2], values[values.shape[0] // 2 :]]

    sent_a = rep_swap(sent_a, 1)
    *state, d_all_b, extra_b, kept_b, sent_b = expert_pass(
        1, where, normed_given, cot_given, mask, pick_rows[1], state, weights
    )
    d_all_b, kept_b, sent_b, sent_a, state = tie(d_all_b, kept_b, sent_b, sent_a, state)
    out_even, out_odd = state
    half_a = add_half(kept_a, sent_a)
    size = half_a.shape[0] // 2
    sent_b, kept_b = in_two(sent_b), in_two(kept_b)
    sent_b[0] = rep_swap(sent_b[0], 1)
    other_a = rep_swap(half_a[size:], 2)
    out_got = swap(out_odd, 1)
    row_even, row_odd = rows_pass(rows, [d_all_a, d_all_b], [extra_a, extra_b], w_gate, w_up, exp_a_in)
    row_odd, other_a, sent_b[0], out_got = tie(row_odd, other_a, sent_b[0], out_got)
    got = swap(row_odd, 1)
    sent_b[1] = rep_swap(later(sent_b[1], row_odd), 1)
    total_a = in_two(add_half(half_a[:size], other_a))
    d_far = scatter_second(row_even, got)
    d_far, sent_b[1] = tie(d_far, sent_b[1])
    pieces = scatter_third(row_even, got, *d_far)
    two_a = [rep_swap(later(total_a[0], d_far), 2)]
    pieces, two_a[0] = tie(pieces, two_a[0])
    early_a = later(total_a, pieces)
    two_a.append(rep_swap(early_a[1], 2))
    one_a = [None, rep_swap(early_a[1], 1)]
    d_resid, thin_send, d_att_send = unmix(
        me, resid_one, upstream, gains, mask, router_all, gates_own, low_out, att_got, pieces, out_given
    )
    d_att_send, two_a[1], one_a[1] = tie(d_att_send, two_a[1], one_a[1])
    d_att_got = lax.all_to_all(d_att_send, "fsdp", split_axis=0, concat_axis=0, tiled=True)
    mine_b = add_half(kept_b[0], sent_b[0])
    half_b = later(in_two(add_half(kept_b[1], sent_b[1])), d_att_send)
    one_a[0] = rep_swap(later(total_a[0], d_att_send), 1)
    other_b = [rep_swap(half_b[0], 2)]
    d_att_got, other_b[0], one_a[0] = tie(d_att_got, other_b[0], one_a[0])
    total_b = [add_half(mine_b[: size // 2], other_b[0])]
    other_b.append(rep_swap(later(half_b[1], d_att_got), 2))
    three_a = [rep_swap(later(two_a[0], d_att_got), 1)]
    d_proj, d_low, thin_even, thin_odd, up_grads = attend_back(
        rows, me, queries, keys, values, att, lse, seg_col, seg_row, cosine, sine, low_qkv, mask, b_attn,
        d_att_got, thin_send, normed_one,
    )
    d_proj, thin_odd, other_b[1], three_a[0] = tie(d_proj, thin_odd, other_b[1], three_a[0])
    thin_got = swap(thin_odd, 1)
    two_b = [rep_swap(later(total_b[0], d_proj), 2)]
    three_a.append(rep_swap(later(two_a[1], d_proj), 1))
    even, odd = unproject(rows, me, d_proj, d_low, given, w_got)
    odd, thin_got, two_b[0], three_a[1] = tie(odd, thin_got, two_b[0], three_a[1])
    total_b.append(later(add_half(mine_b[size // 2 :], other_b[1]), odd))
    got = swap(odd, 1)
    thin_far = scatter_second(thin_even, thin_got)
    one_b = [rep_swap(later(total_b[0], odd), 1)]
    got, thin_far, one_b[0] = tie(got, thin_far, one_b[0])
    thin_pieces = scatter_third(thin_even, thin_got, *thin_far)
    d_far = scatter_second(even, got)
    two_b.append(rep_swap(later(total_b[1], got), 2))
    d_far, thin_pieces, two_b[1] = tie(d_far, thin_pieces, two_b[1])
    pieces = scatter_third(even, got, *d_far)
    thin = jnp.concatenate(
        [sum_pieces(*[piece[: 5 * SR] for piece in thin_pieces]).astype(bf16), up_grads], axis=0
    )
    thin_near = rep_swap(thin, 1)
    out_far = scatter_second(*later((out_even, out_got), d_far))
    grads = unpack(0, where, later([total_a, one_a, two_a, three_a], d_far), inner, local, None)
    pieces, thin_near, out_far, grads = tie(pieces, thin_near, out_far, grads)
    thin = add_half(thin, thin_near)
    thin_last = rep_swap(thin, 2)
    late_b = later([total_b[1], two_b], pieces)
    one_b.append(rep_swap(late_b[0], 1))
    three_b = [rep_swap(part, 1) for part in late_b[1]]
    out_pieces = scatter_third(out_even, out_got, *out_far)
    grad_in = finish(hidden, gains, d_resid, pieces)
    layer_out = layer(resid_one, out_pieces)
    one_b, three_b, thin_last, layer_out, grad_in = tie(one_b, three_b, thin_last, layer_out, grad_in)
    grads = unpack(1, where, [total_b, one_b, two_b, three_b], inner, local, grads)
    grad_a, grad_b = thin_grads(thin, thin_last)
    return (layer_out[None], grad_in[None], grad_a, grad_b, *grads)


def solution(mesh):
    shape = dict(mesh.shape)
    shards = split_layer if shape == {"rep": 4, "fsdp": EVERY} else gathered_layer
    return jax.shard_map(
        shards,
        mesh=mesh,
        in_specs=(
            P("rep", "fsdp", None),
            P("rep", "fsdp"),
            P("rep", "fsdp", None),
            P("rep", None),
            P("rep", "fsdp", None),
            P(None, "fsdp", None),
            P("fsdp", None),
            P("fsdp"),
            P("fsdp"),
            P("fsdp", None),
            P("fsdp", None, None),
            P("fsdp", None, None),
            P("fsdp", None, None),
            P(None, "fsdp", None),
            P(None, "fsdp", None),
            P("fsdp", None, None, None),
            P("fsdp", None, None, None),
            P("fsdp", None, None),
            P("fsdp", None, None),
        ),
        out_specs=(
            P("rep", "fsdp", None),
            P("rep", "fsdp", None),
            P(None, "fsdp", None),
            P(None, "fsdp", None),
            P("fsdp", None, None, None),
            P("fsdp", None, None, None),
            P("fsdp", None, None),
            P("fsdp", None, None),
        ),
        check_vma=False,
    )
```

```python
import functools
import math

import jax
import jax.numpy as jnp
from jax import lax
from jax.experimental import pallas as pl
from jax.experimental.pallas import tpu as pltpu
from jax.sharding import PartitionSpec as P

HD = 128
TOP = 8
R = 16
SETS = 8
SR = 128


EPSILON = 1e-05
MASKED = -1e30


def rms_scale(values):
    return values * lax.rsqrt(jnp.mean(values * values, axis=-1, keepdims=True) + EPSILON)


def norm_back(values, gain_row, upstream_grad):
    result, pull_back = jax.vjp(lambda inner_rows: rms_scale(inner_rows) * gain_row, values)
    return pull_back(upstream_grad)[0]


def rope_tables(positions, head_size):
    half_size = head_size // 2
    inv_freq = jnp.exp(
        jnp.arange(half_size, dtype=jnp.float32) * (-2.0 * math.log(10000.0) / head_size)
    )
    angles = positions.astype(jnp.float32)[:, None] * inv_freq[None, :]
    return (jnp.cos(angles), jnp.sin(angles))


def rotate(values, cosine, sine_table):
    half_size = values.shape[-1] // 2
    front_half = values[..., :half_size]
    back_half = values[..., half_size:]
    cos_rows = cosine[:, None, :]
    sin_rows = sine_table[:, None, :]
    return jnp.concatenate(
        [
            front_half * cos_rows - back_half * sin_rows,
            back_half * cos_rows + front_half * sin_rows,
        ],
        axis=-1,
    )


def gathered_layer(
    hidden_in,
    segments,
    routes,
    doc_sets,
    cotangent,
    w_qkv,
    w_out,
    gain_attn,
    gain_moe,
    router,
    w_gate,
    w_up,
    w_down,
    a_attn,
    b_attn,
    exp_a_in,
    exp_b_in,
    exp_a_down,
    exp_b_down,
):
    shard_count = lax.axis_size("fsdp")
    shard_index = lax.axis_index("fsdp")
    tok_rows = hidden_in.shape[1]
    model_width = hidden_in.shape[2]
    head_count = model_width // HD
    local_experts = w_gate.shape[0]
    experts_all = local_experts * shard_count
    capacity = max(2, 3 * tok_rows * TOP // (2 * experts_all))
    score_scale = HD ** (-0.5)
    (
        attention_weight_full,
        output_weight_full,
        adapter_down_weight,
        adapter_up_weight,
        first_norm_gain_full,
        second_norm_gain_full,
        router_weight_full,
    ) = (
        lax.all_gather(w_qkv, "fsdp", axis=1, tiled=True),
        lax.all_gather(w_out, "fsdp", axis=0, tiled=True),
        lax.all_gather(a_attn, "fsdp", axis=1, tiled=True),
        lax.all_gather(b_attn, "fsdp", axis=1, tiled=True),
        lax.all_gather(gain_attn, "fsdp", axis=0, tiled=True),
        lax.all_gather(gain_moe, "fsdp", axis=0, tiled=True),
        lax.all_gather(router, "fsdp", axis=0, tiled=True),
    )
    gain_one = first_norm_gain_full.astype(jnp.float32)
    gain_two = second_norm_gain_full.astype(jnp.float32)
    seg_local = segments[0]
    set_token = jnp.sum(
        jnp.where(seg_local[:, None] == jnp.arange(SETS)[None, :], doc_sets[0][None, :], 0), axis=1
    )
    document_set_mask = (set_token[:, None] == (jnp.arange(SR) // R)[None, :]).astype(jnp.float32)
    mask_half = document_set_mask.astype(jnp.bfloat16)
    hidden_f = hidden_in[0].astype(jnp.float32)
    first_normed_rows = (rms_scale(hidden_f) * gain_one).astype(jnp.bfloat16)
    attention_rank_branch = (
        jnp.einsum(
            "xj,zje->zxe",
            first_normed_rows,
            adapter_down_weight[:3],
            preferred_element_type=jnp.float32,
        )
        * document_set_mask[None]
    ).astype(jnp.bfloat16)
    projected = jnp.einsum(
        "td,pde->pte", first_normed_rows, attention_weight_full, preferred_element_type=jnp.float32
    ) + jnp.einsum(
        "nzv,nwv->nzw",
        attention_rank_branch,
        adapter_up_weight[:3],
        preferred_element_type=jnp.float32,
    )
    positions = shard_index * tok_rows + jnp.arange(tok_rows)
    cosine, sine_table = rope_tables(positions, HD)
    queries = rotate(projected[0].reshape(tok_rows, head_count, HD), cosine, sine_table).astype(
        jnp.bfloat16
    )
    keys_own = (
        rotate(projected[1].reshape(tok_rows, head_count, HD), cosine, sine_table)
        .astype(jnp.bfloat16)
        .reshape(tok_rows, model_width)
    )
    values_own = projected[2].astype(jnp.bfloat16)
    seg_own = seg_local.astype(jnp.bfloat16)
    run_max = jnp.full((head_count, tok_rows), MASKED, jnp.float32)
    key_piece = lax.all_gather(keys_own, "fsdp", axis=0, tiled=True)
    value_piece = lax.all_gather(values_own, "fsdp", axis=0, tiled=True)
    seg_piece = lax.all_gather(seg_own, "fsdp", axis=0, tiled=True)
    piece_rows = key_piece.shape[0]
    scores = (
        jnp.einsum(
            "qhd,khd->hqk",
            queries,
            key_piece.reshape(piece_rows, head_count, HD),
            preferred_element_type=jnp.float32,
        )
        * score_scale
    )
    same_doc = seg_local[:, None] == seg_piece.astype(jnp.int32)[None, :]
    scores = jnp.where(same_doc[None], scores, MASKED)
    new_max = jnp.maximum(run_max, jnp.max(scores, axis=2))
    exp_scores = jnp.exp(scores - new_max[:, :, None])
    new_sum = jnp.sum(exp_scores, axis=2)
    new_acc = jnp.einsum(
        "hqk,khd->qhd",
        exp_scores.astype(jnp.bfloat16),
        value_piece.reshape(piece_rows, head_count, HD),
        preferred_element_type=jnp.float32,
    )
    folded = (new_max, new_sum, new_acc)
    run_max, run_sum, run_acc = folded
    log_sum = run_max + jnp.log(run_sum)
    attended = run_acc / jnp.transpose(run_sum)[:, :, None]
    attention_rounded_rows = attended.reshape(tok_rows, model_width).astype(jnp.bfloat16)
    output_rank_branch = (
        jnp.dot(attention_rounded_rows, adapter_down_weight[3], preferred_element_type=jnp.float32)
        * document_set_mask
    ).astype(jnp.bfloat16)
    resid_one = hidden_f + (
        jnp.dot(attention_rounded_rows, output_weight_full, preferred_element_type=jnp.float32)
        + jnp.einsum(
            "nd,gd->ng",
            output_rank_branch,
            adapter_up_weight[3],
            preferred_element_type=jnp.float32,
        )
    )
    normed_two = (rms_scale(resid_one) * gain_two).astype(jnp.bfloat16)
    logits = jnp.dot(normed_two, router_weight_full, preferred_element_type=jnp.float32)
    my_routes = routes[0]
    gate_weights = jax.nn.softmax(jnp.take_along_axis(logits, my_routes, axis=1), axis=-1)
    flat_routes = my_routes.reshape(-1)
    one_hot = (flat_routes[:, None] == jnp.arange(experts_all)[None, :]).astype(jnp.int32)
    slot_index = jnp.sum((jnp.cumsum(one_hot, axis=0) - 1) * one_hot, axis=1)
    token_index = jnp.arange(tok_rows * TOP) // TOP
    send_rows = (
        jnp.zeros((experts_all, capacity, model_width), jnp.bfloat16)
        .at[flat_routes, slot_index]
        .set(normed_two[token_index])
    )
    send_sets = (
        jnp.zeros((experts_all, capacity), jnp.bfloat16)
        .at[flat_routes, slot_index]
        .set(set_token[token_index].astype(jnp.bfloat16))
    )
    rows_got = lax.all_to_all(
        send_rows.reshape(shard_count, local_experts, capacity, model_width),
        "fsdp",
        split_axis=0,
        concat_axis=0,
        tiled=True,
    )
    sets_got = lax.all_to_all(
        send_sets.reshape(shard_count, local_experts, capacity),
        "fsdp",
        split_axis=0,
        concat_axis=0,
        tiled=True,
    )
    slot_mask = (sets_got.astype(jnp.int32)[..., None] == jnp.arange(SR) // R).astype(jnp.float32)
    low_in = (
        jnp.einsum("necd,eids->necis", rows_got, exp_a_in, preferred_element_type=jnp.float32)
        * slot_mask[:, :, :, None, :]
    ).astype(jnp.bfloat16)
    gate_h = jnp.einsum(
        "necd,edf->necf", rows_got, w_gate, preferred_element_type=jnp.float32
    ) + jnp.einsum(
        "necs,esf->necf", low_in[:, :, :, 0], exp_b_in[:, 0], preferred_element_type=jnp.float32
    )
    up_h = jnp.einsum(
        "necd,edf->necf", rows_got, w_up, preferred_element_type=jnp.float32
    ) + jnp.einsum(
        "necs,esf->necf", low_in[:, :, :, 1], exp_b_in[:, 1], preferred_element_type=jnp.float32
    )
    activation = (jax.nn.silu(gate_h) * up_h).astype(jnp.bfloat16)
    low_down = (
        jnp.einsum("necf,efs->necs", activation, exp_a_down, preferred_element_type=jnp.float32)
        * slot_mask
    ).astype(jnp.bfloat16)
    expert_out = (
        jnp.einsum("necf,efd->necd", activation, w_down, preferred_element_type=jnp.float32)
        + jnp.einsum("necs,esd->necd", low_down, exp_b_down, preferred_element_type=jnp.float32)
    ).astype(jnp.bfloat16)
    expert_out, rows_got, slot_mask, low_in, gate_h, up_h, activation, low_down = (
        expert_out,
        rows_got,
        slot_mask,
        low_in,
        gate_h,
        up_h,
        activation,
        low_down,
    )
    returned = lax.all_to_all(expert_out, "fsdp", split_axis=0, concat_axis=0, tiled=True)
    route_out = (
        returned.reshape(experts_all, capacity, model_width)[flat_routes, slot_index]
        .reshape(tok_rows, TOP, model_width)
        .astype(jnp.float32)
    )
    layer_value = resid_one + jnp.sum(gate_weights[:, :, None] * route_out, axis=1)
    (
        attention_weight_full,
        output_weight_full,
        adapter_down_weight,
        adapter_up_weight,
        first_norm_gain_full,
        second_norm_gain_full,
        router_weight_full,
    ) = (
        lax.all_gather(w_qkv, "fsdp", axis=1, tiled=True),
        lax.all_gather(w_out, "fsdp", axis=0, tiled=True),
        lax.all_gather(a_attn, "fsdp", axis=1, tiled=True),
        lax.all_gather(b_attn, "fsdp", axis=1, tiled=True),
        lax.all_gather(gain_attn, "fsdp", axis=0, tiled=True),
        lax.all_gather(gain_moe, "fsdp", axis=0, tiled=True),
        lax.all_gather(router, "fsdp", axis=0, tiled=True),
    )
    gain_one = first_norm_gain_full.astype(jnp.float32)
    gain_two = second_norm_gain_full.astype(jnp.float32)
    upstream = cotangent[0].astype(jnp.float32)
    d_route = (gate_weights[:, :, None] * upstream[:, None, :]).astype(jnp.bfloat16)
    d_gates = jnp.sum(upstream[:, None, :] * route_out, axis=2)
    d_chosen = gate_weights * (d_gates - jnp.sum(gate_weights * d_gates, axis=1, keepdims=True))
    d_logits = jnp.sum(
        jnp.where(
            my_routes[:, :, None] == jnp.arange(experts_all)[None, None, :],
            d_chosen[:, :, None],
            0.0,
        ),
        axis=1,
    ).astype(jnp.bfloat16)
    send_grads = (
        jnp.zeros((experts_all, capacity, model_width), jnp.bfloat16)
        .at[flat_routes, slot_index]
        .set(d_route.reshape(tok_rows * TOP, model_width))
    )
    grads_got = lax.all_to_all(
        send_grads.reshape(shard_count, local_experts, capacity, model_width),
        "fsdp",
        split_axis=0,
        concat_axis=0,
        tiled=True,
    )
    slot_half = slot_mask.astype(jnp.bfloat16)
    d_low_down = (
        jnp.einsum(
            "necd,esd->necs", grads_got, exp_b_down, preferred_element_type=jnp.float32
        ).astype(jnp.bfloat16)
        * slot_half
    )
    d_activation = jnp.einsum(
        "necd,efd->necf", grads_got, w_down, preferred_element_type=jnp.float32
    ) + jnp.einsum("necs,efs->necf", d_low_down, exp_a_down, preferred_element_type=jnp.float32)
    silu_value, silu_pull = jax.vjp(
        lambda gate_in, up_in: jax.nn.silu(gate_in) * up_in, gate_h, up_h
    )
    d_gate_h, d_up_h = silu_pull(d_activation)
    d_gate_h = d_gate_h.astype(jnp.bfloat16)
    d_up_h = d_up_h.astype(jnp.bfloat16)
    d_both = jnp.stack([d_gate_h, d_up_h], axis=3)
    d_low_in = (
        jnp.einsum(
            "necif,eisf->necis", d_both, exp_b_in, preferred_element_type=jnp.float32
        ).astype(jnp.bfloat16)
        * slot_half[:, :, :, None, :]
    )
    d_rows = (
        jnp.einsum("necf,edf->necd", d_gate_h, w_gate, preferred_element_type=jnp.float32)
        + jnp.einsum("necf,edf->necd", d_up_h, w_up, preferred_element_type=jnp.float32)
        + jnp.einsum("necis,eids->necd", d_low_in, exp_a_in, preferred_element_type=jnp.float32)
    )
    returned_grads = lax.all_to_all(
        d_rows.astype(jnp.bfloat16), "fsdp", split_axis=0, concat_axis=0, tiled=True
    )
    g_exp_b_down = jnp.einsum(
        "necs,necd->esd", low_down, grads_got, preferred_element_type=jnp.float32
    )
    g_exp_a_down = jnp.einsum(
        "necf,necs->efs", activation, d_low_down, preferred_element_type=jnp.float32
    )
    g_exp_b_in = jnp.einsum("necis,necif->eisf", low_in, d_both, preferred_element_type=jnp.float32)
    g_exp_a_in = jnp.einsum(
        "necd,necis->eids", rows_got, d_low_in, preferred_element_type=jnp.float32
    )
    d_normed_two = jnp.sum(
        returned_grads.reshape(experts_all, capacity, model_width)[flat_routes, slot_index]
        .reshape(tok_rows, TOP, model_width)
        .astype(jnp.float32),
        axis=1,
    ) + jnp.einsum("te,de->td", d_logits, router_weight_full, preferred_element_type=jnp.float32)
    d_resid_one = upstream + norm_back(resid_one, gain_two, d_normed_two)
    branch_gradient = d_resid_one.astype(jnp.bfloat16)
    output_adapter_gradient = (
        jnp.dot(branch_gradient, adapter_up_weight[3], preferred_element_type=jnp.float32).astype(
            jnp.bfloat16
        )
        * mask_half
    )
    d_att = (
        jnp.einsum(
            "te,de->td", branch_gradient, output_weight_full, preferred_element_type=jnp.float32
        )
        + jnp.einsum(
            "cr,ar->ca",
            output_adapter_gradient,
            adapter_down_weight[3],
            preferred_element_type=jnp.float32,
        )
    ).astype(jnp.bfloat16)
    output_up_gradient = jnp.einsum(
        "ts,te->es", output_rank_branch, branch_gradient, preferred_element_type=jnp.float32
    )
    output_down_gradient = jnp.einsum(
        "td,ts->ds",
        attention_rounded_rows,
        output_adapter_gradient,
        preferred_element_type=jnp.float32,
    )
    d_att_heads = d_att.reshape(tok_rows, head_count, HD)
    delta_rows = jnp.transpose(jnp.sum(d_att_heads.astype(jnp.float32) * attended, axis=2))
    key_piece = lax.all_gather(keys_own, "fsdp", axis=0, tiled=True)
    value_piece = lax.all_gather(values_own, "fsdp", axis=0, tiled=True)
    seg_piece = lax.all_gather(seg_own, "fsdp", axis=0, tiled=True)
    piece_rows = key_piece.shape[0]
    key_heads = key_piece.reshape(piece_rows, head_count, HD)
    value_heads = value_piece.reshape(piece_rows, head_count, HD)
    scores = (
        jnp.einsum("qhd,khd->hqk", queries, key_heads, preferred_element_type=jnp.float32)
        * score_scale
    )
    same_doc = seg_local[:, None] == seg_piece.astype(jnp.int32)[None, :]
    scores = jnp.where(same_doc[None], scores, MASKED)
    soft_probs = jnp.exp(scores - log_sum[:, :, None])
    d_probs = jnp.einsum(
        "qhd,khd->hqk", d_att_heads, value_heads, preferred_element_type=jnp.float32
    )
    d_scores = (soft_probs * (d_probs - delta_rows[:, :, None])).astype(jnp.bfloat16)
    soft_probs, d_scores = (soft_probs, d_scores)
    d_query_part = jnp.einsum(
        "hqk,khd->qhd", d_scores, key_heads, preferred_element_type=jnp.float32
    )
    d_key_part = jnp.einsum(
        "hqk,qhd->khd", d_scores, queries, preferred_element_type=jnp.float32
    ).reshape(piece_rows, model_width)
    d_value_part = jnp.einsum(
        "hqk,qhd->khd",
        soft_probs.astype(jnp.bfloat16),
        d_att_heads,
        preferred_element_type=jnp.float32,
    ).reshape(piece_rows, model_width)
    back_state = (d_query_part, d_key_part, d_value_part)
    d_query, d_keys_all, d_values_all = back_state
    d_keys_mine, d_values_mine = (
        lax.psum_scatter(
            d_keys_all.astype(jnp.bfloat16), "fsdp", scatter_dimension=0, tiled=True
        ).astype(jnp.float32),
        lax.psum_scatter(
            d_values_all.astype(jnp.bfloat16), "fsdp", scatter_dimension=0, tiled=True
        ).astype(jnp.float32),
    )
    d_query_pre = (
        rotate(d_query * score_scale, cosine, -sine_table)
        .reshape(tok_rows, model_width)
        .astype(jnp.bfloat16)
    )
    d_key_pre = (
        rotate((d_keys_mine * score_scale).reshape(tok_rows, head_count, HD), cosine, -sine_table)
        .reshape(tok_rows, model_width)
        .astype(jnp.bfloat16)
    )
    projected_gradient = jnp.stack([d_query_pre, d_key_pre, d_values_mine.astype(jnp.bfloat16)])
    projection_adapter_gradient = (
        jnp.einsum(
            "jah,jho->jao",
            projected_gradient,
            adapter_up_weight[:3],
            preferred_element_type=jnp.float32,
        ).astype(jnp.bfloat16)
        * mask_half[None]
    )
    d_normed_one = jnp.einsum(
        "pte,pde->td", projected_gradient, attention_weight_full, preferred_element_type=jnp.float32
    ) + jnp.einsum(
        "czn,cvn->zv",
        projection_adapter_gradient,
        adapter_down_weight[:3],
        preferred_element_type=jnp.float32,
    )
    attention_up_gradient = jnp.einsum(
        "pts,pte->pes",
        attention_rank_branch,
        projected_gradient,
        preferred_element_type=jnp.float32,
    )
    attention_down_gradient = jnp.einsum(
        "td,pts->pds",
        first_normed_rows,
        projection_adapter_gradient,
        preferred_element_type=jnp.float32,
    )
    d_hidden = d_resid_one + norm_back(hidden_f, gain_one, d_normed_one)
    adapter_down_gradient = jnp.concatenate(
        [attention_down_gradient, output_down_gradient[None]], axis=0
    )
    adapter_up_gradient = jnp.concatenate([attention_up_gradient, output_up_gradient[None]], axis=0)
    part_down, part_up = (
        lax.psum_scatter(
            adapter_down_gradient.astype(jnp.bfloat16), "fsdp", scatter_dimension=1, tiled=True
        ).astype(jnp.float32),
        lax.psum_scatter(
            adapter_up_gradient.astype(jnp.bfloat16), "fsdp", scatter_dimension=1, tiled=True
        ).astype(jnp.float32),
    )
    summed = (
        lax.psum(part_down.astype(jnp.bfloat16), "rep").astype(jnp.float32),
        lax.psum(part_up.astype(jnp.bfloat16), "rep").astype(jnp.float32),
        lax.psum(g_exp_a_in.astype(jnp.bfloat16), "rep").astype(jnp.float32),
        lax.psum(g_exp_b_in.astype(jnp.bfloat16), "rep").astype(jnp.float32),
        lax.psum(g_exp_a_down.astype(jnp.bfloat16), "rep").astype(jnp.float32),
        lax.psum(g_exp_b_down.astype(jnp.bfloat16), "rep").astype(jnp.float32),
    )
    return (
        layer_value.astype(jnp.bfloat16)[None],
        d_hidden.astype(jnp.bfloat16)[None],
        summed[0],
        summed[1],
        summed[2],
        summed[3],
        summed[4],
        summed[5],
    )


EVERY = 8
TILE = 256
CUT = 512
ROWS_TILE = 256
ROWS_CUT = 512
VMEM_BYTES = 64000000


def mm(left, right):
    return jnp.dot(left, right, preferred_element_type=jnp.float32)


def mm_nt(left, right):
    return lax.dot_general(left, right, (((1,), (1,)), ((), ())), preferred_element_type=jnp.float32)


def whole():
    return pl.BlockSpec(memory_space=pltpu.VMEM)


def in_place():
    return pl.BlockSpec(memory_space=pl.ANY)


def scalars():
    return pl.BlockSpec(memory_space=pltpu.SMEM)


def params():
    return pltpu.CompilerParams(vmem_limit_bytes=VMEM_BYTES)


def cost(flops, moved):
    return pl.CostEstimate(flops=flops, bytes_accessed=moved, transcendentals=0)


def shape_of(shape, dtype=jnp.bfloat16):
    return jax.ShapeDtypeStruct(shape, dtype)


def swap(values, bits):
    return lax.ppermute(values, "fsdp", [(i, i ^ bits) for i in range(EVERY)])


def tie(*values):
    return lax.optimization_barrier(values)


def gather_first(values):
    return [values, swap(values, 2), swap(values, 4)]


def gather_second(values, side, over):
    half = values.shape[0] // 2
    far = [swap(side[:half], 4), swap(over[half:], 2)]
    return far, swap(values, 1), swap(jnp.concatenate([side, over], axis=0), 1)


def gather_third(first, far, own, pair):
    far = jnp.concatenate(far, axis=0)
    return [*first, far, own, pair, swap(far, 1)]


GATHERED = 7


def blocks_of(refs):
    values, side, over, far, own, pair, last = refs
    rows = values.shape[0]
    return [values, own, side, pair.at[0:rows], over, pair.at[rows : 2 * rows], far, last]


def gather_relative(values):
    first = gather_first(values)
    return gather_third(first, *gather_second(*first))


def add_half(left, right):
    return (left.astype(jnp.float32) + right.astype(jnp.float32)).astype(jnp.bfloat16)


def scatter_second(even, got):
    rows = even.shape[0] // 4
    half = rows // 2
    far = 3 * rows
    return [
        swap(add_half(even[far : far + half], got[far : far + half]), 2),
        swap(add_half(even[far + half :], got[far + half :]), 4),
    ]


def scatter_third(even, got, far_side, far_over):
    rows = even.shape[0] // 4
    half = rows // 2
    f32 = jnp.float32
    side = even[rows : 2 * rows].astype(f32) + got[rows : 2 * rows].astype(f32)
    over = even[2 * rows : 3 * rows].astype(f32) + got[2 * rows : 3 * rows].astype(f32)
    side = jnp.concatenate([side[:half], side[half:] + far_over.astype(f32)], axis=0)
    over = jnp.concatenate([over[:half] + far_side.astype(f32), over[half:]], axis=0)
    return even, got, swap(side.astype(jnp.bfloat16), 2), swap(over.astype(jnp.bfloat16), 4)


def scatter_relative(even, odd):
    got = swap(odd, 1)
    return scatter_third(even, got, *scatter_second(even, got))


def sum_pieces(*pieces):
    return sum([piece.astype(jnp.float32) for piece in pieces[1:]], pieces[0].astype(jnp.float32))


PIECES = 4


def piece_specs(rows, columns, at=0):
    return [pl.BlockSpec((rows, columns), lambda i: (0, at))] * PIECES


def rep_swap(values, bits):
    return lax.ppermute(values, "rep", [(i, i ^ bits) for i in range(4)])


def turn(values, cosine, signed_sine):
    return values * cosine + pltpu.roll(values, HD // 2, 1) * signed_sine


SPOT = 16


def relayout_kernel(wide, source_ref, out_ref):
    for j in range(EVERY):
        out_ref[j, 0] = source_ref[0, :, j * wide : (j + 1) * wide]


def by_columns(values, wide):
    count, rows, width = values.shape
    half = rows // 2
    return pl.pallas_call(
        functools.partial(relayout_kernel, wide),
        grid=(count, 2),
        in_specs=[pl.BlockSpec((1, half, width), lambda i, j: (i, j, 0))],
        out_specs=pl.BlockSpec((EVERY, 1, half, wide), lambda i, j: (0, i, j, 0)),
        out_shape=shape_of((EVERY, count, rows, wide)),
        cost_estimate=cost(1 << 20, 1 << 16),
        name="by_columns",
    )(values)


def project_kernel(
    rows, width, wide,
    me_ref, sets_ref, cos_ref, sin_ref, up_ref, *refs,
):
    f32, bf16 = jnp.float32, jnp.bfloat16
    hidden_hbm, given, w_hbm = blocks_of(refs[:GATHERED]), blocks_of(refs[GATHERED : 2 * GATHERED]), refs[2 * GATHERED]
    refs = refs[2 * GATHERED + 1 :]
    q_ref, k_ref, v_ref, normed_ref, low_ref, mask_ref, col_ref, row_ref, gains_ref, router_ref, *refs = refs
    hidden, extra, weight, down, sems, w_sems = refs
    me, step = me_ref[0], pl.program_id(0)
    thin = 3 * SR
    copies = []
    for j in range(EVERY):
        at = pl.multiple_of((me ^ j) * wide, wide)
        here = slice(j * rows, (j + 1) * rows)
        copies.append(
            [
                pltpu.make_async_copy(hidden_hbm[j], hidden.at[here], sems.at[j, 0]),
                pltpu.make_async_copy(given[j].at[:, 2 * thin :], extra.at[here], sems.at[j, 1]),
                pltpu.make_async_copy(
                    given[j].at[:, 0:thin], down.at[pl.ds(at, rows), :], sems.at[j, 2]
                ),
                pltpu.make_async_copy(
                    given[j].at[:, thin : 2 * thin], down.at[pl.ds(at + rows, rows), :], sems.at[j, 3]
                ),
            ]
        )
    w_copies = [
        pltpu.make_async_copy(
            w_hbm.at[j, i], weight.at[j * wide : (j + 1) * wide, i * wide : (i + 1) * wide], w_sems.at[j, i]
        )
        for i in range(3)
        for j in range(EVERY)
    ]

    @pl.when(step == 0)
    def _():
        for which in (1, 2, 3):
            for group in copies:
                group[which].start()
        for item in w_copies:
            item.start()
        for group in copies:
            group[0].start()
        for group in copies:
            group[1].wait()
        for j in range(EVERY):
            at = pl.multiple_of((me ^ j) * wide, wide)
            for part in range(wide // rows):
                spot = pl.multiple_of(at + part * rows, rows)
                router_ref[pl.ds(spot, rows), :] = extra[j * rows : (j + 1) * rows, part * 128 : (part + 1) * 128]
                for i in range(2):
                    line = extra[j * rows : j * rows + 16, 256:384].astype(f32)
                    gains_ref[i : i + 1, pl.ds(spot, rows)] = line[2 * i + part : 2 * i + part + 1, :]
        for group in copies:
            for which in (2, 3):
                group[which].wait()
        for item in w_copies:
            item.wait()

    for i in range(EVERY // 2):

        @pl.when(step == i)
        def _():
            copies[2 * i][0].wait()
            copies[2 * i + 1][0].wait()

    at = pl.ds(pl.multiple_of(step * TILE, TILE), TILE)
    seg = jnp.broadcast_to(extra[at, 0:1].astype(f32), (TILE, 128))
    col_ref[...] = seg
    row_ref[...] = seg.T[0:8, :]
    chosen = jnp.zeros_like(seg)
    for i in range(SETS):
        chosen = jnp.where(seg == float(i), sets_ref[0, i].astype(f32), chosen)
    lane_set = (lax.broadcasted_iota(jnp.int32, (TILE, SR), 1) // R).astype(f32)
    mask = (chosen == lane_set).astype(f32)
    mask_ref[...] = mask
    values = hidden[at, :].astype(f32)
    scale = lax.rsqrt(jnp.mean(values * values, axis=1, keepdims=True) + EPSILON)
    normed = (values * scale * gains_ref[0:1, :]).astype(bf16)
    normed_ref[...] = normed
    wide_all = mm(normed, weight[...])
    low = (mm(normed, down[...]) * jnp.concatenate([mask] * 3, axis=1)).astype(bf16)
    low_ref[...] = low
    cosine, sine = cos_ref[...], sin_ref[...]
    for i, ref in enumerate((q_ref, k_ref, v_ref)):
        proj = wide_all[:, i * wide : (i + 1) * wide] + mm_nt(low[:, i * SR : (i + 1) * SR], up_ref[i])
        for h in range(wide // HD):
            part = proj[:, h * HD : (h + 1) * HD]
            ref[:, h * HD : (h + 1) * HD] = (turn(part, cosine, sine) if i < 2 else part).astype(bf16)


def by_tile(rows, columns):
    return pl.BlockSpec((rows, columns), lambda i: (i, 0))


def project(me, sets, cosine, sine, up, hidden_given, given, w_got):
    rows, width = hidden_given[0].shape
    wide = width // EVERY
    tokens = rows * EVERY
    f32 = jnp.float32
    return pl.pallas_call(
        functools.partial(project_kernel, rows, width, wide),
        grid=(tokens // TILE,),
        in_specs=[scalars(), scalars(), by_tile(TILE, 128), by_tile(TILE, 128), whole()] + [in_place()] * (2 * GATHERED + 1),
        out_specs=[by_tile(TILE, wide)] * 3
        + [by_tile(TILE, width), by_tile(TILE, 3 * SR), by_tile(TILE, SR), by_tile(TILE, 128)]
        + [
            pl.BlockSpec((8, TILE), lambda i: (0, i)),
            pl.BlockSpec((8, width), lambda i: (0, 0)),
            pl.BlockSpec((width, 128), lambda i: (0, 0)),
        ],
        out_shape=[shape_of((tokens, wide))] * 3
        + [shape_of((tokens, width)), shape_of((tokens, 3 * SR)), shape_of((tokens, SR), f32)]
        + [shape_of((tokens, 128), f32), shape_of((8, tokens), f32), shape_of((8, width), f32), shape_of((width, 128))],
        scratch_shapes=[
            pltpu.VMEM((tokens, width), jnp.bfloat16),
            pltpu.VMEM((tokens, 384), jnp.bfloat16),
            pltpu.VMEM((width, 3 * wide), jnp.bfloat16),
            pltpu.VMEM((width, 3 * SR), jnp.bfloat16),
            pltpu.SemaphoreType.DMA((EVERY, 4)),
            pltpu.SemaphoreType.DMA((EVERY, 3)),
        ],
        compiler_params=params(),
        cost_estimate=cost(1 << 20, 1 << 16),
        name="project",
    )(me, sets, cosine, sine, up, *hidden_given, *given, w_got)


def attend_kernel(rows, me_ref, q_ref, k_ref, v_ref, col_ref, row_ref, att_ref, lse_ref, send_ref):
    f32, bf16 = jnp.float32, jnp.bfloat16
    scale = HD ** (-0.5)
    seg_row = row_ref[0:1, :]
    for h in range(q_ref.shape[1] // HD):
        lanes = slice(h * HD, (h + 1) * HD)
        for c in range(q_ref.shape[0] // TILE):
            at = slice(c * TILE, (c + 1) * TILE)
            scores = mm_nt(q_ref[at, lanes], k_ref[:, lanes]) * scale
            scores = jnp.where(col_ref[at, 0:1] == seg_row, scores, MASKED)
            top = jnp.max(scores, axis=1, keepdims=True)
            weights = jnp.exp(scores - top)
            total = jnp.sum(weights, axis=1, keepdims=True)
            att = mm(weights.astype(bf16), v_ref[:, lanes]) / total
            att_ref[at, lanes] = att
            log_sum = jnp.broadcast_to(top + jnp.log(total), (TILE, HD))
            lse_ref[h : h + 1, at] = log_sum.T[0:1, :]
            for part in range(TILE // rows):
                j = c * (TILE // rows) + part
                send_ref[me_ref[0] ^ j, :, lanes] = att[part * rows : (part + 1) * rows].astype(bf16)


def attend(rows, me, queries, keys, values, seg_col, seg_row):
    tokens, wide = queries.shape
    return pl.pallas_call(
        functools.partial(attend_kernel, rows),
        in_specs=[scalars()] + [whole()] * 5,
        out_specs=[whole()] * 3,
        out_shape=[
            shape_of((tokens, wide), jnp.float32),
            shape_of((8, tokens), jnp.float32),
            shape_of((EVERY, rows, wide)),
        ],
        compiler_params=params(),
        cost_estimate=cost(1 << 20, 1 << 16),
        name="attend",
    )(me, queries, keys, values, seg_col, seg_row)


def output_copies(me, wide, given, weight, down, up, sems):
    width = weight.shape[1]
    copies = []
    for j in range(EVERY):
        at = pl.multiple_of((me ^ j) * wide, wide)
        here = slice(j * wide, (j + 1) * wide)
        copies.append(
            [
                pltpu.make_async_copy(given[j].at[:, width : width + SR], down.at[here, :], sems.at[j, 0]),
                pltpu.make_async_copy(given[j].at[:, width + SR :], up.at[pl.ds(at, wide), :], sems.at[j, 1]),
                pltpu.make_async_copy(given[j].at[:, 0:width], weight.at[here, :], sems.at[j, 2]),
            ]
        )
    return copies


def output_scratch(width):
    return [
        pltpu.VMEM((width, width), jnp.bfloat16),
        pltpu.VMEM((width, SR), jnp.bfloat16),
        pltpu.VMEM((width, SR), jnp.bfloat16),
        pltpu.SemaphoreType.DMA((EVERY, 3)),
    ]


def mix_kernel(
    wide,
    me_ref, hidden_ref, gains_ref, mask_ref, router_ref, named_ref, att_ref, *refs,
):
    f32, bf16 = jnp.float32, jnp.bfloat16
    given = blocks_of(refs[:GATHERED])
    resid_ref, normed_ref, low_ref, gates_ref, weight, down, up, sems = refs[GATHERED:]
    me = me_ref[0]
    width = hidden_ref.shape[1]
    copies = output_copies(me, wide, given, weight, down, up, sems)
    for part in range(3):
        for group in copies:
            group[part].start()
    for part in range(2):
        for group in copies:
            group[part].wait()
    blocks = [att_ref[me ^ j] for j in range(EVERY)]
    low = (mm(jnp.concatenate(blocks, axis=1), down[...]) * mask_ref[...]).astype(bf16)
    low_ref[...] = low
    total = mm_nt(low, up[...])
    for j in range(EVERY):
        copies[j][2].wait()
        total = total + mm(blocks[j], weight[j * wide : (j + 1) * wide, :])
    resid = hidden_ref[...].astype(f32) + total
    resid_ref[...] = resid
    scale = lax.rsqrt(jnp.mean(resid * resid, axis=1, keepdims=True) + EPSILON)
    normed = (resid * scale * gains_ref[1:2, :]).astype(bf16)
    normed_ref[:, 0:width] = normed
    logits = jnp.where(named_ref[...] > 0.5, mm(normed, router_ref[...]), MASKED)
    share = jnp.exp(logits - jnp.max(logits, axis=1, keepdims=True)) * named_ref[...]
    gates = share / jnp.sum(share, axis=1, keepdims=True)
    gates_ref[...] = gates
    high = gates.astype(bf16).astype(f32)
    normed_ref[:, width : width + 128] = (high + pltpu.roll(gates - high, 64, 1)).astype(bf16)


def mix(me, hidden, gains, mask, router, named, att_got, given):
    rows, width = hidden.shape
    wide = width // EVERY
    f32 = jnp.float32
    return pl.pallas_call(
        functools.partial(mix_kernel, wide),
        grid=(1,),
        in_specs=[scalars(), whole(), whole(), pl.BlockSpec((rows, SR), lambda i: (0, 0))]
        + [whole()] * 3
        + [in_place()] * GATHERED,
        out_specs=[whole()] * 4,
        out_shape=[shape_of((rows, width), f32), shape_of((rows, width + 128)), shape_of((rows, SR)),
                   shape_of((rows, 128), f32)],
        scratch_shapes=output_scratch(width),
        compiler_params=params(),
        cost_estimate=cost(1 << 20, 1 << 16),
        name="mix",
    )(me, hidden, gains, mask, router, named, att_got, *given)


def expert_kernel(k, first, width, hidden, blocks, where_ref, mask_ref, pick_ref, *refs):
    f32, bf16 = jnp.float32, jnp.bfloat16
    rows_hbm, cot_hbm = blocks_of(refs[:GATHERED]), blocks_of(refs[GATHERED : 2 * GATHERED])
    refs = refs[2 * GATHERED :]
    if not first:
        prev_out, refs = refs[:2], refs[2:]
    (
        w_gate_hbm, w_up_hbm, w_down_hbm, a_in_hbm, b_in_hbm, a_down_hbm, b_down_hbm,
        out_even, out_odd, d_all_ref, extra_ref, *refs,
    ) = refs
    *grad_refs, rows_s, cot_s, w_in, w_down, silu_s, slope_s, g_a_in, g_b_down, g_b_in, g_a_down, packed, sems, block_sems = refs
    out_refs = (out_even, out_odd)
    step = pl.program_id(0)
    part = TILE // 2
    low_at, thin_at = 2 * hidden, width
    chunks = hidden // CUT
    early, late, given = [], [], []

    def copy(source, target, group):
        group.append(pltpu.make_async_copy(source, target, sems.at[len(early) + len(late)]))

    copy(a_in_hbm.at[k, 0], w_in.at[0:width, low_at : low_at + SR], early)
    copy(a_in_hbm.at[k, 1], w_in.at[0:width, low_at + SR : low_at + 2 * SR], early)
    copy(b_in_hbm.at[k, 0], w_in.at[width : width + SR, 0:hidden], early)
    copy(b_in_hbm.at[k, 1], w_in.at[width : width + SR, hidden:low_at], early)
    for j in range(chunks):
        at = slice(j * CUT, (j + 1) * CUT)
        copy(w_gate_hbm.at[k, :, at], w_in.at[0:width, at], early)
        copy(w_up_hbm.at[k, :, at], w_in.at[0:width, hidden + j * CUT : hidden + (j + 1) * CUT], early)
    copy(a_down_hbm.at[k], w_down.at[0:hidden, thin_at : thin_at + SR], late)
    copy(b_down_hbm.at[k], w_down.at[hidden : hidden + SR, 0:width], late)
    copy(w_down_hbm.at[k], w_down.at[0:hidden, 0:width], late)
    for j in range(blocks):
        at = slice(j * part, (j + 1) * part)
        given.append(pltpu.make_async_copy(rows_hbm[j], rows_s.at[at, :], block_sems.at[j, 0]))
        given.append(pltpu.make_async_copy(cot_hbm[j], cot_s.at[at, :], block_sems.at[j, 1]))

    def wait_for(group, then=(), when=0):
        @pl.when(step == when)
        def _():
            for item in group:
                item.wait()
            for item in then:
                item.start()

    @pl.when(step == 0)
    def _():
        for item in given[0:4] + early[:6]:
            item.start()
        g_a_in[...] = jnp.zeros_like(g_a_in)
        g_b_down[...] = jnp.zeros_like(g_b_down)
        g_b_in[...] = jnp.zeros_like(g_b_in)
        g_a_down[...] = jnp.zeros_like(g_a_down)

    for i in range(1, blocks // 2):
        wait_for(given[4 * i : 4 * i + 4], when=i)
    wait_for([given[0], given[2]] + early[:2], early[6:])
    at_rows = pl.ds(pl.multiple_of(step * TILE, TILE), TILE)
    mask = mask_ref[...]
    mask_two = jnp.concatenate([mask, mask], axis=1)
    rows = rows_s[at_rows, 0:width]
    gate = jnp.sum(rows_s[at_rows, width:].astype(f32) * pick_ref[0:1, :], axis=1, keepdims=True)
    low_in = (mm(rows, w_in[0:width, low_at:]) * mask_two).astype(bf16)
    rows_gate = jnp.concatenate([rows, low_in[:, :SR]], axis=1)
    rows_up = jnp.concatenate([rows, low_in[:, SR:]], axis=1)
    wait_for(early[2:4])
    act_parts = []
    for j in range(chunks):
        wait_for(early[4 + 2 * j : 6 + 2 * j], late if j == 0 else given[4:] if j == 1 else ())
        at = slice(j * CUT, (j + 1) * CUT)
        gate_h = mm(rows_gate, w_in[:, at])
        up_h = mm(rows_up, w_in[:, hidden + j * CUT : hidden + (j + 1) * CUT])
        share = 1.0 / (1.0 + jnp.exp(-gate_h))
        silu = gate_h * share
        silu_s[:, at] = silu
        slope_s[:, at] = up_h * (share * (1.0 + gate_h * (1.0 - share)))
        act_parts.append((silu * up_h).astype(bf16))
    act = jnp.concatenate(act_parts, axis=1)
    wait_for([given[1], given[3]] + late)

    low_down = (mm(act, w_down[0:hidden, thin_at:]) * mask).astype(bf16)
    act_low = jnp.concatenate([act, low_down], axis=1)
    d_gate = jnp.zeros((TILE, 1), f32)
    d_out_parts = []
    for j in range(width // CUT):
        at = slice(j * CUT, (j + 1) * CUT)
        out = mm(act_low, w_down[:, at]).astype(bf16).astype(f32)
        cot = cot_s[at_rows, at].astype(f32)
        d_out_parts.append((gate * cot).astype(bf16))
        weighted = gate * out
        for i in range(2):
            value = weighted[i * part : (i + 1) * part]
            if not first:
                value = value + prev_out[i][:, at].astype(f32)
            out_refs[i][:, at] = value.astype(bf16)
        d_gate = d_gate + jnp.sum(cot * out, axis=1, keepdims=True)
    high = d_gate.astype(bf16).astype(f32)
    extra_ref[...] = high * pick_ref[1:2, :] + (d_gate - high) * pick_ref[2:3, :]

    mask_half = mask.astype(bf16)
    d_out = jnp.concatenate(d_out_parts, axis=1)
    d_low_down = mm_nt(d_out, w_down[hidden:, 0:width]).astype(bf16) * mask_half
    d_out_low = jnp.concatenate([d_out, d_low_down], axis=1)
    d_gate_parts, d_up_parts = [], []
    for j in range(chunks):
        at = slice(j * CUT, (j + 1) * CUT)
        d_act = mm_nt(d_out_low, w_down[at, :])
        d_gate_parts.append((d_act * slope_s[:, at]).astype(bf16))
        d_up_parts.append((d_act * silu_s[:, at]).astype(bf16))
    d_gate_h = jnp.concatenate(d_gate_parts, axis=1)
    d_up_h = jnp.concatenate(d_up_parts, axis=1)
    d_low_gate = mm_nt(d_gate_h, w_in[width:, 0:hidden]).astype(bf16) * mask_half
    d_low_up = mm_nt(d_up_h, w_in[width:, hidden:low_at]).astype(bf16) * mask_half
    d_low_in = jnp.concatenate([d_low_gate, d_low_up], axis=1)
    d_all_ref[:, 0:hidden] = d_gate_h
    d_all_ref[:, hidden:low_at] = d_up_h
    d_all_ref[:, low_at:] = d_low_in
    d_low_in_t, low_down_t, low_in_t, d_low_down_t = d_low_in.T, low_down.T, low_in.T, d_low_down.T
    for j in range(width // CUT):
        at = slice(j * CUT, (j + 1) * CUT)
        g_a_in[:, at] += mm(d_low_in_t, rows[:, at])
        g_b_down[:, at] += mm(low_down_t, d_out[:, at])
    for j in range(chunks):
        at = slice(j * CUT, (j + 1) * CUT)
        g_b_in[0, :, at] += mm(low_in_t[:SR], d_gate_h[:, at])
        g_b_in[1, :, at] += mm(low_in_t[SR:], d_up_h[:, at])
        g_a_down[:, at] += mm(d_low_down_t, act[:, at])

    @pl.when(step == pl.num_programs(0) - 1)
    def _():
        packed[0 : 2 * SR, :] = g_a_in[...].astype(bf16)
        packed[2 * SR : 3 * SR, :] = g_b_down[...].astype(bf16)
        packed[3 * SR : 4 * SR, 0:hidden] = g_b_in[0].astype(bf16)
        packed[3 * SR : 4 * SR, hidden:] = g_b_in[1].astype(bf16)
        packed[4 * SR :, 0:hidden] = g_a_down[: SR // 2].astype(bf16)
        packed[4 * SR :, hidden:] = g_a_down[SR // 2 :].astype(bf16)
        size = packed.shape[0] // 4
        for spot, b in enumerate((0, 2, 1, 3)):
            quarter = packed[pl.ds(pl.multiple_of((where_ref[0] ^ b) * size, 16), size), :]
            per = 4 // len(grad_refs)
            grad_refs[spot // per][(spot % per) * size : (spot % per + 1) * size, :] = quarter


def expert_pass(k, where, rows, cot, mask, picks, prev, weights):
    f32, bf16 = jnp.float32, jnp.bfloat16
    blocks = EVERY
    part, width = cot[0].shape
    hidden = weights[0].shape[2]
    tokens = blocks * part
    shares = 2 if prev is None else 4
    grad_shape = ((4 * SR + SR // 2) // shares, width)
    in_specs = [scalars(), by_tile(TILE, SR), pl.BlockSpec((8, 128), lambda i: (0, 0))] + [in_place()] * (2 * GATHERED)
    operands = [where, mask, picks, *rows, *cot]
    if prev is not None:
        in_specs += [by_tile(part, width)] * 2
        operands += list(prev)
    in_specs += [in_place()] * 7
    flops = 2 * tokens * (4 * width * hidden + 7 * SR * (width + hidden))
    return pl.pallas_call(
        functools.partial(expert_kernel, k, prev is None, width, hidden, blocks),
        grid=(tokens // TILE,),
        in_specs=in_specs,
        out_specs=[by_tile(part, width)] * 2
        + [by_tile(TILE, 2 * hidden + 2 * SR), by_tile(TILE, 128)]
        + [pl.BlockSpec(grad_shape, lambda i: (0, 0))] * shares,
        out_shape=[shape_of((tokens // 2, width))] * 2
        + [shape_of((tokens, 2 * hidden + 2 * SR)), shape_of((tokens, 128), f32)]
        + [shape_of(grad_shape)] * shares,
        scratch_shapes=[
            pltpu.VMEM((tokens, width + 128), bf16),
            pltpu.VMEM((tokens, width), bf16),
            pltpu.VMEM((width + SR, 2 * hidden + 2 * SR), bf16),
            pltpu.VMEM((hidden + SR, width + SR), bf16),
            pltpu.VMEM((TILE, hidden), f32),
            pltpu.VMEM((TILE, hidden), f32),
            pltpu.VMEM((2 * SR, width), f32),
            pltpu.VMEM((SR, width), f32),
            pltpu.VMEM((2, SR, hidden), f32),
            pltpu.VMEM((SR, hidden), f32),
            pltpu.VMEM((4 * SR + SR // 2, width), bf16),
            pltpu.SemaphoreType.DMA((7 + 2 * (hidden // CUT),)),
            pltpu.SemaphoreType.DMA((blocks, 2)),
        ],
        compiler_params=params(),
        cost_estimate=cost(flops, 40 << 20),
        name="expert",
    )(*operands, *weights)


def rows_kernel(part, width, hidden, local, *refs):
    bf16 = jnp.bfloat16
    d_all, extra, (w_gate_hbm, w_up_hbm, a_in_hbm) = refs[:local], refs[local : 2 * local], refs[2 * local : 2 * local + 3]
    even_ref, odd_ref, weight, sems = refs[2 * local + 3 :]
    step = pl.program_id(0)
    span = 2 * hidden + 2 * SR
    chunks = width // ROWS_CUT
    copies = []
    for j in range(chunks):
        at = slice(j * ROWS_CUT, (j + 1) * ROWS_CUT)
        group = []
        for k in range(local):
            base = k * span
            targets = [
                (w_gate_hbm.at[k, at], base, hidden),
                (w_up_hbm.at[k, at], base + hidden, hidden),
                (a_in_hbm.at[k, 0, at], base + 2 * hidden, SR),
                (a_in_hbm.at[k, 1, at], base + 2 * hidden + SR, SR),
            ]
            for i, (source, start, size) in enumerate(targets):
                group.append(
                    pltpu.make_async_copy(source, weight.at[at, start : start + size], sems.at[j, 4 * k + i])
                )
        copies.append(group)

    @pl.when(step == 0)
    def _():
        for group in copies:
            for item in group:
                item.start()

    both = jnp.concatenate([ref[...] for ref in d_all], axis=1)
    for j in range(chunks):

        @pl.when(step == 0)
        def _():
            for item in copies[j]:
                item.wait()

        at = slice(j * ROWS_CUT, (j + 1) * ROWS_CUT)
        value = mm_nt(both, weight[at, :]).astype(bf16)
        for b in range(ROWS_TILE // part):
            (even_ref, odd_ref)[b % 2][b // 2 * part : (b // 2 + 1) * part, at] = value[b * part : (b + 1) * part]
    total = sum([ref[...] for ref in extra[1:]], extra[0][...]).astype(bf16)
    for b in range(ROWS_TILE // part):
        (even_ref, odd_ref)[b % 2][b // 2 * part : (b // 2 + 1) * part, width:] = total[b * part : (b + 1) * part]


def rows_pass(part, d_all, extra, w_gate, w_up, a_in):
    local, width, hidden = w_gate.shape
    tokens, span = d_all[0].shape
    return pl.pallas_call(
        functools.partial(rows_kernel, part, width, hidden, local),
        grid=(tokens // ROWS_TILE,),
        in_specs=[by_tile(ROWS_TILE, span)] * local + [by_tile(ROWS_TILE, 128)] * local + [in_place()] * 3,
        out_specs=[by_tile(ROWS_TILE // 2, width + 128)] * 2,
        out_shape=[shape_of((tokens // 2, width + 128))] * 2,
        scratch_shapes=[
            pltpu.VMEM((width, local * span), jnp.bfloat16),
            pltpu.SemaphoreType.DMA((width // ROWS_CUT, 4 * local)),
        ],
        compiler_params=params(),
        cost_estimate=cost(2 * tokens * width * span * local, 40 << 20),
        name="rows",
    )(*d_all, *extra, w_gate, w_up, a_in)


def norm_grad(values, gain_row, upstream_grad):
    scale = lax.rsqrt(jnp.mean(values * values, axis=1, keepdims=True) + EPSILON)
    inner = gain_row * upstream_grad
    mean = jnp.mean(values * inner, axis=1, keepdims=True)
    return scale * inner - values * (scale * scale * scale * mean)


def unmix_kernel(
    wide,
    me_ref, resid_ref, cot_ref, gains_ref, mask_ref, router_ref, gates_ref, low_ref, att_ref, *refs,
):
    f32, bf16 = jnp.float32, jnp.bfloat16
    pieces, given, refs = refs[:PIECES], blocks_of(refs[PIECES : PIECES + GATHERED]), refs[PIECES + GATHERED :]
    resid_grad_ref, grad_ref, send_ref, weight, down, up, up_grad, sems = refs
    me = me_ref[0]
    width = resid_ref.shape[1]
    copies = output_copies(me, wide, given, weight, down, up, sems)
    for which in (1, 0, 2):
        for group in copies:
            group[which].start()
    resid = resid_ref[...]
    total = sum_pieces(*[ref[...] for ref in pieces])
    extra = total[:, width:]
    gates = gates_ref[...]
    d_gates = extra + pltpu.roll(extra, 64, 1)
    d_chosen = gates * (d_gates - jnp.sum(gates * d_gates, axis=1, keepdims=True))
    d_normed = total[:, :width] + mm_nt(d_chosen.astype(bf16), router_ref[...])
    d_resid = cot_ref[...].astype(f32) + norm_grad(resid, gains_ref[1:2, :], d_normed)
    resid_grad_ref[...] = d_resid
    branch = d_resid.astype(bf16)
    for group in copies:
        group[1].wait()
    d_low = (mm(branch, up[...]).astype(bf16).astype(f32) * mask_ref[...]).astype(bf16)
    low_t, d_low_t = low_ref[...].T, d_low.T
    up_grad[...] = mm(low_t, branch).astype(bf16)
    for group in copies:
        group[0].wait()
    for j in range(EVERY):
        here = slice(j * wide, (j + 1) * wide)
        copies[j][2].wait()
        send_ref[me ^ j] = (mm_nt(branch, weight[here, :]) + mm_nt(d_low, down[here, :])).astype(bf16)
        at = pl.multiple_of((me ^ j) * wide, wide)
        grad_ref[me ^ j, 0:SR, :] = mm(d_low_t, att_ref[me ^ j]).astype(bf16)
        grad_ref[me ^ j, SR:, :] = up_grad[:, pl.ds(at, wide)]


def unmix(me, resid, cot, gains, mask, router, gates, low, att_got, pieces, given):
    rows, width = resid.shape
    wide = width // EVERY
    return pl.pallas_call(
        functools.partial(unmix_kernel, wide),
        grid=(1,),
        in_specs=[scalars()]
        + [whole()] * 3
        + [pl.BlockSpec((rows, SR), lambda i: (0, 0))]
        + [whole()] * 4
        + piece_specs(rows, width + 128)
        + [in_place()] * GATHERED,
        out_specs=[whole()] * 3,
        out_shape=[
            shape_of((rows, width), jnp.float32),
            shape_of((EVERY, 2 * SR, wide)),
            shape_of((EVERY, rows, wide)),
        ],
        scratch_shapes=output_scratch(width)[:3]
        + [pltpu.VMEM((SR, width), jnp.bfloat16)]
        + output_scratch(width)[3:],
        compiler_params=params(),
        cost_estimate=cost(1 << 20, 1 << 16),
        name="unmix",
    )(me, resid, cot, gains, mask, router, gates, low, att_got, *pieces, *given)


def attend_back_kernel(
    rows, wide,
    me_ref, q_ref, k_ref, v_ref, att_ref, lse_ref, col_ref, row_ref, cos_ref, sin_ref, low_ref, mask_ref, up_ref,
    got_ref, normed_hbm, d_proj_ref, d_low_ref, down_grad_ref, up_grad_ref, d_att, normed, sems,
):
    f32, bf16 = jnp.float32, jnp.bfloat16
    tokens = q_ref.shape[0]
    scale = HD ** (-0.5)
    me = me_ref[0]
    bring = pltpu.make_async_copy(normed_hbm, normed, sems.at[0])
    bring.start()
    for j in range(EVERY):
        d_att[j * rows : (j + 1) * rows, :] = got_ref[me ^ j]
    seg_row = row_ref[0:1, :]
    for h in range(wide // HD):
        lanes = slice(h * HD, (h + 1) * HD)
        delta = jnp.sum(d_att[:, lanes].astype(f32) * att_ref[:, lanes], axis=1, keepdims=True)
        delta = jnp.broadcast_to(delta, (tokens, HD)).T[0:1, :]
        log_sum = lse_ref[h : h + 1, :]
        d_query = jnp.zeros((tokens, HD), f32)
        for c in range(tokens // TILE):
            at = slice(c * TILE, (c + 1) * TILE)
            scores = mm_nt(k_ref[at, lanes], q_ref[:, lanes]) * scale - log_sum
            probs = jnp.exp(jnp.where(col_ref[at, 0:1] == seg_row, scores, MASKED))
            d_probs = mm_nt(v_ref[at, lanes], d_att[:, lanes])
            d_scores = (probs * (d_probs - delta)).astype(bf16)
            d_value = mm(probs.astype(bf16), d_att[:, lanes])
            d_key = mm(d_scores, q_ref[:, lanes])
            d_query = d_query + mm(d_scores.T, k_ref[at, lanes])
            d_proj_ref[at, wide + h * HD : wide + (h + 1) * HD] = turn(
                d_key * scale, cos_ref[at, :], -sin_ref[at, :]
            ).astype(bf16)
            d_proj_ref[at, 2 * wide + h * HD : 2 * wide + (h + 1) * HD] = d_value.astype(bf16)
        d_proj_ref[:, lanes] = turn(d_query * scale, cos_ref[...], -sin_ref[...]).astype(bf16)
    for i in range(3):
        part = d_proj_ref[:, i * wide : (i + 1) * wide]
        d_low = (mm(part, up_ref[i]).astype(bf16).astype(f32) * mask_ref[...]).astype(bf16)
        d_low_ref[:, i * SR : (i + 1) * SR] = d_low
        up_grad_ref[i * SR : (i + 1) * SR, :] = mm(low_ref[:, i * SR : (i + 1) * SR].T, part).astype(bf16)
    d_low_t = d_low_ref[...].T
    bring.wait()
    for j in range(EVERY):
        down_grad_ref[j] = mm(d_low_t, normed[:, j * wide : (j + 1) * wide]).astype(bf16)


def attend_back(rows, me, q, k, v, att, lse, seg_col, seg_row, cosine, sine, low, mask, up, got, normed):
    tokens, wide = q.shape
    width = wide * EVERY
    return pl.pallas_call(
        functools.partial(attend_back_kernel, rows, wide),
        in_specs=[scalars()] + [whole()] * 13 + [in_place()],
        out_specs=[whole()] * 4,
        out_shape=[
            shape_of((tokens, 3 * wide)),
            shape_of((tokens, 3 * SR)),
            shape_of((EVERY, 3 * SR, wide)),
            shape_of((3 * SR, wide)),
        ],
        scratch_shapes=[
            pltpu.VMEM((tokens, wide), jnp.bfloat16),
            pltpu.VMEM((tokens, width), jnp.bfloat16),
            pltpu.SemaphoreType.DMA((1,)),
        ],
        compiler_params=params(),
        cost_estimate=cost(1 << 20, 1 << 16),
        name="attend_back",
    )(me, q, k, v, att, lse, seg_col, seg_row, cosine, sine, low, mask, up, got, normed)


def unproject_kernel(rows, width, wide, me_ref, proj_ref, low_ref, *refs):
    bf16 = jnp.bfloat16
    given, w_hbm = blocks_of(refs[:GATHERED]), refs[GATHERED]
    even_ref, odd_ref, weight, sems, w_sems = refs[GATHERED + 1 :]
    me, thin = me_ref[0], 3 * SR

    @pl.when(pl.program_id(0) == 0)
    def _():
        copies = []
        for j in range(EVERY):
            at = pl.multiple_of((me ^ j) * wide, wide)
            for i in range(3):
                copies.append(
                    pltpu.make_async_copy(
                        w_hbm.at[j, i],
                        weight.at[j * wide : (j + 1) * wide, i * wide : (i + 1) * wide],
                        w_sems.at[j, i],
                    )
                )
            for part in range(2):
                start = part * thin
                copies.append(
                    pltpu.make_async_copy(
                        given[j].at[:, start : start + thin],
                        weight.at[pl.ds(at + part * rows, rows), 3 * wide : 3 * wide + thin],
                        sems.at[j, part],
                    )
                )
        for item in copies:
            item.start()
        for item in copies:
            item.wait()

    both = jnp.concatenate([proj_ref[...], low_ref[...]], axis=1)
    for j in range(width // CUT):
        lanes = slice(j * CUT, (j + 1) * CUT)
        value = mm_nt(both, weight[lanes, :]).astype(bf16)
        even_ref[:, lanes] = value[:rows]
        odd_ref[:, lanes] = value[rows:]


def unproject(rows, me, d_proj, d_low, given, w_got):
    tokens = d_proj.shape[0]
    wide = d_proj.shape[1] // 3
    width = wide * EVERY
    return pl.pallas_call(
        functools.partial(unproject_kernel, rows, width, wide),
        grid=(tokens // TILE,),
        in_specs=[scalars(), by_tile(TILE, 3 * wide), by_tile(TILE, 3 * SR)] + [in_place()] * (GATHERED + 1),
        out_specs=[by_tile(rows, width)] * 2,
        out_shape=[shape_of((tokens // 2, width))] * 2,
        scratch_shapes=[
            pltpu.VMEM((width, 3 * wide + 3 * SR), jnp.bfloat16),
            pltpu.SemaphoreType.DMA((EVERY, 2)),
            pltpu.SemaphoreType.DMA((EVERY, 3)),
        ],
        compiler_params=params(),
        cost_estimate=cost(1 << 20, 1 << 16),
        name="unproject",
    )(me, d_proj, d_low, *given, w_got)


def finish_kernel(hidden_ref, gains_ref, resid_grad_ref, *refs):
    pieces, out_ref = refs[:PIECES], refs[PIECES]
    d_normed = sum_pieces(*[ref[...] for ref in pieces])
    back = norm_grad(hidden_ref[...].astype(jnp.float32), gains_ref[0:1, :], d_normed)
    out_ref[...] = (resid_grad_ref[...] + back).astype(jnp.bfloat16)


def finish(hidden, gains, resid_grad, pieces):
    rows, width = hidden.shape
    return pl.pallas_call(
        finish_kernel,
        grid=(1,),
        in_specs=[whole()] * 3 + piece_specs(rows, width),
        out_specs=whole(),
        out_shape=shape_of((rows, width)),
        compiler_params=params(),
        cost_estimate=cost(1 << 20, 1 << 16),
        name="finish",
    )(hidden, gains, resid_grad, *pieces)


def layer_kernel(resid_ref, *refs):
    pieces, out_ref = refs[:PIECES], refs[PIECES]
    out_ref[...] = (resid_ref[...] + sum_pieces(*[ref[...] for ref in pieces])).astype(jnp.bfloat16)


def layer(resid, pieces):
    rows, width = resid.shape
    return pl.pallas_call(
        layer_kernel,
        grid=(1,),
        in_specs=[whole()] + piece_specs(rows, width),
        out_specs=whole(),
        out_shape=shape_of((rows, width)),
        compiler_params=params(),
        cost_estimate=cost(1 << 20, 1 << 16),
        name="layer",
    )(resid, *pieces)


UNPACK_STEPS = 4


def unpack_kernel(hidden, where_ref, *refs):
    f32 = jnp.float32
    parts, refs = refs[:8], refs[-5:]
    a_in_ref, b_in_ref, a_down_ref, b_down_ref, packed = refs
    size = packed.shape[0] // 4
    step = pl.program_id(0)
    wide, thin = packed.shape[1] // UNPACK_STEPS, hidden // UNPACK_STEPS

    @pl.when(step == 0)
    def _():
        for b in range(4):
            for i in range(2):
                spot = pl.multiple_of((where_ref[0] ^ b) * size + i * (size // 2), 8)
                packed[pl.ds(spot, size // 2), :] = parts[2 * b + i][...].astype(f32)

    at = pl.ds(pl.multiple_of(step * wide, 128), wide)
    halves = [pl.ds(pl.multiple_of(i * hidden + step * thin, 128), thin) for i in range(2)]
    for i in range(2):
        a_in_ref[0, i] = packed[i * SR : (i + 1) * SR, at].T
        b_in_ref[0, i] = packed[3 * SR : 4 * SR, halves[i]]
        a_down_ref[0, :, i * (SR // 2) : (i + 1) * (SR // 2)] = packed[4 * SR :, halves[i]].T
    b_down_ref[0] = packed[2 * SR : 3 * SR, at]


def unpack(k, where, quarters, hidden, experts, before):
    quarters = [part for quarter in quarters for part in quarter]
    width = quarters[0].shape[1]
    f32 = jnp.float32
    first = before is None
    shapes = [(experts, 2, width, SR), (experts, 2, SR, hidden), (experts, hidden, SR), (experts, SR, width)]
    given = [] if first else list(before)
    wide, thin = width // UNPACK_STEPS, hidden // UNPACK_STEPS
    return pl.pallas_call(
        functools.partial(unpack_kernel, hidden),
        grid=(UNPACK_STEPS,),
        in_specs=[scalars()] + [whole()] * 8 + [in_place()] * len(given),
        out_specs=[
            pl.BlockSpec((1, 2, wide, SR), lambda i: (k, 0, i, 0)),
            pl.BlockSpec((1, 2, SR, thin), lambda i: (k, 0, 0, i)),
            pl.BlockSpec((1, thin, SR), lambda i: (k, i, 0)),
            pl.BlockSpec((1, SR, wide), lambda i: (k, 0, i)),
        ],
        out_shape=[shape_of(shape, f32) for shape in shapes],
        input_output_aliases={} if first else {9 + i: i for i in range(4)},
        scratch_shapes=[pltpu.VMEM((4 * SR + SR // 2, width), f32)],
        compiler_params=params(),
        cost_estimate=cost(1 << 20, 1 << 16),
        name="unpack",
    )(where, *quarters, *given)


def thin_kernel(late_left, late_right, early_left, early_right, a_ref, b_ref):
    f32 = jnp.float32
    late = late_left[...].astype(f32) + late_right[...].astype(f32)
    early = early_left[...].astype(f32) + early_right[...].astype(f32)
    for i in range(4):
        at = (2 + i) * SR if i < 3 else 0
        a_ref[i] = late[at : at + SR, :].T
        b_ref[i] = (early[i * SR : (i + 1) * SR, :] if i < 3 else late[SR : 2 * SR, :]).T


def thin_grads(late, early):
    wide = late[0].shape[1]
    return pl.pallas_call(
        thin_kernel,
        in_specs=[whole()] * 4,
        out_specs=[whole()] * 2,
        out_shape=[shape_of((4, wide, SR), jnp.float32)] * 2,
        compiler_params=params(),
        cost_estimate=cost(1 << 20, 1 << 16),
        name="thin_grads",
    )(*late, *early)


def split_layer(
    hidden_in,
    segments,
    routes,
    doc_sets,
    cotangent,
    w_qkv,
    w_out,
    gain_attn,
    gain_moe,
    router,
    w_gate,
    w_up,
    w_down,
    a_attn,
    b_attn,
    exp_a_in,
    exp_b_in,
    exp_a_down,
    exp_b_down,
):
    bf16, f32 = jnp.bfloat16, jnp.float32
    index = lax.axis_index("fsdp")
    me = index.astype(jnp.int32).reshape(1)
    where = lax.axis_index("rep").astype(jnp.int32).reshape(1)
    hidden, upstream = hidden_in[0], cotangent[0]
    rows, width = hidden.shape
    wide = width // EVERY
    local, _, inner = w_gate.shape
    experts_all = local * EVERY

    order = index ^ jnp.arange(EVERY)
    positions = (order[:, None] * rows + jnp.arange(rows)[None, :]).reshape(-1)
    cosine, sine = rope_tables(positions, HD)
    cosine, sine = jnp.concatenate([cosine, cosine], axis=1), jnp.concatenate([-sine, sine], axis=1)
    lanes = jnp.arange(128)
    named = jnp.any(routes[0][:, :, None] + SPOT == lanes[None, None, :], axis=1).astype(f32)
    out_own = jnp.concatenate([w_out, a_attn[3], b_attn[3]], axis=1)

    def picks(k):
        high = (lanes == SPOT + 2 * index + k).astype(f32)
        low = (lanes == SPOT + 2 * index + k + 64).astype(f32)
        return jnp.stack([high + low, high, low] + [jnp.zeros_like(high)] * 5)

    hidden_first = gather_first(hidden)
    narrow = jnp.concatenate([a_attn[0], a_attn[1], a_attn[2]], axis=1)
    at_spot = ((0, 0), (SPOT, 128 - SPOT - experts_all))
    meta = jnp.pad(router[:rows], at_spot) + jnp.pad(segments[0].astype(bf16)[:, None], ((0, 0), (0, 127)))
    lines = jnp.concatenate([gain_attn.reshape(2, 128), gain_moe.reshape(2, 128)], axis=0)
    lines = jnp.pad(lines, ((0, rows - 4), (0, 0)))
    given = jnp.concatenate([narrow[:rows], narrow[rows:], meta, jnp.pad(router[rows:], at_spot), lines], axis=1)
    given_first = gather_first(given)
    w_got = lax.all_to_all(by_columns(w_qkv, wide), "fsdp", split_axis=0, concat_axis=0, tiled=True)
    hidden_first, cosine, sine, out_own, named, pick_rows = tie(
        hidden_first, cosine, sine, out_own, named, [picks(0), picks(1)]
    )
    hidden_given = gather_third(hidden_first, *gather_second(*hidden_first))
    given = gather_third(given_first, *gather_second(*given_first))

    hidden_given, given, w_got, out_own = tie(hidden_given, given, w_got, out_own)
    out_first = gather_first(out_own)
    queries, keys, values, normed_one, low_qkv, mask, seg_col, seg_row, gains, router_all = project(
        me, doc_sets, cosine, sine, b_attn, hidden_given, given, w_got
    )
    att, lse, att_send = attend(rows, me, queries, keys, values, seg_col, seg_row)
    att_send, out_first = tie(att_send, out_first)
    att_got = lax.all_to_all(att_send, "fsdp", split_axis=0, concat_axis=0, tiled=True)
    far, *others = gather_second(*out_first)
    cot_first = gather_first(tie(upstream, att_send)[0])
    far, others, att_got, cot_first = tie(far, others, att_got, cot_first)
    out_given = gather_third(out_first, far, *others)
    cot_second = gather_second(*cot_first)
    resid_one, normed_own, low_out, gates_own = mix(
        me, hidden, gains, mask, router_all, named, att_got, out_given
    )
    normed_own, cot_second = tie(normed_own, cot_second)
    normed_given = gather_relative(normed_own)
    cot_given = gather_third(cot_first, *cot_second)

    weights = (w_gate, w_up, w_down, exp_a_in, exp_b_in, exp_a_down, exp_b_down)
    *state, d_all_a, extra_a, kept_a, sent_a = expert_pass(
        0, where, normed_given, cot_given, mask, pick_rows[0], None, weights
    )
    def in_two(values):
        return [values[: values.shape[0] // 2], values[values.shape[0] // 2 :]]

    def later(values, anchor):
        return tie(values, anchor)[0]

    def in_two(values):
        return [values[: values.shape[0] // 2], values[values.shape[0] // 2 :]]

    sent_a = rep_swap(sent_a, 1)
    *state, d_all_b, extra_b, kept_0, kept_1, sent_0, sent_1 = expert_pass(
        1, where, normed_given, cot_given, mask, pick_rows[1], state, weights
    )
    kept_b, sent_b = [kept_0, kept_1], [sent_0, sent_1]
    d_all_b, kept_b, sent_b, sent_a, state = tie(d_all_b, kept_b, sent_b, sent_a, state)
    out_even, out_odd = state
    half_a = add_half(kept_a, sent_a)
    size = half_a.shape[0] // 2
    sent_b[0] = rep_swap(sent_b[0], 1)
    other_a = rep_swap(half_a[size:], 2)
    out_got = swap(out_odd, 1)
    row_even, row_odd = rows_pass(rows, [d_all_a, d_all_b], [extra_a, extra_b], w_gate, w_up, exp_a_in)
    row_odd, other_a, sent_b[0], out_got = tie(row_odd, other_a, sent_b[0], out_got)
    got = swap(row_odd, 1)
    sent_b[1] = rep_swap(later(sent_b[1], row_odd), 1)
    total_a = in_two(add_half(half_a[:size], other_a))
    d_far = scatter_second(row_even, got)
    d_far, sent_b[1] = tie(d_far, sent_b[1])
    pieces = scatter_third(row_even, got, *d_far)
    two_a = [rep_swap(later(total_a[0], d_far), 2)]
    pieces, two_a[0] = tie(pieces, two_a[0])
    early_a = later(total_a, pieces)
    two_a.append(rep_swap(early_a[1], 2))
    one_a = [None, rep_swap(early_a[1], 1)]
    d_resid, thin_send, d_att_send = unmix(
        me, resid_one, upstream, gains, mask, router_all, gates_own, low_out, att_got, pieces, out_given
    )
    d_att_send, two_a[1], one_a[1] = tie(d_att_send, two_a[1], one_a[1])
    d_att_got = lax.all_to_all(d_att_send, "fsdp", split_axis=0, concat_axis=0, tiled=True)
    mine_b = add_half(kept_b[0], sent_b[0])
    half_b = later(in_two(add_half(kept_b[1], sent_b[1])), d_att_send)
    one_a[0] = rep_swap(later(total_a[0], d_att_send), 1)
    other_b = [rep_swap(half_b[0], 2)]
    out_far = scatter_second(*later((out_even, out_got), d_att_send))
    d_att_got, other_b[0], one_a[0], out_far = tie(d_att_got, other_b[0], one_a[0], out_far)
    total_b = [add_half(mine_b[: size // 2], other_b[0])]
    other_b.append(rep_swap(later(half_b[1], d_att_got), 2))
    three_a = [rep_swap(later(two_a[0], d_att_got), 1)]

    def exchange(values):
        return lax.all_to_all(values, "fsdp", split_axis=0, concat_axis=0, tiled=True)

    out_grads = exchange(later(thin_send, d_att_got))
    d_proj, d_low, down_send, up_grads = attend_back(
        rows, me, queries, keys, values, att, lse, seg_col, seg_row, cosine, sine, low_qkv, mask, b_attn,
        d_att_got, normed_one,
    )
    d_proj, down_send, other_b[1], three_a[0], out_grads = tie(d_proj, down_send, other_b[1], three_a[0], out_grads)
    down_grads = exchange(down_send)
    two_b = [rep_swap(later(total_b[0], d_proj), 2)]
    three_a.append(rep_swap(later(two_a[1], d_proj), 1))
    even, odd = unproject(rows, me, d_proj, d_low, given, w_got)
    odd, down_grads, two_b[0], three_a[1] = tie(odd, down_grads, two_b[0], three_a[1])
    got = swap(odd, 1)
    thin = [jnp.sum(part.astype(f32), axis=0).astype(bf16) for part in (out_grads, down_grads)]
    thin = jnp.concatenate(thin, axis=0)
    thin_near = rep_swap(thin, 1)
    total_b.append(later(add_half(mine_b[size // 2 :], other_b[1]), odd))
    two_b.append(rep_swap(total_b[1], 2))
    up_near = rep_swap(later(up_grads, odd), 1)
    d_far = scatter_second(even, got)
    d_far, thin_near, two_b[1], up_near = tie(d_far, thin_near, two_b[1], up_near)
    pieces = scatter_third(even, got, *d_far)
    thin, up_grads = add_half(thin, thin_near), add_half(up_grads, up_near)
    thin_last, up_far = rep_swap(thin, 2), rep_swap(up_grads, 2)
    one_b = [rep_swap(later(total_b[0], d_far), 1)]
    grads = unpack(0, where, later([total_a, one_a, two_a, three_a], d_far), inner, local, None)
    pieces, grads = tie(pieces, grads)
    one_b.append(rep_swap(later(total_b[1], pieces), 1))
    three_b = [rep_swap(part, 1) for part in later(two_b, pieces)]
    grad_in = finish(hidden, gains, d_resid, pieces)
    grad_in, thin_last, up_far, one_b[0] = tie(grad_in, thin_last, up_far, one_b[0])
    grad_a, grad_b = thin_grads([thin, thin_last], [up_grads, up_far])
    out_pieces = scatter_third(*later((out_even, out_got), pieces), *out_far)
    layer_out = layer(resid_one, out_pieces)
    one_b, three_b, layer_out, grad_in, grad_a, grad_b = tie(one_b, three_b, layer_out, grad_in, grad_a, grad_b)
    grads = unpack(1, where, [total_b, one_b, two_b, three_b], inner, local, grads)
    return (layer_out[None], grad_in[None], grad_a, grad_b, *grads)


def solution(mesh):
    shape = dict(mesh.shape)
    shards = split_layer if shape == {"rep": 4, "fsdp": EVERY} else gathered_layer
    return jax.shard_map(
        shards,
        mesh=mesh,
        in_specs=(
            P("rep", "fsdp", None),
            P("rep", "fsdp"),
            P("rep", "fsdp", None),
            P("rep", None),
            P("rep", "fsdp", None),
            P(None, "fsdp", None),
            P("fsdp", None),
            P("fsdp"),
            P("fsdp"),
            P("fsdp", None),
            P("fsdp", None, None),
            P("fsdp", None, None),
            P("fsdp", None, None),
            P(None, "fsdp", None),
            P(None, "fsdp", None),
            P("fsdp", None, None, None),
            P("fsdp", None, None, None),
            P("fsdp", None, None),
            P("fsdp", None, None),
        ),
        out_specs=(
            P("rep", "fsdp", None),
            P("rep", "fsdp", None),
            P(None, "fsdp", None),
            P(None, "fsdp", None),
            P("fsdp", None, None, None),
            P("fsdp", None, None, None),
            P("fsdp", None, None),
            P("fsdp", None, None),
        ),
        check_vma=False,
    )
```

```python
import functools
import math

import jax
import jax.numpy as jnp
from jax import lax
from jax.experimental import pallas as pl
from jax.experimental.pallas import tpu as pltpu
from jax.sharding import PartitionSpec as P

HD = 128
TOP = 8
R = 16
SETS = 8
SR = 128


EPSILON = 1e-05
MASKED = -1e30


def rms_scale(values):
    return values * lax.rsqrt(jnp.mean(values * values, axis=-1, keepdims=True) + EPSILON)


def norm_back(values, gain_row, upstream_grad):
    result, pull_back = jax.vjp(lambda inner_rows: rms_scale(inner_rows) * gain_row, values)
    return pull_back(upstream_grad)[0]


def rope_tables(positions, head_size):
    half_size = head_size // 2
    inv_freq = jnp.exp(
        jnp.arange(half_size, dtype=jnp.float32) * (-2.0 * math.log(10000.0) / head_size)
    )
    angles = positions.astype(jnp.float32)[:, None] * inv_freq[None, :]
    return (jnp.cos(angles), jnp.sin(angles))


def rotate(values, cosine, sine_table):
    half_size = values.shape[-1] // 2
    front_half = values[..., :half_size]
    back_half = values[..., half_size:]
    cos_rows = cosine[:, None, :]
    sin_rows = sine_table[:, None, :]
    return jnp.concatenate(
        [
            front_half * cos_rows - back_half * sin_rows,
            back_half * cos_rows + front_half * sin_rows,
        ],
        axis=-1,
    )


def gathered_layer(
    hidden_in,
    segments,
    routes,
    doc_sets,
    cotangent,
    w_qkv,
    w_out,
    gain_attn,
    gain_moe,
    router,
    w_gate,
    w_up,
    w_down,
    a_attn,
    b_attn,
    exp_a_in,
    exp_b_in,
    exp_a_down,
    exp_b_down,
):
    shard_count = lax.axis_size("fsdp")
    shard_index = lax.axis_index("fsdp")
    tok_rows = hidden_in.shape[1]
    model_width = hidden_in.shape[2]
    head_count = model_width // HD
    local_experts = w_gate.shape[0]
    experts_all = local_experts * shard_count
    capacity = max(2, 3 * tok_rows * TOP // (2 * experts_all))
    score_scale = HD ** (-0.5)
    (
        attention_weight_full,
        output_weight_full,
        adapter_down_weight,
        adapter_up_weight,
        first_norm_gain_full,
        second_norm_gain_full,
        router_weight_full,
    ) = (
        lax.all_gather(w_qkv, "fsdp", axis=1, tiled=True),
        lax.all_gather(w_out, "fsdp", axis=0, tiled=True),
        lax.all_gather(a_attn, "fsdp", axis=1, tiled=True),
        lax.all_gather(b_attn, "fsdp", axis=1, tiled=True),
        lax.all_gather(gain_attn, "fsdp", axis=0, tiled=True),
        lax.all_gather(gain_moe, "fsdp", axis=0, tiled=True),
        lax.all_gather(router, "fsdp", axis=0, tiled=True),
    )
    gain_one = first_norm_gain_full.astype(jnp.float32)
    gain_two = second_norm_gain_full.astype(jnp.float32)
    seg_local = segments[0]
    set_token = jnp.sum(
        jnp.where(seg_local[:, None] == jnp.arange(SETS)[None, :], doc_sets[0][None, :], 0), axis=1
    )
    document_set_mask = (set_token[:, None] == (jnp.arange(SR) // R)[None, :]).astype(jnp.float32)
    mask_half = document_set_mask.astype(jnp.bfloat16)
    hidden_f = hidden_in[0].astype(jnp.float32)
    first_normed_rows = (rms_scale(hidden_f) * gain_one).astype(jnp.bfloat16)
    attention_rank_branch = (
        jnp.einsum(
            "xj,zje->zxe",
            first_normed_rows,
            adapter_down_weight[:3],
            preferred_element_type=jnp.float32,
        )
        * document_set_mask[None]
    ).astype(jnp.bfloat16)
    projected = jnp.einsum(
        "td,pde->pte", first_normed_rows, attention_weight_full, preferred_element_type=jnp.float32
    ) + jnp.einsum(
        "nzv,nwv->nzw",
        attention_rank_branch,
        adapter_up_weight[:3],
        preferred_element_type=jnp.float32,
    )
    positions = shard_index * tok_rows + jnp.arange(tok_rows)
    cosine, sine_table = rope_tables(positions, HD)
    queries = rotate(projected[0].reshape(tok_rows, head_count, HD), cosine, sine_table).astype(
        jnp.bfloat16
    )
    keys_own = (
        rotate(projected[1].reshape(tok_rows, head_count, HD), cosine, sine_table)
        .astype(jnp.bfloat16)
        .reshape(tok_rows, model_width)
    )
    values_own = projected[2].astype(jnp.bfloat16)
    seg_own = seg_local.astype(jnp.bfloat16)
    run_max = jnp.full((head_count, tok_rows), MASKED, jnp.float32)
    key_piece = lax.all_gather(keys_own, "fsdp", axis=0, tiled=True)
    value_piece = lax.all_gather(values_own, "fsdp", axis=0, tiled=True)
    seg_piece = lax.all_gather(seg_own, "fsdp", axis=0, tiled=True)
    piece_rows = key_piece.shape[0]
    scores = (
        jnp.einsum(
            "qhd,khd->hqk",
            queries,
            key_piece.reshape(piece_rows, head_count, HD),
            preferred_element_type=jnp.float32,
        )
        * score_scale
    )
    same_doc = seg_local[:, None] == seg_piece.astype(jnp.int32)[None, :]
    scores = jnp.where(same_doc[None], scores, MASKED)
    new_max = jnp.maximum(run_max, jnp.max(scores, axis=2))
    exp_scores = jnp.exp(scores - new_max[:, :, None])
    new_sum = jnp.sum(exp_scores, axis=2)
    new_acc = jnp.einsum(
        "hqk,khd->qhd",
        exp_scores.astype(jnp.bfloat16),
        value_piece.reshape(piece_rows, head_count, HD),
        preferred_element_type=jnp.float32,
    )
    folded = (new_max, new_sum, new_acc)
    run_max, run_sum, run_acc = folded
    log_sum = run_max + jnp.log(run_sum)
    attended = run_acc / jnp.transpose(run_sum)[:, :, None]
    attention_rounded_rows = attended.reshape(tok_rows, model_width).astype(jnp.bfloat16)
    output_rank_branch = (
        jnp.dot(attention_rounded_rows, adapter_down_weight[3], preferred_element_type=jnp.float32)
        * document_set_mask
    ).astype(jnp.bfloat16)
    resid_one = hidden_f + (
        jnp.dot(attention_rounded_rows, output_weight_full, preferred_element_type=jnp.float32)
        + jnp.einsum(
            "nd,gd->ng",
            output_rank_branch,
            adapter_up_weight[3],
            preferred_element_type=jnp.float32,
        )
    )
    normed_two = (rms_scale(resid_one) * gain_two).astype(jnp.bfloat16)
    logits = jnp.dot(normed_two, router_weight_full, preferred_element_type=jnp.float32)
    my_routes = routes[0]
    gate_weights = jax.nn.softmax(jnp.take_along_axis(logits, my_routes, axis=1), axis=-1)
    flat_routes = my_routes.reshape(-1)
    one_hot = (flat_routes[:, None] == jnp.arange(experts_all)[None, :]).astype(jnp.int32)
    slot_index = jnp.sum((jnp.cumsum(one_hot, axis=0) - 1) * one_hot, axis=1)
    token_index = jnp.arange(tok_rows * TOP) // TOP
    send_rows = (
        jnp.zeros((experts_all, capacity, model_width), jnp.bfloat16)
        .at[flat_routes, slot_index]
        .set(normed_two[token_index])
    )
    send_sets = (
        jnp.zeros((experts_all, capacity), jnp.bfloat16)
        .at[flat_routes, slot_index]
        .set(set_token[token_index].astype(jnp.bfloat16))
    )
    rows_got = lax.all_to_all(
        send_rows.reshape(shard_count, local_experts, capacity, model_width),
        "fsdp",
        split_axis=0,
        concat_axis=0,
        tiled=True,
    )
    sets_got = lax.all_to_all(
        send_sets.reshape(shard_count, local_experts, capacity),
        "fsdp",
        split_axis=0,
        concat_axis=0,
        tiled=True,
    )
    slot_mask = (sets_got.astype(jnp.int32)[..., None] == jnp.arange(SR) // R).astype(jnp.float32)
    low_in = (
        jnp.einsum("necd,eids->necis", rows_got, exp_a_in, preferred_element_type=jnp.float32)
        * slot_mask[:, :, :, None, :]
    ).astype(jnp.bfloat16)
    gate_h = jnp.einsum(
        "necd,edf->necf", rows_got, w_gate, preferred_element_type=jnp.float32
    ) + jnp.einsum(
        "necs,esf->necf", low_in[:, :, :, 0], exp_b_in[:, 0], preferred_element_type=jnp.float32
    )
    up_h = jnp.einsum(
        "necd,edf->necf", rows_got, w_up, preferred_element_type=jnp.float32
    ) + jnp.einsum(
        "necs,esf->necf", low_in[:, :, :, 1], exp_b_in[:, 1], preferred_element_type=jnp.float32
    )
    activation = (jax.nn.silu(gate_h) * up_h).astype(jnp.bfloat16)
    low_down = (
        jnp.einsum("necf,efs->necs", activation, exp_a_down, preferred_element_type=jnp.float32)
        * slot_mask
    ).astype(jnp.bfloat16)
    expert_out = (
        jnp.einsum("necf,efd->necd", activation, w_down, preferred_element_type=jnp.float32)
        + jnp.einsum("necs,esd->necd", low_down, exp_b_down, preferred_element_type=jnp.float32)
    ).astype(jnp.bfloat16)
    expert_out, rows_got, slot_mask, low_in, gate_h, up_h, activation, low_down = (
        expert_out,
        rows_got,
        slot_mask,
        low_in,
        gate_h,
        up_h,
        activation,
        low_down,
    )
    returned = lax.all_to_all(expert_out, "fsdp", split_axis=0, concat_axis=0, tiled=True)
    route_out = (
        returned.reshape(experts_all, capacity, model_width)[flat_routes, slot_index]
        .reshape(tok_rows, TOP, model_width)
        .astype(jnp.float32)
    )
    layer_value = resid_one + jnp.sum(gate_weights[:, :, None] * route_out, axis=1)
    (
        attention_weight_full,
        output_weight_full,
        adapter_down_weight,
        adapter_up_weight,
        first_norm_gain_full,
        second_norm_gain_full,
        router_weight_full,
    ) = (
        lax.all_gather(w_qkv, "fsdp", axis=1, tiled=True),
        lax.all_gather(w_out, "fsdp", axis=0, tiled=True),
        lax.all_gather(a_attn, "fsdp", axis=1, tiled=True),
        lax.all_gather(b_attn, "fsdp", axis=1, tiled=True),
        lax.all_gather(gain_attn, "fsdp", axis=0, tiled=True),
        lax.all_gather(gain_moe, "fsdp", axis=0, tiled=True),
        lax.all_gather(router, "fsdp", axis=0, tiled=True),
    )
    gain_one = first_norm_gain_full.astype(jnp.float32)
    gain_two = second_norm_gain_full.astype(jnp.float32)
    upstream = cotangent[0].astype(jnp.float32)
    d_route = (gate_weights[:, :, None] * upstream[:, None, :]).astype(jnp.bfloat16)
    d_gates = jnp.sum(upstream[:, None, :] * route_out, axis=2)
    d_chosen = gate_weights * (d_gates - jnp.sum(gate_weights * d_gates, axis=1, keepdims=True))
    d_logits = jnp.sum(
        jnp.where(
            my_routes[:, :, None] == jnp.arange(experts_all)[None, None, :],
            d_chosen[:, :, None],
            0.0,
        ),
        axis=1,
    ).astype(jnp.bfloat16)
    send_grads = (
        jnp.zeros((experts_all, capacity, model_width), jnp.bfloat16)
        .at[flat_routes, slot_index]
        .set(d_route.reshape(tok_rows * TOP, model_width))
    )
    grads_got = lax.all_to_all(
        send_grads.reshape(shard_count, local_experts, capacity, model_width),
        "fsdp",
        split_axis=0,
        concat_axis=0,
        tiled=True,
    )
    slot_half = slot_mask.astype(jnp.bfloat16)
    d_low_down = (
        jnp.einsum(
            "necd,esd->necs", grads_got, exp_b_down, preferred_element_type=jnp.float32
        ).astype(jnp.bfloat16)
        * slot_half
    )
    d_activation = jnp.einsum(
        "necd,efd->necf", grads_got, w_down, preferred_element_type=jnp.float32
    ) + jnp.einsum("necs,efs->necf", d_low_down, exp_a_down, preferred_element_type=jnp.float32)
    silu_value, silu_pull = jax.vjp(
        lambda gate_in, up_in: jax.nn.silu(gate_in) * up_in, gate_h, up_h
    )
    d_gate_h, d_up_h = silu_pull(d_activation)
    d_gate_h = d_gate_h.astype(jnp.bfloat16)
    d_up_h = d_up_h.astype(jnp.bfloat16)
    d_both = jnp.stack([d_gate_h, d_up_h], axis=3)
    d_low_in = (
        jnp.einsum(
            "necif,eisf->necis", d_both, exp_b_in, preferred_element_type=jnp.float32
        ).astype(jnp.bfloat16)
        * slot_half[:, :, :, None, :]
    )
    d_rows = (
        jnp.einsum("necf,edf->necd", d_gate_h, w_gate, preferred_element_type=jnp.float32)
        + jnp.einsum("necf,edf->necd", d_up_h, w_up, preferred_element_type=jnp.float32)
        + jnp.einsum("necis,eids->necd", d_low_in, exp_a_in, preferred_element_type=jnp.float32)
    )
    returned_grads = lax.all_to_all(
        d_rows.astype(jnp.bfloat16), "fsdp", split_axis=0, concat_axis=0, tiled=True
    )
    g_exp_b_down = jnp.einsum(
        "necs,necd->esd", low_down, grads_got, preferred_element_type=jnp.float32
    )
    g_exp_a_down = jnp.einsum(
        "necf,necs->efs", activation, d_low_down, preferred_element_type=jnp.float32
    )
    g_exp_b_in = jnp.einsum("necis,necif->eisf", low_in, d_both, preferred_element_type=jnp.float32)
    g_exp_a_in = jnp.einsum(
        "necd,necis->eids", rows_got, d_low_in, preferred_element_type=jnp.float32
    )
    d_normed_two = jnp.sum(
        returned_grads.reshape(experts_all, capacity, model_width)[flat_routes, slot_index]
        .reshape(tok_rows, TOP, model_width)
        .astype(jnp.float32),
        axis=1,
    ) + jnp.einsum("te,de->td", d_logits, router_weight_full, preferred_element_type=jnp.float32)
    d_resid_one = upstream + norm_back(resid_one, gain_two, d_normed_two)
    branch_gradient = d_resid_one.astype(jnp.bfloat16)
    output_adapter_gradient = (
        jnp.dot(branch_gradient, adapter_up_weight[3], preferred_element_type=jnp.float32).astype(
            jnp.bfloat16
        )
        * mask_half
    )
    d_att = (
        jnp.einsum(
            "te,de->td", branch_gradient, output_weight_full, preferred_element_type=jnp.float32
        )
        + jnp.einsum(
            "cr,ar->ca",
            output_adapter_gradient,
            adapter_down_weight[3],
            preferred_element_type=jnp.float32,
        )
    ).astype(jnp.bfloat16)
    output_up_gradient = jnp.einsum(
        "ts,te->es", output_rank_branch, branch_gradient, preferred_element_type=jnp.float32
    )
    output_down_gradient = jnp.einsum(
        "td,ts->ds",
        attention_rounded_rows,
        output_adapter_gradient,
        preferred_element_type=jnp.float32,
    )
    d_att_heads = d_att.reshape(tok_rows, head_count, HD)
    delta_rows = jnp.transpose(jnp.sum(d_att_heads.astype(jnp.float32) * attended, axis=2))
    key_piece = lax.all_gather(keys_own, "fsdp", axis=0, tiled=True)
    value_piece = lax.all_gather(values_own, "fsdp", axis=0, tiled=True)
    seg_piece = lax.all_gather(seg_own, "fsdp", axis=0, tiled=True)
    piece_rows = key_piece.shape[0]
    key_heads = key_piece.reshape(piece_rows, head_count, HD)
    value_heads = value_piece.reshape(piece_rows, head_count, HD)
    scores = (
        jnp.einsum("qhd,khd->hqk", queries, key_heads, preferred_element_type=jnp.float32)
        * score_scale
    )
    same_doc = seg_local[:, None] == seg_piece.astype(jnp.int32)[None, :]
    scores = jnp.where(same_doc[None], scores, MASKED)
    soft_probs = jnp.exp(scores - log_sum[:, :, None])
    d_probs = jnp.einsum(
        "qhd,khd->hqk", d_att_heads, value_heads, preferred_element_type=jnp.float32
    )
    d_scores = (soft_probs * (d_probs - delta_rows[:, :, None])).astype(jnp.bfloat16)
    soft_probs, d_scores = (soft_probs, d_scores)
    d_query_part = jnp.einsum(
        "hqk,khd->qhd", d_scores, key_heads, preferred_element_type=jnp.float32
    )
    d_key_part = jnp.einsum(
        "hqk,qhd->khd", d_scores, queries, preferred_element_type=jnp.float32
    ).reshape(piece_rows, model_width)
    d_value_part = jnp.einsum(
        "hqk,qhd->khd",
        soft_probs.astype(jnp.bfloat16),
        d_att_heads,
        preferred_element_type=jnp.float32,
    ).reshape(piece_rows, model_width)
    back_state = (d_query_part, d_key_part, d_value_part)
    d_query, d_keys_all, d_values_all = back_state
    d_keys_mine, d_values_mine = (
        lax.psum_scatter(
            d_keys_all.astype(jnp.bfloat16), "fsdp", scatter_dimension=0, tiled=True
        ).astype(jnp.float32),
        lax.psum_scatter(
            d_values_all.astype(jnp.bfloat16), "fsdp", scatter_dimension=0, tiled=True
        ).astype(jnp.float32),
    )
    d_query_pre = (
        rotate(d_query * score_scale, cosine, -sine_table)
        .reshape(tok_rows, model_width)
        .astype(jnp.bfloat16)
    )
    d_key_pre = (
        rotate((d_keys_mine * score_scale).reshape(tok_rows, head_count, HD), cosine, -sine_table)
        .reshape(tok_rows, model_width)
        .astype(jnp.bfloat16)
    )
    projected_gradient = jnp.stack([d_query_pre, d_key_pre, d_values_mine.astype(jnp.bfloat16)])
    projection_adapter_gradient = (
        jnp.einsum(
            "jah,jho->jao",
            projected_gradient,
            adapter_up_weight[:3],
            preferred_element_type=jnp.float32,
        ).astype(jnp.bfloat16)
        * mask_half[None]
    )
    d_normed_one = jnp.einsum(
        "pte,pde->td", projected_gradient, attention_weight_full, preferred_element_type=jnp.float32
    ) + jnp.einsum(
        "czn,cvn->zv",
        projection_adapter_gradient,
        adapter_down_weight[:3],
        preferred_element_type=jnp.float32,
    )
    attention_up_gradient = jnp.einsum(
        "pts,pte->pes",
        attention_rank_branch,
        projected_gradient,
        preferred_element_type=jnp.float32,
    )
    attention_down_gradient = jnp.einsum(
        "td,pts->pds",
        first_normed_rows,
        projection_adapter_gradient,
        preferred_element_type=jnp.float32,
    )
    d_hidden = d_resid_one + norm_back(hidden_f, gain_one, d_normed_one)
    adapter_down_gradient = jnp.concatenate(
        [attention_down_gradient, output_down_gradient[None]], axis=0
    )
    adapter_up_gradient = jnp.concatenate([attention_up_gradient, output_up_gradient[None]], axis=0)
    part_down, part_up = (
        lax.psum_scatter(
            adapter_down_gradient.astype(jnp.bfloat16), "fsdp", scatter_dimension=1, tiled=True
        ).astype(jnp.float32),
        lax.psum_scatter(
            adapter_up_gradient.astype(jnp.bfloat16), "fsdp", scatter_dimension=1, tiled=True
        ).astype(jnp.float32),
    )
    summed = (
        lax.psum(part_down.astype(jnp.bfloat16), "rep").astype(jnp.float32),
        lax.psum(part_up.astype(jnp.bfloat16), "rep").astype(jnp.float32),
        lax.psum(g_exp_a_in.astype(jnp.bfloat16), "rep").astype(jnp.float32),
        lax.psum(g_exp_b_in.astype(jnp.bfloat16), "rep").astype(jnp.float32),
        lax.psum(g_exp_a_down.astype(jnp.bfloat16), "rep").astype(jnp.float32),
        lax.psum(g_exp_b_down.astype(jnp.bfloat16), "rep").astype(jnp.float32),
    )
    return (
        layer_value.astype(jnp.bfloat16)[None],
        d_hidden.astype(jnp.bfloat16)[None],
        summed[0],
        summed[1],
        summed[2],
        summed[3],
        summed[4],
        summed[5],
    )


EVERY = 8
TILE = 256
CUT = 512
ROWS_TILE = 256
ROWS_CUT = 512
VMEM_BYTES = 64000000


def mm(left, right):
    return jnp.dot(left, right, preferred_element_type=jnp.float32)


def mm_nt(left, right):
    return lax.dot_general(left, right, (((1,), (1,)), ((), ())), preferred_element_type=jnp.float32)


def whole():
    return pl.BlockSpec(memory_space=pltpu.VMEM)


def in_place():
    return pl.BlockSpec(memory_space=pl.ANY)


def scalars():
    return pl.BlockSpec(memory_space=pltpu.SMEM)


def params():
    return pltpu.CompilerParams(vmem_limit_bytes=VMEM_BYTES)


def cost(flops, moved):
    return pl.CostEstimate(flops=flops, bytes_accessed=moved, transcendentals=0)


def shape_of(shape, dtype=jnp.bfloat16):
    return jax.ShapeDtypeStruct(shape, dtype)


def swap(values, bits):
    return lax.ppermute(values, "fsdp", [(i, i ^ bits) for i in range(EVERY)])


def tie(*values):
    return lax.optimization_barrier(values)


def gather_first(values):
    return [values, swap(values, 2), swap(values, 4)]


def gather_second(values, side, over):
    half = values.shape[0] // 2
    far = [swap(side[:half], 4), swap(over[half:], 2)]
    return far, swap(values, 1), swap(jnp.concatenate([side, over], axis=0), 1)


def gather_third(first, far, own, pair):
    far = jnp.concatenate(far, axis=0)
    return [*first, far, own, pair, swap(far, 1)]


GATHERED = 7


def blocks_of(refs):
    values, side, over, far, own, pair, last = refs
    rows = values.shape[0]
    return [values, own, side, pair.at[0:rows], over, pair.at[rows : 2 * rows], far, last]


def gather_relative(values):
    first = gather_first(values)
    return gather_third(first, *gather_second(*first))


def add_half(left, right):
    return (left.astype(jnp.float32) + right.astype(jnp.float32)).astype(jnp.bfloat16)


def scatter_second(even, got):
    rows = even.shape[0] // 4
    half = rows // 2
    far = 3 * rows
    return [
        swap(add_half(even[far : far + half], got[far : far + half]), 2),
        swap(add_half(even[far + half :], got[far + half :]), 4),
    ]


def scatter_third(even, got, far_side, far_over):
    rows = even.shape[0] // 4
    half = rows // 2
    f32 = jnp.float32
    side = even[rows : 2 * rows].astype(f32) + got[rows : 2 * rows].astype(f32)
    over = even[2 * rows : 3 * rows].astype(f32) + got[2 * rows : 3 * rows].astype(f32)
    side = jnp.concatenate([side[:half], side[half:] + far_over.astype(f32)], axis=0)
    over = jnp.concatenate([over[:half] + far_side.astype(f32), over[half:]], axis=0)
    return even, got, swap(side.astype(jnp.bfloat16), 2), swap(over.astype(jnp.bfloat16), 4)


def scatter_relative(even, odd):
    got = swap(odd, 1)
    return scatter_third(even, got, *scatter_second(even, got))


def sum_pieces(*pieces):
    return sum([piece.astype(jnp.float32) for piece in pieces[1:]], pieces[0].astype(jnp.float32))


PIECES = 4


def piece_specs(rows, columns, at=0):
    return [pl.BlockSpec((rows, columns), lambda i: (0, at))] * PIECES


def rep_swap(values, bits):
    return lax.ppermute(values, "rep", [(i, i ^ bits) for i in range(4)])


def turn(values, cosine, signed_sine):
    return values * cosine + pltpu.roll(values, HD // 2, 1) * signed_sine


SPOT = 16


def relayout_kernel(wide, source_ref, out_ref):
    for j in range(EVERY):
        out_ref[j, 0] = source_ref[0, :, j * wide : (j + 1) * wide]


def by_columns(values, wide):
    count, rows, width = values.shape
    half = rows // 2
    return pl.pallas_call(
        functools.partial(relayout_kernel, wide),
        grid=(count, 2),
        in_specs=[pl.BlockSpec((1, half, width), lambda i, j: (i, j, 0))],
        out_specs=pl.BlockSpec((EVERY, 1, half, wide), lambda i, j: (0, i, j, 0)),
        out_shape=shape_of((EVERY, count, rows, wide)),
        cost_estimate=cost(1 << 20, 1 << 16),
        name="by_columns",
    )(values)


def project_kernel(
    rows, width, wide,
    me_ref, sets_ref, cos_ref, sin_ref, up_ref, *refs,
):
    f32, bf16 = jnp.float32, jnp.bfloat16
    hidden_hbm, given, w_hbm = blocks_of(refs[:GATHERED]), blocks_of(refs[GATHERED : 2 * GATHERED]), refs[2 * GATHERED]
    refs = refs[2 * GATHERED + 1 :]
    q_ref, k_ref, v_ref, normed_ref, low_ref, mask_ref, col_ref, row_ref, gains_ref, router_ref, *refs = refs
    hidden, extra, weight, down, sems, w_sems = refs
    me, step = me_ref[0], pl.program_id(0)
    thin = 3 * SR
    copies = []
    for j in range(EVERY):
        at = pl.multiple_of((me ^ j) * wide, wide)
        here = slice(j * rows, (j + 1) * rows)
        copies.append(
            [
                pltpu.make_async_copy(hidden_hbm[j], hidden.at[here], sems.at[j, 0]),
                pltpu.make_async_copy(given[j].at[:, 2 * thin :], extra.at[here], sems.at[j, 1]),
                pltpu.make_async_copy(
                    given[j].at[:, 0:thin], down.at[pl.ds(at, rows), :], sems.at[j, 2]
                ),
                pltpu.make_async_copy(
                    given[j].at[:, thin : 2 * thin], down.at[pl.ds(at + rows, rows), :], sems.at[j, 3]
                ),
            ]
        )
    w_copies = [
        pltpu.make_async_copy(
            w_hbm.at[j, i], weight.at[j * wide : (j + 1) * wide, i * wide : (i + 1) * wide], w_sems.at[j, i]
        )
        for i in range(3)
        for j in range(EVERY)
    ]

    @pl.when(step == 0)
    def _():
        for which in (1, 2, 3):
            for group in copies:
                group[which].start()
        for item in w_copies:
            item.start()
        for group in copies:
            group[0].start()
        for group in copies:
            group[1].wait()
        for j in range(EVERY):
            at = pl.multiple_of((me ^ j) * wide, wide)
            for part in range(wide // rows):
                spot = pl.multiple_of(at + part * rows, rows)
                router_ref[pl.ds(spot, rows), :] = extra[j * rows : (j + 1) * rows, part * 128 : (part + 1) * 128]
                for i in range(2):
                    line = extra[j * rows : j * rows + 16, 256:384].astype(f32)
                    gains_ref[i : i + 1, pl.ds(spot, rows)] = line[2 * i + part : 2 * i + part + 1, :]
        for group in copies:
            for which in (2, 3):
                group[which].wait()
        for item in w_copies:
            item.wait()

    for i in range(EVERY // 2):

        @pl.when(step == i)
        def _():
            copies[2 * i][0].wait()
            copies[2 * i + 1][0].wait()

    at = pl.ds(pl.multiple_of(step * TILE, TILE), TILE)
    seg = jnp.broadcast_to(extra[at, 0:1].astype(f32), (TILE, 128))
    col_ref[...] = seg
    row_ref[...] = seg.T[0:8, :]
    chosen = jnp.zeros_like(seg)
    for i in range(SETS):
        chosen = jnp.where(seg == float(i), sets_ref[0, i].astype(f32), chosen)
    lane_set = (lax.broadcasted_iota(jnp.int32, (TILE, SR), 1) // R).astype(f32)
    mask = (chosen == lane_set).astype(f32)
    mask_ref[...] = mask
    values = hidden[at, :].astype(f32)
    scale = lax.rsqrt(jnp.mean(values * values, axis=1, keepdims=True) + EPSILON)
    normed = (values * scale * gains_ref[0:1, :]).astype(bf16)
    normed_ref[...] = normed
    wide_all = mm(normed, weight[...])
    low = (mm(normed, down[...]) * jnp.concatenate([mask] * 3, axis=1)).astype(bf16)
    low_ref[...] = low
    cosine, sine = cos_ref[...], sin_ref[...]
    for i, ref in enumerate((q_ref, k_ref, v_ref)):
        proj = wide_all[:, i * wide : (i + 1) * wide] + mm_nt(low[:, i * SR : (i + 1) * SR], up_ref[i])
        for h in range(wide // HD):
            part = proj[:, h * HD : (h + 1) * HD]
            ref[:, h * HD : (h + 1) * HD] = (turn(part, cosine, sine) if i < 2 else part).astype(bf16)


def by_tile(rows, columns):
    return pl.BlockSpec((rows, columns), lambda i: (i, 0))


def project(me, sets, cosine, sine, up, hidden_given, given, w_got):
    rows, width = hidden_given[0].shape
    wide = width // EVERY
    tokens = rows * EVERY
    f32 = jnp.float32
    return pl.pallas_call(
        functools.partial(project_kernel, rows, width, wide),
        grid=(tokens // TILE,),
        in_specs=[scalars(), scalars(), by_tile(TILE, 128), by_tile(TILE, 128), whole()] + [in_place()] * (2 * GATHERED + 1),
        out_specs=[by_tile(TILE, wide)] * 3
        + [by_tile(TILE, width), by_tile(TILE, 3 * SR), by_tile(TILE, SR), by_tile(TILE, 128)]
        + [
            pl.BlockSpec((8, TILE), lambda i: (0, i)),
            pl.BlockSpec((8, width), lambda i: (0, 0)),
            pl.BlockSpec((width, 128), lambda i: (0, 0)),
        ],
        out_shape=[shape_of((tokens, wide))] * 3
        + [shape_of((tokens, width)), shape_of((tokens, 3 * SR)), shape_of((tokens, SR), f32)]
        + [shape_of((tokens, 128), f32), shape_of((8, tokens), f32), shape_of((8, width), f32), shape_of((width, 128))],
        scratch_shapes=[
            pltpu.VMEM((tokens, width), jnp.bfloat16),
            pltpu.VMEM((tokens, 384), jnp.bfloat16),
            pltpu.VMEM((width, 3 * wide), jnp.bfloat16),
            pltpu.VMEM((width, 3 * SR), jnp.bfloat16),
            pltpu.SemaphoreType.DMA((EVERY, 4)),
            pltpu.SemaphoreType.DMA((EVERY, 3)),
        ],
        compiler_params=params(),
        cost_estimate=cost(1 << 20, 1 << 16),
        name="project",
    )(me, sets, cosine, sine, up, *hidden_given, *given, w_got)


def attend_kernel(rows, me_ref, q_ref, k_ref, v_ref, col_ref, row_ref, att_ref, lse_ref, send_ref):
    f32, bf16 = jnp.float32, jnp.bfloat16
    scale = HD ** (-0.5)
    seg_row = row_ref[0:1, :]
    for h in range(q_ref.shape[1] // HD):
        lanes = slice(h * HD, (h + 1) * HD)
        for c in range(q_ref.shape[0] // TILE):
            at = slice(c * TILE, (c + 1) * TILE)
            scores = mm_nt(q_ref[at, lanes], k_ref[:, lanes]) * scale
            scores = jnp.where(col_ref[at, 0:1] == seg_row, scores, MASKED)
            top = jnp.max(scores, axis=1, keepdims=True)
            weights = jnp.exp(scores - top)
            total = jnp.sum(weights, axis=1, keepdims=True)
            att = mm(weights.astype(bf16), v_ref[:, lanes]) / total
            att_ref[at, lanes] = att
            log_sum = jnp.broadcast_to(top + jnp.log(total), (TILE, HD))
            lse_ref[h : h + 1, at] = log_sum.T[0:1, :]
            for part in range(TILE // rows):
                j = c * (TILE // rows) + part
                send_ref[me_ref[0] ^ j, :, lanes] = att[part * rows : (part + 1) * rows].astype(bf16)


def attend(rows, me, queries, keys, values, seg_col, seg_row):
    tokens, wide = queries.shape
    return pl.pallas_call(
        functools.partial(attend_kernel, rows),
        in_specs=[scalars()] + [whole()] * 5,
        out_specs=[whole()] * 3,
        out_shape=[
            shape_of((tokens, wide), jnp.float32),
            shape_of((8, tokens), jnp.float32),
            shape_of((EVERY, rows, wide)),
        ],
        compiler_params=params(),
        cost_estimate=cost(1 << 20, 1 << 16),
        name="attend",
    )(me, queries, keys, values, seg_col, seg_row)


def output_copies(me, wide, given, weight, down, up, sems):
    width = weight.shape[1]
    copies = []
    for j in range(EVERY):
        at = pl.multiple_of((me ^ j) * wide, wide)
        here = slice(j * wide, (j + 1) * wide)
        copies.append(
            [
                pltpu.make_async_copy(given[j].at[:, width : width + SR], down.at[here, :], sems.at[j, 0]),
                pltpu.make_async_copy(given[j].at[:, width + SR :], up.at[pl.ds(at, wide), :], sems.at[j, 1]),
                pltpu.make_async_copy(given[j].at[:, 0:width], weight.at[here, :], sems.at[j, 2]),
            ]
        )
    return copies


def output_scratch(width):
    return [
        pltpu.VMEM((width, width), jnp.bfloat16),
        pltpu.VMEM((width, SR), jnp.bfloat16),
        pltpu.VMEM((width, SR), jnp.bfloat16),
        pltpu.SemaphoreType.DMA((EVERY, 3)),
    ]


def mix_kernel(
    wide,
    me_ref, hidden_ref, gains_ref, mask_ref, router_ref, named_ref, att_ref, *refs,
):
    f32, bf16 = jnp.float32, jnp.bfloat16
    given = blocks_of(refs[:GATHERED])
    resid_ref, normed_ref, low_ref, gates_ref, weight, down, up, sems = refs[GATHERED:]
    me = me_ref[0]
    width = hidden_ref.shape[1]
    copies = output_copies(me, wide, given, weight, down, up, sems)
    for part in range(3):
        for group in copies:
            group[part].start()
    for part in range(2):
        for group in copies:
            group[part].wait()
    blocks = [att_ref[me ^ j] for j in range(EVERY)]
    low = (mm(jnp.concatenate(blocks, axis=1), down[...]) * mask_ref[...]).astype(bf16)
    low_ref[...] = low
    total = mm_nt(low, up[...])
    for j in range(EVERY):
        copies[j][2].wait()
        total = total + mm(blocks[j], weight[j * wide : (j + 1) * wide, :])
    resid = hidden_ref[...].astype(f32) + total
    resid_ref[...] = resid
    scale = lax.rsqrt(jnp.mean(resid * resid, axis=1, keepdims=True) + EPSILON)
    normed = (resid * scale * gains_ref[1:2, :]).astype(bf16)
    normed_ref[:, 0:width] = normed
    logits = jnp.where(named_ref[...] > 0.5, mm(normed, router_ref[...]), MASKED)
    share = jnp.exp(logits - jnp.max(logits, axis=1, keepdims=True)) * named_ref[...]
    gates = share / jnp.sum(share, axis=1, keepdims=True)
    gates_ref[...] = gates
    high = gates.astype(bf16).astype(f32)
    normed_ref[:, width : width + 128] = (high + pltpu.roll(gates - high, 64, 1)).astype(bf16)


def mix(me, hidden, gains, mask, router, named, att_got, given):
    rows, width = hidden.shape
    wide = width // EVERY
    f32 = jnp.float32
    return pl.pallas_call(
        functools.partial(mix_kernel, wide),
        grid=(1,),
        in_specs=[scalars(), whole(), whole(), pl.BlockSpec((rows, SR), lambda i: (0, 0))]
        + [whole()] * 3
        + [in_place()] * GATHERED,
        out_specs=[whole()] * 4,
        out_shape=[shape_of((rows, width), f32), shape_of((rows, width + 128)), shape_of((rows, SR)),
                   shape_of((rows, 128), f32)],
        scratch_shapes=output_scratch(width),
        compiler_params=params(),
        cost_estimate=cost(1 << 20, 1 << 16),
        name="mix",
    )(me, hidden, gains, mask, router, named, att_got, *given)


def expert_kernel(k, first, width, hidden, blocks, where_ref, mask_ref, pick_ref, *refs):
    f32, bf16 = jnp.float32, jnp.bfloat16
    rows_hbm, cot_hbm = blocks_of(refs[:GATHERED]), blocks_of(refs[GATHERED : 2 * GATHERED])
    refs = refs[2 * GATHERED :]
    if not first:
        prev_out, refs = refs[:2], refs[2:]
    (
        w_gate_hbm, w_up_hbm, w_down_hbm, a_in_hbm, b_in_hbm, a_down_hbm, b_down_hbm,
        out_even, out_odd, d_all_ref, extra_ref, *refs,
    ) = refs
    *grad_refs, rows_s, cot_s, w_in, w_down, silu_s, slope_s, g_a_in, g_b_down, g_b_in, g_a_down, packed, sems, block_sems = refs
    out_refs = (out_even, out_odd)
    step = pl.program_id(0)
    part = TILE // 2
    low_at, thin_at = 2 * hidden, width
    chunks = hidden // CUT
    early, late, given = [], [], []

    def copy(source, target, group):
        group.append(pltpu.make_async_copy(source, target, sems.at[len(early) + len(late)]))

    copy(a_in_hbm.at[k, 0], w_in.at[0:width, low_at : low_at + SR], early)
    copy(a_in_hbm.at[k, 1], w_in.at[0:width, low_at + SR : low_at + 2 * SR], early)
    copy(b_in_hbm.at[k, 0], w_in.at[width : width + SR, 0:hidden], early)
    copy(b_in_hbm.at[k, 1], w_in.at[width : width + SR, hidden:low_at], early)
    for j in range(chunks):
        at = slice(j * CUT, (j + 1) * CUT)
        copy(w_gate_hbm.at[k, :, at], w_in.at[0:width, at], early)
        copy(w_up_hbm.at[k, :, at], w_in.at[0:width, hidden + j * CUT : hidden + (j + 1) * CUT], early)
    copy(a_down_hbm.at[k], w_down.at[0:hidden, thin_at : thin_at + SR], late)
    copy(b_down_hbm.at[k], w_down.at[hidden : hidden + SR, 0:width], late)
    copy(w_down_hbm.at[k], w_down.at[0:hidden, 0:width], late)
    for j in range(blocks):
        at = slice(j * part, (j + 1) * part)
        given.append(pltpu.make_async_copy(rows_hbm[j], rows_s.at[at, :], block_sems.at[j, 0]))
        given.append(pltpu.make_async_copy(cot_hbm[j], cot_s.at[at, :], block_sems.at[j, 1]))

    def wait_for(group, then=(), when=0):
        @pl.when(step == when)
        def _():
            for item in group:
                item.wait()
            for item in then:
                item.start()

    @pl.when(step == 0)
    def _():
        for item in given[0:4] + early[:6]:
            item.start()
        g_a_in[...] = jnp.zeros_like(g_a_in)
        g_b_down[...] = jnp.zeros_like(g_b_down)
        g_b_in[...] = jnp.zeros_like(g_b_in)
        g_a_down[...] = jnp.zeros_like(g_a_down)

    for i in range(1, blocks // 2):
        wait_for(given[4 * i : 4 * i + 4], when=i)
    wait_for([given[0], given[2]] + early[:2], early[6:])
    at_rows = pl.ds(pl.multiple_of(step * TILE, TILE), TILE)
    mask = mask_ref[...]
    mask_two = jnp.concatenate([mask, mask], axis=1)
    rows = rows_s[at_rows, 0:width]
    gate = jnp.sum(rows_s[at_rows, width:].astype(f32) * pick_ref[0:1, :], axis=1, keepdims=True)
    low_in = (mm(rows, w_in[0:width, low_at:]) * mask_two).astype(bf16)
    rows_gate = jnp.concatenate([rows, low_in[:, :SR]], axis=1)
    rows_up = jnp.concatenate([rows, low_in[:, SR:]], axis=1)
    wait_for(early[2:4])
    act_parts = []
    for j in range(chunks):
        wait_for(early[4 + 2 * j : 6 + 2 * j], late if j == 0 else given[4:] if j == 1 else ())
        at = slice(j * CUT, (j + 1) * CUT)
        gate_h = mm(rows_gate, w_in[:, at])
        up_h = mm(rows_up, w_in[:, hidden + j * CUT : hidden + (j + 1) * CUT])
        share = 1.0 / (1.0 + jnp.exp(-gate_h))
        silu = gate_h * share
        silu_s[:, at] = silu
        slope_s[:, at] = up_h * (share * (1.0 + gate_h * (1.0 - share)))
        act_parts.append((silu * up_h).astype(bf16))
    act = jnp.concatenate(act_parts, axis=1)
    wait_for([given[1], given[3]] + late)

    low_down = (mm(act, w_down[0:hidden, thin_at:]) * mask).astype(bf16)
    act_low = jnp.concatenate([act, low_down], axis=1)
    d_gate = jnp.zeros((TILE, 1), f32)
    d_out_parts = []
    for j in range(width // CUT):
        at = slice(j * CUT, (j + 1) * CUT)
        out = mm(act_low, w_down[:, at]).astype(bf16).astype(f32)
        cot = cot_s[at_rows, at].astype(f32)
        d_out_parts.append((gate * cot).astype(bf16))
        weighted = gate * out
        for i in range(2):
            value = weighted[i * part : (i + 1) * part]
            if not first:
                value = value + prev_out[i][:, at].astype(f32)
            out_refs[i][:, at] = value.astype(bf16)
        d_gate = d_gate + jnp.sum(cot * out, axis=1, keepdims=True)
    high = d_gate.astype(bf16).astype(f32)
    extra_ref[...] = high * pick_ref[1:2, :] + (d_gate - high) * pick_ref[2:3, :]

    mask_half = mask.astype(bf16)
    d_out = jnp.concatenate(d_out_parts, axis=1)
    d_low_down = mm_nt(d_out, w_down[hidden:, 0:width]).astype(bf16) * mask_half
    d_out_low = jnp.concatenate([d_out, d_low_down], axis=1)
    d_gate_parts, d_up_parts = [], []
    for j in range(chunks):
        at = slice(j * CUT, (j + 1) * CUT)
        d_act = mm_nt(d_out_low, w_down[at, :])
        d_gate_parts.append((d_act * slope_s[:, at]).astype(bf16))
        d_up_parts.append((d_act * silu_s[:, at]).astype(bf16))
    d_gate_h = jnp.concatenate(d_gate_parts, axis=1)
    d_up_h = jnp.concatenate(d_up_parts, axis=1)
    d_low_gate = mm_nt(d_gate_h, w_in[width:, 0:hidden]).astype(bf16) * mask_half
    d_low_up = mm_nt(d_up_h, w_in[width:, hidden:low_at]).astype(bf16) * mask_half
    d_low_in = jnp.concatenate([d_low_gate, d_low_up], axis=1)
    d_all_ref[:, 0:hidden] = d_gate_h
    d_all_ref[:, hidden:low_at] = d_up_h
    d_all_ref[:, low_at:] = d_low_in
    d_low_in_t, low_down_t, low_in_t, d_low_down_t = d_low_in.T, low_down.T, low_in.T, d_low_down.T
    for j in range(width // CUT):
        at = slice(j * CUT, (j + 1) * CUT)
        g_a_in[:, at] += mm(d_low_in_t, rows[:, at])
        g_b_down[:, at] += mm(low_down_t, d_out[:, at])
    for j in range(chunks):
        at = slice(j * CUT, (j + 1) * CUT)
        g_b_in[0, :, at] += mm(low_in_t[:SR], d_gate_h[:, at])
        g_b_in[1, :, at] += mm(low_in_t[SR:], d_up_h[:, at])
        g_a_down[:, at] += mm(d_low_down_t, act[:, at])

    @pl.when(step == pl.num_programs(0) - 1)
    def _():
        packed[0 : 2 * SR, :] = g_a_in[...].astype(bf16)
        packed[2 * SR : 3 * SR, :] = g_b_down[...].astype(bf16)
        packed[3 * SR : 4 * SR, 0:hidden] = g_b_in[0].astype(bf16)
        packed[3 * SR : 4 * SR, hidden:] = g_b_in[1].astype(bf16)
        packed[4 * SR :, 0:hidden] = g_a_down[: SR // 2].astype(bf16)
        packed[4 * SR :, hidden:] = g_a_down[SR // 2 :].astype(bf16)
        size = packed.shape[0] // 4
        for spot, b in enumerate((0, 2, 1, 3)):
            quarter = packed[pl.ds(pl.multiple_of((where_ref[0] ^ b) * size, 16), size), :]
            per = 4 // len(grad_refs)
            grad_refs[spot // per][(spot % per) * size : (spot % per + 1) * size, :] = quarter


def expert_pass(k, where, rows, cot, mask, picks, prev, weights):
    f32, bf16 = jnp.float32, jnp.bfloat16
    blocks = EVERY
    part, width = cot[0].shape
    hidden = weights[0].shape[2]
    tokens = blocks * part
    shares = 2 if prev is None else 4
    grad_shape = ((4 * SR + SR // 2) // shares, width)
    in_specs = [scalars(), by_tile(TILE, SR), pl.BlockSpec((8, 128), lambda i: (0, 0))] + [in_place()] * (2 * GATHERED)
    operands = [where, mask, picks, *rows, *cot]
    if prev is not None:
        in_specs += [by_tile(part, width)] * 2
        operands += list(prev)
    in_specs += [in_place()] * 7
    flops = 2 * tokens * (4 * width * hidden + 7 * SR * (width + hidden))
    return pl.pallas_call(
        functools.partial(expert_kernel, k, prev is None, width, hidden, blocks),
        grid=(tokens // TILE,),
        in_specs=in_specs,
        out_specs=[by_tile(part, width)] * 2
        + [by_tile(TILE, 2 * hidden + 2 * SR), by_tile(TILE, 128)]
        + [pl.BlockSpec(grad_shape, lambda i: (0, 0))] * shares,
        out_shape=[shape_of((tokens // 2, width))] * 2
        + [shape_of((tokens, 2 * hidden + 2 * SR)), shape_of((tokens, 128), f32)]
        + [shape_of(grad_shape)] * shares,
        scratch_shapes=[
            pltpu.VMEM((tokens, width + 128), bf16),
            pltpu.VMEM((tokens, width), bf16),
            pltpu.VMEM((width + SR, 2 * hidden + 2 * SR), bf16),
            pltpu.VMEM((hidden + SR, width + SR), bf16),
            pltpu.VMEM((TILE, hidden), f32),
            pltpu.VMEM((TILE, hidden), f32),
            pltpu.VMEM((2 * SR, width), f32),
            pltpu.VMEM((SR, width), f32),
            pltpu.VMEM((2, SR, hidden), f32),
            pltpu.VMEM((SR, hidden), f32),
            pltpu.VMEM((4 * SR + SR // 2, width), bf16),
            pltpu.SemaphoreType.DMA((7 + 2 * (hidden // CUT),)),
            pltpu.SemaphoreType.DMA((blocks, 2)),
        ],
        compiler_params=params(),
        cost_estimate=cost(flops, 40 << 20),
        name="expert",
    )(*operands, *weights)


def rows_kernel(part, width, hidden, local, *refs):
    bf16 = jnp.bfloat16
    d_all, extra, (w_gate_hbm, w_up_hbm, a_in_hbm) = refs[:local], refs[local : 2 * local], refs[2 * local : 2 * local + 3]
    even_ref, odd_ref, weight, sems = refs[2 * local + 3 :]
    step = pl.program_id(0)
    span = 2 * hidden + 2 * SR
    chunks = width // ROWS_CUT
    copies = []
    for j in range(chunks):
        at = slice(j * ROWS_CUT, (j + 1) * ROWS_CUT)
        group = []
        for k in range(local):
            base = k * span
            targets = [
                (w_gate_hbm.at[k, at], base, hidden),
                (w_up_hbm.at[k, at], base + hidden, hidden),
                (a_in_hbm.at[k, 0, at], base + 2 * hidden, SR),
                (a_in_hbm.at[k, 1, at], base + 2 * hidden + SR, SR),
            ]
            for i, (source, start, size) in enumerate(targets):
                group.append(
                    pltpu.make_async_copy(source, weight.at[at, start : start + size], sems.at[j, 4 * k + i])
                )
        copies.append(group)

    @pl.when(step == 0)
    def _():
        for group in copies:
            for item in group:
                item.start()

    both = jnp.concatenate([ref[...] for ref in d_all], axis=1)
    for j in range(chunks):

        @pl.when(step == 0)
        def _():
            for item in copies[j]:
                item.wait()

        at = slice(j * ROWS_CUT, (j + 1) * ROWS_CUT)
        value = mm_nt(both, weight[at, :]).astype(bf16)
        for b in range(ROWS_TILE // part):
            (even_ref, odd_ref)[b % 2][b // 2 * part : (b // 2 + 1) * part, at] = value[b * part : (b + 1) * part]
    total = sum([ref[...] for ref in extra[1:]], extra[0][...]).astype(bf16)
    for b in range(ROWS_TILE // part):
        (even_ref, odd_ref)[b % 2][b // 2 * part : (b // 2 + 1) * part, width:] = total[b * part : (b + 1) * part]


def rows_pass(part, d_all, extra, w_gate, w_up, a_in):
    local, width, hidden = w_gate.shape
    tokens, span = d_all[0].shape
    return pl.pallas_call(
        functools.partial(rows_kernel, part, width, hidden, local),
        grid=(tokens // ROWS_TILE,),
        in_specs=[by_tile(ROWS_TILE, span)] * local + [by_tile(ROWS_TILE, 128)] * local + [in_place()] * 3,
        out_specs=[by_tile(ROWS_TILE // 2, width + 128)] * 2,
        out_shape=[shape_of((tokens // 2, width + 128))] * 2,
        scratch_shapes=[
            pltpu.VMEM((width, local * span), jnp.bfloat16),
            pltpu.SemaphoreType.DMA((width // ROWS_CUT, 4 * local)),
        ],
        compiler_params=params(),
        cost_estimate=cost(2 * tokens * width * span * local, 40 << 20),
        name="rows",
    )(*d_all, *extra, w_gate, w_up, a_in)


def norm_grad(values, gain_row, upstream_grad):
    scale = lax.rsqrt(jnp.mean(values * values, axis=1, keepdims=True) + EPSILON)
    inner = gain_row * upstream_grad
    mean = jnp.mean(values * inner, axis=1, keepdims=True)
    return scale * inner - values * (scale * scale * scale * mean)


def unmix_kernel(
    wide,
    me_ref, resid_ref, cot_ref, gains_ref, mask_ref, router_ref, gates_ref, low_ref, att_ref, *refs,
):
    f32, bf16 = jnp.float32, jnp.bfloat16
    pieces, given, refs = refs[:PIECES], blocks_of(refs[PIECES : PIECES + GATHERED]), refs[PIECES + GATHERED :]
    resid_grad_ref, grad_ref, send_ref, weight, down, up, up_grad, sems = refs
    me = me_ref[0]
    width = resid_ref.shape[1]
    copies = output_copies(me, wide, given, weight, down, up, sems)
    for which in (1, 0, 2):
        for group in copies:
            group[which].start()
    resid = resid_ref[...]
    total = sum_pieces(*[ref[...] for ref in pieces])
    extra = total[:, width:]
    gates = gates_ref[...]
    d_gates = extra + pltpu.roll(extra, 64, 1)
    d_chosen = gates * (d_gates - jnp.sum(gates * d_gates, axis=1, keepdims=True))
    d_normed = total[:, :width] + mm_nt(d_chosen.astype(bf16), router_ref[...])
    d_resid = cot_ref[...].astype(f32) + norm_grad(resid, gains_ref[1:2, :], d_normed)
    resid_grad_ref[...] = d_resid
    branch = d_resid.astype(bf16)
    for group in copies:
        group[1].wait()
    d_low = (mm(branch, up[...]).astype(bf16).astype(f32) * mask_ref[...]).astype(bf16)
    low_t, d_low_t = low_ref[...].T, d_low.T
    up_grad[...] = mm(low_t, branch).astype(bf16)
    for group in copies:
        group[0].wait()
    for j in range(EVERY):
        here = slice(j * wide, (j + 1) * wide)
        copies[j][2].wait()
        send_ref[me ^ j] = (mm_nt(branch, weight[here, :]) + mm_nt(d_low, down[here, :])).astype(bf16)
        at = pl.multiple_of((me ^ j) * wide, wide)
        grad_ref[me ^ j, 0:SR, :] = mm(d_low_t, att_ref[me ^ j]).astype(bf16)
        grad_ref[me ^ j, SR:, :] = up_grad[:, pl.ds(at, wide)]


def unmix(me, resid, cot, gains, mask, router, gates, low, att_got, pieces, given):
    rows, width = resid.shape
    wide = width // EVERY
    return pl.pallas_call(
        functools.partial(unmix_kernel, wide),
        grid=(1,),
        in_specs=[scalars()]
        + [whole()] * 3
        + [pl.BlockSpec((rows, SR), lambda i: (0, 0))]
        + [whole()] * 4
        + piece_specs(rows, width + 128)
        + [in_place()] * GATHERED,
        out_specs=[whole()] * 3,
        out_shape=[
            shape_of((rows, width), jnp.float32),
            shape_of((EVERY, 2 * SR, wide)),
            shape_of((EVERY, rows, wide)),
        ],
        scratch_shapes=output_scratch(width)[:3]
        + [pltpu.VMEM((SR, width), jnp.bfloat16)]
        + output_scratch(width)[3:],
        compiler_params=params(),
        cost_estimate=cost(1 << 20, 1 << 16),
        name="unmix",
    )(me, resid, cot, gains, mask, router, gates, low, att_got, *pieces, *given)


def attend_back_kernel(
    rows, wide,
    me_ref, q_ref, k_ref, v_ref, att_ref, lse_ref, col_ref, row_ref, cos_ref, sin_ref, low_ref, mask_ref, up_ref,
    got_ref, normed_hbm, d_proj_ref, d_low_ref, down_grad_ref, up_grad_ref, d_att, normed, sems,
):
    f32, bf16 = jnp.float32, jnp.bfloat16
    tokens = q_ref.shape[0]
    scale = HD ** (-0.5)
    me = me_ref[0]
    bring = pltpu.make_async_copy(normed_hbm, normed, sems.at[0])
    bring.start()
    for j in range(EVERY):
        d_att[j * rows : (j + 1) * rows, :] = got_ref[me ^ j]
    seg_row = row_ref[0:1, :]
    for h in range(wide // HD):
        lanes = slice(h * HD, (h + 1) * HD)
        delta = jnp.sum(d_att[:, lanes].astype(f32) * att_ref[:, lanes], axis=1, keepdims=True)
        delta = jnp.broadcast_to(delta, (tokens, HD)).T[0:1, :]
        log_sum = lse_ref[h : h + 1, :]
        d_query = jnp.zeros((tokens, HD), f32)
        for c in range(tokens // TILE):
            at = slice(c * TILE, (c + 1) * TILE)
            scores = mm_nt(k_ref[at, lanes], q_ref[:, lanes]) * scale - log_sum
            probs = jnp.exp(jnp.where(col_ref[at, 0:1] == seg_row, scores, MASKED))
            d_probs = mm_nt(v_ref[at, lanes], d_att[:, lanes])
            d_scores = (probs * (d_probs - delta)).astype(bf16)
            d_value = mm(probs.astype(bf16), d_att[:, lanes])
            d_key = mm(d_scores, q_ref[:, lanes])
            d_query = d_query + mm(d_scores.T, k_ref[at, lanes])
            d_proj_ref[at, wide + h * HD : wide + (h + 1) * HD] = turn(
                d_key * scale, cos_ref[at, :], -sin_ref[at, :]
            ).astype(bf16)
            d_proj_ref[at, 2 * wide + h * HD : 2 * wide + (h + 1) * HD] = d_value.astype(bf16)
        d_proj_ref[:, lanes] = turn(d_query * scale, cos_ref[...], -sin_ref[...]).astype(bf16)
    for i in range(3):
        part = d_proj_ref[:, i * wide : (i + 1) * wide]
        d_low = (mm(part, up_ref[i]).astype(bf16).astype(f32) * mask_ref[...]).astype(bf16)
        d_low_ref[:, i * SR : (i + 1) * SR] = d_low
        up_grad_ref[i * SR : (i + 1) * SR, :] = mm(low_ref[:, i * SR : (i + 1) * SR].T, part).astype(bf16)
    d_low_t = d_low_ref[...].T
    bring.wait()
    for j in range(EVERY):
        down_grad_ref[j] = mm(d_low_t, normed[:, j * wide : (j + 1) * wide]).astype(bf16)


def attend_back(rows, me, q, k, v, att, lse, seg_col, seg_row, cosine, sine, low, mask, up, got, normed):
    tokens, wide = q.shape
    width = wide * EVERY
    return pl.pallas_call(
        functools.partial(attend_back_kernel, rows, wide),
        in_specs=[scalars()] + [whole()] * 13 + [in_place()],
        out_specs=[whole()] * 4,
        out_shape=[
            shape_of((tokens, 3 * wide)),
            shape_of((tokens, 3 * SR)),
            shape_of((EVERY, 3 * SR, wide)),
            shape_of((3 * SR, wide)),
        ],
        scratch_shapes=[
            pltpu.VMEM((tokens, wide), jnp.bfloat16),
            pltpu.VMEM((tokens, width), jnp.bfloat16),
            pltpu.SemaphoreType.DMA((1,)),
        ],
        compiler_params=params(),
        cost_estimate=cost(1 << 20, 1 << 16),
        name="attend_back",
    )(me, q, k, v, att, lse, seg_col, seg_row, cosine, sine, low, mask, up, got, normed)


def unproject_kernel(rows, width, wide, me_ref, proj_ref, low_ref, *refs):
    bf16 = jnp.bfloat16
    given, w_hbm = blocks_of(refs[:GATHERED]), refs[GATHERED]
    even_ref, odd_ref, weight, sems, w_sems = refs[GATHERED + 1 :]
    me, thin = me_ref[0], 3 * SR

    @pl.when(pl.program_id(0) == 0)
    def _():
        copies = []
        for j in range(EVERY):
            at = pl.multiple_of((me ^ j) * wide, wide)
            for i in range(3):
                copies.append(
                    pltpu.make_async_copy(
                        w_hbm.at[j, i],
                        weight.at[j * wide : (j + 1) * wide, i * wide : (i + 1) * wide],
                        w_sems.at[j, i],
                    )
                )
            for part in range(2):
                start = part * thin
                copies.append(
                    pltpu.make_async_copy(
                        given[j].at[:, start : start + thin],
                        weight.at[pl.ds(at + part * rows, rows), 3 * wide : 3 * wide + thin],
                        sems.at[j, part],
                    )
                )
        for item in copies:
            item.start()
        for item in copies:
            item.wait()

    both = jnp.concatenate([proj_ref[...], low_ref[...]], axis=1)
    for j in range(width // CUT):
        lanes = slice(j * CUT, (j + 1) * CUT)
        value = mm_nt(both, weight[lanes, :]).astype(bf16)
        even_ref[:, lanes] = value[:rows]
        odd_ref[:, lanes] = value[rows:]


def unproject(rows, me, d_proj, d_low, given, w_got):
    tokens = d_proj.shape[0]
    wide = d_proj.shape[1] // 3
    width = wide * EVERY
    return pl.pallas_call(
        functools.partial(unproject_kernel, rows, width, wide),
        grid=(tokens // TILE,),
        in_specs=[scalars(), by_tile(TILE, 3 * wide), by_tile(TILE, 3 * SR)] + [in_place()] * (GATHERED + 1),
        out_specs=[by_tile(rows, width)] * 2,
        out_shape=[shape_of((tokens // 2, width))] * 2,
        scratch_shapes=[
            pltpu.VMEM((width, 3 * wide + 3 * SR), jnp.bfloat16),
            pltpu.SemaphoreType.DMA((EVERY, 2)),
            pltpu.SemaphoreType.DMA((EVERY, 3)),
        ],
        compiler_params=params(),
        cost_estimate=cost(1 << 20, 1 << 16),
        name="unproject",
    )(me, d_proj, d_low, *given, w_got)


def finish_kernel(hidden_ref, gains_ref, resid_grad_ref, *refs):
    pieces, out_ref = refs[:PIECES], refs[PIECES]
    d_normed = sum_pieces(*[ref[...] for ref in pieces])
    back = norm_grad(hidden_ref[...].astype(jnp.float32), gains_ref[0:1, :], d_normed)
    out_ref[...] = (resid_grad_ref[...] + back).astype(jnp.bfloat16)


def finish(hidden, gains, resid_grad, pieces):
    rows, width = hidden.shape
    return pl.pallas_call(
        finish_kernel,
        grid=(1,),
        in_specs=[whole()] * 3 + piece_specs(rows, width),
        out_specs=whole(),
        out_shape=shape_of((rows, width)),
        compiler_params=params(),
        cost_estimate=cost(1 << 20, 1 << 16),
        name="finish",
    )(hidden, gains, resid_grad, *pieces)


def layer_kernel(resid_ref, *refs):
    pieces, out_ref = refs[:PIECES], refs[PIECES]
    out_ref[...] = (resid_ref[...] + sum_pieces(*[ref[...] for ref in pieces])).astype(jnp.bfloat16)


def layer(resid, pieces):
    rows, width = resid.shape
    return pl.pallas_call(
        layer_kernel,
        grid=(1,),
        in_specs=[whole()] + piece_specs(rows, width),
        out_specs=whole(),
        out_shape=shape_of((rows, width)),
        compiler_params=params(),
        cost_estimate=cost(1 << 20, 1 << 16),
        name="layer",
    )(resid, *pieces)


def unpack_kernel(hidden, first, where_ref, *refs):
    f32 = jnp.float32
    parts, refs = refs[:8], refs[8:]
    refs = refs if first else refs[4:]
    a_in_ref, b_in_ref, a_down_ref, b_down_ref, packed = refs
    size = packed.shape[0] // 4
    for b in range(4):
        for i in range(2):
            spot = pl.multiple_of((where_ref[0] ^ b) * size + i * (size // 2), 8)
            packed[pl.ds(spot, size // 2), :] = parts[2 * b + i][...].astype(f32)
    for i in range(2):
        a_in_ref[0, i] = packed[i * SR : (i + 1) * SR, :].T
        b_in_ref[0, i] = packed[3 * SR : 4 * SR, i * hidden : (i + 1) * hidden]
    b_down_ref[0] = packed[2 * SR : 3 * SR, :]
    a_down_ref[0, :, 0 : SR // 2] = packed[4 * SR :, 0:hidden].T
    a_down_ref[0, :, SR // 2 :] = packed[4 * SR :, hidden:].T


def unpack(k, where, quarters, hidden, experts, before):
    quarters = [part for quarter in quarters for part in quarter]
    width = quarters[0].shape[1]
    f32 = jnp.float32
    first = before is None
    shapes = [(experts, 2, width, SR), (experts, 2, SR, hidden), (experts, hidden, SR), (experts, SR, width)]
    given = [] if first else list(before)
    return pl.pallas_call(
        functools.partial(unpack_kernel, hidden, first),
        grid=(1,),
        in_specs=[scalars()] + [whole()] * 8 + [in_place()] * len(given),
        out_specs=[
            pl.BlockSpec((1,) + shape[1:], lambda i, n=len(shape): (k,) + (0,) * (n - 1)) for shape in shapes
        ],
        out_shape=[shape_of(shape, f32) for shape in shapes],
        input_output_aliases={} if first else {9 + i: i for i in range(4)},
        scratch_shapes=[pltpu.VMEM((4 * SR + SR // 2, width), f32)],
        compiler_params=params(),
        cost_estimate=cost(1 << 20, 1 << 16),
        name="unpack",
    )(where, *quarters, *given)


def thin_kernel(late_left, late_right, early_left, early_right, a_ref, b_ref):
    f32 = jnp.float32
    late = late_left[...].astype(f32) + late_right[...].astype(f32)
    early = early_left[...].astype(f32) + early_right[...].astype(f32)
    for i in range(4):
        at = (2 + i) * SR if i < 3 else 0
        a_ref[i] = late[at : at + SR, :].T
        b_ref[i] = (early[i * SR : (i + 1) * SR, :] if i < 3 else late[SR : 2 * SR, :]).T


def thin_grads(late, early):
    wide = late[0].shape[1]
    return pl.pallas_call(
        thin_kernel,
        in_specs=[whole()] * 4,
        out_specs=[whole()] * 2,
        out_shape=[shape_of((4, wide, SR), jnp.float32)] * 2,
        compiler_params=params(),
        cost_estimate=cost(1 << 20, 1 << 16),
        name="thin_grads",
    )(*late, *early)


def split_layer(
    hidden_in,
    segments,
    routes,
    doc_sets,
    cotangent,
    w_qkv,
    w_out,
    gain_attn,
    gain_moe,
    router,
    w_gate,
    w_up,
    w_down,
    a_attn,
    b_attn,
    exp_a_in,
    exp_b_in,
    exp_a_down,
    exp_b_down,
):
    bf16, f32 = jnp.bfloat16, jnp.float32
    index = lax.axis_index("fsdp")
    me = index.astype(jnp.int32).reshape(1)
    where = lax.axis_index("rep").astype(jnp.int32).reshape(1)
    hidden, upstream = hidden_in[0], cotangent[0]
    rows, width = hidden.shape
    wide = width // EVERY
    local, _, inner = w_gate.shape
    experts_all = local * EVERY

    order = index ^ jnp.arange(EVERY)
    positions = (order[:, None] * rows + jnp.arange(rows)[None, :]).reshape(-1)
    cosine, sine = rope_tables(positions, HD)
    cosine, sine = jnp.concatenate([cosine, cosine], axis=1), jnp.concatenate([-sine, sine], axis=1)
    lanes = jnp.arange(128)
    named = jnp.any(routes[0][:, :, None] + SPOT == lanes[None, None, :], axis=1).astype(f32)
    out_own = jnp.concatenate([w_out, a_attn[3], b_attn[3]], axis=1)

    def picks(k):
        high = (lanes == SPOT + 2 * index + k).astype(f32)
        low = (lanes == SPOT + 2 * index + k + 64).astype(f32)
        return jnp.stack([high + low, high, low] + [jnp.zeros_like(high)] * 5)

    hidden_first = gather_first(hidden)
    narrow = jnp.concatenate([a_attn[0], a_attn[1], a_attn[2]], axis=1)
    at_spot = ((0, 0), (SPOT, 128 - SPOT - experts_all))
    meta = jnp.pad(router[:rows], at_spot) + jnp.pad(segments[0].astype(bf16)[:, None], ((0, 0), (0, 127)))
    lines = jnp.concatenate([gain_attn.reshape(2, 128), gain_moe.reshape(2, 128)], axis=0)
    lines = jnp.pad(lines, ((0, rows - 4), (0, 0)))
    given = jnp.concatenate([narrow[:rows], narrow[rows:], meta, jnp.pad(router[rows:], at_spot), lines], axis=1)
    given_first = gather_first(given)
    w_got = lax.all_to_all(by_columns(w_qkv, wide), "fsdp", split_axis=0, concat_axis=0, tiled=True)
    hidden_first, cosine, sine, out_own, named, pick_rows = tie(
        hidden_first, cosine, sine, out_own, named, [picks(0), picks(1)]
    )
    hidden_given = gather_third(hidden_first, *gather_second(*hidden_first))
    given = gather_third(given_first, *gather_second(*given_first))

    hidden_given, given, w_got, out_own = tie(hidden_given, given, w_got, out_own)
    out_first = gather_first(out_own)
    queries, keys, values, normed_one, low_qkv, mask, seg_col, seg_row, gains, router_all = project(
        me, doc_sets, cosine, sine, b_attn, hidden_given, given, w_got
    )
    att, lse, att_send = attend(rows, me, queries, keys, values, seg_col, seg_row)
    att_send, out_first = tie(att_send, out_first)
    att_got = lax.all_to_all(att_send, "fsdp", split_axis=0, concat_axis=0, tiled=True)
    far, *others = gather_second(*out_first)
    cot_first = gather_first(tie(upstream, others)[0])
    far, others, att_got, cot_first = tie(far, others, att_got, cot_first)
    out_given = gather_third(out_first, far, *others)
    cot_second = gather_second(*cot_first)
    resid_one, normed_own, low_out, gates_own = mix(
        me, hidden, gains, mask, router_all, named, att_got, out_given
    )
    normed_own, cot_second = tie(normed_own, cot_second)
    normed_given = gather_relative(normed_own)
    cot_given = gather_third(cot_first, *cot_second)

    weights = (w_gate, w_up, w_down, exp_a_in, exp_b_in, exp_a_down, exp_b_down)
    *state, d_all_a, extra_a, kept_a, sent_a = expert_pass(
        0, where, normed_given, cot_given, mask, pick_rows[0], None, weights
    )
    def in_two(values):
        return [values[: values.shape[0] // 2], values[values.shape[0] // 2 :]]

    def later(values, anchor):
        return tie(values, anchor)[0]

    def in_two(values):
        return [values[: values.shape[0] // 2], values[values.shape[0] // 2 :]]

    sent_a = rep_swap(sent_a, 1)
    *state, d_all_b, extra_b, kept_0, kept_1, sent_0, sent_1 = expert_pass(
        1, where, normed_given, cot_given, mask, pick_rows[1], state, weights
    )
    kept_b, sent_b = [kept_0, kept_1], [sent_0, sent_1]
    d_all_b, kept_b, sent_b, sent_a, state = tie(d_all_b, kept_b, sent_b, sent_a, state)
    out_even, out_odd = state
    half_a = add_half(kept_a, sent_a)
    size = half_a.shape[0] // 2
    sent_b[0] = rep_swap(sent_b[0], 1)
    other_a = rep_swap(half_a[size:], 2)
    out_got = swap(out_odd, 1)
    row_even, row_odd = rows_pass(rows, [d_all_a, d_all_b], [extra_a, extra_b], w_gate, w_up, exp_a_in)
    row_odd, other_a, sent_b[0], out_got = tie(row_odd, other_a, sent_b[0], out_got)
    got = swap(row_odd, 1)
    sent_b[1] = rep_swap(later(sent_b[1], row_odd), 1)
    total_a = in_two(add_half(half_a[:size], other_a))
    d_far = scatter_second(row_even, got)
    d_far, sent_b[1] = tie(d_far, sent_b[1])
    pieces = scatter_third(row_even, got, *d_far)
    two_a = [rep_swap(later(total_a[0], d_far), 2)]
    pieces, two_a[0] = tie(pieces, two_a[0])
    early_a = later(total_a, pieces)
    two_a.append(rep_swap(early_a[1], 2))
    one_a = [None, rep_swap(early_a[1], 1)]
    d_resid, thin_send, d_att_send = unmix(
        me, resid_one, upstream, gains, mask, router_all, gates_own, low_out, att_got, pieces, out_given
    )
    d_att_send, two_a[1], one_a[1] = tie(d_att_send, two_a[1], one_a[1])
    d_att_got = lax.all_to_all(d_att_send, "fsdp", split_axis=0, concat_axis=0, tiled=True)
    mine_b = add_half(kept_b[0], sent_b[0])
    half_b = later(in_two(add_half(kept_b[1], sent_b[1])), d_att_send)
    one_a[0] = rep_swap(later(total_a[0], d_att_send), 1)
    other_b = [rep_swap(half_b[0], 2)]
    out_far = scatter_second(*later((out_even, out_got), d_att_send))
    d_att_got, other_b[0], one_a[0], out_far = tie(d_att_got, other_b[0], one_a[0], out_far)
    total_b = [add_half(mine_b[: size // 2], other_b[0])]
    other_b.append(rep_swap(later(half_b[1], d_att_got), 2))
    three_a = [rep_swap(later(two_a[0], d_att_got), 1)]

    def exchange(values):
        return lax.all_to_all(values, "fsdp", split_axis=0, concat_axis=0, tiled=True)

    out_grads = exchange(later(thin_send, d_att_got))
    d_proj, d_low, down_send, up_grads = attend_back(
        rows, me, queries, keys, values, att, lse, seg_col, seg_row, cosine, sine, low_qkv, mask, b_attn,
        d_att_got, normed_one,
    )
    d_proj, down_send, other_b[1], three_a[0], out_grads = tie(d_proj, down_send, other_b[1], three_a[0], out_grads)
    down_grads = exchange(down_send)
    two_b = [rep_swap(later(total_b[0], d_proj), 2)]
    three_a.append(rep_swap(later(two_a[1], d_proj), 1))
    even, odd = unproject(rows, me, d_proj, d_low, given, w_got)
    odd, down_grads, two_b[0], three_a[1] = tie(odd, down_grads, two_b[0], three_a[1])
    got = swap(odd, 1)
    thin = [jnp.sum(part.astype(f32), axis=0).astype(bf16) for part in (out_grads, down_grads)]
    thin = jnp.concatenate(thin, axis=0)
    thin_near = rep_swap(thin, 1)
    total_b.append(later(add_half(mine_b[size // 2 :], other_b[1]), odd))
    two_b.append(rep_swap(total_b[1], 2))
    up_near = rep_swap(later(up_grads, odd), 1)
    d_far = scatter_second(even, got)
    d_far, thin_near, two_b[1], up_near = tie(d_far, thin_near, two_b[1], up_near)
    pieces = scatter_third(even, got, *d_far)
    thin, up_grads = add_half(thin, thin_near), add_half(up_grads, up_near)
    thin_last, up_far = rep_swap(thin, 2), rep_swap(up_grads, 2)
    one_b = [rep_swap(later(total_b[0], d_far), 1)]
    grads = unpack(0, where, later([total_a, one_a, two_a, three_a], d_far), inner, local, None)
    pieces, grads = tie(pieces, grads)
    one_b.append(rep_swap(later(total_b[1], pieces), 1))
    three_b = [rep_swap(part, 1) for part in later(two_b, pieces)]
    grad_in = finish(hidden, gains, d_resid, pieces)
    grad_in, thin_last, up_far, one_b[0] = tie(grad_in, thin_last, up_far, one_b[0])
    grad_a, grad_b = thin_grads([thin, thin_last], [up_grads, up_far])
    out_pieces = scatter_third(*later((out_even, out_got), pieces), *out_far)
    layer_out = layer(resid_one, out_pieces)
    one_b, three_b, layer_out, grad_in, grad_a, grad_b = tie(one_b, three_b, layer_out, grad_in, grad_a, grad_b)
    grads = unpack(1, where, [total_b, one_b, two_b, three_b], inner, local, grads)
    return (layer_out[None], grad_in[None], grad_a, grad_b, *grads)


def solution(mesh):
    shape = dict(mesh.shape)
    shards = split_layer if shape == {"rep": 4, "fsdp": EVERY} else gathered_layer
    return jax.shard_map(
        shards,
        mesh=mesh,
        in_specs=(
            P("rep", "fsdp", None),
            P("rep", "fsdp"),
            P("rep", "fsdp", None),
            P("rep", None),
            P("rep", "fsdp", None),
            P(None, "fsdp", None),
            P("fsdp", None),
            P("fsdp"),
            P("fsdp"),
            P("fsdp", None),
            P("fsdp", None, None),
            P("fsdp", None, None),
            P("fsdp", None, None),
            P(None, "fsdp", None),
            P(None, "fsdp", None),
            P("fsdp", None, None, None),
            P("fsdp", None, None, None),
            P("fsdp", None, None),
            P("fsdp", None, None),
        ),
        out_specs=(
            P("rep", "fsdp", None),
            P("rep", "fsdp", None),
            P(None, "fsdp", None),
            P(None, "fsdp", None),
            P("fsdp", None, None, None),
            P("fsdp", None, None, None),
            P("fsdp", None, None),
            P("fsdp", None, None),
        ),
        check_vma=False,
    )
```

```python
import functools
import math

import jax
import jax.numpy as jnp
from jax import lax
from jax.experimental import pallas as pl
from jax.experimental.pallas import tpu as pltpu
from jax.sharding import PartitionSpec as P

HD = 128
TOP = 8
R = 16
SETS = 8
SR = 128


EPSILON = 1e-05
MASKED = -1e30


def rms_scale(values):
    return values * lax.rsqrt(jnp.mean(values * values, axis=-1, keepdims=True) + EPSILON)


def norm_back(values, gain_row, upstream_grad):
    result, pull_back = jax.vjp(lambda inner_rows: rms_scale(inner_rows) * gain_row, values)
    return pull_back(upstream_grad)[0]


def rope_tables(positions, head_size):
    half_size = head_size // 2
    inv_freq = jnp.exp(
        jnp.arange(half_size, dtype=jnp.float32) * (-2.0 * math.log(10000.0) / head_size)
    )
    angles = positions.astype(jnp.float32)[:, None] * inv_freq[None, :]
    return (jnp.cos(angles), jnp.sin(angles))


def rotate(values, cosine, sine_table):
    half_size = values.shape[-1] // 2
    front_half = values[..., :half_size]
    back_half = values[..., half_size:]
    cos_rows = cosine[:, None, :]
    sin_rows = sine_table[:, None, :]
    return jnp.concatenate(
        [
            front_half * cos_rows - back_half * sin_rows,
            back_half * cos_rows + front_half * sin_rows,
        ],
        axis=-1,
    )


def gathered_layer(
    hidden_in,
    segments,
    routes,
    doc_sets,
    cotangent,
    w_qkv,
    w_out,
    gain_attn,
    gain_moe,
    router,
    w_gate,
    w_up,
    w_down,
    a_attn,
    b_attn,
    exp_a_in,
    exp_b_in,
    exp_a_down,
    exp_b_down,
):
    shard_count = lax.axis_size("fsdp")
    shard_index = lax.axis_index("fsdp")
    tok_rows = hidden_in.shape[1]
    model_width = hidden_in.shape[2]
    head_count = model_width // HD
    local_experts = w_gate.shape[0]
    experts_all = local_experts * shard_count
    capacity = max(2, 3 * tok_rows * TOP // (2 * experts_all))
    score_scale = HD ** (-0.5)
    (
        attention_weight_full,
        output_weight_full,
        adapter_down_weight,
        adapter_up_weight,
        first_norm_gain_full,
        second_norm_gain_full,
        router_weight_full,
    ) = (
        lax.all_gather(w_qkv, "fsdp", axis=1, tiled=True),
        lax.all_gather(w_out, "fsdp", axis=0, tiled=True),
        lax.all_gather(a_attn, "fsdp", axis=1, tiled=True),
        lax.all_gather(b_attn, "fsdp", axis=1, tiled=True),
        lax.all_gather(gain_attn, "fsdp", axis=0, tiled=True),
        lax.all_gather(gain_moe, "fsdp", axis=0, tiled=True),
        lax.all_gather(router, "fsdp", axis=0, tiled=True),
    )
    gain_one = first_norm_gain_full.astype(jnp.float32)
    gain_two = second_norm_gain_full.astype(jnp.float32)
    seg_local = segments[0]
    set_token = jnp.sum(
        jnp.where(seg_local[:, None] == jnp.arange(SETS)[None, :], doc_sets[0][None, :], 0), axis=1
    )
    document_set_mask = (set_token[:, None] == (jnp.arange(SR) // R)[None, :]).astype(jnp.float32)
    mask_half = document_set_mask.astype(jnp.bfloat16)
    hidden_f = hidden_in[0].astype(jnp.float32)
    first_normed_rows = (rms_scale(hidden_f) * gain_one).astype(jnp.bfloat16)
    attention_rank_branch = (
        jnp.einsum(
            "xj,zje->zxe",
            first_normed_rows,
            adapter_down_weight[:3],
            preferred_element_type=jnp.float32,
        )
        * document_set_mask[None]
    ).astype(jnp.bfloat16)
    projected = jnp.einsum(
        "td,pde->pte", first_normed_rows, attention_weight_full, preferred_element_type=jnp.float32
    ) + jnp.einsum(
        "nzv,nwv->nzw",
        attention_rank_branch,
        adapter_up_weight[:3],
        preferred_element_type=jnp.float32,
    )
    positions = shard_index * tok_rows + jnp.arange(tok_rows)
    cosine, sine_table = rope_tables(positions, HD)
    queries = rotate(projected[0].reshape(tok_rows, head_count, HD), cosine, sine_table).astype(
        jnp.bfloat16
    )
    keys_own = (
        rotate(projected[1].reshape(tok_rows, head_count, HD), cosine, sine_table)
        .astype(jnp.bfloat16)
        .reshape(tok_rows, model_width)
    )
    values_own = projected[2].astype(jnp.bfloat16)
    seg_own = seg_local.astype(jnp.bfloat16)
    run_max = jnp.full((head_count, tok_rows), MASKED, jnp.float32)
    key_piece = lax.all_gather(keys_own, "fsdp", axis=0, tiled=True)
    value_piece = lax.all_gather(values_own, "fsdp", axis=0, tiled=True)
    seg_piece = lax.all_gather(seg_own, "fsdp", axis=0, tiled=True)
    piece_rows = key_piece.shape[0]
    scores = (
        jnp.einsum(
            "qhd,khd->hqk",
            queries,
            key_piece.reshape(piece_rows, head_count, HD),
            preferred_element_type=jnp.float32,
        )
        * score_scale
    )
    same_doc = seg_local[:, None] == seg_piece.astype(jnp.int32)[None, :]
    scores = jnp.where(same_doc[None], scores, MASKED)
    new_max = jnp.maximum(run_max, jnp.max(scores, axis=2))
    exp_scores = jnp.exp(scores - new_max[:, :, None])
    new_sum = jnp.sum(exp_scores, axis=2)
    new_acc = jnp.einsum(
        "hqk,khd->qhd",
        exp_scores.astype(jnp.bfloat16),
        value_piece.reshape(piece_rows, head_count, HD),
        preferred_element_type=jnp.float32,
    )
    folded = (new_max, new_sum, new_acc)
    run_max, run_sum, run_acc = folded
    log_sum = run_max + jnp.log(run_sum)
    attended = run_acc / jnp.transpose(run_sum)[:, :, None]
    attention_rounded_rows = attended.reshape(tok_rows, model_width).astype(jnp.bfloat16)
    output_rank_branch = (
        jnp.dot(attention_rounded_rows, adapter_down_weight[3], preferred_element_type=jnp.float32)
        * document_set_mask
    ).astype(jnp.bfloat16)
    resid_one = hidden_f + (
        jnp.dot(attention_rounded_rows, output_weight_full, preferred_element_type=jnp.float32)
        + jnp.einsum(
            "nd,gd->ng",
            output_rank_branch,
            adapter_up_weight[3],
            preferred_element_type=jnp.float32,
        )
    )
    normed_two = (rms_scale(resid_one) * gain_two).astype(jnp.bfloat16)
    logits = jnp.dot(normed_two, router_weight_full, preferred_element_type=jnp.float32)
    my_routes = routes[0]
    gate_weights = jax.nn.softmax(jnp.take_along_axis(logits, my_routes, axis=1), axis=-1)
    flat_routes = my_routes.reshape(-1)
    one_hot = (flat_routes[:, None] == jnp.arange(experts_all)[None, :]).astype(jnp.int32)
    slot_index = jnp.sum((jnp.cumsum(one_hot, axis=0) - 1) * one_hot, axis=1)
    token_index = jnp.arange(tok_rows * TOP) // TOP
    send_rows = (
        jnp.zeros((experts_all, capacity, model_width), jnp.bfloat16)
        .at[flat_routes, slot_index]
        .set(normed_two[token_index])
    )
    send_sets = (
        jnp.zeros((experts_all, capacity), jnp.bfloat16)
        .at[flat_routes, slot_index]
        .set(set_token[token_index].astype(jnp.bfloat16))
    )
    rows_got = lax.all_to_all(
        send_rows.reshape(shard_count, local_experts, capacity, model_width),
        "fsdp",
        split_axis=0,
        concat_axis=0,
        tiled=True,
    )
    sets_got = lax.all_to_all(
        send_sets.reshape(shard_count, local_experts, capacity),
        "fsdp",
        split_axis=0,
        concat_axis=0,
        tiled=True,
    )
    slot_mask = (sets_got.astype(jnp.int32)[..., None] == jnp.arange(SR) // R).astype(jnp.float32)
    low_in = (
        jnp.einsum("necd,eids->necis", rows_got, exp_a_in, preferred_element_type=jnp.float32)
        * slot_mask[:, :, :, None, :]
    ).astype(jnp.bfloat16)
    gate_h = jnp.einsum(
        "necd,edf->necf", rows_got, w_gate, preferred_element_type=jnp.float32
    ) + jnp.einsum(
        "necs,esf->necf", low_in[:, :, :, 0], exp_b_in[:, 0], preferred_element_type=jnp.float32
    )
    up_h = jnp.einsum(
        "necd,edf->necf", rows_got, w_up, preferred_element_type=jnp.float32
    ) + jnp.einsum(
        "necs,esf->necf", low_in[:, :, :, 1], exp_b_in[:, 1], preferred_element_type=jnp.float32
    )
    activation = (jax.nn.silu(gate_h) * up_h).astype(jnp.bfloat16)
    low_down = (
        jnp.einsum("necf,efs->necs", activation, exp_a_down, preferred_element_type=jnp.float32)
        * slot_mask
    ).astype(jnp.bfloat16)
    expert_out = (
        jnp.einsum("necf,efd->necd", activation, w_down, preferred_element_type=jnp.float32)
        + jnp.einsum("necs,esd->necd", low_down, exp_b_down, preferred_element_type=jnp.float32)
    ).astype(jnp.bfloat16)
    expert_out, rows_got, slot_mask, low_in, gate_h, up_h, activation, low_down = (
        expert_out,
        rows_got,
        slot_mask,
        low_in,
        gate_h,
        up_h,
        activation,
        low_down,
    )
    returned = lax.all_to_all(expert_out, "fsdp", split_axis=0, concat_axis=0, tiled=True)
    route_out = (
        returned.reshape(experts_all, capacity, model_width)[flat_routes, slot_index]
        .reshape(tok_rows, TOP, model_width)
        .astype(jnp.float32)
    )
    layer_value = resid_one + jnp.sum(gate_weights[:, :, None] * route_out, axis=1)
    (
        attention_weight_full,
        output_weight_full,
        adapter_down_weight,
        adapter_up_weight,
        first_norm_gain_full,
        second_norm_gain_full,
        router_weight_full,
    ) = (
        lax.all_gather(w_qkv, "fsdp", axis=1, tiled=True),
        lax.all_gather(w_out, "fsdp", axis=0, tiled=True),
        lax.all_gather(a_attn, "fsdp", axis=1, tiled=True),
        lax.all_gather(b_attn, "fsdp", axis=1, tiled=True),
        lax.all_gather(gain_attn, "fsdp", axis=0, tiled=True),
        lax.all_gather(gain_moe, "fsdp", axis=0, tiled=True),
        lax.all_gather(router, "fsdp", axis=0, tiled=True),
    )
    gain_one = first_norm_gain_full.astype(jnp.float32)
    gain_two = second_norm_gain_full.astype(jnp.float32)
    upstream = cotangent[0].astype(jnp.float32)
    d_route = (gate_weights[:, :, None] * upstream[:, None, :]).astype(jnp.bfloat16)
    d_gates = jnp.sum(upstream[:, None, :] * route_out, axis=2)
    d_chosen = gate_weights * (d_gates - jnp.sum(gate_weights * d_gates, axis=1, keepdims=True))
    d_logits = jnp.sum(
        jnp.where(
            my_routes[:, :, None] == jnp.arange(experts_all)[None, None, :],
            d_chosen[:, :, None],
            0.0,
        ),
        axis=1,
    ).astype(jnp.bfloat16)
    send_grads = (
        jnp.zeros((experts_all, capacity, model_width), jnp.bfloat16)
        .at[flat_routes, slot_index]
        .set(d_route.reshape(tok_rows * TOP, model_width))
    )
    grads_got = lax.all_to_all(
        send_grads.reshape(shard_count, local_experts, capacity, model_width),
        "fsdp",
        split_axis=0,
        concat_axis=0,
        tiled=True,
    )
    slot_half = slot_mask.astype(jnp.bfloat16)
    d_low_down = (
        jnp.einsum(
            "necd,esd->necs", grads_got, exp_b_down, preferred_element_type=jnp.float32
        ).astype(jnp.bfloat16)
        * slot_half
    )
    d_activation = jnp.einsum(
        "necd,efd->necf", grads_got, w_down, preferred_element_type=jnp.float32
    ) + jnp.einsum("necs,efs->necf", d_low_down, exp_a_down, preferred_element_type=jnp.float32)
    silu_value, silu_pull = jax.vjp(
        lambda gate_in, up_in: jax.nn.silu(gate_in) * up_in, gate_h, up_h
    )
    d_gate_h, d_up_h = silu_pull(d_activation)
    d_gate_h = d_gate_h.astype(jnp.bfloat16)
    d_up_h = d_up_h.astype(jnp.bfloat16)
    d_both = jnp.stack([d_gate_h, d_up_h], axis=3)
    d_low_in = (
        jnp.einsum(
            "necif,eisf->necis", d_both, exp_b_in, preferred_element_type=jnp.float32
        ).astype(jnp.bfloat16)
        * slot_half[:, :, :, None, :]
    )
    d_rows = (
        jnp.einsum("necf,edf->necd", d_gate_h, w_gate, preferred_element_type=jnp.float32)
        + jnp.einsum("necf,edf->necd", d_up_h, w_up, preferred_element_type=jnp.float32)
        + jnp.einsum("necis,eids->necd", d_low_in, exp_a_in, preferred_element_type=jnp.float32)
    )
    returned_grads = lax.all_to_all(
        d_rows.astype(jnp.bfloat16), "fsdp", split_axis=0, concat_axis=0, tiled=True
    )
    g_exp_b_down = jnp.einsum(
        "necs,necd->esd", low_down, grads_got, preferred_element_type=jnp.float32
    )
    g_exp_a_down = jnp.einsum(
        "necf,necs->efs", activation, d_low_down, preferred_element_type=jnp.float32
    )
    g_exp_b_in = jnp.einsum("necis,necif->eisf", low_in, d_both, preferred_element_type=jnp.float32)
    g_exp_a_in = jnp.einsum(
        "necd,necis->eids", rows_got, d_low_in, preferred_element_type=jnp.float32
    )
    d_normed_two = jnp.sum(
        returned_grads.reshape(experts_all, capacity, model_width)[flat_routes, slot_index]
        .reshape(tok_rows, TOP, model_width)
        .astype(jnp.float32),
        axis=1,
    ) + jnp.einsum("te,de->td", d_logits, router_weight_full, preferred_element_type=jnp.float32)
    d_resid_one = upstream + norm_back(resid_one, gain_two, d_normed_two)
    branch_gradient = d_resid_one.astype(jnp.bfloat16)
    output_adapter_gradient = (
        jnp.dot(branch_gradient, adapter_up_weight[3], preferred_element_type=jnp.float32).astype(
            jnp.bfloat16
        )
        * mask_half
    )
    d_att = (
        jnp.einsum(
            "te,de->td", branch_gradient, output_weight_full, preferred_element_type=jnp.float32
        )
        + jnp.einsum(
            "cr,ar->ca",
            output_adapter_gradient,
            adapter_down_weight[3],
            preferred_element_type=jnp.float32,
        )
    ).astype(jnp.bfloat16)
    output_up_gradient = jnp.einsum(
        "ts,te->es", output_rank_branch, branch_gradient, preferred_element_type=jnp.float32
    )
    output_down_gradient = jnp.einsum(
        "td,ts->ds",
        attention_rounded_rows,
        output_adapter_gradient,
        preferred_element_type=jnp.float32,
    )
    d_att_heads = d_att.reshape(tok_rows, head_count, HD)
    delta_rows = jnp.transpose(jnp.sum(d_att_heads.astype(jnp.float32) * attended, axis=2))
    key_piece = lax.all_gather(keys_own, "fsdp", axis=0, tiled=True)
    value_piece = lax.all_gather(values_own, "fsdp", axis=0, tiled=True)
    seg_piece = lax.all_gather(seg_own, "fsdp", axis=0, tiled=True)
    piece_rows = key_piece.shape[0]
    key_heads = key_piece.reshape(piece_rows, head_count, HD)
    value_heads = value_piece.reshape(piece_rows, head_count, HD)
    scores = (
        jnp.einsum("qhd,khd->hqk", queries, key_heads, preferred_element_type=jnp.float32)
        * score_scale
    )
    same_doc = seg_local[:, None] == seg_piece.astype(jnp.int32)[None, :]
    scores = jnp.where(same_doc[None], scores, MASKED)
    soft_probs = jnp.exp(scores - log_sum[:, :, None])
    d_probs = jnp.einsum(
        "qhd,khd->hqk", d_att_heads, value_heads, preferred_element_type=jnp.float32
    )
    d_scores = (soft_probs * (d_probs - delta_rows[:, :, None])).astype(jnp.bfloat16)
    soft_probs, d_scores = (soft_probs, d_scores)
    d_query_part = jnp.einsum(
        "hqk,khd->qhd", d_scores, key_heads, preferred_element_type=jnp.float32
    )
    d_key_part = jnp.einsum(
        "hqk,qhd->khd", d_scores, queries, preferred_element_type=jnp.float32
    ).reshape(piece_rows, model_width)
    d_value_part = jnp.einsum(
        "hqk,qhd->khd",
        soft_probs.astype(jnp.bfloat16),
        d_att_heads,
        preferred_element_type=jnp.float32,
    ).reshape(piece_rows, model_width)
    back_state = (d_query_part, d_key_part, d_value_part)
    d_query, d_keys_all, d_values_all = back_state
    d_keys_mine, d_values_mine = (
        lax.psum_scatter(
            d_keys_all.astype(jnp.bfloat16), "fsdp", scatter_dimension=0, tiled=True
        ).astype(jnp.float32),
        lax.psum_scatter(
            d_values_all.astype(jnp.bfloat16), "fsdp", scatter_dimension=0, tiled=True
        ).astype(jnp.float32),
    )
    d_query_pre = (
        rotate(d_query * score_scale, cosine, -sine_table)
        .reshape(tok_rows, model_width)
        .astype(jnp.bfloat16)
    )
    d_key_pre = (
        rotate((d_keys_mine * score_scale).reshape(tok_rows, head_count, HD), cosine, -sine_table)
        .reshape(tok_rows, model_width)
        .astype(jnp.bfloat16)
    )
    projected_gradient = jnp.stack([d_query_pre, d_key_pre, d_values_mine.astype(jnp.bfloat16)])
    projection_adapter_gradient = (
        jnp.einsum(
            "jah,jho->jao",
            projected_gradient,
            adapter_up_weight[:3],
            preferred_element_type=jnp.float32,
        ).astype(jnp.bfloat16)
        * mask_half[None]
    )
    d_normed_one = jnp.einsum(
        "pte,pde->td", projected_gradient, attention_weight_full, preferred_element_type=jnp.float32
    ) + jnp.einsum(
        "czn,cvn->zv",
        projection_adapter_gradient,
        adapter_down_weight[:3],
        preferred_element_type=jnp.float32,
    )
    attention_up_gradient = jnp.einsum(
        "pts,pte->pes",
        attention_rank_branch,
        projected_gradient,
        preferred_element_type=jnp.float32,
    )
    attention_down_gradient = jnp.einsum(
        "td,pts->pds",
        first_normed_rows,
        projection_adapter_gradient,
        preferred_element_type=jnp.float32,
    )
    d_hidden = d_resid_one + norm_back(hidden_f, gain_one, d_normed_one)
    adapter_down_gradient = jnp.concatenate(
        [attention_down_gradient, output_down_gradient[None]], axis=0
    )
    adapter_up_gradient = jnp.concatenate([attention_up_gradient, output_up_gradient[None]], axis=0)
    part_down, part_up = (
        lax.psum_scatter(
            adapter_down_gradient.astype(jnp.bfloat16), "fsdp", scatter_dimension=1, tiled=True
        ).astype(jnp.float32),
        lax.psum_scatter(
            adapter_up_gradient.astype(jnp.bfloat16), "fsdp", scatter_dimension=1, tiled=True
        ).astype(jnp.float32),
    )
    summed = (
        lax.psum(part_down.astype(jnp.bfloat16), "rep").astype(jnp.float32),
        lax.psum(part_up.astype(jnp.bfloat16), "rep").astype(jnp.float32),
        lax.psum(g_exp_a_in.astype(jnp.bfloat16), "rep").astype(jnp.float32),
        lax.psum(g_exp_b_in.astype(jnp.bfloat16), "rep").astype(jnp.float32),
        lax.psum(g_exp_a_down.astype(jnp.bfloat16), "rep").astype(jnp.float32),
        lax.psum(g_exp_b_down.astype(jnp.bfloat16), "rep").astype(jnp.float32),
    )
    return (
        layer_value.astype(jnp.bfloat16)[None],
        d_hidden.astype(jnp.bfloat16)[None],
        summed[0],
        summed[1],
        summed[2],
        summed[3],
        summed[4],
        summed[5],
    )


EVERY = 8
TILE = 256
CUT = 512
ROWS_TILE = 256
ROWS_CUT = 512
VMEM_BYTES = 64000000


def mm(left, right):
    return jnp.dot(left, right, preferred_element_type=jnp.float32)


def mm_nt(left, right):
    return lax.dot_general(left, right, (((1,), (1,)), ((), ())), preferred_element_type=jnp.float32)


def whole():
    return pl.BlockSpec(memory_space=pltpu.VMEM)


def in_place():
    return pl.BlockSpec(memory_space=pl.ANY)


def scalars():
    return pl.BlockSpec(memory_space=pltpu.SMEM)


def params():
    return pltpu.CompilerParams(vmem_limit_bytes=VMEM_BYTES)


def cost(flops, moved):
    return pl.CostEstimate(flops=flops, bytes_accessed=moved, transcendentals=0)


def shape_of(shape, dtype=jnp.bfloat16):
    return jax.ShapeDtypeStruct(shape, dtype)


def swap(values, bits):
    return lax.ppermute(values, "fsdp", [(i, i ^ bits) for i in range(EVERY)])


def tie(*values):
    return lax.optimization_barrier(values)


def gather_first(values):
    return [values, swap(values, 2), swap(values, 4)]


def gather_second(values, side, over):
    half = values.shape[0] // 2
    far = [swap(side[:half], 4), swap(over[half:], 2)]
    return far, swap(values, 1), swap(jnp.concatenate([side, over], axis=0), 1)


def gather_third(first, far, own, pair):
    far = jnp.concatenate(far, axis=0)
    return [*first, far, own, pair, swap(far, 1)]


GATHERED = 7


def blocks_of(refs):
    values, side, over, far, own, pair, last = refs
    rows = values.shape[0]
    return [values, own, side, pair.at[0:rows], over, pair.at[rows : 2 * rows], far, last]


def gather_relative(values):
    first = gather_first(values)
    return gather_third(first, *gather_second(*first))


def add_half(left, right):
    return (left.astype(jnp.float32) + right.astype(jnp.float32)).astype(jnp.bfloat16)


def scatter_second(even, got):
    rows = even.shape[0] // 4
    half = rows // 2
    far = 3 * rows
    return [
        swap(add_half(even[far : far + half], got[far : far + half]), 2),
        swap(add_half(even[far + half :], got[far + half :]), 4),
    ]


def scatter_third(even, got, far_side, far_over):
    rows = even.shape[0] // 4
    half = rows // 2
    f32 = jnp.float32
    side = even[rows : 2 * rows].astype(f32) + got[rows : 2 * rows].astype(f32)
    over = even[2 * rows : 3 * rows].astype(f32) + got[2 * rows : 3 * rows].astype(f32)
    side = jnp.concatenate([side[:half], side[half:] + far_over.astype(f32)], axis=0)
    over = jnp.concatenate([over[:half] + far_side.astype(f32), over[half:]], axis=0)
    return even, got, swap(side.astype(jnp.bfloat16), 2), swap(over.astype(jnp.bfloat16), 4)


def scatter_relative(even, odd):
    got = swap(odd, 1)
    return scatter_third(even, got, *scatter_second(even, got))


def sum_pieces(*pieces):
    return sum([piece.astype(jnp.float32) for piece in pieces[1:]], pieces[0].astype(jnp.float32))


PIECES = 4


def piece_specs(rows, columns, at=0):
    return [pl.BlockSpec((rows, columns), lambda i: (0, at))] * PIECES


def rep_swap(values, bits):
    return lax.ppermute(values, "rep", [(i, i ^ bits) for i in range(4)])


def turn(values, cosine, signed_sine):
    return values * cosine + pltpu.roll(values, HD // 2, 1) * signed_sine


SPOT = 16


def relayout_kernel(wide, source_ref, out_ref):
    for j in range(EVERY):
        out_ref[j, 0] = source_ref[0, :, j * wide : (j + 1) * wide]


def by_columns(values, wide):
    count, rows, width = values.shape
    half = rows // 2
    return pl.pallas_call(
        functools.partial(relayout_kernel, wide),
        grid=(count, 2),
        in_specs=[pl.BlockSpec((1, half, width), lambda i, j: (i, j, 0))],
        out_specs=pl.BlockSpec((EVERY, 1, half, wide), lambda i, j: (0, i, j, 0)),
        out_shape=shape_of((EVERY, count, rows, wide)),
        cost_estimate=cost(1 << 20, 1 << 16),
        name="by_columns",
    )(values)


def pack_kernel(rows, maps_ref, extra_ref, out_ref):
    for part in range(2):
        for i in range(3):
            at = (3 * part + i) * SR
            out_ref[:, at : at + SR] = maps_ref[i, part * rows : (part + 1) * rows, :]
    out_ref[:, 6 * SR :] = extra_ref[...]


def pack(maps, extra):
    rows, lanes = extra.shape
    return pl.pallas_call(
        functools.partial(pack_kernel, rows),
        in_specs=[whole()] * 2,
        out_specs=whole(),
        out_shape=shape_of((rows, 6 * SR + lanes)),
        compiler_params=params(),
        cost_estimate=cost(1 << 20, 1 << 16),
        name="pack",
    )(maps, extra)


def project_kernel(
    rows, width, wide,
    me_ref, sets_ref, cos_ref, sin_ref, up_ref, *refs,
):
    f32, bf16 = jnp.float32, jnp.bfloat16
    hidden_hbm, given, w_hbm = blocks_of(refs[:GATHERED]), blocks_of(refs[GATHERED : 2 * GATHERED]), refs[2 * GATHERED]
    refs = refs[2 * GATHERED + 1 :]
    q_ref, k_ref, v_ref, normed_ref, low_ref, mask_ref, col_ref, row_ref, gains_ref, router_ref, *refs = refs
    hidden, extra, weight, down, sems, w_sems = refs
    me, step = me_ref[0], pl.program_id(0)
    thin = 3 * SR
    copies = []
    for j in range(EVERY):
        at = pl.multiple_of((me ^ j) * wide, wide)
        here = slice(j * rows, (j + 1) * rows)
        copies.append(
            [
                pltpu.make_async_copy(hidden_hbm[j], hidden.at[here], sems.at[j, 0]),
                pltpu.make_async_copy(given[j].at[:, 2 * thin :], extra.at[here], sems.at[j, 1]),
                pltpu.make_async_copy(
                    given[j].at[:, 0:thin], down.at[pl.ds(at, rows), :], sems.at[j, 2]
                ),
                pltpu.make_async_copy(
                    given[j].at[:, thin : 2 * thin], down.at[pl.ds(at + rows, rows), :], sems.at[j, 3]
                ),
            ]
        )
    w_copies = [
        pltpu.make_async_copy(
            w_hbm.at[j, i], weight.at[j * wide : (j + 1) * wide, i * wide : (i + 1) * wide], w_sems.at[j, i]
        )
        for i in range(3)
        for j in range(EVERY)
    ]

    @pl.when(step == 0)
    def _():
        for which in (1, 2, 3):
            for group in copies:
                group[which].start()
        for item in w_copies:
            item.start()
        for group in copies:
            group[0].start()
        for group in copies:
            group[1].wait()
        for j in range(EVERY):
            at = pl.multiple_of((me ^ j) * wide, wide)
            for part in range(wide // rows):
                spot = pl.multiple_of(at + part * rows, rows)
                router_ref[pl.ds(spot, rows), :] = extra[j * rows : (j + 1) * rows, part * 128 : (part + 1) * 128]
                for i in range(2):
                    line = extra[j * rows : j * rows + 16, 256:384].astype(f32)
                    gains_ref[i : i + 1, pl.ds(spot, rows)] = line[2 * i + part : 2 * i + part + 1, :]
        for group in copies:
            for which in (2, 3):
                group[which].wait()
        for item in w_copies:
            item.wait()

    for i in range(EVERY // 2):

        @pl.when(step == i)
        def _():
            copies[2 * i][0].wait()
            copies[2 * i + 1][0].wait()

    at = pl.ds(pl.multiple_of(step * TILE, TILE), TILE)
    seg = jnp.broadcast_to(extra[at, 0:1].astype(f32), (TILE, 128))
    col_ref[...] = seg
    row_ref[...] = seg.T[0:8, :]
    chosen = jnp.zeros_like(seg)
    for i in range(SETS):
        chosen = jnp.where(seg == float(i), sets_ref[0, i].astype(f32), chosen)
    lane_set = (lax.broadcasted_iota(jnp.int32, (TILE, SR), 1) // R).astype(f32)
    mask = (chosen == lane_set).astype(f32)
    mask_ref[...] = mask
    values = hidden[at, :].astype(f32)
    scale = lax.rsqrt(jnp.mean(values * values, axis=1, keepdims=True) + EPSILON)
    normed = (values * scale * gains_ref[0:1, :]).astype(bf16)
    normed_ref[...] = normed
    wide_all = mm(normed, weight[...])
    low = (mm(normed, down[...]) * jnp.concatenate([mask] * 3, axis=1)).astype(bf16)
    low_ref[...] = low
    cosine, sine = cos_ref[...], sin_ref[...]
    for i, ref in enumerate((q_ref, k_ref, v_ref)):
        proj = wide_all[:, i * wide : (i + 1) * wide] + mm_nt(low[:, i * SR : (i + 1) * SR], up_ref[i])
        for h in range(wide // HD):
            part = proj[:, h * HD : (h + 1) * HD]
            ref[:, h * HD : (h + 1) * HD] = (turn(part, cosine, sine) if i < 2 else part).astype(bf16)


def by_tile(rows, columns):
    return pl.BlockSpec((rows, columns), lambda i: (i, 0))


def project(me, sets, cosine, sine, up, hidden_given, given, w_got):
    rows, width = hidden_given[0].shape
    wide = width // EVERY
    tokens = rows * EVERY
    f32 = jnp.float32
    return pl.pallas_call(
        functools.partial(project_kernel, rows, width, wide),
        grid=(tokens // TILE,),
        in_specs=[scalars(), scalars(), by_tile(TILE, 128), by_tile(TILE, 128), whole()] + [in_place()] * (2 * GATHERED + 1),
        out_specs=[by_tile(TILE, wide)] * 3
        + [by_tile(TILE, width), by_tile(TILE, 3 * SR), by_tile(TILE, SR), by_tile(TILE, 128)]
        + [
            pl.BlockSpec((8, TILE), lambda i: (0, i)),
            pl.BlockSpec((8, width), lambda i: (0, 0)),
            pl.BlockSpec((width, 128), lambda i: (0, 0)),
        ],
        out_shape=[shape_of((tokens, wide))] * 3
        + [shape_of((tokens, width)), shape_of((tokens, 3 * SR)), shape_of((tokens, SR), f32)]
        + [shape_of((tokens, 128), f32), shape_of((8, tokens), f32), shape_of((8, width), f32), shape_of((width, 128))],
        scratch_shapes=[
            pltpu.VMEM((tokens, width), jnp.bfloat16),
            pltpu.VMEM((tokens, 384), jnp.bfloat16),
            pltpu.VMEM((width, 3 * wide), jnp.bfloat16),
            pltpu.VMEM((width, 3 * SR), jnp.bfloat16),
            pltpu.SemaphoreType.DMA((EVERY, 4)),
            pltpu.SemaphoreType.DMA((EVERY, 3)),
        ],
        compiler_params=params(),
        cost_estimate=cost(1 << 20, 1 << 16),
        name="project",
    )(me, sets, cosine, sine, up, *hidden_given, *given, w_got)


def attend_kernel(rows, me_ref, q_ref, k_ref, v_ref, col_ref, row_ref, att_ref, lse_ref, send_ref):
    f32, bf16 = jnp.float32, jnp.bfloat16
    scale = HD ** (-0.5)
    seg_row = row_ref[0:1, :]
    for h in range(q_ref.shape[1] // HD):
        lanes = slice(h * HD, (h + 1) * HD)
        for c in range(q_ref.shape[0] // TILE):
            at = slice(c * TILE, (c + 1) * TILE)
            scores = mm_nt(q_ref[at, lanes], k_ref[:, lanes]) * scale
            scores = jnp.where(col_ref[at, 0:1] == seg_row, scores, MASKED)
            top = jnp.max(scores, axis=1, keepdims=True)
            weights = jnp.exp(scores - top)
            total = jnp.sum(weights, axis=1, keepdims=True)
            att = mm(weights.astype(bf16), v_ref[:, lanes]) / total
            att_ref[at, lanes] = att
            log_sum = jnp.broadcast_to(top + jnp.log(total), (TILE, HD))
            lse_ref[h : h + 1, at] = log_sum.T[0:1, :]
            for part in range(TILE // rows):
                j = c * (TILE // rows) + part
                send_ref[me_ref[0] ^ j, :, lanes] = att[part * rows : (part + 1) * rows].astype(bf16)


def attend(rows, me, queries, keys, values, seg_col, seg_row):
    tokens, wide = queries.shape
    return pl.pallas_call(
        functools.partial(attend_kernel, rows),
        in_specs=[scalars()] + [whole()] * 5,
        out_specs=[whole()] * 3,
        out_shape=[
            shape_of((tokens, wide), jnp.float32),
            shape_of((8, tokens), jnp.float32),
            shape_of((EVERY, rows, wide)),
        ],
        compiler_params=params(),
        cost_estimate=cost(1 << 20, 1 << 16),
        name="attend",
    )(me, queries, keys, values, seg_col, seg_row)


def output_copies(me, wide, given, weight, down, up, sems):
    width = weight.shape[1]
    copies = []
    for j in range(EVERY):
        at = pl.multiple_of((me ^ j) * wide, wide)
        here = slice(j * wide, (j + 1) * wide)
        copies.append(
            [
                pltpu.make_async_copy(given[j].at[:, width : width + SR], down.at[here, :], sems.at[j, 0]),
                pltpu.make_async_copy(given[j].at[:, width + SR :], up.at[pl.ds(at, wide), :], sems.at[j, 1]),
                pltpu.make_async_copy(given[j].at[:, 0:width], weight.at[here, :], sems.at[j, 2]),
            ]
        )
    return copies


def output_scratch(width):
    return [
        pltpu.VMEM((width, width), jnp.bfloat16),
        pltpu.VMEM((width, SR), jnp.bfloat16),
        pltpu.VMEM((width, SR), jnp.bfloat16),
        pltpu.SemaphoreType.DMA((EVERY, 3)),
    ]


def mix_kernel(
    wide,
    me_ref, hidden_ref, gains_ref, mask_ref, router_ref, named_ref, att_ref, *refs,
):
    f32, bf16 = jnp.float32, jnp.bfloat16
    given = blocks_of(refs[:GATHERED])
    resid_ref, normed_ref, low_ref, gates_ref, weight, down, up, sems = refs[GATHERED:]
    me = me_ref[0]
    width = hidden_ref.shape[1]
    copies = output_copies(me, wide, given, weight, down, up, sems)
    for part in range(3):
        for group in copies:
            group[part].start()
    for part in range(2):
        for group in copies:
            group[part].wait()
    blocks = [att_ref[me ^ j] for j in range(EVERY)]
    low = (mm(jnp.concatenate(blocks, axis=1), down[...]) * mask_ref[...]).astype(bf16)
    low_ref[...] = low
    total = mm_nt(low, up[...])
    for j in range(EVERY):
        copies[j][2].wait()
        total = total + mm(blocks[j], weight[j * wide : (j + 1) * wide, :])
    resid = hidden_ref[...].astype(f32) + total
    resid_ref[...] = resid
    scale = lax.rsqrt(jnp.mean(resid * resid, axis=1, keepdims=True) + EPSILON)
    normed = (resid * scale * gains_ref[1:2, :]).astype(bf16)
    normed_ref[:, 0:width] = normed
    logits = jnp.where(named_ref[...] > 0.5, mm(normed, router_ref[...]), MASKED)
    share = jnp.exp(logits - jnp.max(logits, axis=1, keepdims=True)) * named_ref[...]
    gates = share / jnp.sum(share, axis=1, keepdims=True)
    gates_ref[...] = gates
    high = gates.astype(bf16).astype(f32)
    normed_ref[:, width : width + 128] = (high + pltpu.roll(gates - high, 64, 1)).astype(bf16)


def mix(me, hidden, gains, mask, router, named, att_got, given):
    rows, width = hidden.shape
    wide = width // EVERY
    f32 = jnp.float32
    return pl.pallas_call(
        functools.partial(mix_kernel, wide),
        grid=(1,),
        in_specs=[scalars(), whole(), whole(), pl.BlockSpec((rows, SR), lambda i: (0, 0))]
        + [whole()] * 3
        + [in_place()] * GATHERED,
        out_specs=[whole()] * 4,
        out_shape=[shape_of((rows, width), f32), shape_of((rows, width + 128)), shape_of((rows, SR)),
                   shape_of((rows, 128), f32)],
        scratch_shapes=output_scratch(width),
        compiler_params=params(),
        cost_estimate=cost(1 << 20, 1 << 16),
        name="mix",
    )(me, hidden, gains, mask, router, named, att_got, *given)


def expert_kernel(k, first, width, hidden, blocks, where_ref, mask_ref, pick_ref, *refs):
    f32, bf16 = jnp.float32, jnp.bfloat16
    rows_hbm, cot_hbm = blocks_of(refs[:GATHERED]), blocks_of(refs[GATHERED : 2 * GATHERED])
    refs = refs[2 * GATHERED :]
    if not first:
        prev_out, refs = refs[:2], refs[2:]
    (
        w_gate_hbm, w_up_hbm, w_down_hbm, a_in_hbm, b_in_hbm, a_down_hbm, b_down_hbm,
        out_even, out_odd, d_all_ref, extra_ref, *refs,
    ) = refs
    *grad_refs, rows_s, cot_s, w_in, w_down, silu_s, slope_s, g_a_in, g_b_down, g_b_in, g_a_down, packed, sems, block_sems = refs
    out_refs = (out_even, out_odd)
    step = pl.program_id(0)
    part = TILE // 2
    low_at, thin_at = 2 * hidden, width
    chunks = hidden // CUT
    early, late, given = [], [], []

    def copy(source, target, group):
        group.append(pltpu.make_async_copy(source, target, sems.at[len(early) + len(late)]))

    copy(a_in_hbm.at[k, 0], w_in.at[0:width, low_at : low_at + SR], early)
    copy(a_in_hbm.at[k, 1], w_in.at[0:width, low_at + SR : low_at + 2 * SR], early)
    copy(b_in_hbm.at[k, 0], w_in.at[width : width + SR, 0:hidden], early)
    copy(b_in_hbm.at[k, 1], w_in.at[width : width + SR, hidden:low_at], early)
    for j in range(chunks):
        at = slice(j * CUT, (j + 1) * CUT)
        copy(w_gate_hbm.at[k, :, at], w_in.at[0:width, at], early)
        copy(w_up_hbm.at[k, :, at], w_in.at[0:width, hidden + j * CUT : hidden + (j + 1) * CUT], early)
    copy(a_down_hbm.at[k], w_down.at[0:hidden, thin_at : thin_at + SR], late)
    copy(b_down_hbm.at[k], w_down.at[hidden : hidden + SR, 0:width], late)
    copy(w_down_hbm.at[k], w_down.at[0:hidden, 0:width], late)
    for j in range(blocks):
        at = slice(j * part, (j + 1) * part)
        given.append(pltpu.make_async_copy(rows_hbm[j], rows_s.at[at, :], block_sems.at[j, 0]))
        given.append(pltpu.make_async_copy(cot_hbm[j], cot_s.at[at, :], block_sems.at[j, 1]))

    def wait_for(group, then=(), when=0):
        @pl.when(step == when)
        def _():
            for item in group:
                item.wait()
            for item in then:
                item.start()

    @pl.when(step == 0)
    def _():
        for item in given[0:4] + early[:6]:
            item.start()
        g_a_in[...] = jnp.zeros_like(g_a_in)
        g_b_down[...] = jnp.zeros_like(g_b_down)
        g_b_in[...] = jnp.zeros_like(g_b_in)
        g_a_down[...] = jnp.zeros_like(g_a_down)

    for i in range(1, blocks // 2):
        wait_for(given[4 * i : 4 * i + 4], when=i)
    wait_for([given[0], given[2]] + early[:2], early[6:])
    at_rows = pl.ds(pl.multiple_of(step * TILE, TILE), TILE)
    mask = mask_ref[...]
    mask_two = jnp.concatenate([mask, mask], axis=1)
    rows = rows_s[at_rows, 0:width]
    gate = jnp.sum(rows_s[at_rows, width:].astype(f32) * pick_ref[0:1, :], axis=1, keepdims=True)
    low_in = (mm(rows, w_in[0:width, low_at:]) * mask_two).astype(bf16)
    rows_gate = jnp.concatenate([rows, low_in[:, :SR]], axis=1)
    rows_up = jnp.concatenate([rows, low_in[:, SR:]], axis=1)
    wait_for(early[2:4])
    act_parts = []
    for j in range(chunks):
        wait_for(early[4 + 2 * j : 6 + 2 * j], late if j == 0 else given[4:] if j == 1 else ())
        at = slice(j * CUT, (j + 1) * CUT)
        gate_h = mm(rows_gate, w_in[:, at])
        up_h = mm(rows_up, w_in[:, hidden + j * CUT : hidden + (j + 1) * CUT])
        share = 1.0 / (1.0 + jnp.exp(-gate_h))
        silu = gate_h * share
        silu_s[:, at] = silu
        slope_s[:, at] = up_h * (share * (1.0 + gate_h * (1.0 - share)))
        act_parts.append((silu * up_h).astype(bf16))
    act = jnp.concatenate(act_parts, axis=1)
    wait_for([given[1], given[3]] + late)

    low_down = (mm(act, w_down[0:hidden, thin_at:]) * mask).astype(bf16)
    act_low = jnp.concatenate([act, low_down], axis=1)
    d_gate = jnp.zeros((TILE, 1), f32)
    d_out_parts = []
    for j in range(width // CUT):
        at = slice(j * CUT, (j + 1) * CUT)
        out = mm(act_low, w_down[:, at]).astype(bf16).astype(f32)
        cot = cot_s[at_rows, at].astype(f32)
        d_out_parts.append((gate * cot).astype(bf16))
        weighted = gate * out
        for i in range(2):
            value = weighted[i * part : (i + 1) * part]
            if not first:
                value = value + prev_out[i][:, at].astype(f32)
            out_refs[i][:, at] = value.astype(bf16)
        d_gate = d_gate + jnp.sum(cot * out, axis=1, keepdims=True)
    high = d_gate.astype(bf16).astype(f32)
    extra_ref[...] = high * pick_ref[1:2, :] + (d_gate - high) * pick_ref[2:3, :]

    mask_half = mask.astype(bf16)
    d_out = jnp.concatenate(d_out_parts, axis=1)
    d_low_down = mm_nt(d_out, w_down[hidden:, 0:width]).astype(bf16) * mask_half
    d_out_low = jnp.concatenate([d_out, d_low_down], axis=1)
    d_gate_parts, d_up_parts = [], []
    for j in range(chunks):
        at = slice(j * CUT, (j + 1) * CUT)
        d_act = mm_nt(d_out_low, w_down[at, :])
        d_gate_parts.append((d_act * slope_s[:, at]).astype(bf16))
        d_up_parts.append((d_act * silu_s[:, at]).astype(bf16))
    d_gate_h = jnp.concatenate(d_gate_parts, axis=1)
    d_up_h = jnp.concatenate(d_up_parts, axis=1)
    d_low_gate = mm_nt(d_gate_h, w_in[width:, 0:hidden]).astype(bf16) * mask_half
    d_low_up = mm_nt(d_up_h, w_in[width:, hidden:low_at]).astype(bf16) * mask_half
    d_low_in = jnp.concatenate([d_low_gate, d_low_up], axis=1)
    d_all_ref[:, 0:hidden] = d_gate_h
    d_all_ref[:, hidden:low_at] = d_up_h
    d_all_ref[:, low_at:] = d_low_in
    d_low_in_t, low_down_t, low_in_t, d_low_down_t = d_low_in.T, low_down.T, low_in.T, d_low_down.T
    for j in range(width // CUT):
        at = slice(j * CUT, (j + 1) * CUT)
        g_a_in[:, at] += mm(d_low_in_t, rows[:, at])
        g_b_down[:, at] += mm(low_down_t, d_out[:, at])
    for j in range(chunks):
        at = slice(j * CUT, (j + 1) * CUT)
        g_b_in[0, :, at] += mm(low_in_t[:SR], d_gate_h[:, at])
        g_b_in[1, :, at] += mm(low_in_t[SR:], d_up_h[:, at])
        g_a_down[:, at] += mm(d_low_down_t, act[:, at])

    @pl.when(step == pl.num_programs(0) - 1)
    def _():
        packed[0 : 2 * SR, :] = g_a_in[...].astype(bf16)
        packed[2 * SR : 3 * SR, :] = g_b_down[...].astype(bf16)
        packed[3 * SR : 4 * SR, 0:hidden] = g_b_in[0].astype(bf16)
        packed[3 * SR : 4 * SR, hidden:] = g_b_in[1].astype(bf16)
        packed[4 * SR :, 0:hidden] = g_a_down[: SR // 2].astype(bf16)
        packed[4 * SR :, hidden:] = g_a_down[SR // 2 :].astype(bf16)
        size = packed.shape[0] // 4
        for spot, b in enumerate((0, 2, 1, 3)):
            quarter = packed[pl.ds(pl.multiple_of((where_ref[0] ^ b) * size, 16), size), :]
            per = 4 // len(grad_refs)
            grad_refs[spot // per][(spot % per) * size : (spot % per + 1) * size, :] = quarter


def expert_pass(k, where, rows, cot, mask, picks, prev, weights):
    f32, bf16 = jnp.float32, jnp.bfloat16
    blocks = EVERY
    part, width = cot[0].shape
    hidden = weights[0].shape[2]
    tokens = blocks * part
    shares = 2 if prev is None else 4
    grad_shape = ((4 * SR + SR // 2) // shares, width)
    in_specs = [scalars(), by_tile(TILE, SR), pl.BlockSpec((8, 128), lambda i: (0, 0))] + [in_place()] * (2 * GATHERED)
    operands = [where, mask, picks, *rows, *cot]
    if prev is not None:
        in_specs += [by_tile(part, width)] * 2
        operands += list(prev)
    in_specs += [in_place()] * 7
    flops = 2 * tokens * (4 * width * hidden + 7 * SR * (width + hidden))
    return pl.pallas_call(
        functools.partial(expert_kernel, k, prev is None, width, hidden, blocks),
        grid=(tokens // TILE,),
        in_specs=in_specs,
        out_specs=[by_tile(part, width)] * 2
        + [by_tile(TILE, 2 * hidden + 2 * SR), by_tile(TILE, 128)]
        + [pl.BlockSpec(grad_shape, lambda i: (0, 0))] * shares,
        out_shape=[shape_of((tokens // 2, width))] * 2
        + [shape_of((tokens, 2 * hidden + 2 * SR)), shape_of((tokens, 128), f32)]
        + [shape_of(grad_shape)] * shares,
        scratch_shapes=[
            pltpu.VMEM((tokens, width + 128), bf16),
            pltpu.VMEM((tokens, width), bf16),
            pltpu.VMEM((width + SR, 2 * hidden + 2 * SR), bf16),
            pltpu.VMEM((hidden + SR, width + SR), bf16),
            pltpu.VMEM((TILE, hidden), f32),
            pltpu.VMEM((TILE, hidden), f32),
            pltpu.VMEM((2 * SR, width), f32),
            pltpu.VMEM((SR, width), f32),
            pltpu.VMEM((2, SR, hidden), f32),
            pltpu.VMEM((SR, hidden), f32),
            pltpu.VMEM((4 * SR + SR // 2, width), bf16),
            pltpu.SemaphoreType.DMA((7 + 2 * (hidden // CUT),)),
            pltpu.SemaphoreType.DMA((blocks, 2)),
        ],
        compiler_params=params(),
        cost_estimate=cost(flops, 40 << 20),
        name="expert",
    )(*operands, *weights)


def rows_kernel(part, width, hidden, local, *refs):
    bf16 = jnp.bfloat16
    d_all, extra, (w_gate_hbm, w_up_hbm, a_in_hbm) = refs[:local], refs[local : 2 * local], refs[2 * local : 2 * local + 3]
    even_ref, odd_ref, weight, sems = refs[2 * local + 3 :]
    step = pl.program_id(0)
    span = 2 * hidden + 2 * SR
    chunks = width // ROWS_CUT
    copies = []
    for j in range(chunks):
        at = slice(j * ROWS_CUT, (j + 1) * ROWS_CUT)
        group = []
        for k in range(local):
            base = k * span
            targets = [
                (w_gate_hbm.at[k, at], base, hidden),
                (w_up_hbm.at[k, at], base + hidden, hidden),
                (a_in_hbm.at[k, 0, at], base + 2 * hidden, SR),
                (a_in_hbm.at[k, 1, at], base + 2 * hidden + SR, SR),
            ]
            for i, (source, start, size) in enumerate(targets):
                group.append(
                    pltpu.make_async_copy(source, weight.at[at, start : start + size], sems.at[j, 4 * k + i])
                )
        copies.append(group)

    @pl.when(step == 0)
    def _():
        for group in copies:
            for item in group:
                item.start()

    both = jnp.concatenate([ref[...] for ref in d_all], axis=1)
    for j in range(chunks):

        @pl.when(step == 0)
        def _():
            for item in copies[j]:
                item.wait()

        at = slice(j * ROWS_CUT, (j + 1) * ROWS_CUT)
        value = mm_nt(both, weight[at, :]).astype(bf16)
        for b in range(ROWS_TILE // part):
            (even_ref, odd_ref)[b % 2][b // 2 * part : (b // 2 + 1) * part, at] = value[b * part : (b + 1) * part]
    total = sum([ref[...] for ref in extra[1:]], extra[0][...]).astype(bf16)
    for b in range(ROWS_TILE // part):
        (even_ref, odd_ref)[b % 2][b // 2 * part : (b // 2 + 1) * part, width:] = total[b * part : (b + 1) * part]


def rows_pass(part, d_all, extra, w_gate, w_up, a_in):
    local, width, hidden = w_gate.shape
    tokens, span = d_all[0].shape
    return pl.pallas_call(
        functools.partial(rows_kernel, part, width, hidden, local),
        grid=(tokens // ROWS_TILE,),
        in_specs=[by_tile(ROWS_TILE, span)] * local + [by_tile(ROWS_TILE, 128)] * local + [in_place()] * 3,
        out_specs=[by_tile(ROWS_TILE // 2, width + 128)] * 2,
        out_shape=[shape_of((tokens // 2, width + 128))] * 2,
        scratch_shapes=[
            pltpu.VMEM((width, local * span), jnp.bfloat16),
            pltpu.SemaphoreType.DMA((width // ROWS_CUT, 4 * local)),
        ],
        compiler_params=params(),
        cost_estimate=cost(2 * tokens * width * span * local, 40 << 20),
        name="rows",
    )(*d_all, *extra, w_gate, w_up, a_in)


def norm_grad(values, gain_row, upstream_grad):
    scale = lax.rsqrt(jnp.mean(values * values, axis=1, keepdims=True) + EPSILON)
    inner = gain_row * upstream_grad
    mean = jnp.mean(values * inner, axis=1, keepdims=True)
    return scale * inner - values * (scale * scale * scale * mean)


def unmix_kernel(
    wide,
    me_ref, resid_ref, cot_ref, gains_ref, mask_ref, router_ref, gates_ref, low_ref, att_ref, *refs,
):
    f32, bf16 = jnp.float32, jnp.bfloat16
    pieces, given, refs = refs[:PIECES], blocks_of(refs[PIECES : PIECES + GATHERED]), refs[PIECES + GATHERED :]
    resid_grad_ref, grad_ref, send_ref, weight, down, up, up_grad, sems = refs
    me = me_ref[0]
    width = resid_ref.shape[1]
    copies = output_copies(me, wide, given, weight, down, up, sems)
    for which in (1, 0, 2):
        for group in copies:
            group[which].start()
    resid = resid_ref[...]
    total = sum_pieces(*[ref[...] for ref in pieces])
    extra = total[:, width:]
    gates = gates_ref[...]
    d_gates = extra + pltpu.roll(extra, 64, 1)
    d_chosen = gates * (d_gates - jnp.sum(gates * d_gates, axis=1, keepdims=True))
    d_normed = total[:, :width] + mm_nt(d_chosen.astype(bf16), router_ref[...])
    d_resid = cot_ref[...].astype(f32) + norm_grad(resid, gains_ref[1:2, :], d_normed)
    resid_grad_ref[...] = d_resid
    branch = d_resid.astype(bf16)
    for group in copies:
        group[1].wait()
    d_low = (mm(branch, up[...]).astype(bf16).astype(f32) * mask_ref[...]).astype(bf16)
    low_t, d_low_t = low_ref[...].T, d_low.T
    up_grad[...] = mm(low_t, branch).astype(bf16)
    for group in copies:
        group[0].wait()
    for j in range(EVERY):
        here = slice(j * wide, (j + 1) * wide)
        copies[j][2].wait()
        send_ref[me ^ j] = (mm_nt(branch, weight[here, :]) + mm_nt(d_low, down[here, :])).astype(bf16)
        at = pl.multiple_of((me ^ j) * wide, wide)
        grad_ref[me ^ j, 0:SR, :] = mm(d_low_t, att_ref[me ^ j]).astype(bf16)
        grad_ref[me ^ j, SR:, :] = up_grad[:, pl.ds(at, wide)]


def unmix(me, resid, cot, gains, mask, router, gates, low, att_got, pieces, given):
    rows, width = resid.shape
    wide = width // EVERY
    return pl.pallas_call(
        functools.partial(unmix_kernel, wide),
        grid=(1,),
        in_specs=[scalars()]
        + [whole()] * 3
        + [pl.BlockSpec((rows, SR), lambda i: (0, 0))]
        + [whole()] * 4
        + piece_specs(rows, width + 128)
        + [in_place()] * GATHERED,
        out_specs=[whole()] * 3,
        out_shape=[
            shape_of((rows, width), jnp.float32),
            shape_of((EVERY, 2 * SR, wide)),
            shape_of((EVERY, rows, wide)),
        ],
        scratch_shapes=output_scratch(width)[:3]
        + [pltpu.VMEM((SR, width), jnp.bfloat16)]
        + output_scratch(width)[3:],
        compiler_params=params(),
        cost_estimate=cost(1 << 20, 1 << 16),
        name="unmix",
    )(me, resid, cot, gains, mask, router, gates, low, att_got, *pieces, *given)


def attend_back_kernel(
    rows, wide,
    me_ref, q_ref, k_ref, v_ref, att_ref, lse_ref, col_ref, row_ref, cos_ref, sin_ref, low_ref, mask_ref, up_ref,
    got_ref, normed_hbm, d_proj_ref, d_low_ref, down_grad_ref, up_grad_ref, d_att, normed, sems,
):
    f32, bf16 = jnp.float32, jnp.bfloat16
    tokens = q_ref.shape[0]
    scale = HD ** (-0.5)
    me = me_ref[0]
    bring = pltpu.make_async_copy(normed_hbm, normed, sems.at[0])
    bring.start()
    for j in range(EVERY):
        d_att[j * rows : (j + 1) * rows, :] = got_ref[me ^ j]
    seg_row = row_ref[0:1, :]
    for h in range(wide // HD):
        lanes = slice(h * HD, (h + 1) * HD)
        delta = jnp.sum(d_att[:, lanes].astype(f32) * att_ref[:, lanes], axis=1, keepdims=True)
        delta = jnp.broadcast_to(delta, (tokens, HD)).T[0:1, :]
        log_sum = lse_ref[h : h + 1, :]
        d_query = jnp.zeros((tokens, HD), f32)
        for c in range(tokens // TILE):
            at = slice(c * TILE, (c + 1) * TILE)
            scores = mm_nt(k_ref[at, lanes], q_ref[:, lanes]) * scale - log_sum
            probs = jnp.exp(jnp.where(col_ref[at, 0:1] == seg_row, scores, MASKED))
            d_probs = mm_nt(v_ref[at, lanes], d_att[:, lanes])
            d_scores = (probs * (d_probs - delta)).astype(bf16)
            d_value = mm(probs.astype(bf16), d_att[:, lanes])
            d_key = mm(d_scores, q_ref[:, lanes])
            d_query = d_query + mm(d_scores.T, k_ref[at, lanes])
            d_proj_ref[at, wide + h * HD : wide + (h + 1) * HD] = turn(
                d_key * scale, cos_ref[at, :], -sin_ref[at, :]
            ).astype(bf16)
            d_proj_ref[at, 2 * wide + h * HD : 2 * wide + (h + 1) * HD] = d_value.astype(bf16)
        d_proj_ref[:, lanes] = turn(d_query * scale, cos_ref[...], -sin_ref[...]).astype(bf16)
    for i in range(3):
        part = d_proj_ref[:, i * wide : (i + 1) * wide]
        d_low = (mm(part, up_ref[i]).astype(bf16).astype(f32) * mask_ref[...]).astype(bf16)
        d_low_ref[:, i * SR : (i + 1) * SR] = d_low
        up_grad_ref[i * SR : (i + 1) * SR, :] = mm(low_ref[:, i * SR : (i + 1) * SR].T, part).astype(bf16)
    d_low_t = d_low_ref[...].T
    bring.wait()
    for j in range(EVERY):
        down_grad_ref[j] = mm(d_low_t, normed[:, j * wide : (j + 1) * wide]).astype(bf16)


def attend_back(rows, me, q, k, v, att, lse, seg_col, seg_row, cosine, sine, low, mask, up, got, normed):
    tokens, wide = q.shape
    width = wide * EVERY
    return pl.pallas_call(
        functools.partial(attend_back_kernel, rows, wide),
        in_specs=[scalars()] + [whole()] * 13 + [in_place()],
        out_specs=[whole()] * 4,
        out_shape=[
            shape_of((tokens, 3 * wide)),
            shape_of((tokens, 3 * SR)),
            shape_of((EVERY, 3 * SR, wide)),
            shape_of((3 * SR, wide)),
        ],
        scratch_shapes=[
            pltpu.VMEM((tokens, wide), jnp.bfloat16),
            pltpu.VMEM((tokens, width), jnp.bfloat16),
            pltpu.SemaphoreType.DMA((1,)),
        ],
        compiler_params=params(),
        cost_estimate=cost(1 << 20, 1 << 16),
        name="attend_back",
    )(me, q, k, v, att, lse, seg_col, seg_row, cosine, sine, low, mask, up, got, normed)


def unproject_kernel(rows, width, wide, me_ref, proj_ref, low_ref, *refs):
    bf16 = jnp.bfloat16
    given, w_hbm = blocks_of(refs[:GATHERED]), refs[GATHERED]
    even_ref, odd_ref, weight, sems, w_sems = refs[GATHERED + 1 :]
    me, thin = me_ref[0], 3 * SR

    @pl.when(pl.program_id(0) == 0)
    def _():
        copies = []
        for j in range(EVERY):
            at = pl.multiple_of((me ^ j) * wide, wide)
            for i in range(3):
                copies.append(
                    pltpu.make_async_copy(
                        w_hbm.at[j, i],
                        weight.at[j * wide : (j + 1) * wide, i * wide : (i + 1) * wide],
                        w_sems.at[j, i],
                    )
                )
            for part in range(2):
                start = part * thin
                copies.append(
                    pltpu.make_async_copy(
                        given[j].at[:, start : start + thin],
                        weight.at[pl.ds(at + part * rows, rows), 3 * wide : 3 * wide + thin],
                        sems.at[j, part],
                    )
                )
        for item in copies:
            item.start()
        for item in copies:
            item.wait()

    both = jnp.concatenate([proj_ref[...], low_ref[...]], axis=1)
    for j in range(width // CUT):
        lanes = slice(j * CUT, (j + 1) * CUT)
        value = mm_nt(both, weight[lanes, :]).astype(bf16)
        even_ref[:, lanes] = value[:rows]
        odd_ref[:, lanes] = value[rows:]


def unproject(rows, me, d_proj, d_low, given, w_got):
    tokens = d_proj.shape[0]
    wide = d_proj.shape[1] // 3
    width = wide * EVERY
    return pl.pallas_call(
        functools.partial(unproject_kernel, rows, width, wide),
        grid=(tokens // TILE,),
        in_specs=[scalars(), by_tile(TILE, 3 * wide), by_tile(TILE, 3 * SR)] + [in_place()] * (GATHERED + 1),
        out_specs=[by_tile(rows, width)] * 2,
        out_shape=[shape_of((tokens // 2, width))] * 2,
        scratch_shapes=[
            pltpu.VMEM((width, 3 * wide + 3 * SR), jnp.bfloat16),
            pltpu.SemaphoreType.DMA((EVERY, 2)),
            pltpu.SemaphoreType.DMA((EVERY, 3)),
        ],
        compiler_params=params(),
        cost_estimate=cost(1 << 20, 1 << 16),
        name="unproject",
    )(me, d_proj, d_low, *given, w_got)


def finish_kernel(hidden_ref, gains_ref, resid_grad_ref, *refs):
    pieces, out_ref = refs[:PIECES], refs[PIECES]
    d_normed = sum_pieces(*[ref[...] for ref in pieces])
    back = norm_grad(hidden_ref[...].astype(jnp.float32), gains_ref[0:1, :], d_normed)
    out_ref[...] = (resid_grad_ref[...] + back).astype(jnp.bfloat16)


def finish(hidden, gains, resid_grad, pieces):
    rows, width = hidden.shape
    return pl.pallas_call(
        finish_kernel,
        grid=(1,),
        in_specs=[whole()] * 3 + piece_specs(rows, width),
        out_specs=whole(),
        out_shape=shape_of((rows, width)),
        compiler_params=params(),
        cost_estimate=cost(1 << 20, 1 << 16),
        name="finish",
    )(hidden, gains, resid_grad, *pieces)


def layer_kernel(resid_ref, *refs):
    pieces, out_ref = refs[:PIECES], refs[PIECES]
    out_ref[...] = (resid_ref[...] + sum_pieces(*[ref[...] for ref in pieces])).astype(jnp.bfloat16)


def layer(resid, pieces):
    rows, width = resid.shape
    return pl.pallas_call(
        layer_kernel,
        grid=(1,),
        in_specs=[whole()] + piece_specs(rows, width),
        out_specs=whole(),
        out_shape=shape_of((rows, width)),
        compiler_params=params(),
        cost_estimate=cost(1 << 20, 1 << 16),
        name="layer",
    )(resid, *pieces)


def unpack_kernel(hidden, first, where_ref, *refs):
    f32 = jnp.float32
    parts, refs = refs[:8], refs[8:]
    refs = refs if first else refs[4:]
    a_in_ref, b_in_ref, a_down_ref, b_down_ref, packed = refs
    size = packed.shape[0] // 4
    for b in range(4):
        for i in range(2):
            spot = pl.multiple_of((where_ref[0] ^ b) * size + i * (size // 2), 8)
            packed[pl.ds(spot, size // 2), :] = parts[2 * b + i][...].astype(f32)
    for i in range(2):
        a_in_ref[0, i] = packed[i * SR : (i + 1) * SR, :].T
        b_in_ref[0, i] = packed[3 * SR : 4 * SR, i * hidden : (i + 1) * hidden]
    b_down_ref[0] = packed[2 * SR : 3 * SR, :]
    a_down_ref[0, :, 0 : SR // 2] = packed[4 * SR :, 0:hidden].T
    a_down_ref[0, :, SR // 2 :] = packed[4 * SR :, hidden:].T


def unpack(k, where, quarters, hidden, experts, before):
    quarters = [part for quarter in quarters for part in quarter]
    width = quarters[0].shape[1]
    f32 = jnp.float32
    first = before is None
    shapes = [(experts, 2, width, SR), (experts, 2, SR, hidden), (experts, hidden, SR), (experts, SR, width)]
    given = [] if first else list(before)
    return pl.pallas_call(
        functools.partial(unpack_kernel, hidden, first),
        grid=(1,),
        in_specs=[scalars()] + [whole()] * 8 + [in_place()] * len(given),
        out_specs=[
            pl.BlockSpec((1,) + shape[1:], lambda i, n=len(shape): (k,) + (0,) * (n - 1)) for shape in shapes
        ],
        out_shape=[shape_of(shape, f32) for shape in shapes],
        input_output_aliases={} if first else {9 + i: i for i in range(4)},
        scratch_shapes=[pltpu.VMEM((4 * SR + SR // 2, width), f32)],
        compiler_params=params(),
        cost_estimate=cost(1 << 20, 1 << 16),
        name="unpack",
    )(where, *quarters, *given)


def thin_kernel(late_left, late_right, early_left, early_right, a_ref, b_ref):
    f32 = jnp.float32
    late = late_left[...].astype(f32) + late_right[...].astype(f32)
    early = early_left[...].astype(f32) + early_right[...].astype(f32)
    for i in range(4):
        at = (2 + i) * SR if i < 3 else 0
        a_ref[i] = late[at : at + SR, :].T
        b_ref[i] = (early[i * SR : (i + 1) * SR, :] if i < 3 else late[SR : 2 * SR, :]).T


def thin_grads(late, early):
    wide = late[0].shape[1]
    return pl.pallas_call(
        thin_kernel,
        in_specs=[whole()] * 4,
        out_specs=[whole()] * 2,
        out_shape=[shape_of((4, wide, SR), jnp.float32)] * 2,
        compiler_params=params(),
        cost_estimate=cost(1 << 20, 1 << 16),
        name="thin_grads",
    )(*late, *early)


def split_layer(
    hidden_in,
    segments,
    routes,
    doc_sets,
    cotangent,
    w_qkv,
    w_out,
    gain_attn,
    gain_moe,
    router,
    w_gate,
    w_up,
    w_down,
    a_attn,
    b_attn,
    exp_a_in,
    exp_b_in,
    exp_a_down,
    exp_b_down,
):
    bf16, f32 = jnp.bfloat16, jnp.float32
    index = lax.axis_index("fsdp")
    me = index.astype(jnp.int32).reshape(1)
    where = lax.axis_index("rep").astype(jnp.int32).reshape(1)
    hidden, upstream = hidden_in[0], cotangent[0]
    rows, width = hidden.shape
    wide = width // EVERY
    local, _, inner = w_gate.shape
    experts_all = local * EVERY

    order = index ^ jnp.arange(EVERY)
    positions = (order[:, None] * rows + jnp.arange(rows)[None, :]).reshape(-1)
    cosine, sine = rope_tables(positions, HD)
    cosine, sine = jnp.concatenate([cosine, cosine], axis=1), jnp.concatenate([-sine, sine], axis=1)
    lanes = jnp.arange(128)
    named = jnp.any(routes[0][:, :, None] + SPOT == lanes[None, None, :], axis=1).astype(f32)
    out_own = jnp.concatenate([w_out, a_attn[3], b_attn[3]], axis=1)

    def picks(k):
        high = (lanes == SPOT + 2 * index + k).astype(f32)
        low = (lanes == SPOT + 2 * index + k + 64).astype(f32)
        return jnp.stack([high + low, high, low] + [jnp.zeros_like(high)] * 5)

    hidden_first = gather_first(hidden)
    at_spot = ((0, 0), (SPOT, 128 - SPOT - experts_all))
    meta = jnp.pad(router[:rows], at_spot) + jnp.pad(segments[0].astype(bf16)[:, None], ((0, 0), (0, 127)))
    lines = jnp.concatenate([gain_attn.reshape(2, 128), gain_moe.reshape(2, 128)], axis=0)
    lines = jnp.pad(lines, ((0, rows - 4), (0, 0)))
    given = pack(a_attn, jnp.concatenate([meta, jnp.pad(router[rows:], at_spot), lines], axis=1))
    given_first = gather_first(given)
    w_got = lax.all_to_all(by_columns(w_qkv, wide), "fsdp", split_axis=0, concat_axis=0, tiled=True)
    hidden_first, cosine, sine, out_own, named, pick_rows = tie(
        hidden_first, cosine, sine, out_own, named, [picks(0), picks(1)]
    )
    hidden_given = gather_third(hidden_first, *gather_second(*hidden_first))
    given = gather_third(given_first, *gather_second(*given_first))

    hidden_given, given, w_got, out_own = tie(hidden_given, given, w_got, out_own)
    out_first = gather_first(out_own)
    queries, keys, values, normed_one, low_qkv, mask, seg_col, seg_row, gains, router_all = project(
        me, doc_sets, cosine, sine, b_attn, hidden_given, given, w_got
    )
    att, lse, att_send = attend(rows, me, queries, keys, values, seg_col, seg_row)
    att_send, out_first = tie(att_send, out_first)
    att_got = lax.all_to_all(att_send, "fsdp", split_axis=0, concat_axis=0, tiled=True)
    far, *others = gather_second(*out_first)
    cot_first = gather_first(tie(upstream, others)[0])
    far, others, att_got, cot_first = tie(far, others, att_got, cot_first)
    out_given = gather_third(out_first, far, *others)
    cot_second = gather_second(*cot_first)
    resid_one, normed_own, low_out, gates_own = mix(
        me, hidden, gains, mask, router_all, named, att_got, out_given
    )
    normed_own, cot_second = tie(normed_own, cot_second)
    normed_given = gather_relative(normed_own)
    cot_given = gather_third(cot_first, *cot_second)

    weights = (w_gate, w_up, w_down, exp_a_in, exp_b_in, exp_a_down, exp_b_down)
    *state, d_all_a, extra_a, kept_a, sent_a = expert_pass(
        0, where, normed_given, cot_given, mask, pick_rows[0], None, weights
    )
    def in_two(values):
        return [values[: values.shape[0] // 2], values[values.shape[0] // 2 :]]

    def later(values, anchor):
        return tie(values, anchor)[0]

    def in_two(values):
        return [values[: values.shape[0] // 2], values[values.shape[0] // 2 :]]

    sent_a = rep_swap(sent_a, 1)
    *state, d_all_b, extra_b, kept_0, kept_1, sent_0, sent_1 = expert_pass(
        1, where, normed_given, cot_given, mask, pick_rows[1], state, weights
    )
    kept_b, sent_b = [kept_0, kept_1], [sent_0, sent_1]
    d_all_b, kept_b, sent_b, sent_a, state = tie(d_all_b, kept_b, sent_b, sent_a, state)
    out_even, out_odd = state
    half_a = add_half(kept_a, sent_a)
    size = half_a.shape[0] // 2
    sent_b[0] = rep_swap(sent_b[0], 1)
    other_a = rep_swap(half_a[size:], 2)
    out_got = swap(out_odd, 1)
    row_even, row_odd = rows_pass(rows, [d_all_a, d_all_b], [extra_a, extra_b], w_gate, w_up, exp_a_in)
    row_odd, other_a, sent_b[0], out_got = tie(row_odd, other_a, sent_b[0], out_got)
    got = swap(row_odd, 1)
    sent_b[1] = rep_swap(later(sent_b[1], row_odd), 1)
    total_a = in_two(add_half(half_a[:size], other_a))
    d_far = scatter_second(row_even, got)
    d_far, sent_b[1] = tie(d_far, sent_b[1])
    pieces = scatter_third(row_even, got, *d_far)
    two_a = [rep_swap(later(total_a[0], d_far), 2)]
    pieces, two_a[0] = tie(pieces, two_a[0])
    early_a = later(total_a, pieces)
    two_a.append(rep_swap(early_a[1], 2))
    one_a = [None, rep_swap(early_a[1], 1)]
    d_resid, thin_send, d_att_send = unmix(
        me, resid_one, upstream, gains, mask, router_all, gates_own, low_out, att_got, pieces, out_given
    )
    d_att_send, two_a[1], one_a[1] = tie(d_att_send, two_a[1], one_a[1])
    d_att_got = lax.all_to_all(d_att_send, "fsdp", split_axis=0, concat_axis=0, tiled=True)
    mine_b = add_half(kept_b[0], sent_b[0])
    half_b = later(in_two(add_half(kept_b[1], sent_b[1])), d_att_send)
    one_a[0] = rep_swap(later(total_a[0], d_att_send), 1)
    other_b = [rep_swap(half_b[0], 2)]
    out_far = scatter_second(*later((out_even, out_got), d_att_send))
    d_att_got, other_b[0], one_a[0], out_far = tie(d_att_got, other_b[0], one_a[0], out_far)
    total_b = [add_half(mine_b[: size // 2], other_b[0])]
    other_b.append(rep_swap(later(half_b[1], d_att_got), 2))
    three_a = [rep_swap(later(two_a[0], d_att_got), 1)]

    def exchange(values):
        return lax.all_to_all(values, "fsdp", split_axis=0, concat_axis=0, tiled=True)

    out_grads = exchange(later(thin_send, d_att_got))
    d_proj, d_low, down_send, up_grads = attend_back(
        rows, me, queries, keys, values, att, lse, seg_col, seg_row, cosine, sine, low_qkv, mask, b_attn,
        d_att_got, normed_one,
    )
    d_proj, down_send, other_b[1], three_a[0], out_grads = tie(d_proj, down_send, other_b[1], three_a[0], out_grads)
    down_grads = exchange(down_send)
    two_b = [rep_swap(later(total_b[0], d_proj), 2)]
    three_a.append(rep_swap(later(two_a[1], d_proj), 1))
    even, odd = unproject(rows, me, d_proj, d_low, given, w_got)
    odd, down_grads, two_b[0], three_a[1] = tie(odd, down_grads, two_b[0], three_a[1])
    got = swap(odd, 1)
    thin = [jnp.sum(part.astype(f32), axis=0).astype(bf16) for part in (out_grads, down_grads)]
    thin = jnp.concatenate(thin, axis=0)
    thin_near = rep_swap(thin, 1)
    total_b.append(later(add_half(mine_b[size // 2 :], other_b[1]), odd))
    two_b.append(rep_swap(total_b[1], 2))
    up_near = rep_swap(later(up_grads, odd), 1)
    d_far = scatter_second(even, got)
    d_far, thin_near, two_b[1], up_near = tie(d_far, thin_near, two_b[1], up_near)
    pieces = scatter_third(even, got, *d_far)
    thin, up_grads = add_half(thin, thin_near), add_half(up_grads, up_near)
    thin_last, up_far = rep_swap(thin, 2), rep_swap(up_grads, 2)
    one_b = [rep_swap(later(total_b[0], d_far), 1)]
    grads = unpack(0, where, later([total_a, one_a, two_a, three_a], d_far), inner, local, None)
    pieces, grads = tie(pieces, grads)
    one_b.append(rep_swap(later(total_b[1], pieces), 1))
    three_b = [rep_swap(part, 1) for part in later(two_b, pieces)]
    grad_in = finish(hidden, gains, d_resid, pieces)
    grad_in, thin_last, up_far, one_b[0] = tie(grad_in, thin_last, up_far, one_b[0])
    grad_a, grad_b = thin_grads([thin, thin_last], [up_grads, up_far])
    out_pieces = scatter_third(*later((out_even, out_got), pieces), *out_far)
    layer_out = layer(resid_one, out_pieces)
    one_b, three_b, layer_out, grad_in, grad_a, grad_b = tie(one_b, three_b, layer_out, grad_in, grad_a, grad_b)
    grads = unpack(1, where, [total_b, one_b, two_b, three_b], inner, local, grads)
    return (layer_out[None], grad_in[None], grad_a, grad_b, *grads)


def solution(mesh):
    shape = dict(mesh.shape)
    shards = split_layer if shape == {"rep": 4, "fsdp": EVERY} else gathered_layer
    return jax.shard_map(
        shards,
        mesh=mesh,
        in_specs=(
            P("rep", "fsdp", None),
            P("rep", "fsdp"),
            P("rep", "fsdp", None),
            P("rep", None),
            P("rep", "fsdp", None),
            P(None, "fsdp", None),
            P("fsdp", None),
            P("fsdp"),
            P("fsdp"),
            P("fsdp", None),
            P("fsdp", None, None),
            P("fsdp", None, None),
            P("fsdp", None, None),
            P(None, "fsdp", None),
            P(None, "fsdp", None),
            P("fsdp", None, None, None),
            P("fsdp", None, None, None),
            P("fsdp", None, None),
            P("fsdp", None, None),
        ),
        out_specs=(
            P("rep", "fsdp", None),
            P("rep", "fsdp", None),
            P(None, "fsdp", None),
            P(None, "fsdp", None),
            P("fsdp", None, None, None),
            P("fsdp", None, None, None),
            P("fsdp", None, None),
            P("fsdp", None, None),
        ),
        check_vma=False,
    )
```
